32 devices in a mesh: dp: 8 (over y, x, core), tensor: 4 (over z).
Axes of the slice: x: 2, y: 2, z: 4, core: 2. Of those that a mesh axis runs over, the one named last changes fastest.
Arguments:
- hidden_in: bfloat16 [8, 256, 2048], P(None, 'dp'), may hold values from -6 to 6
- cotangent: bfloat16 [8, 256, 2048], P('dp'), may hold values from -6 to 6
- lengths: int32 [8], replicated, may hold values from 1 to 256, 1536 in all
- dealing: int32 [8], replicated, may hold values from 0 to 7, each once
- attn_routes: int32 [8, 256, 2], replicated, may hold values from 0 to 3, all different within a row; in each aligned block of 256 rows (0 to 255, 256 to 511, ..., all dimensions but the last counted through in order) at most 192 rows name the same one
- ffn_routes: int32 [8, 256, 2], replicated, may hold values from 0 to 3, all different within a row; in each aligned block of 256 rows (0 to 255, 256 to 511, ..., all dimensions but the last counted through in order) at most 192 rows name the same one
- attn_gain: float32 [2048], replicated, may hold values from 0.5 to 1.5
- attn_router: bfloat16 [2048, 4], replicated, may hold values from -0.0625 to 0.0625
- kv_weight: bfloat16 [2, 2048, 2048], P(None, 'dp', 'tensor'), may hold values from -0.125 to 0.125
- query_weight: bfloat16 [4, 2048, 2048], P(None, 'dp', 'tensor'), may hold values from -0.125 to 0.125
- proj_weight: bfloat16 [4, 2048, 2048], P(None, 'tensor', 'dp'), may hold values from -1 to 1
- ffn_gain: float32 [2048], replicated, may hold values from 0.5 to 1.5
- ffn_router: bfloat16 [2048, 4], replicated, may hold values from -0.0625 to 0.0625
- expert_in: bfloat16 [4, 2048, 2, 5632], P(None, 'dp', None, 'tensor'), may hold values from -0.125 to 0.125
- expert_out: bfloat16 [4, 5632, 2048], P(None, 'tensor', 'dp'), may hold values from -0.109375 to 0.109375
Outputs:
- layer_out: bfloat16 [8, 256, 2048], P(None, 'dp')
- input_grad: bfloat16 [8, 256, 2048], P(None, 'dp')
- attngain_grad: float32 [2048], replicated
- attnrouter_grad: float32 [2048, 4], replicated
- kv_grad: float32 [2, 2048, 2048], P(None, 'dp', 'tensor')
- query_grad: float32 [4, 2048, 2048], P(None, 'dp', 'tensor')
- proj_grad: float32 [4, 2048, 2048], P(None, 'tensor', 'dp')
- ffngain_grad: float32 [2048], replicated
- ffnrouter_grad: float32 [2048, 4], replicated
- expertin_grad: float32 [4, 2048, 2, 5632], P(None, 'dp', None, 'tensor')
- expertout_grad: float32 [4, 5632, 2048], P(None, 'tensor', 'dp')
The draws below stay inside these ranges and needn't reach their ends.
Inputs may be any that keep to these rules, and one draw needn't show every extreme that they name: `attn_routes`: within each sequence's 256 rows no expert is named by more than 192 rows, a bound that some block reaches; a row names 2 different experts. `ffn_routes`: within each sequence's 256 rows no expert is named by more than 192 rows, a bound that some block reaches; a row names 2 different experts. `lengths`: the longest sequence has 256 positions. `dealing`: each sequence appears once.
All inputs are finite; a program needn't handle non-finite values.
Results may differ from the reference program's by a relative error of at most 0.02.
Values may be sent and summed in bfloat16 or wider, within the bound.
No kernel may reach another device: no remote copies, remote signals or barrier semaphores. Data moves between devices by JAX's collectives and lax.ppermute only.
A program may use at most 384 MiB of HBM per device.

```python
import math
import jax
import jax.numpy as jnp
import numpy as np
from jax import lax

D = 2048
HEADS = 16
HD = 128
FF = 5632
TOP = 2
EA = 4
EF = 4
LMAX = 256
CAP = 192
NSEQ = 8


def level_of(own_key, extent, cuts, least, largest):
    def one(position, parts):
        draws = jax.random.uniform(jax.random.fold_in(jax.random.fold_in(own_key, 6), position), (parts,), jnp.float32, least / len(cuts), largest / len(cuts))
        return jnp.repeat(jnp.exp(draws), extent[position] // parts).reshape((-1,) + (1,) * (len(extent) - position - 1))

    factor_of = one(*cuts[0])
    for cut in cuts[1:]:
        factor_of = factor_of * one(*cut)
    return factor_of


def length_profile(amount, total, limit, lean):
    portions = [(1 << 20) // math.isqrt(rank ** lean) + 1 for rank in range(2, amount + 1)]
    spare, given = total - limit - (amount - 1), [1] * (amount - 1)
    while spare > 0:
        free = [i for i in range(amount - 1) if given[i] < limit]
        mass, remaining = sum([portions[i] for i in free]), spare
        for i in free:
            addition = min(limit - given[i], max(1, remaining * portions[i] // mass), spare)
            given[i] = given[i] + addition
            spare = spare - addition
    return np.array([limit] + given)


def uneven_parts(rng, amount, total, limit, slope):
    if amount == 2:
        one = jax.random.randint(rng, (), max(1, total - limit), min(limit, total - 1) + 1)
        return jnp.stack([one, total - one])
    sizes = jnp.asarray(length_profile(amount, total, limit, slope), jnp.int32)
    pairs = (amount - 1) // 2
    donor, taker = sizes[1:1 + 2 * pairs:2], sizes[2:2 + 2 * pairs:2]
    slack = jnp.minimum(donor - 1, limit - taker)
    shifted = jax.random.randint(jax.random.fold_in(rng, 1), (pairs,), 0, 1 << 20) % (slack + 1)
    sizes = sizes.at[1:1 + 2 * pairs:2].set(donor - shifted).at[2:2 + 2 * pairs:2].set(taker + shifted)
    return sizes[jax.random.permutation(jax.random.fold_in(rng, 2), amount)]


def routed_block(rng, own, number, rows, number_of, top, bound, lean):
    order = jax.random.permutation(rng, number_of)
    heavy_load, ordinary = load_shares(number_of, rows * top, bound, lean, True), load_shares(number_of, rows * top, bound, lean, False)
    places = jnp.arange(number_of)

    def named(tallies, rotation):
        used = int((tallies > 0).sum())
        fixed = max(1, used // 4)
        moved = fixed + (places - fixed + rotation * (used - fixed)) % max(1, number_of - fixed)
        return jnp.zeros((number_of,), jnp.int32).at[order[jnp.where(places < fixed, places, moved)]].set(jnp.asarray(tallies, jnp.int32))

    tallies = jnp.where(number % 4 == 0, named(heavy_load, number // 4), named(ordinary, number - number // 4 - 1))
    mixed = jax.random.permutation(jax.random.fold_in(own, 3), number_of)
    donor, receiver = mixed[0:number_of // 2 * 2:2], mixed[1:number_of // 2 * 2:2]
    slack = jnp.minimum(tallies[donor] - 1, bound - tallies[receiver]) // 2
    slack = jnp.where((donor == order[0]) | (receiver == order[0]) | (tallies[receiver] == 0), 0, jnp.maximum(slack, 0))
    moved = jax.random.randint(jax.random.fold_in(own, 4), (number_of // 2,), 0, 1 << 20) % (slack + 1)
    tallies = tallies.at[donor].add(-moved).at[receiver].add(moved)
    members = jnp.searchsorted(jnp.cumsum(tallies), jnp.arange(rows * top), side="right").astype(jnp.int32)
    table = members.reshape(top, rows).T
    table = table[jax.random.permutation(jax.random.fold_in(own, 1), rows)]
    rotation = jax.random.randint(jax.random.fold_in(own, 2), (rows, 1), 0, top)
    return jnp.take_along_axis(table, (jnp.arange(top)[None, :] + rotation) % top, axis=1)


def load_shares(count, total, most, slope, full):
    portions = [(1 << 20) // math.isqrt(grade ** slope) + 1 for grade in range(1, count + 1)]
    largest = most if full else min(most, max(-(-total // count), total * portions[0] // sum(portions)))
    least = 1 if total - largest >= count - 1 else 0
    given, rest = [largest] + [least] * (count - 1), total - largest - least * (count - 1)
    while rest > 0:
        free = [i for i in range(1, count) if given[i] < largest] or [i for i in range(1, count) if given[i] < most]
        mass, budget = sum([portions[i] for i in free]), rest
        for i in free:
            addition = min(most - given[i], max(1, budget * portions[i] // mass), rest)
            given[i] = given[i] + addition
            rest = rest - addition
    return np.array(given)


def noise(key, extent, spread, most, split=(), kind=jnp.bfloat16):
    entries = jax.random.normal(key, extent, jnp.float32) * spread
    if len(split) > 0:
        entries = level_of(key, extent, split, -0.22, 0.18) * entries
    return jnp.clip(entries, min=-most, max=most).astype(kind)


def setup_inputs(seed: int = 0) -> dict:
    seeds = jax.random.split(jax.random.key(seed), 16)
    hidden_in = noise(seeds[0], (NSEQ, LMAX, D), 1.0, 6.0, ((1, 8),))
    cotangent = noise(seeds[1], (NSEQ, LMAX, D), 1.0, 6.0, ((0, 8),))
    lengths = uneven_parts(seeds[2], NSEQ, NSEQ * LMAX * 3 // 4, LMAX, 1).astype(jnp.int32)
    dealing = jax.random.permutation(seeds[3], NSEQ).astype(jnp.int32)
    attn_routes_keys = jax.random.split(jax.random.fold_in(seeds[4], 1), NSEQ * LMAX // LMAX)
    attn_routes_turns = jax.random.permutation(jax.random.fold_in(seeds[4], 3), NSEQ * LMAX // LMAX)
    attn_routes = jax.vmap(lambda own, number: routed_block(jax.random.fold_in(seeds[4], 2), own, number, LMAX, EA, TOP, CAP, 1))(attn_routes_keys, attn_routes_turns).reshape((NSEQ, LMAX, TOP))
    ffn_routes_keys = jax.random.split(jax.random.fold_in(seeds[5], 1), NSEQ * LMAX // LMAX)
    ffn_routes_turns = jax.random.permutation(jax.random.fold_in(seeds[5], 3), NSEQ * LMAX // LMAX)
    ffn_routes = jax.vmap(lambda own, number: routed_block(jax.random.fold_in(seeds[5], 2), own, number, LMAX, EF, TOP, CAP, 1))(ffn_routes_keys, ffn_routes_turns).reshape((NSEQ, LMAX, TOP))
    attn_gain = jnp.clip(1.0 + 0.1 * jax.random.normal(seeds[6], (D,), jnp.float32), 0.5, 1.5)
    attn_router = noise(seeds[7], (D, EA), (4 * D) ** -0.5, 0.0625)
    kv_weight = noise(seeds[8], (2, D, HEADS * HD), D ** -0.5, 0.125, ((1, 8), (2, 4)))
    query_weight = noise(seeds[9], (EA, D, HEADS * HD), D ** -0.5, 0.125, ((1, 8), (2, 4)))
    proj_weight = noise(seeds[10], (EA, HEADS * HD, D), (HEADS * HD // 64) ** -0.5, 1.0, ((1, 4), (2, 8)))
    ffn_gain = jnp.clip(1.0 + 0.1 * jax.random.normal(seeds[11], (D,), jnp.float32), 0.5, 1.5)
    ffn_router = noise(seeds[12], (D, EF), (4 * D) ** -0.5, 0.0625)
    expert_in = noise(seeds[13], (EF, D, 2, FF), D ** -0.5, 0.125, ((1, 8), (3, 4)))
    expert_out = noise(seeds[14], (EF, FF, D), (FF // 2) ** -0.5, 0.109375, ((1, 4), (2, 8)))
    return dict(hidden_in=hidden_in, cotangent=cotangent, lengths=lengths, dealing=dealing, attn_routes=attn_routes, ffn_routes=ffn_routes, attn_gain=attn_gain, attn_router=attn_router, kv_weight=kv_weight, query_weight=query_weight, proj_weight=proj_weight, ffn_gain=ffn_gain, ffn_router=ffn_router, expert_in=expert_in, expert_out=expert_out)


EPSILON = 1e-06
ROPE_BASE = 10000.0
BEST = lax.Precision.HIGHEST

@jax.custom_vjp
def low(v):
    return lax.optimization_barrier(v.astype(jnp.bfloat16)).astype(jnp.float32)

@jax.custom_vjp
def low_back(v):
    return v

def low_keep(v):
    return (low(v), None)

def low_pass(kept, grad):
    return (grad,)

def back_keep(v):
    return (v, None)

def back_low(kept, grad):
    return (low(grad),)
low.defvjp(low_keep, low_pass)
low_back.defvjp(back_keep, back_low)

def both_round(value):
    return low(low_back(value))

def rotate(values, positions, head_count, direction):
    head_width = values.shape[-1] // head_count
    half_width = head_width // 2
    frequency = ROPE_BASE ** (-2.0 * jnp.arange(half_width, dtype=jnp.float32) / head_width)
    angles = positions.astype(jnp.float32)[:, None] * frequency[None, :]
    cosine = jnp.cos(angles)[:, None, :]
    sine_part = direction * jnp.sin(angles)[:, None, :]
    shaped = values.reshape(values.shape[0], head_count, head_width)
    front_half = shaped[:, :, :half_width]
    back_half = shaped[:, :, half_width:]
    turned = jnp.concatenate([front_half * cosine - back_half * sine_part, back_half * cosine + front_half * sine_part], axis=-1)
    return turned.reshape(values.shape)

def dispatch_table(routes, experts, capacity):
    flat_routes = routes.reshape(-1)
    one_hot = (flat_routes[:, None] == jnp.arange(experts, dtype=jnp.int32)[None, :]).astype(jnp.int32)
    places = lax.optimization_barrier(jnp.sum((jnp.cumsum(one_hot, axis=0) - 1) * one_hot, axis=1))
    targets = (flat_routes * capacity + places).astype(jnp.int32)
    sources = jnp.zeros((experts * capacity,), jnp.int32).at[targets].set(jnp.arange(flat_routes.shape[0], dtype=jnp.int32))
    return (targets, sources)

def sequence_forward(inputs, gain_a, router_a, kv_w, query_w, proj_w, gain_f, router_f, in_w, out_w, seq_len, attn_route, ffn_route):
    positions = jnp.arange(LMAX, dtype=jnp.int32)
    valid_rows = (positions < seq_len).astype(jnp.float32)[:, None]
    allowed = (positions[None, :] <= positions[:, None]) & (positions[None, :] < seq_len)
    rms_one = lax.rsqrt(lax.optimization_barrier(jnp.mean(inputs * inputs, axis=-1, keepdims=True)) + EPSILON)
    attn_input = low(inputs * rms_one * gain_a)
    attn_logits = jnp.dot(attn_input, router_a, precision=BEST)
    attn_gates = jax.nn.softmax(jnp.take_along_axis(attn_logits, attn_route, axis=1), axis=-1)
    key_raw = low_back(jnp.dot(attn_input, kv_w[0], precision=BEST))
    keys = low(rotate(key_raw, positions, HEADS, 1.0)).reshape(LMAX, HEADS, HD)
    values = both_round(jnp.dot(attn_input, kv_w[1], precision=BEST)).reshape(LMAX, HEADS, HD)
    query_all = jnp.einsum('td,edh->teh', attn_input, query_w, precision=BEST)
    query_raw = low_back(jnp.take_along_axis(query_all, attn_route[:, :, None], axis=1))
    slot_positions = jnp.repeat(positions, TOP)
    queries = low(rotate(query_raw.reshape(LMAX * TOP, HEADS * HD), slot_positions, HEADS, 1.0)).reshape(LMAX, TOP, HEADS, HD)
    scores = low_back(jnp.einsum('qkhd,uhd->khqu', queries, keys, precision=BEST) * HD ** (-0.5))
    scores = jnp.where(allowed[None, None], scores, -jnp.inf)
    attn_probs = low(jax.nn.softmax(scores, axis=-1))
    mixed_heads = both_round(jnp.einsum('khqu,uhd->qkhd', attn_probs, values, precision=BEST)).reshape(LMAX, TOP, HEADS * HD)
    proj_all = jnp.einsum('tkh,ehd->tked', mixed_heads, proj_w, precision=BEST)
    attn_slots = low_back(jnp.take_along_axis(proj_all, attn_route[:, :, None, None], axis=2)[:, :, 0])
    after_attn = inputs + valid_rows * lax.optimization_barrier(jnp.sum(attn_gates[..., None] * attn_slots, axis=1))
    rms_two = lax.rsqrt(lax.optimization_barrier(jnp.mean(after_attn * after_attn, axis=-1, keepdims=True)) + EPSILON)
    ffn_input = low(after_attn * rms_two * gain_f)
    ffn_logits = jnp.dot(ffn_input, router_f, precision=BEST)
    ffn_gates = jax.nn.softmax(jnp.take_along_axis(ffn_logits, ffn_route, axis=1), axis=-1)
    targets, sources = dispatch_table(ffn_route, EF, CAP)
    grouped = ffn_input[sources // TOP].reshape(EF, CAP, D)
    gate_up = jnp.einsum('ecd,edjf->ecjf', grouped, in_w, precision=BEST)
    gate_pre = low_back(gate_up[:, :, 0])
    up_pre = low_back(gate_up[:, :, 1])
    hidden = low(jax.nn.silu(gate_pre) * up_pre)
    group_out = jnp.einsum('ecf,efd->ecd', hidden, out_w, precision=BEST)
    ffn_slots = low_back(group_out.reshape(EF * CAP, D)[targets].reshape(LMAX, TOP, D))
    return after_attn + valid_rows * lax.optimization_barrier(jnp.sum(ffn_gates[..., None] * ffn_slots, axis=1))

def reference(hidden_in, cotangent, lengths, dealing, attn_routes, ffn_routes, attn_gain, attn_router, kv_weight, query_weight, proj_weight, ffn_gain, ffn_router, expert_in, expert_out):
    count = dealing.shape[0]
    inverse = jnp.zeros((count,), jnp.int32).at[dealing].set(jnp.arange(count, dtype=jnp.int32))
    shared = (attn_gain.astype(jnp.float32), attn_router.astype(jnp.float32), kv_weight.astype(jnp.float32), query_weight.astype(jnp.float32), proj_weight.astype(jnp.float32), ffn_gain.astype(jnp.float32), ffn_router.astype(jnp.float32), expert_in.astype(jnp.float32), expert_out.astype(jnp.float32))

    def one_sequence(totals, items):
        seq_input, seq_cot, seq_len, attn_route, ffn_route = items

        def forward(inputs, gain_a, router_a, kv_w, query_w, proj_w, gain_f, router_f, in_w, out_w):
            return sequence_forward(inputs, gain_a, router_a, kv_w, query_w, proj_w, gain_f, router_f, in_w, out_w, seq_len, attn_route, ffn_route)
        outputs, pullback = jax.vjp(forward, seq_input.astype(jnp.float32), shared[0], shared[1], shared[2], shared[3], shared[4], shared[5], shared[6], shared[7], shared[8])
        grads = pullback(seq_cot.astype(jnp.float32))
        totals = tuple((total + grad for total, grad in zip(totals, grads[1:])))
        return (totals, (outputs.astype(jnp.bfloat16), grads[0].astype(jnp.bfloat16)))
    start = tuple((jnp.zeros_like(weight_arr) for weight_arr in shared))
    totals, (outputs, input_grads) = lax.scan(one_sequence, start, (hidden_in, cotangent[inverse], lengths, attn_routes, ffn_routes))
    return (outputs, input_grads, totals[0], totals[1], totals[2], totals[3], totals[4], totals[5], totals[6], totals[7], totals[8])
```

```python
import functools

import jax
import jax.numpy as jnp
from jax import lax
from jax.experimental import pallas as pl
from jax.experimental.pallas import tpu as pltpu
from jax.sharding import PartitionSpec as P

HD = 128
EPSILON = 1e-06
ROPE_BASE = 10000.0
BEST = lax.Precision.HIGHEST
F32 = jnp.float32
BF16 = jnp.bfloat16
VMEM_BYTES = 60 * 1024 * 1024


def nn(a, b):
    return lax.dot_general(a, b, (((1,), (0,)), ((), ())), preferred_element_type=F32)


def nt(a, b, precision=None):
    return lax.dot_general(
        a, b, (((1,), (1,)), ((), ())), preferred_element_type=F32, precision=precision
    )


def tn(a, b):
    return lax.dot_general(a, b, (((0,), (0,)), ((), ())), preferred_element_type=F32)


def lane_sums(values):
    ones = jnp.ones((8, values.shape[1]), F32)
    return nt(ones, values, BEST)


def run(body, name, grid, meta, ins, outs, scratch=(), flops=0):
    in_specs = []
    moved = 0
    for array, block, index in ins:
        if block is None:
            rank = array.ndim
            in_specs.append(pl.BlockSpec(array.shape, lambda *a, rank=rank: (0,) * rank))
        else:
            in_specs.append(pl.BlockSpec(block, index))
        moved += array.size * array.dtype.itemsize
    out_specs = []
    out_shape = []
    for shape, dtype, block, index in outs:
        if block is None:
            rank = len(shape)
            out_specs.append(pl.BlockSpec(shape, lambda *a, rank=rank: (0,) * rank))
        else:
            out_specs.append(pl.BlockSpec(block, index))
        out_shape.append(jax.ShapeDtypeStruct(shape, dtype))
        size = jnp.dtype(dtype).itemsize
        for extent in shape:
            size *= extent
        moved += size
    return pl.pallas_call(
        body,
        name=name,
        grid_spec=pltpu.PrefetchScalarGridSpec(
            num_scalar_prefetch=1,
            grid=grid,
            in_specs=in_specs,
            out_specs=out_specs,
            scratch_shapes=list(scratch),
        ),
        out_shape=out_shape,
        compiler_params=pltpu.CompilerParams(
            dimension_semantics=("arbitrary",) * len(grid), vmem_limit_bytes=VMEM_BYTES
        ),
        cost_estimate=pl.CostEstimate(flops=flops, bytes_accessed=moved, transcendentals=0),
    )(meta, *[array for array, _, _ in ins])


def pick(low_id, high_id, expert, low_value, high_value):
    zero = jnp.zeros_like(low_value)
    return jnp.where(
        low_id == expert, low_value, jnp.where(high_id == expert, high_value, zero)
    )


def two_slots(low_id, high_id, products):
    low_value = products[0]
    for expert in range(1, len(products) - 1):
        low_value = jnp.where(low_id == expert, products[expert], low_value)
    high_value = products[1]
    for expert in range(2, len(products)):
        high_value = jnp.where(high_id == expert, products[expert], high_value)
    return low_value, high_value


def turn(values, cosine, sine):
    return values * cosine + pltpu.roll(values, HD // 2, 1) * sine


def local(
    hidden_in,
    cotangent,
    lengths,
    dealing,
    attn_routes,
    ffn_routes,
    attn_gain,
    attn_router,
    kv_weight,
    query_weight,
    proj_weight,
    ffn_gain,
    ffn_router,
    expert_in,
    expert_out,
    *,
    dp,
    tp,
):
    seqs = dealing.shape[0]
    seq_len = cotangent.shape[1]
    held = cotangent.shape[0]
    per = hidden_in.shape[1]
    width = hidden_in.shape[2]
    heads = query_weight.shape[2] // HD
    groups = heads
    parts = dp // groups
    ds = width // dp
    hw = heads * HD
    rows_all = seqs * seq_len
    rows = rows_all * 3 // 4
    rp = rows // parts
    blk = rp // groups
    experts = query_weight.shape[0]
    ff = expert_out.shape[1]
    scale = HD ** (-0.5)
    pieces = range(parts)

    index = lax.axis_index("dp")
    z = lax.axis_index("tensor")
    g = index // parts
    c = index % parts
    meta = jnp.stack([g, c, g, g ^ 1, g ^ 2, g ^ 3]).astype(jnp.int32)

    def by_group(value, mask):
        pairs = [(a, ((a // parts) ^ mask) * parts + a % parts) for a in range(dp)]
        return lax.ppermute(value, "dp", pairs)

    def by_part(value, mask):
        pairs = [(a, (a // parts) * parts + ((a % parts) ^ mask)) for a in range(dp)]
        return lax.ppermute(value, "dp", pairs)

    def to_next(value):
        pairs = [(a, a + 1) for a in range(dp) if a % parts < parts - 1]
        return lax.ppermute(value, "dp", pairs)

    def to_previous(value):
        pairs = [(a, a - 1) for a in range(dp) if a % parts > 0]
        return lax.ppermute(value, "dp", pairs)

    def by_z(value, mask):
        return lax.ppermute(value, "tensor", [(a, a ^ mask) for a in range(tp)])

    def sum_groups(value):
        value = value + by_group(value, 1)
        return value + by_group(value, 2)

    def sum_z(value):
        value = value + by_z(value, 1)
        return value + by_z(value, 3)

    def wide_sum_z(value):
        inner = lax.ppermute(value, "tensor", [(0, 1), (3, 2)])
        value = (value.astype(F32) + inner.astype(F32)).astype(BF16)
        other = lax.ppermute(value, "tensor", [(1, 2), (2, 1)])
        value = (value.astype(F32) + other.astype(F32)).astype(BF16)
        outer = lax.ppermute(value, "tensor", [(1, 0), (2, 3)])
        return jnp.where((z == 1) | (z == 2), value, outer)

    def reduce_groups(first, second):
        ra = by_group(first[3], 1)
        rb = by_group(second[3], 2)
        ax = by_group(first[1], 1)
        by = by_group(second[2], 2)
        ay = by_group((first[2].astype(F32) + ra.astype(F32)).astype(BF16), 2)
        bx = by_group((second[1].astype(F32) + rb.astype(F32)).astype(BF16), 1)
        return (first[0], ax, ay), (second[0], bx, by)

    def gather_groups(first, second):
        ax, bx = by_group(first, 1), by_group(second, 1)
        ay, by = by_group(first, 2), by_group(second, 2)
        ad, bd = by_group(ax, 2), by_group(by, 1)
        return (first, ax, ay, ad), (second, bx, by, bd)

    def row_of(offset):
        return lambda *a: (a[-1][2 + offset], 0)

    ends = jnp.cumsum(lengths)
    starts = ends - lengths
    inverse = jnp.sum(
        (dealing[None, :] == jnp.arange(seqs, dtype=jnp.int32)[:, None])
        * jnp.arange(seqs, dtype=jnp.int32)[None, :],
        axis=1,
    )

    def places(part):
        packed = part * rp + jnp.arange(rp, dtype=jnp.int32)
        begun = starts[None, :] <= packed[:, None]
        first = jnp.max(jnp.where(begun, starts[None, :], 0), axis=1)
        seq = jnp.sum(begun.astype(jnp.int32), axis=1) - 1
        at = packed - first
        slot = jnp.sum(
            jnp.where(seq[:, None] == jnp.arange(seqs, dtype=jnp.int32)[None, :], inverse[None, :], 0),
            axis=1,
        )
        x_row = (at // per) * (seqs * per) + seq * per + at % per
        d_row = slot * seq_len + at
        return seq, at, first, x_row, d_row

    seq, at, first, x_row, d_row = places(c)

    x_send = hidden_in.reshape(seqs * per, dp, ds).transpose(1, 0, 2)
    x_all = lax.all_to_all(x_send, "dp", 0, 0, tiled=True).reshape(rows_all, ds)
    d_send = cotangent.reshape(held * seq_len, dp, ds).transpose(1, 0, 2)
    d_all = lax.all_to_all(d_send, "dp", 0, 0, tiled=True).reshape(rows_all, ds)
    x_pieces = [x_all[x_row]]
    d_pieces = [d_all[d_row]]
    for s in pieces[1:]:
        _, _, _, other_x, other_d = places(c ^ s)
        x_pieces.append(by_part(x_all[other_x], s))
        d_pieces.append(by_part(d_all[other_d], s))

    def spread(vector):
        tall = vector.reshape((groups, parts, ds) + vector.shape[1:])[g]
        return jnp.stack([tall[c ^ s] for s in pieces])

    gain_a = spread(attn_gain)[:, None, :]
    gain_f = spread(ffn_gain)[:, None, :]
    pad = ((0, 0), (0, 8 - experts), (0, 0))
    router_a = jnp.pad(spread(attn_router).transpose(0, 2, 1), pad)
    router_f = jnp.pad(spread(ffn_router).transpose(0, 2, 1), pad)

    in_own = expert_in.swapaxes(1, 2)
    wq = [query_weight] + [by_part(query_weight, s) for s in pieces[1:]]
    wkv = [kv_weight] + [by_part(kv_weight, s) for s in pieces[1:]]
    wp = [proj_weight] + [by_part(proj_weight, s) for s in pieces[1:]]
    wo = [expert_out] + [by_part(expert_out, s) for s in pieces[1:]]
    wi = [in_own] + [by_part(in_own, s) for s in pieces[1:]]

    routes = jnp.concatenate(
        [attn_routes.reshape(rows_all, 2), ffn_routes.reshape(rows_all, 2)], axis=1
    )
    here = (seq * seq_len + at)[:, None] == jnp.arange(rows_all, dtype=jnp.int32)[None, :]
    mine = jnp.dot(here.astype(BF16), routes.astype(BF16), preferred_element_type=F32)
    low_a, high_a = jnp.minimum(mine[:, 0], mine[:, 1]), jnp.maximum(mine[:, 0], mine[:, 1])
    low_f, high_f = jnp.minimum(mine[:, 2], mine[:, 3]), jnp.maximum(mine[:, 2], mine[:, 3])
    window = (first - c * rp + seq_len).astype(F32)
    nil = jnp.zeros_like(window)
    sel = jnp.stack([low_a, high_a, low_f, high_f, window, nil, nil, nil], axis=1)
    half = HD // 2
    frequency = ROPE_BASE ** (-2.0 * jnp.arange(half, dtype=F32) / HD)
    angles = at.astype(F32)[:, None] * frequency[None, :]
    cosine = jnp.concatenate([jnp.cos(angles)] * 2, axis=1)
    sine = jnp.sin(angles)
    sine = jnp.concatenate([-sine, sine], axis=1)

    def gate_columns(stats, low_id, high_id):
        rms = lax.rsqrt(stats[experts] / width + EPSILON)
        ids = jnp.arange(experts, dtype=F32)[:, None]
        logits = stats[:experts]
        low_logit = jnp.sum(jnp.where(low_id[None] == ids, logits, 0.0), axis=0) * rms
        high_logit = jnp.sum(jnp.where(high_id[None] == ids, logits, 0.0), axis=0) * rms
        gap = low_logit - high_logit
        low_gate, high_gate = jax.nn.sigmoid(gap), jax.nn.sigmoid(-gap)
        zero = jnp.zeros_like(rms)
        flat = jnp.stack([rms, low_gate, high_gate, gap, zero, zero, zero, zero])
        return flat, flat.T

    def dhidden_body(m, *refs):
        d_refs, w_refs = refs[:parts], refs[parts : 2 * parts]
        sel_ref, a_ref, b_ref = refs[2 * parts :]
        products = []
        for e in range(experts):
            products.append(sum(nt(d_refs[s][...], w_refs[s][e]) for s in pieces))
        low, high = two_slots(sel_ref[:, 2:3], sel_ref[:, 3:4], products)
        a_ref[...] = low.astype(BF16)
        b_ref[...] = high.astype(BF16)

    def dhidden(r):
        ins = [(d, (blk, ds), row_of(r)) for d in d_pieces]
        ins += [(w, None, None) for w in wo]
        ins += [(sel, (blk, 8), row_of(r))]
        outs = [((blk, ff), BF16, None, None)] * 2
        return run(
            dhidden_body, "dhidden", (1,), meta, ins, outs,
            flops=2 * blk * experts * parts * ds * ff,
        )

    dh = [dhidden(r) for r in range(4)]
    dh_a, dh_b = reduce_groups([v[0] for v in dh], [v[1] for v in dh])

    tile = 256

    def qkv_body(m, *refs):
        x_refs = refs[:parts]
        gain_ref, router_ref = refs[parts : parts + 2]
        q_refs = refs[parts + 2 : 2 * parts + 2]
        kv_refs = refs[2 * parts + 2 : 3 * parts + 2]
        sel_ref = refs[3 * parts + 2]
        outs = refs[3 * parts + 3 : 3 * parts + 11]
        stats_ref, scr = refs[3 * parts + 11 :]
        us = []
        logits = jnp.zeros((8, tile), F32)
        squares = jnp.zeros((8, tile), F32)
        for s in pieces:
            xf = x_refs[s][...].astype(F32)
            us.append((xf * gain_ref[s]).astype(BF16))
            logits += nt(router_ref[s], us[s])
            squares += lane_sums(xf * xf)
        line = lax.broadcasted_iota(jnp.int32, (8, tile), 0)
        stats_ref[...] = jnp.where(line < experts, logits, squares)
        products = []
        for e in range(experts):
            products.append(sum(nn(us[s], q_refs[s][e]) for s in pieces))
        low, high = two_slots(sel_ref[:, 0:1], sel_ref[:, 1:2], products)
        keys = sum(nn(us[s], kv_refs[s][0]) for s in pieces)
        values = sum(nn(us[s], kv_refs[s][1]) for s in pieces)
        for k, value in enumerate((low, high, keys, values)):
            value = value.astype(BF16)
            for h in range(heads):
                scr[h, :, k * HD : (k + 1) * HD] = value[:, h * HD : (h + 1) * HD]
        for r in range(4):
            block = scr[m[2 + r]]
            outs[2 * r][...] = block[:, : 2 * HD]
            outs[2 * r + 1][...] = block[:, 2 * HD :]

    ins = [(x, (tile, ds), lambda i, m: (i, 0)) for x in x_pieces]
    ins += [(gain_a, None, None), (router_a, None, None)]
    ins += [(w, None, None) for w in wq + wkv]
    ins += [(sel, (tile, 8), lambda i, m: (i, 0))]
    outs = [((rp, 2 * HD), BF16, (tile, 2 * HD), lambda i, m: (i, 0))] * 8
    outs += [((8, rp), F32, (8, tile), lambda i, m: (0, i))]
    qkv = run(
        qkv_body, "qkv", (rp // tile,), meta, ins, outs,
        [pltpu.VMEM((heads, tile, 4 * HD), BF16)],
        flops=2 * rp * (experts + 2) * parts * ds * hw,
    )
    q_sum, kv_sum = reduce_groups(qkv[0:8:2], qkv[1:8:2])
    stats_a = sum_groups(qkv[8])
    flat_a, cols_a = gate_columns(stats_a, low_a, high_a)

    def rope_body(m, a0, a1, a2, b0, b1, b2, cols, cos_ref, sin_ref, q_ref, kv_ref):
        rms = cols[:, 0:1]
        cos, sin = cos_ref[...], sin_ref[...]
        q = (a0[...].astype(F32) + a1[...].astype(F32) + a2[...].astype(F32)) * rms
        kv = (b0[...].astype(F32) + b1[...].astype(F32) + b2[...].astype(F32)) * rms
        q_ref[:, :HD] = turn(q[:, :HD], cos, sin).astype(BF16)
        q_ref[:, HD:] = turn(q[:, HD:], cos, sin).astype(BF16)
        kv_ref[:, :HD] = turn(kv[:, :HD], cos, sin).astype(BF16)
        kv_ref[:, HD:] = kv[:, HD:].astype(BF16)

    ins = [(v, (tile, 2 * HD), lambda i, m: (i, 0)) for v in q_sum + kv_sum]
    ins += [(cols_a, (tile, 8), lambda i, m: (i, 0))]
    ins += [(v, (tile, HD), lambda i, m: (i, 0)) for v in (cosine, sine)]
    outs = [((rp, 2 * HD), BF16, (tile, 2 * HD), lambda i, m: (i, 0))] * 2
    q_rot, kv_rot = run(rope_body, "rope", (rp // tile,), meta, ins, outs)
    halo = to_next(kv_rot[rp - seq_len :])

    qt = 128
    span = seq_len + qt

    def window_mask(i, low_key):
        u = i * qt + lax.broadcasted_iota(jnp.int32, (qt, span), 1)
        t = seq_len + i * qt + lax.broadcasted_iota(jnp.int32, (qt, span), 0)
        return (u >= low_key.astype(jnp.int32)) & (u <= t)

    def softmax_of(query, key, allowed):
        score = jnp.where(allowed, nt(query, key) * scale, -1e30)
        top = jnp.max(score, axis=1, keepdims=True)
        raised = jnp.exp(score - top)
        return raised / jnp.sum(raised, axis=1, keepdims=True)

    def attend_body(m, q_ref, kv_ref, halo_ref, sel_ref, cols, ga, gb, ma, mb, ext):
        i = pl.program_id(0)

        @pl.when(i == 0)
        def _():
            ext[:seq_len, :] = halo_ref[...]
            ext[seq_len:, :] = kv_ref[...]

        near = ext[pl.ds(pl.multiple_of(i * qt, qt), span), :]
        allowed = window_mask(i, sel_ref[:, 4:5])
        for k, (g_ref, m_ref) in enumerate(((ga, ma), (gb, mb))):
            probs = softmax_of(q_ref[:, k * HD : (k + 1) * HD], near[:, :HD], allowed)
            mixed = nn(probs.astype(BF16), near[:, HD:]).astype(BF16)
            m_ref[...] = mixed
            g_ref[...] = (mixed.astype(F32) * cols[:, 1 + k : 2 + k]).astype(BF16)

    def qrow(i, m):
        return (i, 0)

    ins = [(q_rot, (qt, 2 * HD), qrow), (kv_rot, None, None), (halo, None, None)]
    ins += [(sel, (qt, 8), qrow), (cols_a, (qt, 8), qrow)]
    outs = [((rp, HD), BF16, (qt, HD), qrow)] * 4
    gated_a, gated_b, mixed_a, mixed_b = run(
        attend_body, "attend", (rp // qt,), meta, ins, outs,
        [pltpu.VMEM((seq_len + rp, 2 * HD), BF16)],
        flops=8 * rp * span * HD,
    )
    gm_a, gm_b = gather_groups(gated_a, gated_b)

    chunks = 4
    zr = rp // chunks

    def proj_body(m, *refs):
        a_refs, b_refs = refs[:4], refs[4:8]
        sel_ref = refs[8]
        w_refs = refs[9 : 9 + parts]
        out_ref, lo, hi = refs[9 + parts :]
        for r in range(4):
            lanes = pl.ds(pl.multiple_of(m[2 + r] * HD, HD), HD)
            lo[:, lanes] = a_refs[r][...]
            hi[:, lanes] = b_refs[r][...]
        acc = [None] * parts
        for e in range(experts):
            x = pick(sel_ref[:, 0:1], sel_ref[:, 1:2], e, lo[...], hi[...])
            for s in pieces:
                term = nn(x, w_refs[s][e])
                acc[s] = term if e == 0 else acc[s] + term
        for s in pieces:
            out_ref[s] = acc[s].astype(BF16)

    def project(k):
        at_chunk = lambda i, m: (k, 0)
        ins = [(v, (zr, HD), at_chunk) for v in gm_a + gm_b]
        ins += [(sel, (zr, 8), at_chunk)]
        ins += [(w, None, None) for w in wp]
        return run(
            proj_body, "proj", (1,), meta, ins, [((parts, zr, ds), BF16, None, None)],
            [pltpu.VMEM((zr, hw), BF16)] * 2,
            flops=2 * zr * experts * hw * parts * ds,
        )[0]

    attn_totals = [wide_sum_z(project(k)) for k in range(chunks)]

    def norm_body(m, *refs):
        t_refs = refs[:chunks]
        x_refs = refs[chunks : chunks + parts]
        gain_ref, router_ref, after_ref, u_ref, stats_ref = refs[chunks + parts :]
        for k in range(chunks):
            span_k = slice(k * zr, (k + 1) * zr)
            for s in pieces:
                after_ref[s, span_k] = x_refs[s][span_k, :].astype(F32) + t_refs[k][s].astype(F32)
        logits = jnp.zeros((8, rp), F32)
        squares = jnp.zeros((8, rp), F32)
        for s in pieces:
            af = after_ref[s]
            u = (af * gain_ref[s]).astype(BF16)
            u_ref[s] = u
            logits += nt(router_ref[s], u)
            squares += lane_sums(af * af)
        line = lax.broadcasted_iota(jnp.int32, (8, rp), 0)
        stats_ref[...] = jnp.where(line < experts, logits, squares)

    ins = [(t, None, None) for t in attn_totals + x_pieces]
    ins += [(gain_f, None, None), (router_f, None, None)]
    outs = [
        ((parts, rp, ds), F32, None, None),
        ((parts, rp, ds), BF16, None, None),
        ((8, rp), F32, None, None),
    ]
    after, u_f, stats_part = run(norm_body, "norm", (1,), meta, ins, outs)
    stats_f = sum_groups(stats_part)
    flat_f, cols_f = gate_columns(stats_f, low_f, high_f)

    def up_body(m, *refs):
        u_ref = refs[0]
        w_refs = refs[1 : 1 + parts]
        sel_ref, a_ref, b_ref = refs[1 + parts :]
        products = []
        for e in range(experts):
            products.append(sum(nn(u_ref[s], w_refs[s][e, 0]) for s in pieces))
        low, high = two_slots(sel_ref[:, 2:3], sel_ref[:, 3:4], products)
        a_ref[0] = low.astype(BF16)
        b_ref[0] = high.astype(BF16)

    def up(r):
        ins = [(u_f, (parts, blk, ds), lambda j, m: (0, m[2 + r], 0))]
        ins += [(w, (experts, 1, ds, ff), lambda j, m: (0, j, 0, 0)) for w in wi]
        ins += [(sel, (blk, 8), row_of(r))]
        outs = [((2, blk, ff), BF16, (1, blk, ff), lambda j, m: (j, 0, 0))] * 2
        return run(
            up_body, "up", (2,), meta, ins, outs, flops=4 * blk * experts * parts * ds * ff
        )

    ups = [None] * 4
    for r in (3, 1, 2, 0):
        ups[r] = up(r)
    gu_a, gu_b = reduce_groups([v[0] for v in ups], [v[1] for v in ups])

    ft = HD

    def mid_body(m, *refs):
        gu = (refs[0:3], refs[3:6])
        dhr = (refs[6:9], refs[9:12])
        cols = refs[12]
        outs, dots = refs[13:15], refs[15]
        j = pl.program_id(0)

        @pl.when(j == 0)
        def _():
            dots[...] = jnp.zeros_like(dots)

        rms = cols[:, 0:1]
        line = lax.broadcasted_iota(jnp.int32, (8, blk), 0)
        inner = jnp.zeros((blk, ft), F32)
        found = []
        for k in range(2):
            gate = cols[:, 1 + k : 2 + k]
            gp = sum(v[0].astype(F32) for v in gu[k]) * rms
            up_pre = sum(v[1].astype(F32) for v in gu[k]) * rms
            raw = sum(v[...].astype(F32) for v in dhr[k])
            sg = jax.nn.sigmoid(gp)
            act = (gp * sg * up_pre).astype(BF16).astype(F32)
            grad = raw * gate
            dgp = (grad * up_pre * sg * (1.0 + gp * (1.0 - sg))).astype(BF16)
            dup = (grad * gp * sg).astype(BF16)
            outs[k][0] = (act * gate).astype(BF16)
            outs[k][1] = dgp
            outs[k][2] = dup
            found.append(act * raw)
            inner += dgp.astype(F32) * gp + dup.astype(F32) * up_pre
        sums = jnp.where(
            line == 0, lane_sums(found[0]), jnp.where(line == 1, lane_sums(found[1]), lane_sums(inner))
        )
        dots[...] += sums

    ins = [(v, (2, blk, ft), lambda j, m: (0, 0, j)) for v in gu_a + gu_b]
    ins += [(v, (blk, ft), lambda j, m: (0, j)) for v in dh_a + dh_b]
    ins += [(cols_f, (blk, 8), row_of(0))]
    outs = [((3, blk, ff), BF16, (3, blk, ft), lambda j, m: (0, 0, j))] * 2
    outs += [((8, blk), F32, None, None)]
    act_a, act_b, dots_f = run(mid_body, "mid", (ff // ft,), meta, ins, outs)
    ag_a, ag_b = gather_groups(act_a, act_b)

    dots_f = sum_z(dots_f)
    dots_f = jnp.stack([dots_f, by_group(dots_f, 1), by_group(dots_f, 2), by_group(dots_f, 3)])
    dots_f = jnp.take(dots_f, g ^ jnp.arange(4, dtype=jnp.int32), axis=0)
    dots_f = dots_f.transpose(1, 0, 2).reshape(8, rp)

    def back_columns(flat, dots, low_id, high_id):
        delta = flat[1] * flat[2] * (dots[0] - dots[1])
        inner = (dots[2] + delta * flat[3]) / width
        ids = jnp.arange(experts, dtype=F32)[:, None]
        dlogit = jnp.where(low_id[None] == ids, delta[None], 0.0) - jnp.where(
            high_id[None] == ids, delta[None], 0.0
        )
        zero = jnp.zeros((1, rp), F32)
        return jnp.concatenate(
            [dlogit, inner[None], flat[0:1]] + [zero] * (6 - experts), axis=0
        ).T

    back_f = back_columns(flat_f, dots_f, low_f, high_f)

    def dx_body(m, *refs):
        a_ref, b_ref = refs[:2]
        w_refs = refs[2 : 2 + parts]
        sel_ref, out_ref, acc = refs[2 + parts :]
        e = pl.program_id(0)
        expert = e.astype(F32)
        gate = pick(sel_ref[:, 2:3], sel_ref[:, 3:4], expert, a_ref[1], b_ref[1])
        upper = pick(sel_ref[:, 2:3], sel_ref[:, 3:4], expert, a_ref[2], b_ref[2])

        @pl.when(e == 0)
        def _():
            acc[...] = jnp.zeros_like(acc)

        for s in pieces:
            acc[s] += nt(gate, w_refs[s][0, 0]) + nt(upper, w_refs[s][0, 1])

        @pl.when(e == experts - 1)
        def _():
            out_ref[...] = acc[...].astype(BF16)

    def dx(r):
        ins = [(ag_a[r], None, None), (ag_b[r], None, None)]
        ins += [(w, (1, 2, ds, ff), lambda e, m: (e, 0, 0, 0)) for w in wi]
        ins += [(sel, (blk, 8), row_of(r))]
        return run(
            dx_body, "dx", (experts,), meta, ins, [((parts, blk, ds), BF16, None, None)],
            [pltpu.VMEM((parts, blk, ds), F32)], flops=4 * blk * experts * parts * ds * ff,
        )[0]

    dx_totals = [wide_sum_z(dx(r)) for r in range(4)]

    def down_body(m, *refs):
        a_ref, b_ref = refs[:2]
        w_refs = refs[2 : 2 + parts]
        sel_ref, out_ref, acc = refs[2 + parts :]
        e = pl.program_id(0)
        x = pick(sel_ref[:, 2:3], sel_ref[:, 3:4], e.astype(F32), a_ref[0], b_ref[0])

        @pl.when(e == 0)
        def _():
            acc[...] = jnp.zeros_like(acc)

        for s in pieces:
            acc[s] += nn(x, w_refs[s][0])

        @pl.when(e == experts - 1)
        def _():
            out_ref[...] = acc[...].astype(BF16)

    def down(r):
        whole = lambda e, m: (0, 0, 0)
        ins = [(ag_a[r], (1, blk, ff), whole), (ag_b[r], (1, blk, ff), whole)]
        ins += [(w, (1, ff, ds), lambda e, m: (e, 0, 0)) for w in wo]
        ins += [(sel, (blk, 8), row_of(r))]
        return run(
            down_body, "down", (experts,), meta, ins, [((parts, blk, ds), BF16, None, None)],
            [pltpu.VMEM((parts, blk, ds), F32)], flops=2 * blk * experts * parts * ds * ff,
        )[0]

    def norm_back_body(low_precision_out, m, *refs):
        t_refs = refs[:4]
        after_ref = refs[4]
        up_refs = refs[5 : 5 + parts]
        gain_ref, router_ref, back = refs[5 + parts : 8 + parts]
        outs = refs[8 + parts :]
        small = outs[-1]
        for s in pieces:
            gain = gain_ref[s]
            router = router_ref[s].astype(F32)
            gain_sum = jnp.zeros((1, ds), F32)
            router_sum = [jnp.zeros((1, ds), F32)] * experts
            for r in range(4):
                if low_precision_out:
                    span_r = pl.ds(pl.multiple_of(m[2 + r] * blk, blk), blk)
                else:
                    span_r = slice(r * blk, (r + 1) * blk)
                up_value = up_refs[s][span_r, :] if low_precision_out else up_refs[0][s, span_r, :]
                x = after_ref[s, span_r, :].astype(F32)
                cols = back[span_r, :]
                rms = cols[:, experts + 1 : experts + 2]
                grad = t_refs[r][s].astype(F32)
                for e in range(experts):
                    grad += cols[:, e : e + 1] * router[e : e + 1]
                normed = x * rms
                token = (normed * gain).astype(BF16).astype(F32)
                gain_sum += jnp.sum(grad * normed, axis=0, keepdims=True)
                for e in range(experts):
                    router_sum[e] = router_sum[e] + jnp.sum(
                        token * cols[:, e : e + 1], axis=0, keepdims=True
                    )
                dn = grad * gain
                total = up_value.astype(F32) + rms * (
                    dn - normed * cols[:, experts : experts + 1]
                )
                if low_precision_out:
                    outs[0][s, span_r, :] = total
                    outs[1][s, span_r, :] = total.astype(BF16)
                else:
                    outs[0][s, span_r, :] = total.astype(BF16)
            for e in range(experts):
                small[e, s] = router_sum[e][0]
            small[experts, s] = gain_sum[0]

    ins = [(t, None, None) for t in dx_totals]
    ins += [(after, None, None)] + [(d, None, None) for d in d_pieces]
    ins += [(gain_f, None, None), (router_f, None, None), (back_f, None, None)]
    outs = [
        ((parts, rp, ds), F32, None, None),
        ((parts, rp, ds), BF16, None, None),
        ((experts + 1, parts, ds), F32, None, None),
    ]
    dafter, dafter_low, small_f = run(
        functools.partial(norm_back_body, True), "norm_back", (1,), meta, ins, outs
    )

    def whole_vectors(small):
        full = jnp.zeros((experts + 1, dp, ds), F32)
        for s in pieces:
            full = lax.dynamic_update_slice_in_dim(
                full, small[:, s : s + 1], g * parts + (c ^ s), axis=1
            )
        mask = 1
        while mask < dp:
            full = full + lax.ppermute(full, "dp", [(a, a ^ mask) for a in range(dp)])
            mask *= 2
        full = full.reshape(experts + 1, width)
        return full[:experts].T, full[experts]

    ffnrouter_grad, ffngain_grad = whole_vectors(small_f)

    def dmix_body(m, *refs):
        d_ref = refs[0]
        w_refs = refs[1 : 1 + parts]
        sel_ref = refs[1 + parts]
        outs = refs[2 + parts : 10 + parts]
        scr = refs[10 + parts]
        products = []
        for e in range(experts):
            products.append(sum(nt(d_ref[s], w_refs[s][e]) for s in pieces))
        low, high = two_slots(sel_ref[:, 0:1], sel_ref[:, 1:2], products)
        for k, value in enumerate((low, high)):
            value = value.astype(BF16)
            for h in range(heads):
                scr[h, :, k * HD : (k + 1) * HD] = value[:, h * HD : (h + 1) * HD]
        for r in range(4):
            block = scr[m[2 + r]]
            outs[2 * r][...] = block[:, :HD]
            outs[2 * r + 1][...] = block[:, HD:]

    ins = [(dafter_low, (parts, tile, ds), lambda i, m: (0, i, 0))]
    ins += [(w, None, None) for w in wp]
    ins += [(sel, (tile, 8), lambda i, m: (i, 0))]
    outs = [((rp, HD), BF16, (tile, HD), lambda i, m: (i, 0))] * 8
    dm = run(
        dmix_body, "dmix", (rp // tile,), meta, ins, outs,
        [pltpu.VMEM((heads, tile, 2 * HD), BF16)],
        flops=2 * rp * experts * parts * ds * hw,
    )
    dm_a, dm_b = reduce_groups(dm[0:8:2], dm[1:8:2])

    def attend_back_body(m, *refs):
        q_ref, kv_ref, halo_ref, sel_ref, cols, cos_ref, sin_ref = refs[:7]
        d_refs = (refs[7:10], refs[10:13])
        mix_refs = refs[13:15]
        dq_ref, own_ref, far_ref, dots_ref, ext, acc = refs[15:]
        i = pl.program_id(0)

        @pl.when(i == 0)
        def _():
            ext[:seq_len, :] = halo_ref[...]
            ext[seq_len:, :] = kv_ref[...]
            acc[...] = jnp.zeros_like(acc)

        near_rows = pl.ds(pl.multiple_of(i * qt, qt), span)
        near = ext[near_rows, :]
        allowed = window_mask(i, sel_ref[:, 4:5])
        line = lax.broadcasted_iota(jnp.int32, (8, qt), 0)
        inner = jnp.zeros((qt, HD), F32)
        found = []
        dk = jnp.zeros((span, HD), F32)
        dv = jnp.zeros((span, HD), F32)
        for k in range(2):
            query = q_ref[:, k * HD : (k + 1) * HD]
            probs = softmax_of(query, near[:, :HD], allowed)
            raw = sum(v[...].astype(F32) for v in d_refs[k])
            dmixed = (raw * cols[:, 1 + k : 2 + k]).astype(BF16)
            found.append(raw * mix_refs[k][...].astype(F32))
            dv += tn(probs.astype(BF16), dmixed)
            dprob = nt(dmixed, near[:, HD:])
            rest = jnp.sum(probs * dprob, axis=1, keepdims=True)
            dscore = (probs * (dprob - rest)).astype(BF16)
            dk += tn(dscore, query) * scale
            dquery = nn(dscore, near[:, :HD]) * scale
            inner += dquery * query.astype(F32)
            dq_ref[:, k * HD : (k + 1) * HD] = turn(dquery, cos_ref[...], -sin_ref[...]).astype(BF16)
        acc[near_rows, :HD] += dk
        acc[near_rows, HD:] += dv
        dots_ref[...] = jnp.where(
            line == 0, lane_sums(found[0]), jnp.where(line == 1, lane_sums(found[1]), lane_sums(inner))
        )

        @pl.when(i == rp // qt - 1)
        def _():
            far_ref[...] = acc[:seq_len, :]
            own_ref[...] = acc[seq_len:, :]

    ins = [(q_rot, (qt, 2 * HD), qrow), (kv_rot, None, None), (halo, None, None)]
    ins += [(sel, (qt, 8), qrow), (cols_a, (qt, 8), qrow)]
    ins += [(cosine, (qt, HD), qrow), (sine, (qt, HD), qrow)]
    ins += [(v, (qt, HD), qrow) for v in dm_a + dm_b + (mixed_a, mixed_b)]
    outs = [
        ((rp, 2 * HD), BF16, (qt, 2 * HD), qrow),
        ((rp, 2 * HD), F32, None, None),
        ((seq_len, 2 * HD), F32, None, None),
        ((8, rp), F32, (8, qt), lambda i, m: (0, i)),
    ]
    dq, dkv_own, dkv_far, dots_q = run(
        attend_back_body, "attend_back", (rp // qt,), meta, ins, outs,
        [pltpu.VMEM((seq_len + rp, 2 * HD), BF16), pltpu.VMEM((seq_len + rp, 2 * HD), F32)],
        flops=20 * rp * span * HD,
    )
    dkv_in = to_previous(dkv_far)

    def dkv_body(m, own_ref, in_ref, kv_ref, cos_ref, sin_ref, out_ref, dots_ref):
        head = rp - seq_len
        for rows_here in (slice(0, head), slice(head, rp)):
            value = own_ref[rows_here, :]
            if rows_here.start == head:
                value = value + in_ref[...]
            out_ref[rows_here, :HD] = turn(
                value[:, :HD], cos_ref[rows_here, :], -sin_ref[rows_here, :]
            ).astype(BF16)
            out_ref[rows_here, HD:] = value[:, HD:].astype(BF16)
            dots_ref[:, rows_here] = lane_sums(value * kv_ref[rows_here, :].astype(F32))

    ins = [(v, None, None) for v in (dkv_own, dkv_in, kv_rot, cosine, sine)]
    outs = [((rp, 2 * HD), BF16, None, None), ((8, rp), F32, None, None)]
    dkv, dots_kv = run(dkv_body, "dkv", (1,), meta, ins, outs)
    third = jnp.arange(8)[:, None] == 2
    dots_a = sum_z(sum_groups(dots_q + jnp.where(third, dots_kv, 0.0)))
    back_a = back_columns(flat_a, dots_a, low_a, high_a)
    da_a, da_b = gather_groups(dq, dkv)

    def place_heads(m, refs, lo, hi):
        for r in range(4):
            lanes = pl.ds(pl.multiple_of(m[2 + r] * HD, HD), HD)
            lo[:, lanes] = refs[r][:, :HD]
            hi[:, lanes] = refs[r][:, HD:]

    def dattn_body(m, *refs):
        a_refs, b_refs = refs[:4], refs[4:8]
        sel_ref = refs[8]
        q_refs = refs[9 : 9 + parts]
        kv_refs = refs[9 + parts : 9 + 2 * parts]
        out_ref, lo, hi, dk, dv = refs[9 + 2 * parts :]
        place_heads(m, a_refs, lo, hi)
        place_heads(m, b_refs, dk, dv)
        acc = [nt(dk[...], kv_refs[s][0]) + nt(dv[...], kv_refs[s][1]) for s in pieces]
        for e in range(experts):
            x = pick(sel_ref[:, 0:1], sel_ref[:, 1:2], e, lo[...], hi[...])
            for s in pieces:
                acc[s] += nt(x, q_refs[s][e])
        for s in pieces:
            out_ref[s] = acc[s].astype(BF16)

    def dattn(k):
        at_chunk = lambda i, m: (k, 0)
        ins = [(v, (zr, 2 * HD), at_chunk) for v in da_a + da_b]
        ins += [(sel, (zr, 8), at_chunk)]
        ins += [(w, None, None) for w in wq + wkv]
        return run(
            dattn_body, "dattn", (1,), meta, ins, [((parts, zr, ds), BF16, None, None)],
            [pltpu.VMEM((zr, hw), BF16)] * 4,
            flops=2 * zr * (experts + 2) * hw * parts * ds,
        )[0]

    da_totals = [wide_sum_z(dattn(k)) for k in range(chunks)]
    x_stack = jnp.stack(x_pieces)
    ins = [(t, None, None) for t in da_totals]
    ins += [(x_stack, None, None)] + [(dafter, None, None)] * parts
    ins += [(gain_a, None, None), (router_a, None, None), (back_a, None, None)]
    outs = [((parts, rp, ds), BF16, None, None), ((experts + 1, parts, ds), F32, None, None)]
    dinput, small_a = run(
        functools.partial(norm_back_body, False), "norm_back_first", (1,), meta, ins, outs
    )
    attnrouter_grad, attngain_grad = whole_vectors(small_a)

    def exchange(grad_of):
        received = [by_part(grad_of(s, None), s) for s in pieces[1:]]
        return grad_of(0, received)

    ffn_input = (after * flat_f[0][None, :, None] * gain_f).astype(BF16)
    attn_input = (x_stack.astype(F32) * flat_a[0][None, :, None] * gain_a).astype(BF16)

    def dwin_body(count, m, *refs):
        a_refs, b_refs = refs[:4], refs[4:8]
        sel_ref, x_ref = refs[8:10]
        add_refs = refs[10 : 10 + count]
        out_ref, xs, ids, mt = refs[10 + count :]
        j, e = pl.program_id(0), pl.program_id(1)

        @pl.when((j == 0) & (e == 0))
        def _():
            for r in range(4):
                src = pl.ds(pl.multiple_of(m[2 + r] * blk, blk), blk)
                xs[r * blk : (r + 1) * blk, :] = x_ref[0, src, :]
                ids[r * blk : (r + 1) * blk, :] = sel_ref[src, :]

        expert = e.astype(F32)
        for r in range(4):
            here_r = slice(r * blk, (r + 1) * blk)
            mt[here_r, :] = pick(
                ids[here_r, 2:3], ids[here_r, 3:4], expert, a_refs[r][0], b_refs[r][0]
            )
        acc = tn(xs[...], mt[...])
        for ref in add_refs:
            acc = acc + ref[0, 0].astype(F32)
        out_ref[0, 0] = acc.astype(out_ref.dtype)

    def dwin(s, received):
        adds = received or []
        spot = lambda j, e, m: (e, j, 0, 0)
        ins = [(v, (1, blk, ff), lambda j, e, m: (1 + j, 0, 0)) for v in ag_a + ag_b]
        ins += [(sel, None, None), (ffn_input, (1, rp, ds), lambda j, e, m: (s, 0, 0))]
        ins += [(v, (1, 1, ds, ff), spot) for v in adds]
        dtype = BF16 if received is None else F32
        outs = [((experts, 2, ds, ff), dtype, (1, 1, ds, ff), spot)]
        return run(
            functools.partial(dwin_body, len(adds)), "dwin", (2, experts), meta, ins, outs,
            [pltpu.VMEM((rp, ds), BF16), pltpu.VMEM((rp, 8), F32), pltpu.VMEM((rp, ff), BF16)],
            flops=4 * rp * experts * ds * ff,
        )[0]

    def dwout_body(count, m, *refs):
        a_refs, b_refs = refs[:4], refs[4:8]
        sel_ref, d_ref = refs[8:10]
        add_refs = refs[10 : 10 + count]
        out_ref, xs, ids, mt = refs[10 + count :]
        e = pl.program_id(0)

        @pl.when(e == 0)
        def _():
            for r in range(4):
                src = pl.ds(pl.multiple_of(m[2 + r] * blk, blk), blk)
                xs[r * blk : (r + 1) * blk, :] = d_ref[src, :]
                ids[r * blk : (r + 1) * blk, :] = sel_ref[src, :]

        expert = e.astype(F32)
        for r in range(4):
            here_r = slice(r * blk, (r + 1) * blk)
            mt[here_r, :] = pick(
                ids[here_r, 2:3], ids[here_r, 3:4], expert, a_refs[r][0], b_refs[r][0]
            )
        acc = tn(mt[...], xs[...])
        for ref in add_refs:
            acc = acc + ref[0].astype(F32)
        out_ref[0] = acc.astype(out_ref.dtype)

    def dwout(s, received):
        adds = received or []
        spot = lambda e, m: (e, 0, 0)
        ins = [(v, (1, blk, ff), lambda e, m: (0, 0, 0)) for v in ag_a + ag_b]
        ins += [(sel, None, None), (d_pieces[s], None, None)]
        ins += [(v, (1, ff, ds), spot) for v in adds]
        dtype = BF16 if received is None else F32
        outs = [((experts, ff, ds), dtype, (1, ff, ds), spot)]
        return run(
            functools.partial(dwout_body, len(adds)), "dwout", (experts,), meta, ins, outs,
            [pltpu.VMEM((rp, ds), BF16), pltpu.VMEM((rp, 8), F32), pltpu.VMEM((rp, ff), BF16)],
            flops=2 * rp * experts * ds * ff,
        )[0]

    def dwproj_body(count, m, *refs):
        a_refs, b_refs = refs[:4], refs[4:8]
        sel_ref, d_ref = refs[8:10]
        add_refs = refs[10 : 10 + count]
        out_ref, lo, hi = refs[10 + count :]
        e = pl.program_id(0)

        @pl.when(e == 0)
        def _():
            for r in range(4):
                lanes = pl.ds(pl.multiple_of(m[2 + r] * HD, HD), HD)
                lo[:, lanes] = a_refs[r][...]
                hi[:, lanes] = b_refs[r][...]

        x = pick(sel_ref[:, 0:1], sel_ref[:, 1:2], e.astype(F32), lo[...], hi[...])
        acc = tn(x, d_ref[0])
        for ref in add_refs:
            acc = acc + ref[0].astype(F32)
        out_ref[0] = acc.astype(out_ref.dtype)

    def dwproj(s, received):
        adds = received or []
        spot = lambda e, m: (e, 0, 0)
        ins = [(v, None, None) for v in gm_a + gm_b]
        ins += [(sel, None, None), (dafter_low, (1, rp, ds), lambda e, m: (s, 0, 0))]
        ins += [(v, (1, hw, ds), spot) for v in adds]
        dtype = BF16 if received is None else F32
        return run(
            functools.partial(dwproj_body, len(adds)), "dwproj", (experts,), meta, ins,
            [((experts, hw, ds), dtype, (1, hw, ds), spot)],
            [pltpu.VMEM((rp, hw), BF16)] * 2,
            flops=2 * rp * experts * hw * ds,
        )[0]

    def dwqkv_body(count, m, *refs):
        a_refs, b_refs = refs[:4], refs[4:8]
        sel_ref, x_ref = refs[8:10]
        add_q, add_kv = refs[10 : 10 + count], refs[10 + count : 10 + 2 * count]
        q_ref, kv_ref, lo, hi, dk, dv = refs[10 + 2 * count :]
        e = pl.program_id(0)

        @pl.when(e == 0)
        def _():
            place_heads(m, a_refs, lo, hi)
            place_heads(m, b_refs, dk, dv)

        @pl.when(e < experts)
        def _():
            x = pick(sel_ref[:, 0:1], sel_ref[:, 1:2], e.astype(F32), lo[...], hi[...])
            acc = tn(x_ref[0], x)
            for ref in add_q:
                acc = acc + ref[0].astype(F32)
            q_ref[0] = acc.astype(q_ref.dtype)

        for k, grad in enumerate((dk, dv)):

            @pl.when(e == experts + k)
            def _():
                acc = tn(x_ref[0], grad[...])
                for ref in add_kv:
                    acc = acc + ref[0].astype(F32)
                kv_ref[0] = acc.astype(kv_ref.dtype)

    def dwqkv(s, received):
        adds_q = [v[0] for v in received or []]
        adds_kv = [v[1] for v in received or []]
        q_spot = lambda e, m: (jnp.minimum(e, experts - 1), 0, 0)
        kv_spot = lambda e, m: (jnp.maximum(e - experts, 0), 0, 0)
        ins = [(v, None, None) for v in da_a + da_b]
        ins += [(sel, None, None), (attn_input, (1, rp, ds), lambda e, m: (s, 0, 0))]
        ins += [(v, (1, ds, hw), q_spot) for v in adds_q]
        ins += [(v, (1, ds, hw), kv_spot) for v in adds_kv]
        dtype = BF16 if received is None else F32
        outs = [
            ((experts, ds, hw), dtype, (1, ds, hw), q_spot),
            ((2, ds, hw), dtype, (1, ds, hw), kv_spot),
        ]
        return run(
            functools.partial(dwqkv_body, len(adds_q)), "dwqkv", (experts + 2,), meta, ins, outs,
            [pltpu.VMEM((rp, hw), BF16)] * 4,
            flops=2 * rp * (experts + 2) * hw * ds,
        )

    expertout_grad = exchange(dwout)
    expertin_grad = exchange(dwin).swapaxes(1, 2)
    proj_grad = exchange(dwproj)
    sent = [tuple(by_part(v, s) for v in dwqkv(s, None)) for s in pieces[1:]]
    query_grad, kv_grad = dwqkv(0, sent)

    down_totals = [wide_sum_z(down(r)) for r in range(4)]

    def finish_body(m, *refs):
        t_refs, after_ref, out_ref = refs[:4], refs[4], refs[5]
        for r in range(4):
            span_r = pl.ds(pl.multiple_of(m[2 + r] * blk, blk), blk)
            for s in pieces:
                out_ref[s, span_r, :] = (
                    after_ref[s, span_r, :] + t_refs[r][s].astype(F32)
                ).astype(BF16)

    ins = [(t, None, None) for t in down_totals] + [(after, None, None)]
    out_rows = run(
        finish_body, "finish", (1,), meta, ins, [((parts, rp, ds), BF16, None, None)]
    )[0]

    place = jnp.arange(seq_len, dtype=jnp.int32).reshape(dp, 1, per)
    seq_ids = jnp.arange(seqs, dtype=jnp.int32).reshape(1, seqs, 1)
    valid = place < lengths.reshape(1, seqs, 1)
    packed = jnp.where(valid, starts.reshape(1, seqs, 1) + place, 0)
    from_row = (((packed // rp) ^ c) * rp + packed % rp).reshape(-1)
    cot_row = (inverse.reshape(1, seqs, 1) * seq_len + place).reshape(-1)
    valid = valid.reshape(-1)[:, None]

    def unpack(value, otherwise):
        mine_all = [value[0]] + [by_part(value[s], s) for s in pieces[1:]]
        spread_rows = jnp.concatenate(mine_all, axis=0)[from_row]
        spread_rows = jnp.where(valid, spread_rows, otherwise)
        landed = lax.all_to_all(
            spread_rows.reshape(dp, seqs * per, ds), "dp", 0, 0, tiled=True
        )
        return landed.transpose(1, 0, 2).reshape(seqs, per, width)

    layer_out = unpack(out_rows, x_all)
    input_grad = unpack(dinput, d_all[cot_row])
    return (
        layer_out,
        input_grad,
        attngain_grad,
        attnrouter_grad,
        kv_grad,
        query_grad,
        proj_grad,
        ffngain_grad,
        ffnrouter_grad,
        expertin_grad,
        expertout_grad,
    )


def solution(mesh):
    placed = (
        P(None, "dp", None),
        P("dp", None, None),
        P(),
        P(),
        P(),
        P(),
        P(),
        P(),
        P(None, "dp", "tensor"),
        P(None, "dp", "tensor"),
        P(None, "tensor", "dp"),
        P(),
        P(),
        P(None, "dp", None, "tensor"),
        P(None, "tensor", "dp"),
    )
    return jax.shard_map(
        functools.partial(local, dp=mesh.shape["dp"], tp=mesh.shape["tensor"]),
        mesh=mesh,
        in_specs=placed,
        out_specs=(
            P(None, "dp", None),
            P(None, "dp", None),
            P(),
            P(),
            P(None, "dp", "tensor"),
            P(None, "dp", "tensor"),
            P(None, "tensor", "dp"),
            P(),
            P(),
            P(None, "dp", None, "tensor"),
            P(None, "tensor", "dp"),
        ),
        check_vma=False,
    )
```

```python
import functools

import jax
import jax.numpy as jnp
from jax import lax
from jax.experimental import pallas as pl
from jax.experimental.pallas import tpu as pltpu
from jax.sharding import PartitionSpec as P

HD = 128
EPSILON = 1e-06
ROPE_BASE = 10000.0
BEST = lax.Precision.HIGHEST
F32 = jnp.float32
BF16 = jnp.bfloat16
VMEM_BYTES = 60 * 1024 * 1024


def nn(a, b):
    return lax.dot_general(a, b, (((1,), (0,)), ((), ())), preferred_element_type=F32)


def nt(a, b, precision=None):
    return lax.dot_general(
        a, b, (((1,), (1,)), ((), ())), preferred_element_type=F32, precision=precision
    )


def tn(a, b):
    return lax.dot_general(a, b, (((0,), (0,)), ((), ())), preferred_element_type=F32)


def lane_sums(values):
    ones = jnp.ones((8, values.shape[1]), F32)
    return nt(ones, values, BEST)


def run(body, name, grid, meta, ins, outs, scratch=(), flops=0):
    in_specs = []
    moved = 0
    for array, block, index in ins:
        if block is None:
            rank = array.ndim
            in_specs.append(pl.BlockSpec(array.shape, lambda *a, rank=rank: (0,) * rank))
        else:
            in_specs.append(pl.BlockSpec(block, index))
        moved += array.size * array.dtype.itemsize
    out_specs = []
    out_shape = []
    for shape, dtype, block, index in outs:
        if block is None:
            rank = len(shape)
            out_specs.append(pl.BlockSpec(shape, lambda *a, rank=rank: (0,) * rank))
        else:
            out_specs.append(pl.BlockSpec(block, index))
        out_shape.append(jax.ShapeDtypeStruct(shape, dtype))
        size = jnp.dtype(dtype).itemsize
        for extent in shape:
            size *= extent
        moved += size
    return pl.pallas_call(
        body,
        name=name,
        grid_spec=pltpu.PrefetchScalarGridSpec(
            num_scalar_prefetch=1,
            grid=grid,
            in_specs=in_specs,
            out_specs=out_specs,
            scratch_shapes=list(scratch),
        ),
        out_shape=out_shape,
        compiler_params=pltpu.CompilerParams(
            dimension_semantics=("arbitrary",) * len(grid), vmem_limit_bytes=VMEM_BYTES
        ),
        cost_estimate=pl.CostEstimate(flops=flops, bytes_accessed=moved, transcendentals=0),
    )(meta, *[array for array, _, _ in ins])


def pick(low_id, high_id, expert, low_value, high_value):
    zero = jnp.zeros_like(low_value)
    return jnp.where(
        low_id == expert, low_value, jnp.where(high_id == expert, high_value, zero)
    )


def two_slots(low_id, high_id, products):
    low_value = products[0]
    for expert in range(1, len(products) - 1):
        low_value = jnp.where(low_id == expert, products[expert], low_value)
    high_value = products[1]
    for expert in range(2, len(products)):
        high_value = jnp.where(high_id == expert, products[expert], high_value)
    return low_value, high_value


def turn(values, cosine, sine):
    return values * cosine + pltpu.roll(values, HD // 2, 1) * sine


def local(
    hidden_in,
    cotangent,
    lengths,
    dealing,
    attn_routes,
    ffn_routes,
    attn_gain,
    attn_router,
    kv_weight,
    query_weight,
    proj_weight,
    ffn_gain,
    ffn_router,
    expert_in,
    expert_out,
    *,
    dp,
    tp,
):
    seqs = dealing.shape[0]
    seq_len = cotangent.shape[1]
    held = cotangent.shape[0]
    per = hidden_in.shape[1]
    width = hidden_in.shape[2]
    heads = query_weight.shape[2] // HD
    groups = heads
    parts = dp // groups
    ds = width // dp
    hw = heads * HD
    rows_all = seqs * seq_len
    rows = rows_all * 3 // 4
    rp = rows // parts
    blk = rp // groups
    experts = query_weight.shape[0]
    ff = expert_out.shape[1]
    scale = HD ** (-0.5)
    pieces = range(parts)

    index = lax.axis_index("dp")
    z = lax.axis_index("tensor")
    g = index // parts
    c = index % parts
    mine = ((z == 1) | (z == 2)).astype(jnp.int32)
    theirs = 1 - mine
    spots = [g, c, g, g ^ 1, g ^ 2, g ^ 3, mine, theirs]
    spots += [g ^ mine, g ^ theirs, g ^ (2 + mine), g ^ (2 + theirs)]
    spots += [g ^ (2 * mine), g ^ (2 * mine + 1), g ^ (2 * theirs), g ^ (2 * theirs + 1)]
    spots += [mine, theirs, 2 + mine, 2 + theirs]
    meta = jnp.stack(spots).astype(jnp.int32)
    BY_CHUNK, BY_HALF, IN_ORDER = 8, 12, 16

    def after(value, *others):
        return lax.optimization_barrier((value,) + others)[0]

    def both(a, b):
        return (a.astype(F32) + b.astype(F32)).astype(BF16)

    def by_group(value, mask):
        pairs = [(a, ((a // parts) ^ mask) * parts + a % parts) for a in range(dp)]
        return lax.ppermute(value, "dp", pairs)

    def by_part(value, mask):
        pairs = [(a, (a // parts) * parts + ((a % parts) ^ mask)) for a in range(dp)]
        return lax.ppermute(value, "dp", pairs)

    def to_next(value):
        pairs = [(a, a + 1) for a in range(dp) if a % parts < parts - 1]
        return lax.ppermute(value, "dp", pairs)

    def to_previous(value):
        pairs = [(a, a - 1) for a in range(dp) if a % parts > 0]
        return lax.ppermute(value, "dp", pairs)

    def by_z(value, mask):
        return lax.ppermute(value, "tensor", [(a, a ^ mask) for a in range(tp)])

    def sum_groups(value):
        value = value + by_group(value, 1)
        return value + by_group(value, 2)

    def sum_z(value):
        value = value + by_z(value, 1)
        return value + by_z(value, 3)

    def wide_sum_z(keep, send):
        half = both(keep, by_z(send, 1))
        half = both(half, by_z(half, 3))
        return half, by_z(half, 1)

    def reduce_groups(first, second):
        ra = by_group(first[3], 1)
        rb = by_group(second[3], 2)
        ax = by_group(first[1], 1)
        by = by_group(second[2], 2)
        ay = by_group(both(first[2], ra), 2)
        bx = by_group(both(second[1], rb), 1)
        return (first[0], ax, ay), (second[0], bx, by)

    def gather_groups(first, second):
        ax, bx = by_group(first, 1), by_group(second, 1)
        ay, by = by_group(first, 2), by_group(second, 2)
        ad, bd = by_group(ax, 2), by_group(by, 1)
        return (first, ax, ay, ad), (second, bx, by, bd)

    def row_of(offset):
        return lambda *a: (a[-1][2 + offset], 0)

    def at_row(m, spot, count):
        return pl.ds(pl.multiple_of(m[spot] * count, count), count)

    wide = ds % 128 == 0

    def nn_pieces(x, weights):
        if not wide:
            return [nn(x, w) for w in weights]
        value = nn(x, jnp.concatenate(weights, axis=1))
        return [value[:, s * ds : (s + 1) * ds] for s in pieces]

    def nt_pieces(x, weights):
        if not wide:
            return [nt(x, w) for w in weights]
        value = nt(x, jnp.concatenate(weights, axis=0))
        return [value[:, s * ds : (s + 1) * ds] for s in pieces]

    ends = jnp.cumsum(lengths)
    starts = ends - lengths
    inverse = jnp.sum(
        (dealing[None, :] == jnp.arange(seqs, dtype=jnp.int32)[:, None])
        * jnp.arange(seqs, dtype=jnp.int32)[None, :],
        axis=1,
    )

    def places(part):
        packed = part * rp + jnp.arange(rp, dtype=jnp.int32)
        begun = starts[None, :] <= packed[:, None]
        first = jnp.max(jnp.where(begun, starts[None, :], 0), axis=1)
        seq = jnp.sum(begun.astype(jnp.int32), axis=1) - 1
        at = packed - first
        slot = jnp.sum(
            jnp.where(seq[:, None] == jnp.arange(seqs, dtype=jnp.int32)[None, :], inverse[None, :], 0),
            axis=1,
        )
        x_row = (at // per) * (seqs * per) + seq * per + at % per
        d_row = slot * seq_len + at
        return seq, at, first, x_row, d_row

    seq, at, first, x_row, d_row = places(c)

    x_send = hidden_in.reshape(seqs * per, dp, ds).transpose(1, 0, 2)
    x_all = lax.all_to_all(x_send, "dp", 0, 0, tiled=True).reshape(rows_all, ds)
    d_send = cotangent.reshape(held * seq_len, dp, ds).transpose(1, 0, 2)
    d_all = lax.all_to_all(d_send, "dp", 0, 0, tiled=True).reshape(rows_all, ds)
    x_pieces = [x_all[x_row]]
    d_pieces = [d_all[d_row]]
    for s in pieces[1:]:
        _, _, _, other_x, other_d = places(c ^ s)
        x_pieces.append(by_part(x_all[other_x], s))
        d_pieces.append(by_part(d_all[other_d], s))

    def spread(vector):
        tall = vector.reshape((groups, parts, ds) + vector.shape[1:])[g]
        return jnp.stack([tall[c ^ s] for s in pieces])

    gain_a = spread(attn_gain)[:, None, :]
    gain_f = spread(ffn_gain)[:, None, :]
    pad = ((0, 0), (0, 8 - experts), (0, 0))
    router_a = jnp.pad(spread(attn_router).transpose(0, 2, 1), pad)
    router_f = jnp.pad(spread(ffn_router).transpose(0, 2, 1), pad)

    in_own = expert_in.swapaxes(1, 2)
    wq = [query_weight] + [by_part(query_weight, s) for s in pieces[1:]]
    wkv = [kv_weight] + [by_part(kv_weight, s) for s in pieces[1:]]
    wp = [proj_weight] + [by_part(proj_weight, s) for s in pieces[1:]]
    wo = [expert_out] + [by_part(expert_out, s) for s in pieces[1:]]
    wi = [in_own] + [by_part(in_own, s) for s in pieces[1:]]

    routes = jnp.concatenate(
        [attn_routes.reshape(rows_all, 2), ffn_routes.reshape(rows_all, 2)], axis=1
    )
    here = (seq * seq_len + at)[:, None] == jnp.arange(rows_all, dtype=jnp.int32)[None, :]
    mine = jnp.dot(here.astype(BF16), routes.astype(BF16), preferred_element_type=F32)
    low_a, high_a = jnp.minimum(mine[:, 0], mine[:, 1]), jnp.maximum(mine[:, 0], mine[:, 1])
    low_f, high_f = jnp.minimum(mine[:, 2], mine[:, 3]), jnp.maximum(mine[:, 2], mine[:, 3])
    window = (first - c * rp + seq_len).astype(F32)
    nil = jnp.zeros_like(window)
    sel = jnp.stack([low_a, high_a, low_f, high_f, window, nil, nil, nil], axis=1)
    half = HD // 2
    frequency = ROPE_BASE ** (-2.0 * jnp.arange(half, dtype=F32) / HD)
    angles = at.astype(F32)[:, None] * frequency[None, :]
    cosine = jnp.concatenate([jnp.cos(angles)] * 2, axis=1)
    sine = jnp.sin(angles)
    sine = jnp.concatenate([-sine, sine], axis=1)

    def gate_columns(stats, low_id, high_id):
        rms = lax.rsqrt(stats[experts] / width + EPSILON)
        ids = jnp.arange(experts, dtype=F32)[:, None]
        logits = stats[:experts]
        low_logit = jnp.sum(jnp.where(low_id[None] == ids, logits, 0.0), axis=0) * rms
        high_logit = jnp.sum(jnp.where(high_id[None] == ids, logits, 0.0), axis=0) * rms
        gap = low_logit - high_logit
        low_gate, high_gate = jax.nn.sigmoid(gap), jax.nn.sigmoid(-gap)
        zero = jnp.zeros_like(rms)
        flat = jnp.stack([rms, low_gate, high_gate, gap, zero, zero, zero, zero])
        return flat, flat.T

    def rows_pair(refs):
        return jnp.concatenate([ref[...] for ref in refs], axis=0)

    def dhidden_body(m, *refs):
        d_refs = refs[: 2 * parts]
        w_refs, sel_refs = refs[2 * parts : 3 * parts], refs[3 * parts : 3 * parts + 2]
        outs = refs[3 * parts + 2 :]
        ids = rows_pair(sel_refs)
        rows_of = [rows_pair(d_refs[2 * s : 2 * s + 2]) for s in pieces]
        products = []
        for e in range(experts):
            products.append(sum(nt(rows_of[s], w_refs[s][e]) for s in pieces))
        low, high = two_slots(ids[:, 2:3], ids[:, 3:4], products)
        low, high = low.astype(BF16), high.astype(BF16)
        for step, pair in enumerate(((3, 1), (2, 0))):

            @pl.when(pl.program_id(0) == step)
            def _():
                for k, r in enumerate(pair):
                    outs[2 * r][...] = low[k * blk : (k + 1) * blk]
                    outs[2 * r + 1][...] = high[k * blk : (k + 1) * blk]

    def dhidden(meta):
        spots = [lambda i, m: (m[5 - i], 0), lambda i, m: (m[3 - i], 0)]
        ins = [(d, (blk, ds), spot) for d in d_pieces for spot in spots]
        ins += [(w, None, None) for w in wo]
        ins += [(sel, (blk, 8), spot) for spot in spots]
        outs = [((blk, ff), BF16, None, None)] * 8
        return run(
            dhidden_body, "dhidden", (2,), meta, ins, outs,
            flops=2 * rp * experts * parts * ds * ff,
        )

    tile = 256

    def qkv_body(m, *refs):
        x_refs = refs[:parts]
        gain_ref, router_ref = refs[parts : parts + 2]
        q_refs = refs[parts + 2 : 2 * parts + 2]
        kv_refs = refs[2 * parts + 2 : 3 * parts + 2]
        sel_ref = refs[3 * parts + 2]
        outs = refs[3 * parts + 3 : 3 * parts + 11]
        stats_ref, scr = refs[3 * parts + 11 :]
        us = []
        logits = jnp.zeros((8, tile), F32)
        squares = jnp.zeros((8, tile), F32)
        for s in pieces:
            xf = x_refs[s][...].astype(F32)
            us.append((xf * gain_ref[s]).astype(BF16))
            logits += nt(router_ref[s], us[s])
            squares += lane_sums(xf * xf)
        line = lax.broadcasted_iota(jnp.int32, (8, tile), 0)
        stats_ref[...] = jnp.where(line < experts, logits, squares)
        products = []
        for e in range(experts):
            products.append(sum(nn(us[s], q_refs[s][e]) for s in pieces))
        low, high = two_slots(sel_ref[:, 0:1], sel_ref[:, 1:2], products)
        keys = sum(nn(us[s], kv_refs[s][0]) for s in pieces)
        values = sum(nn(us[s], kv_refs[s][1]) for s in pieces)
        for k, value in enumerate((low, high, keys, values)):
            value = value.astype(BF16)
            for h in range(heads):
                scr[h, :, k * HD : (k + 1) * HD] = value[:, h * HD : (h + 1) * HD]
        for r in range(4):
            block = scr[m[2 + r]]
            outs[2 * r][...] = block[:, : 2 * HD]
            outs[2 * r + 1][...] = block[:, 2 * HD :]

    ins = [(x, (tile, ds), lambda i, m: (i, 0)) for x in x_pieces]
    ins += [(gain_a, None, None), (router_a, None, None)]
    ins += [(w, None, None) for w in wq + wkv]
    ins += [(sel, (tile, 8), lambda i, m: (i, 0))]
    outs = [((rp, 2 * HD), BF16, (tile, 2 * HD), lambda i, m: (i, 0))] * 8
    outs += [((8, rp), F32, (8, tile), lambda i, m: (0, i))]
    qkv = run(
        qkv_body, "qkv", (rp // tile,), meta, ins, outs,
        [pltpu.VMEM((heads, tile, 4 * HD), BF16)],
        flops=2 * rp * (experts + 2) * parts * ds * hw,
    )
    dh = dhidden(after(meta, qkv[8]))
    q_sum, kv_sum = reduce_groups(qkv[0:8:2], qkv[1:8:2])
    dh_a, dh_b = reduce_groups(dh[0:8:2], dh[1:8:2])
    stats_a = sum_groups(qkv[8])
    flat_a, cols_a = gate_columns(stats_a, low_a, high_a)

    def rope_body(m, a0, a1, a2, b0, b1, b2, cols, cos_ref, sin_ref, q_ref, kv_ref):
        rms = cols[:, 0:1]
        cos, sin = cos_ref[...], sin_ref[...]
        q = (a0[...].astype(F32) + a1[...].astype(F32) + a2[...].astype(F32)) * rms
        kv = (b0[...].astype(F32) + b1[...].astype(F32) + b2[...].astype(F32)) * rms
        q_ref[:, :HD] = turn(q[:, :HD], cos, sin).astype(BF16)
        q_ref[:, HD:] = turn(q[:, HD:], cos, sin).astype(BF16)
        kv_ref[:, :HD] = turn(kv[:, :HD], cos, sin).astype(BF16)
        kv_ref[:, HD:] = kv[:, HD:].astype(BF16)

    ins = [(v, (tile, 2 * HD), lambda i, m: (i, 0)) for v in q_sum + kv_sum]
    ins += [(cols_a, (tile, 8), lambda i, m: (i, 0))]
    ins += [(v, (tile, HD), lambda i, m: (i, 0)) for v in (cosine, sine)]
    outs = [((rp, 2 * HD), BF16, (tile, 2 * HD), lambda i, m: (i, 0))] * 2
    q_rot, kv_rot = run(rope_body, "rope", (rp // tile,), meta, ins, outs)
    halo = to_next(kv_rot[rp - seq_len :])

    qt = 128
    span = seq_len + qt

    def window_mask(i, low_key):
        u = i * qt + lax.broadcasted_iota(jnp.int32, (qt, span), 1)
        t = seq_len + i * qt + lax.broadcasted_iota(jnp.int32, (qt, span), 0)
        return (u >= low_key.astype(jnp.int32)) & (u <= t)

    def softmax_of(query, key, allowed):
        score = jnp.where(allowed, nt(query, key) * scale, -1e30)
        top = jnp.max(score, axis=1, keepdims=True)
        raised = jnp.exp(score - top)
        return raised / jnp.sum(raised, axis=1, keepdims=True)

    def attend_body(m, q_ref, kv_ref, halo_ref, sel_ref, cols, ga, gb, ma, mb, ext):
        i = pl.program_id(0)

        @pl.when(i == 0)
        def _():
            ext[:seq_len, :] = halo_ref[...]
            ext[seq_len:, :] = kv_ref[...]

        near = ext[pl.ds(pl.multiple_of(i * qt, qt), span), :]
        allowed = window_mask(i, sel_ref[:, 4:5])
        for k, (g_ref, m_ref) in enumerate(((ga, ma), (gb, mb))):
            probs = softmax_of(q_ref[:, k * HD : (k + 1) * HD], near[:, :HD], allowed)
            mixed = nn(probs.astype(BF16), near[:, HD:]).astype(BF16)
            m_ref[...] = mixed
            g_ref[...] = (mixed.astype(F32) * cols[:, 1 + k : 2 + k]).astype(BF16)

    def qrow(i, m):
        return (i, 0)

    ins = [(q_rot, (qt, 2 * HD), qrow), (kv_rot, None, None), (halo, None, None)]
    ins += [(sel, (qt, 8), qrow), (cols_a, (qt, 8), qrow)]
    outs = [((rp, HD), BF16, (qt, HD), qrow)] * 4
    gated_a, gated_b, mixed_a, mixed_b = run(
        attend_body, "attend", (rp // qt,), meta, ins, outs,
        [pltpu.VMEM((seq_len + rp, 2 * HD), BF16)],
        flops=8 * rp * span * HD,
    )
    gm_a, gm_b = gather_groups(gated_a, gated_b)

    chunks = 2
    zr = rp // chunks // 2
    hold = [((parts, zr, ds), BF16, None, None)] * 2

    def store_halves(i, refs, s, value):
        @pl.when(i == 0)
        def _():
            refs[1][s] = value

        @pl.when(i == 1)
        def _():
            refs[0][s] = value

    def proj_body(m, *refs):
        a_refs, b_refs = refs[:4], refs[4:8]
        sel_ref = refs[8]
        w_refs = refs[9 : 9 + parts]
        outs, xs = refs[9 + parts : 11 + parts], refs[11 + parts]
        for r in range(4):
            lanes = pl.ds(pl.multiple_of(m[2 + r] * HD, HD), HD)
            for e in range(experts):
                xs[e, :, lanes] = pick(
                    sel_ref[:, 0:1], sel_ref[:, 1:2], e, a_refs[r][...], b_refs[r][...]
                )
        acc = nn_pieces(xs[0], [w[0] for w in w_refs])
        for e in range(1, experts):
            for s, value in enumerate(nn_pieces(xs[e], [w[e] for w in w_refs])):
                acc[s] += value
        for s in pieces:
            store_halves(pl.program_id(0), outs, s, acc[s].astype(BF16))

    def project(k):
        half = lambda i, m: (2 * k + m[7 - i], 0)
        ins = [(v, (zr, HD), half) for v in gm_a + gm_b]
        ins += [(sel, (zr, 8), half)]
        ins += [(w, None, None) for w in wp]
        return run(
            proj_body, "proj", (2,), meta, ins, hold,
            [pltpu.VMEM((experts, zr, hw), BF16)],
            flops=4 * zr * experts * hw * parts * ds,
        )

    attn_totals = [half for k in range(chunks) for half in wide_sum_z(*project(k))]

    def norm_body(m, *refs):
        t_refs = refs[: 2 * chunks]
        x_refs = refs[2 * chunks : 2 * chunks + parts]
        gain_ref, router_ref, after_ref, u_ref, stats_ref = refs[2 * chunks + parts :]
        for k in range(2 * chunks):
            span_k = at_row(m, IN_ORDER + k, zr)
            for s in pieces:
                after_ref[s, span_k, :] = x_refs[s][span_k, :].astype(F32) + t_refs[k][s].astype(F32)
        logits = jnp.zeros((8, rp), F32)
        squares = jnp.zeros((8, rp), F32)
        for s in pieces:
            af = after_ref[s]
            u = (af * gain_ref[s]).astype(BF16)
            u_ref[s] = u
            logits += nt(router_ref[s], u)
            squares += lane_sums(af * af)
        line = lax.broadcasted_iota(jnp.int32, (8, rp), 0)
        stats_ref[...] = jnp.where(line < experts, logits, squares)

    ins = [(t, None, None) for t in attn_totals + x_pieces]
    ins += [(gain_f, None, None), (router_f, None, None)]
    outs = [
        ((parts, rp, ds), F32, None, None),
        ((parts, rp, ds), BF16, None, None),
        ((8, rp), F32, None, None),
    ]
    after_rows, u_f, stats_part = run(norm_body, "norm", (1,), meta, ins, outs)
    stats_f = sum_groups(stats_part)
    flat_f, cols_f = gate_columns(stats_f, low_f, high_f)

    def up_body(m, *refs):
        u_refs, w_refs = refs[:2], refs[2 : 2 + parts]
        sel_refs = refs[2 + parts : 4 + parts]
        outs = refs[4 + parts :]
        ids = rows_pair(sel_refs)
        rows_of = [jnp.concatenate([u[s] for u in u_refs], axis=0) for s in pieces]
        products = []
        for e in range(experts):
            products.append(sum(nn(rows_of[s], w_refs[s][e, 0]) for s in pieces))
        low, high = two_slots(ids[:, 2:3], ids[:, 3:4], products)
        low, high = low.astype(BF16), high.astype(BF16)
        for k in range(2):
            outs[2 * k][0] = low[k * blk : (k + 1) * blk]
            outs[2 * k + 1][0] = high[k * blk : (k + 1) * blk]

    def up(pair, meta):
        def block_of(r):
            return lambda j, m: (0, m[2 + r], 0)

        ins = [(u_f, (parts, blk, ds), block_of(r)) for r in pair]
        ins += [(w, (experts, 1, ds, ff), lambda j, m: (0, j, 0, 0)) for w in wi]
        ins += [(sel, (blk, 8), row_of(r)) for r in pair]
        outs = [((2, blk, ff), BF16, (1, blk, ff), lambda j, m: (j, 0, 0))] * 4
        return run(
            up_body, "up", (2,), meta, ins, outs, flops=8 * blk * experts * parts * ds * ff
        )

    up_far = up((3, 1), meta)
    up_near = up((2, 0), after(meta, up_far[0]))
    gu_a, gu_b = reduce_groups(
        (up_near[2], up_far[2], up_near[0], up_far[0]),
        (up_near[3], up_far[3], up_near[1], up_far[1]),
    )

    mt_rows = blk // 3

    def mid_body(m, *refs):
        gu = (refs[0:3], refs[3:6])
        dhr = (refs[6:9], refs[9:12])
        cols = refs[12]
        acts, grads, dots = refs[13:15], refs[15:17], refs[17]
        rms = cols[:, 0:1]
        column = lax.broadcasted_iota(jnp.int32, (mt_rows, 8), 1)
        found = []
        inner = jnp.zeros((mt_rows, 1), F32)
        for k in range(2):
            gate = cols[:, 1 + k : 2 + k]
            gp = sum(v[0].astype(F32) for v in gu[k]) * rms
            up_pre = sum(v[1].astype(F32) for v in gu[k]) * rms
            raw = sum(v[...].astype(F32) for v in dhr[k])
            sg = jax.nn.sigmoid(gp)
            act = (gp * sg * up_pre).astype(BF16).astype(F32)
            grad = raw * gate
            dgp = (grad * up_pre * sg * (1.0 + gp * (1.0 - sg))).astype(BF16)
            dup = (grad * gp * sg).astype(BF16)
            acts[k][...] = (act * gate).astype(BF16)
            grads[k][0] = dgp
            grads[k][1] = dup
            found.append(jnp.sum(act * raw, axis=1, keepdims=True))
            inner += jnp.sum(
                dgp.astype(F32) * gp + dup.astype(F32) * up_pre, axis=1, keepdims=True
            )
        zero = jnp.zeros((mt_rows, 8), F32)
        for k, value in enumerate(found + [inner]):
            zero = jnp.where(column == k, value, zero)
        dots[...] = zero

    rows_3 = lambda i, m: (0, i, 0)
    rows_2 = lambda i, m: (i, 0)
    ins = [(v, (2, mt_rows, ff), rows_3) for v in gu_a + gu_b]
    ins += [(v, (mt_rows, ff), rows_2) for v in dh_a + dh_b]
    ins += [(cols_f, (mt_rows, 8), lambda i, m: (3 * m[2] + i, 0))]
    outs = [((blk, ff), BF16, (mt_rows, ff), rows_2)] * 2
    outs += [((2, blk, ff), BF16, (2, mt_rows, ff), rows_3)] * 2
    outs += [((blk, 8), F32, (mt_rows, 8), rows_2)]
    act_a, act_b, grad_a, grad_b, dots_f = run(mid_body, "mid", (3,), meta, ins, outs)
    gg_a, gg_b = gather_groups(grad_a, grad_b)
    late = after(act_a, gg_a[1], gg_a[2]), after(act_b, gg_b[1], gg_b[2])
    ag_a, ag_b = gather_groups(*late)
    dots_f = dots_f.T

    dots_f = sum_z(dots_f)
    dots_f = jnp.stack([dots_f, by_group(dots_f, 1), by_group(dots_f, 2), by_group(dots_f, 3)])
    dots_f = jnp.take(dots_f, g ^ jnp.arange(4, dtype=jnp.int32), axis=0)
    dots_f = dots_f.transpose(1, 0, 2).reshape(8, rp)

    def back_columns(flat, dots, low_id, high_id):
        delta = flat[1] * flat[2] * (dots[0] - dots[1])
        inner = (dots[2] + delta * flat[3]) / width
        ids = jnp.arange(experts, dtype=F32)[:, None]
        dlogit = jnp.where(low_id[None] == ids, delta[None], 0.0) - jnp.where(
            high_id[None] == ids, delta[None], 0.0
        )
        zero = jnp.zeros((1, rp), F32)
        return jnp.concatenate(
            [dlogit, inner[None], flat[0:1]] + [zero] * (6 - experts), axis=0
        ).T

    back_f = back_columns(flat_f, dots_f, low_f, high_f)

    def dx_body(m, *refs):
        a_refs, b_refs = refs[:2], refs[2:4]
        w_refs = refs[4 : 4 + parts]
        sel_refs = refs[4 + parts : 6 + parts]
        keep_ref, send_ref, acc, xs = refs[6 + parts :]
        e = pl.program_id(0)
        expert = e.astype(F32)

        @pl.when(e == 0)
        def _():
            acc[...] = jnp.zeros_like(acc)

        for j in range(2):
            for k in range(2):
                ids = sel_refs[k]
                xs[k * blk : (k + 1) * blk, :] = pick(
                    ids[:, 2:3], ids[:, 3:4], expert, a_refs[k][j], b_refs[k][j]
                )
            for s, value in enumerate(nt_pieces(xs[...], [w[0, j] for w in w_refs])):
                acc[s] += value

        @pl.when(e == experts - 1)
        def _():
            keep_ref[...] = acc[:, at_row(m, 6, blk), :].astype(BF16)
            send_ref[...] = acc[:, at_row(m, 7, blk), :].astype(BF16)

    def dx(pair, meta):
        ins = [(v[r], None, None) for v in (gg_a, gg_b) for r in pair]
        ins += [(w, (1, 2, ds, ff), lambda e, m: (e, 0, 0, 0)) for w in wi]
        ins += [(sel, (blk, 8), row_of(r)) for r in pair]
        return run(
            dx_body, "dx", (experts,), meta, ins, [((parts, blk, ds), BF16, None, None)] * 2,
            [pltpu.VMEM((parts, 2 * blk, ds), F32), pltpu.VMEM((2 * blk, ff), BF16)],
            flops=8 * blk * experts * parts * ds * ff,
        )

    dx_near = dx((0, 1), meta)
    dx_far = dx((2, 3), meta)
    dx_totals = wide_sum_z(*dx_near) + wide_sum_z(*dx_far)

    def down_body(m, *refs):
        a_refs, b_refs = refs[:4], refs[4:8]
        w_refs = refs[8 : 8 + parts]
        sel_refs = refs[8 + parts : 12 + parts]
        keep_ref, send_ref, acc, xs = refs[12 + parts :]
        e = pl.program_id(0)

        @pl.when(e == 0)
        def _():
            acc[...] = jnp.zeros_like(acc)

        for r in range(4):
            ids = sel_refs[r]
            xs[r * blk : (r + 1) * blk, :] = pick(
                ids[:, 2:3], ids[:, 3:4], e.astype(F32), a_refs[r][...], b_refs[r][...]
            )
        for s, value in enumerate(nn_pieces(xs[...], [w[0] for w in w_refs])):
            acc[s] += value

        @pl.when(e == experts - 1)
        def _():
            keep_ref[...] = acc[:, at_row(m, 6, 2 * blk), :].astype(BF16)
            send_ref[...] = acc[:, at_row(m, 7, 2 * blk), :].astype(BF16)

    def down(meta):
        ins = [(v, None, None) for v in ag_a + ag_b]
        ins += [(w, (1, ff, ds), lambda e, m: (e, 0, 0)) for w in wo]
        ins += [(sel, (blk, 8), row_of(r)) for r in range(4)]
        return run(
            down_body, "down", (experts,), meta, ins,
            [((parts, 2 * blk, ds), BF16, None, None)] * 2,
            [pltpu.VMEM((parts, rp, ds), F32), pltpu.VMEM((rp, ff), BF16)],
            flops=2 * rp * experts * parts * ds * ff,
        )

    def norm_back_body(low_precision_out, m, *refs):
        t_refs = refs[:4]
        after_ref = refs[4]
        ups = parts if low_precision_out else 1
        up_refs = refs[5 : 5 + ups]
        gain_ref, router_ref, back = refs[5 + ups : 8 + ups]
        outs = refs[8 + ups :]
        small = outs[-1]
        for s in pieces:
            gain = gain_ref[s]
            router = router_ref[s].astype(F32)
            gain_sum = jnp.zeros((1, ds), F32)
            router_sum = [jnp.zeros((1, ds), F32)] * experts
            for r in range(4):
                span_r = at_row(m, (BY_CHUNK if low_precision_out else IN_ORDER) + r, blk)
                up_value = up_refs[s][span_r, :] if low_precision_out else up_refs[0][s, span_r, :]
                x = after_ref[s, span_r, :].astype(F32)
                cols = back[span_r, :]
                rms = cols[:, experts + 1 : experts + 2]
                grad = t_refs[r][s].astype(F32)
                for e in range(experts):
                    grad += cols[:, e : e + 1] * router[e : e + 1]
                normed = x * rms
                token = (normed * gain).astype(BF16).astype(F32)
                gain_sum += jnp.sum(grad * normed, axis=0, keepdims=True)
                for e in range(experts):
                    router_sum[e] = router_sum[e] + jnp.sum(
                        token * cols[:, e : e + 1], axis=0, keepdims=True
                    )
                dn = grad * gain
                total = up_value.astype(F32) + rms * (
                    dn - normed * cols[:, experts : experts + 1]
                )
                if low_precision_out:
                    outs[0][s, span_r, :] = total
                    outs[1][s, span_r, :] = total.astype(BF16)
                else:
                    outs[0][s, span_r, :] = total.astype(BF16)
            for e in range(experts):
                small[e, s] = router_sum[e][0]
            small[experts, s] = gain_sum[0]

    ins = [(t, None, None) for t in dx_totals]
    ins += [(after_rows, None, None)] + [(d, None, None) for d in d_pieces]
    ins += [(gain_f, None, None), (router_f, None, None), (back_f, None, None)]
    outs = [
        ((parts, rp, ds), F32, None, None),
        ((parts, rp, ds), BF16, None, None),
        ((experts + 1, parts, ds), F32, None, None),
    ]
    dafter, dafter_low, small_f = run(
        functools.partial(norm_back_body, True), "norm_back", (1,), meta, ins, outs
    )

    def whole_vectors(small):
        full = jnp.zeros((experts + 1, dp, ds), F32)
        for s in pieces:
            full = lax.dynamic_update_slice_in_dim(
                full, small[:, s : s + 1], g * parts + (c ^ s), axis=1
            )
        mask = 1
        while mask < dp:
            full = full + lax.ppermute(full, "dp", [(a, a ^ mask) for a in range(dp)])
            mask *= 2
        full = full.reshape(experts + 1, width)
        return full[:experts].T, full[experts]

    ffnrouter_grad, ffngain_grad = whole_vectors(small_f)

    def dmix_body(m, *refs):
        d_ref = refs[0]
        w_refs = refs[1 : 1 + parts]
        sel_ref = refs[1 + parts]
        outs = refs[2 + parts : 10 + parts]
        scr = refs[10 + parts]
        products = []
        for e in range(experts):
            products.append(sum(nt(d_ref[s], w_refs[s][e]) for s in pieces))
        low, high = two_slots(sel_ref[:, 0:1], sel_ref[:, 1:2], products)
        for k, value in enumerate((low, high)):
            value = value.astype(BF16)
            for h in range(heads):
                scr[h, :, k * HD : (k + 1) * HD] = value[:, h * HD : (h + 1) * HD]
        for r in range(4):
            block = scr[m[2 + r]]
            outs[2 * r][...] = block[:, :HD]
            outs[2 * r + 1][...] = block[:, HD:]

    ins = [(dafter_low, (parts, tile, ds), lambda i, m: (0, i, 0))]
    ins += [(w, None, None) for w in wp]
    ins += [(sel, (tile, 8), lambda i, m: (i, 0))]
    outs = [((rp, HD), BF16, (tile, HD), lambda i, m: (i, 0))] * 8
    dm = run(
        dmix_body, "dmix", (rp // tile,), meta, ins, outs,
        [pltpu.VMEM((heads, tile, 2 * HD), BF16)],
        flops=2 * rp * experts * parts * ds * hw,
    )
    dm_a, dm_b = reduce_groups(dm[0:8:2], dm[1:8:2])

    def attend_back_body(m, *refs):
        q_ref, kv_ref, halo_ref, sel_ref, cols, cos_ref, sin_ref = refs[:7]
        d_refs = (refs[7:10], refs[10:13])
        mix_refs = refs[13:15]
        dq_ref, own_ref, far_ref, dots_ref, ext, acc = refs[15:]
        i = pl.program_id(0)

        @pl.when(i == 0)
        def _():
            ext[:seq_len, :] = halo_ref[...]
            ext[seq_len:, :] = kv_ref[...]
            acc[...] = jnp.zeros_like(acc)

        near_rows = pl.ds(pl.multiple_of(i * qt, qt), span)
        near = ext[near_rows, :]
        allowed = window_mask(i, sel_ref[:, 4:5])
        line = lax.broadcasted_iota(jnp.int32, (8, qt), 0)
        inner = jnp.zeros((qt, HD), F32)
        found = []
        dk = jnp.zeros((span, HD), F32)
        dv = jnp.zeros((span, HD), F32)
        for k in range(2):
            query = q_ref[:, k * HD : (k + 1) * HD]
            probs = softmax_of(query, near[:, :HD], allowed)
            raw = sum(v[...].astype(F32) for v in d_refs[k])
            dmixed = (raw * cols[:, 1 + k : 2 + k]).astype(BF16)
            found.append(raw * mix_refs[k][...].astype(F32))
            dv += tn(probs.astype(BF16), dmixed)
            dprob = nt(dmixed, near[:, HD:])
            rest = jnp.sum(probs * dprob, axis=1, keepdims=True)
            dscore = (probs * (dprob - rest)).astype(BF16)
            dk += tn(dscore, query) * scale
            dquery = nn(dscore, near[:, :HD]) * scale
            inner += dquery * query.astype(F32)
            dq_ref[:, k * HD : (k + 1) * HD] = turn(dquery, cos_ref[...], -sin_ref[...]).astype(BF16)
        acc[near_rows, :HD] += dk
        acc[near_rows, HD:] += dv
        dots_ref[...] = jnp.where(
            line == 0, lane_sums(found[0]), jnp.where(line == 1, lane_sums(found[1]), lane_sums(inner))
        )

        @pl.when(i == rp // qt - 1)
        def _():
            far_ref[...] = acc[:seq_len, :]
            own_ref[...] = acc[seq_len:, :]

    ins = [(q_rot, (qt, 2 * HD), qrow), (kv_rot, None, None), (halo, None, None)]
    ins += [(sel, (qt, 8), qrow), (cols_a, (qt, 8), qrow)]
    ins += [(cosine, (qt, HD), qrow), (sine, (qt, HD), qrow)]
    ins += [(v, (qt, HD), qrow) for v in dm_a + dm_b + (mixed_a, mixed_b)]
    outs = [
        ((rp, 2 * HD), BF16, (qt, 2 * HD), qrow),
        ((rp, 2 * HD), F32, None, None),
        ((seq_len, 2 * HD), F32, None, None),
        ((8, rp), F32, (8, qt), lambda i, m: (0, i)),
    ]
    dq, dkv_own, dkv_far, dots_q = run(
        attend_back_body, "attend_back", (rp // qt,), meta, ins, outs,
        [pltpu.VMEM((seq_len + rp, 2 * HD), BF16), pltpu.VMEM((seq_len + rp, 2 * HD), F32)],
        flops=20 * rp * span * HD,
    )
    dkv_in = to_previous(dkv_far)

    def dkv_body(m, own_ref, in_ref, kv_ref, cos_ref, sin_ref, out_ref, dots_ref):
        head = rp - seq_len
        for rows_here in (slice(0, head), slice(head, rp)):
            value = own_ref[rows_here, :]
            if rows_here.start == head:
                value = value + in_ref[...]
            out_ref[rows_here, :HD] = turn(
                value[:, :HD], cos_ref[rows_here, :], -sin_ref[rows_here, :]
            ).astype(BF16)
            out_ref[rows_here, HD:] = value[:, HD:].astype(BF16)
            dots_ref[:, rows_here] = lane_sums(value * kv_ref[rows_here, :].astype(F32))

    ins = [(v, None, None) for v in (dkv_own, dkv_in, kv_rot, cosine, sine)]
    outs = [((rp, 2 * HD), BF16, None, None), ((8, rp), F32, None, None)]
    dkv, dots_kv = run(dkv_body, "dkv", (1,), meta, ins, outs)
    third = jnp.arange(8)[:, None] == 2
    dots_a = sum_z(sum_groups(dots_q + jnp.where(third, dots_kv, 0.0)))
    back_a = back_columns(flat_a, dots_a, low_a, high_a)
    da_a, da_b = gather_groups(dq, dkv)

    def place_heads(m, refs, lo, hi):
        for r in range(4):
            lanes = pl.ds(pl.multiple_of(m[2 + r] * HD, HD), HD)
            lo[:, lanes] = refs[r][:, :HD]
            hi[:, lanes] = refs[r][:, HD:]

    def dattn_body(m, *refs):
        a_refs, b_refs = refs[:4], refs[4:8]
        sel_ref = refs[8]
        q_refs = refs[9 : 9 + parts]
        kv_refs = refs[9 + parts : 9 + 2 * parts]
        outs = refs[9 + 2 * parts : 11 + 2 * parts]
        lo, hi, dk, dv = refs[11 + 2 * parts :]
        place_heads(m, a_refs, lo, hi)
        place_heads(m, b_refs, dk, dv)
        acc = nt_pieces(dk[...], [w[0] for w in kv_refs])
        for s, value in enumerate(nt_pieces(dv[...], [w[1] for w in kv_refs])):
            acc[s] += value
        for e in range(experts):
            x = pick(sel_ref[:, 0:1], sel_ref[:, 1:2], e, lo[...], hi[...])
            for s, value in enumerate(nt_pieces(x, [w[e] for w in q_refs])):
                acc[s] += value
        for s in pieces:
            store_halves(pl.program_id(0), outs, s, acc[s].astype(BF16))

    def dattn(k):
        half = lambda i, m: (2 * k + m[7 - i], 0)
        ins = [(v, (zr, 2 * HD), half) for v in da_a + da_b]
        ins += [(sel, (zr, 8), half)]
        ins += [(w, None, None) for w in wq + wkv]
        return run(
            dattn_body, "dattn", (2,), meta, ins, hold,
            [pltpu.VMEM((zr, hw), BF16)] * 4,
            flops=4 * zr * (experts + 2) * hw * parts * ds,
        )

    da_totals = [half for k in range(chunks) for half in wide_sum_z(*dattn(k))]
    x_stack = jnp.stack(x_pieces)
    ins = [(t, None, None) for t in da_totals]
    ins += [(x_stack, None, None), (dafter, None, None)]
    ins += [(gain_a, None, None), (router_a, None, None), (back_a, None, None)]
    outs = [((parts, rp, ds), BF16, None, None), ((experts + 1, parts, ds), F32, None, None)]
    dinput, small_a = run(
        functools.partial(norm_back_body, False), "norm_back_first", (1,), meta, ins, outs
    )
    attnrouter_grad, attngain_grad = whole_vectors(small_a)

    def exchange(sums):
        total = sums[0].astype(F32)
        for s in pieces[1:]:
            total = total + by_part(sums[s], s).astype(F32)
        return total

    ffn_input = (after_rows * flat_f[0][None, :, None] * gain_f).astype(BF16)
    attn_input = (x_stack.astype(F32) * flat_a[0][None, :, None] * gain_a).astype(BF16)

    def t_left(xs, value):
        if not wide:
            return [tn(x, value) for x in xs]
        total = tn(jnp.concatenate(xs, axis=1), value)
        return [total[s * ds : (s + 1) * ds] for s in pieces]

    def t_right(value, xs):
        if not wide:
            return [tn(value, x) for x in xs]
        total = tn(value, jnp.concatenate(xs, axis=1))
        return [total[:, s * ds : (s + 1) * ds] for s in pieces]

    def sort_rows(m, sel_ref, x_refs, xs, ids):
        for r in range(4):
            src, here_r = at_row(m, 2 + r, blk), slice(r * blk, (r + 1) * blk)
            for s in pieces:
                xs[s, here_r, :] = x_refs[s][src, :]
            ids[here_r, :] = sel_ref[src, :]

    def dwin_body(m, *refs):
        a_refs, b_refs = refs[:4], refs[4:8]
        sel_ref, x_ref = refs[8:10]
        outs = refs[10 : 10 + parts]
        xs, ids, mt = refs[10 + parts :]
        j, e = pl.program_id(0), pl.program_id(1)

        @pl.when((j == 0) & (e == 0))
        def _():
            sort_rows(m, sel_ref, [x_ref.at[s] for s in pieces], xs, ids)

        expert = e.astype(F32)
        for r in range(4):
            here_r = slice(r * blk, (r + 1) * blk)
            mt[here_r, :] = pick(
                ids[here_r, 2:3], ids[here_r, 3:4], expert, a_refs[r][0], b_refs[r][0]
            )
        for s, value in enumerate(t_left([xs[s] for s in pieces], mt[...])):
            outs[s][0, 0] = value.astype(BF16)

    def dwin(meta):
        spot = lambda j, e, m: (e, j, 0, 0)
        ins = [(v, (1, blk, ff), lambda j, e, m: (j, 0, 0)) for v in gg_a + gg_b]
        ins += [(sel, None, None), (ffn_input, None, None)]
        outs = [((experts, 2, ds, ff), BF16, (1, 1, ds, ff), spot)] * parts
        return run(
            dwin_body, "dwin", (2, experts), meta, ins, outs,
            [pltpu.VMEM((parts, rp, ds), BF16), pltpu.VMEM((rp, 8), F32), pltpu.VMEM((rp, ff), BF16)],
            flops=4 * rp * experts * parts * ds * ff,
        )

    def dwout_body(m, *refs):
        a_refs, b_refs = refs[:4], refs[4:8]
        sel_ref, d_refs = refs[8], refs[9 : 9 + parts]
        outs = refs[9 + parts : 9 + 2 * parts]
        xs, ids, mt = refs[9 + 2 * parts :]
        e = pl.program_id(0)

        @pl.when(e == 0)
        def _():
            sort_rows(m, sel_ref, d_refs, xs, ids)

        expert = e.astype(F32)
        for r in range(4):
            here_r = slice(r * blk, (r + 1) * blk)
            mt[here_r, :] = pick(
                ids[here_r, 2:3], ids[here_r, 3:4], expert, a_refs[r][...], b_refs[r][...]
            )
        for s, value in enumerate(t_right(mt[...], [xs[s] for s in pieces])):
            outs[s][0] = value.astype(BF16)

    def dwout(meta):
        spot = lambda e, m: (e, 0, 0)
        ins = [(v, None, None) for v in ag_a + ag_b]
        ins += [(sel, None, None)] + [(d, None, None) for d in d_pieces]
        outs = [((experts, ff, ds), BF16, (1, ff, ds), spot)] * parts
        return run(
            dwout_body, "dwout", (experts,), meta, ins, outs,
            [pltpu.VMEM((parts, rp, ds), BF16), pltpu.VMEM((rp, 8), F32), pltpu.VMEM((rp, ff), BF16)],
            flops=2 * rp * experts * parts * ds * ff,
        )

    def dwproj_body(m, *refs):
        a_refs, b_refs = refs[:4], refs[4:8]
        sel_ref, d_ref = refs[8:10]
        outs = refs[10 : 10 + parts]
        lo, hi = refs[10 + parts :]
        e = pl.program_id(0)

        @pl.when(e == 0)
        def _():
            for r in range(4):
                lanes = pl.ds(pl.multiple_of(m[2 + r] * HD, HD), HD)
                lo[:, lanes] = a_refs[r][...]
                hi[:, lanes] = b_refs[r][...]

        x = pick(sel_ref[:, 0:1], sel_ref[:, 1:2], e.astype(F32), lo[...], hi[...])
        for s, value in enumerate(t_right(x, [d_ref[s] for s in pieces])):
            outs[s][0] = value.astype(BF16)

    def dwproj(meta):
        ins = [(v, None, None) for v in gm_a + gm_b]
        ins += [(sel, None, None), (dafter_low, None, None)]
        return run(
            dwproj_body, "dwproj", (experts,), meta, ins,
            [((experts, hw, ds), BF16, (1, hw, ds), lambda e, m: (e, 0, 0))] * parts,
            [pltpu.VMEM((rp, hw), BF16)] * 2,
            flops=2 * rp * experts * hw * parts * ds,
        )

    def dwqkv_body(m, *refs):
        a_refs, b_refs = refs[:4], refs[4:8]
        sel_ref, x_ref = refs[8:10]
        q_outs, kv_outs = refs[10 : 10 + parts], refs[10 + parts : 10 + 2 * parts]
        lo, hi, dk, dv = refs[10 + 2 * parts :]
        e = pl.program_id(0)
        xs = [x_ref.at[s] for s in pieces]

        @pl.when(e == 0)
        def _():
            place_heads(m, a_refs, lo, hi)
            place_heads(m, b_refs, dk, dv)

        @pl.when(e < experts)
        def _():
            x = pick(sel_ref[:, 0:1], sel_ref[:, 1:2], e.astype(F32), lo[...], hi[...])
            for s, value in enumerate(t_left([v[...] for v in xs], x)):
                q_outs[s][0] = value.astype(BF16)

        for k, grad in enumerate((dk, dv)):

            @pl.when(e == experts + k)
            def _():
                for s, value in enumerate(t_left([v[...] for v in xs], grad[...])):
                    kv_outs[s][0] = value.astype(BF16)

    def dwqkv(meta):
        q_spot = lambda e, m: (jnp.minimum(e, experts - 1), 0, 0)
        kv_spot = lambda e, m: (jnp.maximum(e - experts, 0), 0, 0)
        ins = [(v, None, None) for v in da_a + da_b]
        ins += [(sel, None, None), (attn_input, None, None)]
        outs = [((experts, ds, hw), BF16, (1, ds, hw), q_spot)] * parts
        outs += [((2, ds, hw), BF16, (1, ds, hw), kv_spot)] * parts
        return run(
            dwqkv_body, "dwqkv", (experts + 2,), meta, ins, outs,
            [pltpu.VMEM((rp, hw), BF16)] * 4,
            flops=2 * rp * (experts + 2) * hw * parts * ds,
        )

    expertin_grad = exchange(dwin(meta)).swapaxes(1, 2)
    expertout_grad = exchange(dwout(meta))
    proj_grad = exchange(dwproj(meta))
    sums = dwqkv(meta)
    query_grad, kv_grad = exchange(sums[:parts]), exchange(sums[parts:])

    down_totals = wide_sum_z(*down(meta))

    def finish_body(m, *refs):
        t_refs, after_ref, out_ref = refs[:2], refs[2], refs[3]
        for k in range(4):
            span_k = at_row(m, BY_HALF + k, blk)
            for s in pieces:
                total = t_refs[k // 2][s, (k % 2) * blk : (k % 2 + 1) * blk, :]
                out_ref[s, span_k, :] = (
                    after_ref[s, span_k, :] + total.astype(F32)
                ).astype(BF16)

    ins = [(t, None, None) for t in down_totals] + [(after_rows, None, None)]
    out_rows = run(
        finish_body, "finish", (1,), meta, ins, [((parts, rp, ds), BF16, None, None)]
    )[0]

    place = jnp.arange(seq_len, dtype=jnp.int32).reshape(dp, 1, per)
    seq_ids = jnp.arange(seqs, dtype=jnp.int32).reshape(1, seqs, 1)
    valid = place < lengths.reshape(1, seqs, 1)
    packed = jnp.where(valid, starts.reshape(1, seqs, 1) + place, 0)
    from_row = (((packed // rp) ^ c) * rp + packed % rp).reshape(-1)
    cot_row = (inverse.reshape(1, seqs, 1) * seq_len + place).reshape(-1)
    valid = valid.reshape(-1)[:, None]

    found_row = jnp.where(valid, from_row[:, None], -1)
    ut = rows_all // dp

    def unpack_body(m, at_ref, other_ref, *refs):
        v_refs, out_ref = refs[:parts], refs[parts]
        at = at_ref[...]
        lane = lax.broadcasted_iota(jnp.int32, (ut, rp), 1)
        total = jnp.zeros((ut, ds), F32)
        for s in pieces:
            hot = jnp.where(at - s * rp == lane, 1.0, 0.0).astype(BF16)
            total += nn(hot, v_refs[s][...])
        out_ref[...] = jnp.where(at >= 0, total, other_ref[...].astype(F32)).astype(BF16)

    def unpack(value, otherwise):
        mine_all = [value[0]] + [by_part(value[s], s) for s in pieces[1:]]
        ins = [(found_row, (ut, 1), lambda i, m: (i, 0))]
        ins += [(otherwise, (ut, ds), lambda i, m: (i, 0))]
        ins += [(v, None, None) for v in mine_all]
        spread_rows = run(
            unpack_body, "unpack", (dp,), meta, ins,
            [((rows_all, ds), BF16, (ut, ds), lambda i, m: (i, 0))],
            flops=2 * rows_all * rp * parts * ds,
        )[0]
        landed = lax.all_to_all(
            spread_rows.reshape(dp, seqs * per, ds), "dp", 0, 0, tiled=True
        )
        return landed.transpose(1, 0, 2).reshape(seqs, per, width)

    layer_out = unpack(out_rows, x_all)
    input_grad = unpack(dinput, d_all[cot_row])
    return (
        layer_out,
        input_grad,
        attngain_grad,
        attnrouter_grad,
        kv_grad,
        query_grad,
        proj_grad,
        ffngain_grad,
        ffnrouter_grad,
        expertin_grad,
        expertout_grad,
    )


def solution(mesh):
    placed = (
        P(None, "dp", None),
        P("dp", None, None),
        P(),
        P(),
        P(),
        P(),
        P(),
        P(),
        P(None, "dp", "tensor"),
        P(None, "dp", "tensor"),
        P(None, "tensor", "dp"),
        P(),
        P(),
        P(None, "dp", None, "tensor"),
        P(None, "tensor", "dp"),
    )
    return jax.shard_map(
        functools.partial(local, dp=mesh.shape["dp"], tp=mesh.shape["tensor"]),
        mesh=mesh,
        in_specs=placed,
        out_specs=(
            P(None, "dp", None),
            P(None, "dp", None),
            P(),
            P(),
            P(None, "dp", "tensor"),
            P(None, "dp", "tensor"),
            P(None, "tensor", "dp"),
            P(),
            P(),
            P(None, "dp", None, "tensor"),
            P(None, "tensor", "dp"),
        ),
        check_vma=False,
    )
```

```python
import functools

import jax
import jax.numpy as jnp
from jax import lax
from jax.experimental import pallas as pl
from jax.experimental.pallas import tpu as pltpu
from jax.sharding import PartitionSpec as P

HD = 128
EPSILON = 1e-06
ROPE_BASE = 10000.0
BEST = lax.Precision.HIGHEST
F32 = jnp.float32
BF16 = jnp.bfloat16
VMEM_BYTES = 60 * 1024 * 1024


def nn(a, b):
    return lax.dot_general(a, b, (((1,), (0,)), ((), ())), preferred_element_type=F32)


def nt(a, b, precision=None):
    return lax.dot_general(
        a, b, (((1,), (1,)), ((), ())), preferred_element_type=F32, precision=precision
    )


def tn(a, b):
    return lax.dot_general(a, b, (((0,), (0,)), ((), ())), preferred_element_type=F32)


def lane_sums(values):
    ones = jnp.ones((8, values.shape[1]), F32)
    return nt(ones, values, BEST)


def run(body, name, grid, meta, ins, outs, scratch=(), flops=0):
    in_specs = []
    moved = 0
    for array, block, index in ins:
        if block is None:
            rank = array.ndim
            in_specs.append(pl.BlockSpec(array.shape, lambda *a, rank=rank: (0,) * rank))
        else:
            in_specs.append(pl.BlockSpec(block, index))
        moved += array.size * array.dtype.itemsize
    out_specs = []
    out_shape = []
    for shape, dtype, block, index in outs:
        if block is None:
            rank = len(shape)
            out_specs.append(pl.BlockSpec(shape, lambda *a, rank=rank: (0,) * rank))
        else:
            out_specs.append(pl.BlockSpec(block, index))
        out_shape.append(jax.ShapeDtypeStruct(shape, dtype))
        size = jnp.dtype(dtype).itemsize
        for extent in shape:
            size *= extent
        moved += size
    return pl.pallas_call(
        body,
        name=name,
        grid_spec=pltpu.PrefetchScalarGridSpec(
            num_scalar_prefetch=1,
            grid=grid,
            in_specs=in_specs,
            out_specs=out_specs,
            scratch_shapes=list(scratch),
        ),
        out_shape=out_shape,
        compiler_params=pltpu.CompilerParams(
            dimension_semantics=("arbitrary",) * len(grid), vmem_limit_bytes=VMEM_BYTES
        ),
        cost_estimate=pl.CostEstimate(flops=flops, bytes_accessed=moved, transcendentals=0),
    )(meta, *[array for array, _, _ in ins])


def pick(low_id, high_id, expert, low_value, high_value):
    zero = jnp.zeros_like(low_value)
    return jnp.where(
        low_id == expert, low_value, jnp.where(high_id == expert, high_value, zero)
    )


def two_slots(low_id, high_id, products):
    low_value = products[0]
    for expert in range(1, len(products) - 1):
        low_value = jnp.where(low_id == expert, products[expert], low_value)
    high_value = products[1]
    for expert in range(2, len(products)):
        high_value = jnp.where(high_id == expert, products[expert], high_value)
    return low_value, high_value


def turn(values, cosine, sine):
    return values * cosine + pltpu.roll(values, HD // 2, 1) * sine


def local(
    hidden_in,
    cotangent,
    lengths,
    dealing,
    attn_routes,
    ffn_routes,
    attn_gain,
    attn_router,
    kv_weight,
    query_weight,
    proj_weight,
    ffn_gain,
    ffn_router,
    expert_in,
    expert_out,
    *,
    dp,
    tp,
):
    seqs = dealing.shape[0]
    seq_len = cotangent.shape[1]
    held = cotangent.shape[0]
    per = hidden_in.shape[1]
    width = hidden_in.shape[2]
    heads = query_weight.shape[2] // HD
    groups = heads
    parts = dp // groups
    ds = width // dp
    hw = heads * HD
    rows_all = seqs * seq_len
    rows = rows_all * 3 // 4
    rp = rows // parts
    blk = rp // groups
    experts = query_weight.shape[0]
    ff = expert_out.shape[1]
    scale = HD ** (-0.5)
    pieces = range(parts)

    index = lax.axis_index("dp")
    z = lax.axis_index("tensor")
    g = index // parts
    c = index % parts
    mine = ((z == 1) | (z == 2)).astype(jnp.int32)
    theirs = 1 - mine
    spots = [g, c, g, g ^ 1, g ^ 2, g ^ 3, mine, theirs]
    spots += [g ^ mine, g ^ theirs, g ^ (2 + mine), g ^ (2 + theirs)]
    spots += [g ^ (2 * mine), g ^ (2 * mine + 1), g ^ (2 * theirs), g ^ (2 * theirs + 1)]
    spots += [mine, theirs, 2 + mine, 2 + theirs]
    meta = jnp.stack(spots).astype(jnp.int32)
    BY_CHUNK, BY_HALF, IN_ORDER = 8, 12, 16

    def after(value, *others):
        return lax.optimization_barrier((value,) + others)[0]

    def both(a, b):
        return (a.astype(F32) + b.astype(F32)).astype(BF16)

    def by_group(value, mask):
        pairs = [(a, ((a // parts) ^ mask) * parts + a % parts) for a in range(dp)]
        return lax.ppermute(value, "dp", pairs)

    def by_part(value, mask):
        pairs = [(a, (a // parts) * parts + ((a % parts) ^ mask)) for a in range(dp)]
        return lax.ppermute(value, "dp", pairs)

    def to_next(value):
        pairs = [(a, a + 1) for a in range(dp) if a % parts < parts - 1]
        return lax.ppermute(value, "dp", pairs)

    def to_previous(value):
        pairs = [(a, a - 1) for a in range(dp) if a % parts > 0]
        return lax.ppermute(value, "dp", pairs)

    def by_z(value, mask):
        return lax.ppermute(value, "tensor", [(a, a ^ mask) for a in range(tp)])

    def sum_groups(value):
        value = value + by_group(value, 1)
        return value + by_group(value, 2)

    def sum_z(value):
        value = value + by_z(value, 1)
        return value + by_z(value, 3)

    def wide_sum_z(keep, send):
        half = both(keep, by_z(send, 1))
        half = both(half, by_z(half, 3))
        return half, by_z(half, 1)

    def reduce_groups(first, second, early=None, late=None):
        if early is not None:
            first, second, _ = lax.optimization_barrier((tuple(first), tuple(second), early))
        ra = by_group(first[3], 1)
        rb = by_group(second[3], 2)
        ax = by_group(first[1], 1)
        by = by_group(second[2], 2)
        along_y, along_x = both(first[2], ra), both(second[1], rb)
        if late is not None:
            along_y, along_x, _ = lax.optimization_barrier((along_y, along_x, late))
        ay = by_group(along_y, 2)
        bx = by_group(along_x, 1)
        return (first[0], ax, ay), (second[0], bx, by), (along_y, along_x)

    def gather_groups(first, second):
        ax, bx = by_group(first, 1), by_group(second, 1)
        ay, by = by_group(first, 2), by_group(second, 2)
        ad, bd = by_group(ax, 2), by_group(by, 1)
        return (first, ax, ay, ad), (second, bx, by, bd)

    def row_of(offset):
        return lambda *a: (a[-1][2 + offset], 0)

    def at_row(m, spot, count):
        return pl.ds(pl.multiple_of(m[spot] * count, count), count)

    wide = ds % 128 == 0

    def nn_pieces(x, weights):
        if not wide:
            return [nn(x, w) for w in weights]
        value = nn(x, jnp.concatenate(weights, axis=1))
        return [value[:, s * ds : (s + 1) * ds] for s in pieces]

    def nt_pieces(x, weights):
        if not wide:
            return [nt(x, w) for w in weights]
        value = nt(x, jnp.concatenate(weights, axis=0))
        return [value[:, s * ds : (s + 1) * ds] for s in pieces]

    ends = jnp.cumsum(lengths)
    starts = ends - lengths
    inverse = jnp.sum(
        (dealing[None, :] == jnp.arange(seqs, dtype=jnp.int32)[:, None])
        * jnp.arange(seqs, dtype=jnp.int32)[None, :],
        axis=1,
    )

    table = jnp.concatenate([starts, lengths, inverse, c[None]]).astype(jnp.int32)

    def places(part):
        packed = part * rp + jnp.arange(rp, dtype=jnp.int32)
        begun = starts[None, :] <= packed[:, None]
        first = jnp.max(jnp.where(begun, starts[None, :], 0), axis=1)
        seq = jnp.sum(begun.astype(jnp.int32), axis=1) - 1
        return seq, packed - first, first

    seq, at, first = places(c)

    def slot_rows(m, j):
        return pl.ds(pl.multiple_of(m[2 * seqs + j] * seq_len, seq_len), seq_len)

    def part_rows(m, s):
        return pl.ds(pl.multiple_of((m[3 * seqs] ^ s) * rp, rp), rp)

    def block_rows(p, j):
        return pl.ds(pl.multiple_of((p * seqs + j) * per, per), per)

    def near_rows(m, j):
        shift = m[j] & 7
        return pl.ds(pl.multiple_of(m[j] - shift, 8), seq_len + 8), shift

    def pack_body(dealt, m, all_ref, *refs):
        outs = refs[:parts]
        source, packed, whole = refs[parts:]
        source[...] = all_ref[...].astype(F32)

        line = lax.broadcasted_iota(jnp.int32, (seq_len + 8, ds), 0)

        def one(j, carry):
            if dealt:
                whole[:seq_len, :] = source[slot_rows(m, j), :]
            else:
                for p in range(dp):
                    whole[p * per : (p + 1) * per, :] = source[block_rows(p, j), :]
            window, shift = near_rows(m, j)
            moved = pltpu.roll(whole[...], shift, 0)
            packed[window, :] = jnp.where(line < shift, packed[window, :], moved)
            return carry

        lax.fori_loop(0, seqs, one, 0)
        for s in pieces:
            outs[s][...] = packed[part_rows(m, s), :].astype(BF16)

    def pack(value, dealt):
        own = run(
            functools.partial(pack_body, dealt), "pack", (1,), table, [(value, None, None)],
            [((rp, ds), BF16, None, None)] * parts,
            [pltpu.VMEM((n, ds), F32) for n in (rows_all, rows + seq_len + 8, seq_len + 8)],
        )
        return [own[0]] + [by_part(own[s], s) for s in pieces[1:]]

    x_send = hidden_in.reshape(seqs * per, dp, ds).transpose(1, 0, 2)
    x_all = lax.all_to_all(x_send, "dp", 0, 0, tiled=True).reshape(rows_all, ds)
    x_pieces = pack(x_all, False)
    d_send = cotangent.reshape(held * seq_len, dp, ds).transpose(1, 0, 2)
    d_all = lax.all_to_all(d_send, "dp", 0, 0, tiled=True).reshape(rows_all, ds)
    d_pieces = pack(d_all, True)

    def spread(vector):
        tall = vector.reshape((groups, parts, ds) + vector.shape[1:])[g]
        return jnp.stack([tall[c ^ s] for s in pieces])

    gain_a = spread(attn_gain)[:, None, :]
    gain_f = spread(ffn_gain)[:, None, :]
    pad = ((0, 0), (0, 8 - experts), (0, 0))
    router_a = jnp.pad(spread(attn_router).transpose(0, 2, 1), pad)
    router_f = jnp.pad(spread(ffn_router).transpose(0, 2, 1), pad)

    in_own = expert_in.swapaxes(1, 2)
    wq = [query_weight] + [by_part(query_weight, s) for s in pieces[1:]]
    wkv = [kv_weight] + [by_part(kv_weight, s) for s in pieces[1:]]
    wp = [proj_weight] + [by_part(proj_weight, s) for s in pieces[1:]]
    wo = [expert_out] + [by_part(expert_out, s) for s in pieces[1:]]
    wi = [in_own] + [by_part(in_own, s) for s in pieces[1:]]

    routes = jnp.concatenate(
        [attn_routes.reshape(rows_all, 2), ffn_routes.reshape(rows_all, 2)], axis=1
    )
    here = (seq * seq_len + at)[:, None] == jnp.arange(rows_all, dtype=jnp.int32)[None, :]
    mine = jnp.dot(here.astype(BF16), routes.astype(BF16), preferred_element_type=F32)
    low_a, high_a = jnp.minimum(mine[:, 0], mine[:, 1]), jnp.maximum(mine[:, 0], mine[:, 1])
    low_f, high_f = jnp.minimum(mine[:, 2], mine[:, 3]), jnp.maximum(mine[:, 2], mine[:, 3])
    window = (first - c * rp + seq_len).astype(F32)
    nil = jnp.zeros_like(window)
    sel = jnp.stack([low_a, high_a, low_f, high_f, window, nil, nil, nil], axis=1)
    half = HD // 2
    frequency = ROPE_BASE ** (-2.0 * jnp.arange(half, dtype=F32) / HD)
    angles = at.astype(F32)[:, None] * frequency[None, :]
    cosine = jnp.concatenate([jnp.cos(angles)] * 2, axis=1)
    sine = jnp.sin(angles)
    sine = jnp.concatenate([-sine, sine], axis=1)

    def gate_columns(stats, low_id, high_id):
        rms = lax.rsqrt(stats[experts] / width + EPSILON)
        ids = jnp.arange(experts, dtype=F32)[:, None]
        logits = stats[:experts]
        low_logit = jnp.sum(jnp.where(low_id[None] == ids, logits, 0.0), axis=0) * rms
        high_logit = jnp.sum(jnp.where(high_id[None] == ids, logits, 0.0), axis=0) * rms
        gap = low_logit - high_logit
        low_gate, high_gate = jax.nn.sigmoid(gap), jax.nn.sigmoid(-gap)
        zero = jnp.zeros_like(rms)
        flat = jnp.stack([rms, low_gate, high_gate, gap, zero, zero, zero, zero])
        return flat, flat.T

    def rows_pair(refs):
        return jnp.concatenate([ref[...] for ref in refs], axis=0)

    def dhidden_body(m, *refs):
        d_refs = refs[: 2 * parts]
        w_refs, sel_refs = refs[2 * parts : 3 * parts], refs[3 * parts : 3 * parts + 2]
        outs = refs[3 * parts + 2 :]
        ids = rows_pair(sel_refs)
        rows_of = [rows_pair(d_refs[2 * s : 2 * s + 2]) for s in pieces]
        products = []
        for e in range(experts):
            products.append(sum(nt(rows_of[s], w_refs[s][e]) for s in pieces))
        low, high = two_slots(ids[:, 2:3], ids[:, 3:4], products)
        low, high = low.astype(BF16), high.astype(BF16)
        for step, pair in enumerate(((3, 1), (2, 0))):

            @pl.when(pl.program_id(0) == step)
            def _():
                for k, r in enumerate(pair):
                    outs[2 * r][...] = low[k * blk : (k + 1) * blk]
                    outs[2 * r + 1][...] = high[k * blk : (k + 1) * blk]

    def dhidden(meta):
        spots = [lambda i, m: (m[5 - i], 0), lambda i, m: (m[3 - i], 0)]
        ins = [(d, (blk, ds), spot) for d in d_pieces for spot in spots]
        ins += [(w, None, None) for w in wo]
        ins += [(sel, (blk, 8), spot) for spot in spots]
        outs = [((blk, ff), BF16, None, None)] * 8
        return run(
            dhidden_body, "dhidden", (2,), meta, ins, outs,
            flops=2 * rp * experts * parts * ds * ff,
        )

    tile = 256

    def qkv_body(m, *refs):
        x_refs = refs[:parts]
        gain_ref, router_ref = refs[parts : parts + 2]
        q_refs = refs[parts + 2 : 2 * parts + 2]
        kv_refs = refs[2 * parts + 2 : 3 * parts + 2]
        sel_ref = refs[3 * parts + 2]
        outs = refs[3 * parts + 3 : 3 * parts + 11]
        stats_ref, scr = refs[3 * parts + 11 :]
        us = []
        logits = jnp.zeros((8, tile), F32)
        squares = jnp.zeros((8, tile), F32)
        for s in pieces:
            xf = x_refs[s][...].astype(F32)
            us.append((xf * gain_ref[s]).astype(BF16))
            logits += nt(router_ref[s], us[s])
            squares += lane_sums(xf * xf)
        line = lax.broadcasted_iota(jnp.int32, (8, tile), 0)
        stats_ref[...] = jnp.where(line < experts, logits, squares)
        products = []
        for e in range(experts):
            products.append(sum(nn(us[s], q_refs[s][e]) for s in pieces))
        low, high = two_slots(sel_ref[:, 0:1], sel_ref[:, 1:2], products)
        keys = sum(nn(us[s], kv_refs[s][0]) for s in pieces)
        values = sum(nn(us[s], kv_refs[s][1]) for s in pieces)
        for k, value in enumerate((low, high, keys, values)):
            value = value.astype(BF16)
            for h in range(heads):
                scr[h, :, k * HD : (k + 1) * HD] = value[:, h * HD : (h + 1) * HD]
        for r in range(4):
            block = scr[m[2 + r]]
            outs[2 * r][...] = block[:, : 2 * HD]
            outs[2 * r + 1][...] = block[:, 2 * HD :]

    ins = [(x, (tile, ds), lambda i, m: (i, 0)) for x in x_pieces]
    ins += [(gain_a, None, None), (router_a, None, None)]
    ins += [(w, None, None) for w in wq + wkv]
    ins += [(sel, (tile, 8), lambda i, m: (i, 0))]
    outs = [((rp, 2 * HD), BF16, (tile, 2 * HD), lambda i, m: (i, 0))] * 8
    outs += [((8, rp), F32, (8, tile), lambda i, m: (0, i))]
    qkv = run(
        qkv_body, "qkv", (rp // tile,), meta, ins, outs,
        [pltpu.VMEM((heads, tile, 4 * HD), BF16)],
        flops=2 * rp * (experts + 2) * parts * ds * hw,
    )
    dh = dhidden(after(meta, qkv[8]))
    q_sum, kv_sum, sent = reduce_groups(qkv[0:8:2], qkv[1:8:2])
    stats_a = sum_groups(qkv[8])
    flat_a, cols_a = gate_columns(stats_a, low_a, high_a)

    def rope_body(m, a0, a1, a2, b0, b1, b2, cols, cos_ref, sin_ref, q_ref, kv_ref):
        rms = cols[:, 0:1]
        cos, sin = cos_ref[...], sin_ref[...]
        q = (a0[...].astype(F32) + a1[...].astype(F32) + a2[...].astype(F32)) * rms
        kv = (b0[...].astype(F32) + b1[...].astype(F32) + b2[...].astype(F32)) * rms
        q_ref[:, :HD] = turn(q[:, :HD], cos, sin).astype(BF16)
        q_ref[:, HD:] = turn(q[:, HD:], cos, sin).astype(BF16)
        kv_ref[:, :HD] = turn(kv[:, :HD], cos, sin).astype(BF16)
        kv_ref[:, HD:] = kv[:, HD:].astype(BF16)

    ins = [(v, (tile, 2 * HD), lambda i, m: (i, 0)) for v in q_sum + kv_sum]
    ins += [(cols_a, (tile, 8), lambda i, m: (i, 0))]
    ins += [(v, (tile, HD), lambda i, m: (i, 0)) for v in (cosine, sine)]
    outs = [((rp, 2 * HD), BF16, (tile, 2 * HD), lambda i, m: (i, 0))] * 2
    q_rot, kv_rot = run(rope_body, "rope", (rp // tile,), after(meta, dh[0]), ins, outs)
    halo = to_next(kv_rot[rp - seq_len :])

    qt = 128
    span = seq_len + qt

    def window_mask(i, low_key):
        u = i * qt + lax.broadcasted_iota(jnp.int32, (qt, span), 1)
        t = seq_len + i * qt + lax.broadcasted_iota(jnp.int32, (qt, span), 0)
        return (u >= low_key.astype(jnp.int32)) & (u <= t)

    def softmax_of(query, key, allowed):
        score = jnp.where(allowed, nt(query, key) * scale, -1e30)
        top = jnp.max(score, axis=1, keepdims=True)
        raised = jnp.exp(score - top)
        return raised / jnp.sum(raised, axis=1, keepdims=True)

    def attend_body(m, q_ref, kv_ref, halo_ref, sel_ref, cols, ga, gb, ma, mb, ext):
        i = pl.program_id(0)

        @pl.when(i == 0)
        def _():
            ext[:seq_len, :] = halo_ref[...]
            ext[seq_len:, :] = kv_ref[...]

        near = ext[pl.ds(pl.multiple_of(i * qt, qt), span), :]
        allowed = window_mask(i, sel_ref[:, 4:5])
        for k, (g_ref, m_ref) in enumerate(((ga, ma), (gb, mb))):
            probs = softmax_of(q_ref[:, k * HD : (k + 1) * HD], near[:, :HD], allowed)
            mixed = nn(probs.astype(BF16), near[:, HD:]).astype(BF16)
            m_ref[...] = mixed
            g_ref[...] = (mixed.astype(F32) * cols[:, 1 + k : 2 + k]).astype(BF16)

    def qrow(i, m):
        return (i, 0)

    ins = [(q_rot, (qt, 2 * HD), qrow), (kv_rot, None, None), (halo, None, None)]
    ins += [(sel, (qt, 8), qrow), (cols_a, (qt, 8), qrow)]
    outs = [((rp, HD), BF16, (qt, HD), qrow)] * 4
    gated_a, gated_b, mixed_a, mixed_b = run(
        attend_body, "attend", (rp // qt,), meta, ins, outs,
        [pltpu.VMEM((seq_len + rp, 2 * HD), BF16)],
        flops=8 * rp * span * HD,
    )
    gm_a, gm_b = gather_groups(gated_a, gated_b)
    dh_a, dh_b, _ = reduce_groups(
        dh[0:8:2], dh[1:8:2], early=sent, late=(gm_a[1], gm_b[2])
    )

    chunks = 2
    zr = rp // chunks // 2
    hold = [((parts, zr, ds), BF16, None, None)] * 2

    def store_halves(i, refs, s, value):
        @pl.when(i == 0)
        def _():
            refs[1][s] = value

        @pl.when(i == 1)
        def _():
            refs[0][s] = value

    def proj_body(m, *refs):
        a_refs, b_refs = refs[:4], refs[4:8]
        sel_ref = refs[8]
        w_refs = refs[9 : 9 + parts]
        outs, xs = refs[9 + parts : 11 + parts], refs[11 + parts]
        for r in range(4):
            lanes = pl.ds(pl.multiple_of(m[2 + r] * HD, HD), HD)
            for e in range(experts):
                xs[e, :, lanes] = pick(
                    sel_ref[:, 0:1], sel_ref[:, 1:2], e, a_refs[r][...], b_refs[r][...]
                )
        acc = nn_pieces(xs[0], [w[0] for w in w_refs])
        for e in range(1, experts):
            for s, value in enumerate(nn_pieces(xs[e], [w[e] for w in w_refs])):
                acc[s] += value
        for s in pieces:
            store_halves(pl.program_id(0), outs, s, acc[s].astype(BF16))

    def project(k):
        half = lambda i, m: (2 * k + m[7 - i], 0)
        ins = [(v, (zr, HD), half) for v in gm_a + gm_b]
        ins += [(sel, (zr, 8), half)]
        ins += [(w, None, None) for w in wp]
        return run(
            proj_body, "proj", (2,), meta, ins, hold,
            [pltpu.VMEM((experts, zr, hw), BF16)],
            flops=4 * zr * experts * hw * parts * ds,
        )

    attn_totals = [half for k in range(chunks) for half in wide_sum_z(*project(k))]

    def norm_body(m, *refs):
        t_refs = refs[: 2 * chunks]
        x_refs = refs[2 * chunks : 2 * chunks + parts]
        gain_ref, router_ref, after_ref, u_ref, stats_ref = refs[2 * chunks + parts :]
        for k in range(2 * chunks):
            span_k = at_row(m, IN_ORDER + k, zr)
            for s in pieces:
                after_ref[s, span_k, :] = x_refs[s][span_k, :].astype(F32) + t_refs[k][s].astype(F32)
        logits = jnp.zeros((8, rp), F32)
        squares = jnp.zeros((8, rp), F32)
        for s in pieces:
            af = after_ref[s]
            u = (af * gain_ref[s]).astype(BF16)
            u_ref[s] = u
            logits += nt(router_ref[s], u)
            squares += lane_sums(af * af)
        line = lax.broadcasted_iota(jnp.int32, (8, rp), 0)
        stats_ref[...] = jnp.where(line < experts, logits, squares)

    ins = [(t, None, None) for t in attn_totals + x_pieces]
    ins += [(gain_f, None, None), (router_f, None, None)]
    outs = [
        ((parts, rp, ds), F32, None, None),
        ((parts, rp, ds), BF16, None, None),
        ((8, rp), F32, None, None),
    ]
    after_rows, u_f, stats_part = run(norm_body, "norm", (1,), meta, ins, outs)
    stats_f = sum_groups(stats_part)
    flat_f, cols_f = gate_columns(stats_f, low_f, high_f)

    def up_body(m, *refs):
        u_refs, w_refs = refs[:2], refs[2 : 2 + parts]
        sel_refs = refs[2 + parts : 4 + parts]
        outs = refs[4 + parts :]
        ids = rows_pair(sel_refs)
        rows_of = [jnp.concatenate([u[s] for u in u_refs], axis=0) for s in pieces]
        products = []
        for e in range(experts):
            products.append(sum(nn(rows_of[s], w_refs[s][e, 0]) for s in pieces))
        low, high = two_slots(ids[:, 2:3], ids[:, 3:4], products)
        low, high = low.astype(BF16), high.astype(BF16)
        for k in range(2):
            outs[2 * k][0] = low[k * blk : (k + 1) * blk]
            outs[2 * k + 1][0] = high[k * blk : (k + 1) * blk]

    def up(pair, meta):
        def block_of(r):
            return lambda j, m: (0, m[2 + r], 0)

        ins = [(u_f, (parts, blk, ds), block_of(r)) for r in pair]
        ins += [(w, (experts, 1, ds, ff), lambda j, m: (0, j, 0, 0)) for w in wi]
        ins += [(sel, (blk, 8), row_of(r)) for r in pair]
        outs = [((2, blk, ff), BF16, (1, blk, ff), lambda j, m: (j, 0, 0))] * 4
        return run(
            up_body, "up", (2,), meta, ins, outs, flops=8 * blk * experts * parts * ds * ff
        )

    up_far = up((3, 1), meta)
    up_near = up((2, 0), after(meta, up_far[0]))
    gu_a, gu_b, _ = reduce_groups(
        (up_near[2], up_far[2], up_near[0], up_far[0]),
        (up_near[3], up_far[3], up_near[1], up_far[1]),
    )

    mt_rows = blk // 3

    def mid_body(m, *refs):
        gu = (refs[0:3], refs[3:6])
        dhr = (refs[6:9], refs[9:12])
        cols = refs[12]
        acts, grads, dots = refs[13:15], refs[15:17], refs[17]
        rms = cols[:, 0:1]
        column = lax.broadcasted_iota(jnp.int32, (mt_rows, 8), 1)
        found = []
        inner = jnp.zeros((mt_rows, 1), F32)
        for k in range(2):
            gate = cols[:, 1 + k : 2 + k]
            gp = sum(v[0].astype(F32) for v in gu[k]) * rms
            up_pre = sum(v[1].astype(F32) for v in gu[k]) * rms
            raw = sum(v[...].astype(F32) for v in dhr[k])
            sg = jax.nn.sigmoid(gp)
            act = (gp * sg * up_pre).astype(BF16).astype(F32)
            grad = raw * gate
            dgp = (grad * up_pre * sg * (1.0 + gp * (1.0 - sg))).astype(BF16)
            dup = (grad * gp * sg).astype(BF16)
            acts[k][...] = (act * gate).astype(BF16)
            grads[k][0] = dgp
            grads[k][1] = dup
            found.append(jnp.sum(act * raw, axis=1, keepdims=True))
            inner += jnp.sum(
                dgp.astype(F32) * gp + dup.astype(F32) * up_pre, axis=1, keepdims=True
            )
        zero = jnp.zeros((mt_rows, 8), F32)
        for k, value in enumerate(found + [inner]):
            zero = jnp.where(column == k, value, zero)
        dots[...] = zero

    rows_3 = lambda i, m: (0, i, 0)
    rows_2 = lambda i, m: (i, 0)
    ins = [(v, (2, mt_rows, ff), rows_3) for v in gu_a + gu_b]
    ins += [(v, (mt_rows, ff), rows_2) for v in dh_a + dh_b]
    ins += [(cols_f, (mt_rows, 8), lambda i, m: (3 * m[2] + i, 0))]
    outs = [((blk, ff), BF16, (mt_rows, ff), rows_2)] * 2
    outs += [((2, blk, ff), BF16, (2, mt_rows, ff), rows_3)] * 2
    outs += [((blk, 8), F32, (mt_rows, 8), rows_2)]
    act_a, act_b, grad_a, grad_b, dots_f = run(mid_body, "mid", (3,), meta, ins, outs)
    gg_a, gg_b = gather_groups(grad_a, grad_b)
    late = after(act_a, gg_a[1], gg_a[2]), after(act_b, gg_b[1], gg_b[2])
    ag_a, ag_b = gather_groups(*late)
    dots_f = dots_f.T

    dots_f = after(sum_z(dots_f), gg_a[3], gg_b[3])
    dots_f = jnp.stack([dots_f, by_group(dots_f, 1), by_group(dots_f, 2), by_group(dots_f, 3)])
    dots_f = jnp.take(dots_f, g ^ jnp.arange(4, dtype=jnp.int32), axis=0)
    dots_f = dots_f.transpose(1, 0, 2).reshape(8, rp)

    def back_columns(flat, dots, low_id, high_id):
        delta = flat[1] * flat[2] * (dots[0] - dots[1])
        inner = (dots[2] + delta * flat[3]) / width
        ids = jnp.arange(experts, dtype=F32)[:, None]
        dlogit = jnp.where(low_id[None] == ids, delta[None], 0.0) - jnp.where(
            high_id[None] == ids, delta[None], 0.0
        )
        zero = jnp.zeros((1, rp), F32)
        return jnp.concatenate(
            [dlogit, inner[None], flat[0:1]] + [zero] * (6 - experts), axis=0
        ).T

    back_f = back_columns(flat_f, dots_f, low_f, high_f)

    def dx_body(m, *refs):
        a_refs, b_refs = refs[:2], refs[2:4]
        w_refs = refs[4 : 4 + parts]
        sel_refs = refs[4 + parts : 6 + parts]
        keep_ref, send_ref, acc, xs = refs[6 + parts :]
        e = pl.program_id(0)
        expert = e.astype(F32)

        @pl.when(e == 0)
        def _():
            acc[...] = jnp.zeros_like(acc)

        for j in range(2):
            for k in range(2):
                ids = sel_refs[k]
                xs[k * blk : (k + 1) * blk, :] = pick(
                    ids[:, 2:3], ids[:, 3:4], expert, a_refs[k][j], b_refs[k][j]
                )
            for s, value in enumerate(nt_pieces(xs[...], [w[0, j] for w in w_refs])):
                acc[s] += value

        @pl.when(e == experts - 1)
        def _():
            keep_ref[...] = acc[:, at_row(m, 6, blk), :].astype(BF16)
            send_ref[...] = acc[:, at_row(m, 7, blk), :].astype(BF16)

    def dx(pair, meta):
        ins = [(v[r], None, None) for v in (gg_a, gg_b) for r in pair]
        ins += [(w, (1, 2, ds, ff), lambda e, m: (e, 0, 0, 0)) for w in wi]
        ins += [(sel, (blk, 8), row_of(r)) for r in pair]
        return run(
            dx_body, "dx", (experts,), meta, ins, [((parts, blk, ds), BF16, None, None)] * 2,
            [pltpu.VMEM((parts, 2 * blk, ds), F32), pltpu.VMEM((2 * blk, ff), BF16)],
            flops=8 * blk * experts * parts * ds * ff,
        )

    dx_near = dx((0, 1), meta)
    dx_far = dx((2, 3), meta)
    dx_totals = wide_sum_z(*dx_near) + wide_sum_z(*dx_far)

    def down_body(m, *refs):
        a_refs, b_refs = refs[:4], refs[4:8]
        w_refs = refs[8 : 8 + parts]
        sel_refs = refs[8 + parts : 12 + parts]
        keep_ref, send_ref, acc, xs = refs[12 + parts :]
        e = pl.program_id(0)

        @pl.when(e == 0)
        def _():
            acc[...] = jnp.zeros_like(acc)

        for r in range(4):
            ids = sel_refs[r]
            xs[r * blk : (r + 1) * blk, :] = pick(
                ids[:, 2:3], ids[:, 3:4], e.astype(F32), a_refs[r][...], b_refs[r][...]
            )
        for s, value in enumerate(nn_pieces(xs[...], [w[0] for w in w_refs])):
            acc[s] += value

        @pl.when(e == experts - 1)
        def _():
            keep_ref[...] = acc[:, at_row(m, 6, 2 * blk), :].astype(BF16)
            send_ref[...] = acc[:, at_row(m, 7, 2 * blk), :].astype(BF16)

    def down(meta):
        ins = [(v, None, None) for v in ag_a + ag_b]
        ins += [(w, (1, ff, ds), lambda e, m: (e, 0, 0)) for w in wo]
        ins += [(sel, (blk, 8), row_of(r)) for r in range(4)]
        return run(
            down_body, "down", (experts,), meta, ins,
            [((parts, 2 * blk, ds), BF16, None, None)] * 2,
            [pltpu.VMEM((parts, rp, ds), F32), pltpu.VMEM((rp, ff), BF16)],
            flops=2 * rp * experts * parts * ds * ff,
        )

    def norm_back_body(low_precision_out, m, *refs):
        t_refs = refs[:4]
        after_ref = refs[4]
        ups = parts if low_precision_out else 1
        up_refs = refs[5 : 5 + ups]
        gain_ref, router_ref, back = refs[5 + ups : 8 + ups]
        outs = refs[8 + ups :]
        small = outs[-1]
        for s in pieces:
            gain = gain_ref[s]
            router = router_ref[s].astype(F32)
            gain_sum = jnp.zeros((1, ds), F32)
            router_sum = [jnp.zeros((1, ds), F32)] * experts
            for r in range(4):
                span_r = at_row(m, (BY_CHUNK if low_precision_out else IN_ORDER) + r, blk)
                up_value = up_refs[s][span_r, :] if low_precision_out else up_refs[0][s, span_r, :]
                x = after_ref[s, span_r, :].astype(F32)
                cols = back[span_r, :]
                rms = cols[:, experts + 1 : experts + 2]
                grad = t_refs[r][s].astype(F32)
                for e in range(experts):
                    grad += cols[:, e : e + 1] * router[e : e + 1]
                normed = x * rms
                token = (normed * gain).astype(BF16).astype(F32)
                gain_sum += jnp.sum(grad * normed, axis=0, keepdims=True)
                for e in range(experts):
                    router_sum[e] = router_sum[e] + jnp.sum(
                        token * cols[:, e : e + 1], axis=0, keepdims=True
                    )
                dn = grad * gain
                total = up_value.astype(F32) + rms * (
                    dn - normed * cols[:, experts : experts + 1]
                )
                if low_precision_out:
                    outs[0][s, span_r, :] = total
                    outs[1][s, span_r, :] = total.astype(BF16)
                else:
                    outs[0][s, span_r, :] = total.astype(BF16)
            for e in range(experts):
                small[e, s] = router_sum[e][0]
            small[experts, s] = gain_sum[0]

    ins = [(t, None, None) for t in dx_totals]
    ins += [(after_rows, None, None)] + [(d, None, None) for d in d_pieces]
    ins += [(gain_f, None, None), (router_f, None, None), (back_f, None, None)]
    outs = [
        ((parts, rp, ds), F32, None, None),
        ((parts, rp, ds), BF16, None, None),
        ((experts + 1, parts, ds), F32, None, None),
    ]
    dafter, dafter_low, small_f = run(
        functools.partial(norm_back_body, True), "norm_back", (1,), meta, ins, outs
    )

    def whole_vectors(small):
        full = jnp.zeros((experts + 1, dp, ds), F32)
        for s in pieces:
            full = lax.dynamic_update_slice_in_dim(
                full, small[:, s : s + 1], g * parts + (c ^ s), axis=1
            )
        mask = 1
        while mask < dp:
            full = full + lax.ppermute(full, "dp", [(a, a ^ mask) for a in range(dp)])
            mask *= 2
        full = full.reshape(experts + 1, width)
        return full[:experts].T, full[experts]

    ffnrouter_grad, ffngain_grad = whole_vectors(small_f)

    def dmix_body(m, *refs):
        d_ref = refs[0]
        w_refs = refs[1 : 1 + parts]
        sel_ref = refs[1 + parts]
        outs = refs[2 + parts : 10 + parts]
        scr = refs[10 + parts]
        products = []
        for e in range(experts):
            products.append(sum(nt(d_ref[s], w_refs[s][e]) for s in pieces))
        low, high = two_slots(sel_ref[:, 0:1], sel_ref[:, 1:2], products)
        for k, value in enumerate((low, high)):
            value = value.astype(BF16)
            for h in range(heads):
                scr[h, :, k * HD : (k + 1) * HD] = value[:, h * HD : (h + 1) * HD]
        for r in range(4):
            block = scr[m[2 + r]]
            outs[2 * r][...] = block[:, :HD]
            outs[2 * r + 1][...] = block[:, HD:]

    ins = [(dafter_low, (parts, tile, ds), lambda i, m: (0, i, 0))]
    ins += [(w, None, None) for w in wp]
    ins += [(sel, (tile, 8), lambda i, m: (i, 0))]
    outs = [((rp, HD), BF16, (tile, HD), lambda i, m: (i, 0))] * 8
    dm = run(
        dmix_body, "dmix", (rp // tile,), meta, ins, outs,
        [pltpu.VMEM((heads, tile, 2 * HD), BF16)],
        flops=2 * rp * experts * parts * ds * hw,
    )
    dm_a, dm_b, _ = reduce_groups(dm[0:8:2], dm[1:8:2])

    def attend_back_body(m, *refs):
        q_ref, kv_ref, halo_ref, sel_ref, cols, cos_ref, sin_ref = refs[:7]
        d_refs = (refs[7:10], refs[10:13])
        mix_refs = refs[13:15]
        dq_ref, own_ref, far_ref, dots_ref, ext, acc = refs[15:]
        i = pl.program_id(0)

        @pl.when(i == 0)
        def _():
            ext[:seq_len, :] = halo_ref[...]
            ext[seq_len:, :] = kv_ref[...]
            acc[...] = jnp.zeros_like(acc)

        near_rows = pl.ds(pl.multiple_of(i * qt, qt), span)
        near = ext[near_rows, :]
        allowed = window_mask(i, sel_ref[:, 4:5])
        line = lax.broadcasted_iota(jnp.int32, (8, qt), 0)
        inner = jnp.zeros((qt, HD), F32)
        found = []
        dk = jnp.zeros((span, HD), F32)
        dv = jnp.zeros((span, HD), F32)
        for k in range(2):
            query = q_ref[:, k * HD : (k + 1) * HD]
            probs = softmax_of(query, near[:, :HD], allowed)
            raw = sum(v[...].astype(F32) for v in d_refs[k])
            dmixed = (raw * cols[:, 1 + k : 2 + k]).astype(BF16)
            found.append(raw * mix_refs[k][...].astype(F32))
            dv += tn(probs.astype(BF16), dmixed)
            dprob = nt(dmixed, near[:, HD:])
            rest = jnp.sum(probs * dprob, axis=1, keepdims=True)
            dscore = (probs * (dprob - rest)).astype(BF16)
            dk += tn(dscore, query) * scale
            dquery = nn(dscore, near[:, :HD]) * scale
            inner += dquery * query.astype(F32)
            dq_ref[:, k * HD : (k + 1) * HD] = turn(dquery, cos_ref[...], -sin_ref[...]).astype(BF16)
        acc[near_rows, :HD] += dk
        acc[near_rows, HD:] += dv
        dots_ref[...] = jnp.where(
            line == 0, lane_sums(found[0]), jnp.where(line == 1, lane_sums(found[1]), lane_sums(inner))
        )

        @pl.when(i == rp // qt - 1)
        def _():
            far_ref[...] = acc[:seq_len, :]
            own_ref[...] = acc[seq_len:, :]

    ins = [(q_rot, (qt, 2 * HD), qrow), (kv_rot, None, None), (halo, None, None)]
    ins += [(sel, (qt, 8), qrow), (cols_a, (qt, 8), qrow)]
    ins += [(cosine, (qt, HD), qrow), (sine, (qt, HD), qrow)]
    ins += [(v, (qt, HD), qrow) for v in dm_a + dm_b + (mixed_a, mixed_b)]
    outs = [
        ((rp, 2 * HD), BF16, (qt, 2 * HD), qrow),
        ((rp, 2 * HD), F32, None, None),
        ((seq_len, 2 * HD), F32, None, None),
        ((8, rp), F32, (8, qt), lambda i, m: (0, i)),
    ]
    dq, dkv_own, dkv_far, dots_q = run(
        attend_back_body, "attend_back", (rp // qt,), meta, ins, outs,
        [pltpu.VMEM((seq_len + rp, 2 * HD), BF16), pltpu.VMEM((seq_len + rp, 2 * HD), F32)],
        flops=20 * rp * span * HD,
    )
    dkv_in = to_previous(dkv_far)

    def dkv_body(m, own_ref, in_ref, kv_ref, cos_ref, sin_ref, out_ref, dots_ref):
        head = rp - seq_len
        for rows_here in (slice(0, head), slice(head, rp)):
            value = own_ref[rows_here, :]
            if rows_here.start == head:
                value = value + in_ref[...]
            out_ref[rows_here, :HD] = turn(
                value[:, :HD], cos_ref[rows_here, :], -sin_ref[rows_here, :]
            ).astype(BF16)
            out_ref[rows_here, HD:] = value[:, HD:].astype(BF16)
            dots_ref[:, rows_here] = lane_sums(value * kv_ref[rows_here, :].astype(F32))

    ins = [(v, None, None) for v in (dkv_own, dkv_in, kv_rot, cosine, sine)]
    outs = [((rp, 2 * HD), BF16, None, None), ((8, rp), F32, None, None)]
    dkv, dots_kv = run(dkv_body, "dkv", (1,), meta, ins, outs)
    third = jnp.arange(8)[:, None] == 2
    dots_a = sum_z(sum_groups(dots_q + jnp.where(third, dots_kv, 0.0)))
    back_a = back_columns(flat_a, dots_a, low_a, high_a)
    da_a, da_b = gather_groups(dq, dkv)

    def place_heads(m, refs, lo, hi):
        for r in range(4):
            lanes = pl.ds(pl.multiple_of(m[2 + r] * HD, HD), HD)
            lo[:, lanes] = refs[r][:, :HD]
            hi[:, lanes] = refs[r][:, HD:]

    def dattn_body(m, *refs):
        a_refs, b_refs = refs[:4], refs[4:8]
        sel_ref = refs[8]
        q_refs = refs[9 : 9 + parts]
        kv_refs = refs[9 + parts : 9 + 2 * parts]
        outs = refs[9 + 2 * parts : 11 + 2 * parts]
        lo, hi, dk, dv = refs[11 + 2 * parts :]
        place_heads(m, a_refs, lo, hi)
        place_heads(m, b_refs, dk, dv)
        acc = nt_pieces(dk[...], [w[0] for w in kv_refs])
        for s, value in enumerate(nt_pieces(dv[...], [w[1] for w in kv_refs])):
            acc[s] += value
        for e in range(experts):
            x = pick(sel_ref[:, 0:1], sel_ref[:, 1:2], e, lo[...], hi[...])
            for s, value in enumerate(nt_pieces(x, [w[e] for w in q_refs])):
                acc[s] += value
        for s in pieces:
            store_halves(pl.program_id(0), outs, s, acc[s].astype(BF16))

    def dattn(k):
        half = lambda i, m: (2 * k + m[7 - i], 0)
        ins = [(v, (zr, 2 * HD), half) for v in da_a + da_b]
        ins += [(sel, (zr, 8), half)]
        ins += [(w, None, None) for w in wq + wkv]
        return run(
            dattn_body, "dattn", (2,), meta, ins, hold,
            [pltpu.VMEM((zr, hw), BF16)] * 4,
            flops=4 * zr * (experts + 2) * hw * parts * ds,
        )

    da_totals = [half for k in range(chunks) for half in wide_sum_z(*dattn(k))]
    x_stack = jnp.stack(x_pieces)
    ins = [(t, None, None) for t in da_totals]
    ins += [(x_stack, None, None), (dafter, None, None)]
    ins += [(gain_a, None, None), (router_a, None, None), (back_a, None, None)]
    outs = [((parts, rp, ds), BF16, None, None), ((experts + 1, parts, ds), F32, None, None)]
    dinput, small_a = run(
        functools.partial(norm_back_body, False), "norm_back_first", (1,), meta, ins, outs
    )
    attnrouter_grad, attngain_grad = whole_vectors(small_a)

    def exchange(sums):
        total = sums[0].astype(F32)
        for s in pieces[1:]:
            total = total + by_part(sums[s], s).astype(F32)
        return total

    ffn_input = (after_rows * flat_f[0][None, :, None] * gain_f).astype(BF16)
    attn_input = (x_stack.astype(F32) * flat_a[0][None, :, None] * gain_a).astype(BF16)

    def t_left(xs, value):
        if not wide:
            return [tn(x, value) for x in xs]
        total = tn(jnp.concatenate(xs, axis=1), value)
        return [total[s * ds : (s + 1) * ds] for s in pieces]

    def t_right(value, xs):
        if not wide:
            return [tn(value, x) for x in xs]
        total = tn(value, jnp.concatenate(xs, axis=1))
        return [total[:, s * ds : (s + 1) * ds] for s in pieces]

    def sort_rows(m, sel_ref, x_refs, xs, ids):
        for r in range(4):
            src, here_r = at_row(m, 2 + r, blk), slice(r * blk, (r + 1) * blk)
            for s in pieces:
                xs[s, here_r, :] = x_refs[s][src, :]
            ids[here_r, :] = sel_ref[src, :]

    def dwin_body(m, *refs):
        a_refs, b_refs = refs[:4], refs[4:8]
        sel_ref, x_ref = refs[8:10]
        outs = refs[10 : 10 + parts]
        xs, ids, mt = refs[10 + parts :]
        j, e = pl.program_id(0), pl.program_id(1)

        @pl.when((j == 0) & (e == 0))
        def _():
            sort_rows(m, sel_ref, [x_ref.at[s] for s in pieces], xs, ids)

        expert = e.astype(F32)
        for r in range(4):
            here_r = slice(r * blk, (r + 1) * blk)
            mt[here_r, :] = pick(
                ids[here_r, 2:3], ids[here_r, 3:4], expert, a_refs[r][0], b_refs[r][0]
            )
        for s, value in enumerate(t_left([xs[s] for s in pieces], mt[...])):
            outs[s][0, 0] = value.astype(BF16)

    def dwin(meta):
        spot = lambda j, e, m: (e, j, 0, 0)
        ins = [(v, (1, blk, ff), lambda j, e, m: (j, 0, 0)) for v in gg_a + gg_b]
        ins += [(sel, None, None), (ffn_input, None, None)]
        outs = [((experts, 2, ds, ff), BF16, (1, 1, ds, ff), spot)] * parts
        return run(
            dwin_body, "dwin", (2, experts), meta, ins, outs,
            [pltpu.VMEM((parts, rp, ds), BF16), pltpu.VMEM((rp, 8), F32), pltpu.VMEM((rp, ff), BF16)],
            flops=4 * rp * experts * parts * ds * ff,
        )

    def dwout_body(m, *refs):
        a_refs, b_refs = refs[:4], refs[4:8]
        sel_ref, d_refs = refs[8], refs[9 : 9 + parts]
        outs = refs[9 + parts : 9 + 2 * parts]
        xs, ids, mt = refs[9 + 2 * parts :]
        e = pl.program_id(0)

        @pl.when(e == 0)
        def _():
            sort_rows(m, sel_ref, d_refs, xs, ids)

        expert = e.astype(F32)
        for r in range(4):
            here_r = slice(r * blk, (r + 1) * blk)
            mt[here_r, :] = pick(
                ids[here_r, 2:3], ids[here_r, 3:4], expert, a_refs[r][...], b_refs[r][...]
            )
        for s, value in enumerate(t_right(mt[...], [xs[s] for s in pieces])):
            outs[s][0] = value.astype(BF16)

    def dwout(meta):
        spot = lambda e, m: (e, 0, 0)
        ins = [(v, None, None) for v in ag_a + ag_b]
        ins += [(sel, None, None)] + [(d, None, None) for d in d_pieces]
        outs = [((experts, ff, ds), BF16, (1, ff, ds), spot)] * parts
        return run(
            dwout_body, "dwout", (experts,), meta, ins, outs,
            [pltpu.VMEM((parts, rp, ds), BF16), pltpu.VMEM((rp, 8), F32), pltpu.VMEM((rp, ff), BF16)],
            flops=2 * rp * experts * parts * ds * ff,
        )

    def dwproj_body(m, *refs):
        a_refs, b_refs = refs[:4], refs[4:8]
        sel_ref, d_ref = refs[8:10]
        outs = refs[10 : 10 + parts]
        lo, hi = refs[10 + parts :]
        e = pl.program_id(0)

        @pl.when(e == 0)
        def _():
            for r in range(4):
                lanes = pl.ds(pl.multiple_of(m[2 + r] * HD, HD), HD)
                lo[:, lanes] = a_refs[r][...]
                hi[:, lanes] = b_refs[r][...]

        x = pick(sel_ref[:, 0:1], sel_ref[:, 1:2], e.astype(F32), lo[...], hi[...])
        for s, value in enumerate(t_right(x, [d_ref[s] for s in pieces])):
            outs[s][0] = value.astype(BF16)

    def dwproj(meta):
        ins = [(v, None, None) for v in gm_a + gm_b]
        ins += [(sel, None, None), (dafter_low, None, None)]
        return run(
            dwproj_body, "dwproj", (experts,), meta, ins,
            [((experts, hw, ds), BF16, (1, hw, ds), lambda e, m: (e, 0, 0))] * parts,
            [pltpu.VMEM((rp, hw), BF16)] * 2,
            flops=2 * rp * experts * hw * parts * ds,
        )

    def dwqkv_body(m, *refs):
        a_refs, b_refs = refs[:4], refs[4:8]
        sel_ref, x_ref = refs[8:10]
        q_outs, kv_outs = refs[10 : 10 + parts], refs[10 + parts : 10 + 2 * parts]
        lo, hi, dk, dv = refs[10 + 2 * parts :]
        e = pl.program_id(0)
        xs = [x_ref.at[s] for s in pieces]

        @pl.when(e == 0)
        def _():
            place_heads(m, a_refs, lo, hi)
            place_heads(m, b_refs, dk, dv)

        @pl.when(e < experts)
        def _():
            x = pick(sel_ref[:, 0:1], sel_ref[:, 1:2], e.astype(F32), lo[...], hi[...])
            for s, value in enumerate(t_left([v[...] for v in xs], x)):
                q_outs[s][0] = value.astype(BF16)

        for k, grad in enumerate((dk, dv)):

            @pl.when(e == experts + k)
            def _():
                for s, value in enumerate(t_left([v[...] for v in xs], grad[...])):
                    kv_outs[s][0] = value.astype(BF16)

    def dwqkv(meta):
        q_spot = lambda e, m: (jnp.minimum(e, experts - 1), 0, 0)
        kv_spot = lambda e, m: (jnp.maximum(e - experts, 0), 0, 0)
        ins = [(v, None, None) for v in da_a + da_b]
        ins += [(sel, None, None), (attn_input, None, None)]
        outs = [((experts, ds, hw), BF16, (1, ds, hw), q_spot)] * parts
        outs += [((2, ds, hw), BF16, (1, ds, hw), kv_spot)] * parts
        return run(
            dwqkv_body, "dwqkv", (experts + 2,), meta, ins, outs,
            [pltpu.VMEM((rp, hw), BF16)] * 4,
            flops=2 * rp * (experts + 2) * hw * parts * ds,
        )

    tiles = ff // HD

    def fold_body(m, *refs):
        add_refs, out_ref = refs[:parts], refs[parts]
        for j in range(2):
            total = add_refs[0][0, j].astype(F32)
            for ref in add_refs[1:]:
                total = total + ref[0, j].astype(F32)
            for t in range(tiles):
                out_ref[0, pl.ds(2 * t + j, ds, stride=2 * tiles), :] = total[
                    :, t * HD : (t + 1) * HD
                ]

    def fold(sums):
        got = [sums[0]] + [by_part(sums[s], s) for s in pieces[1:]]
        spot = lambda e, m: (e, 0, 0, 0)
        ins = [(v, (1, 2, ds, ff), spot) for v in got]
        outs = [((experts, 2 * tiles * ds, HD), F32, (1, 2 * tiles * ds, HD), lambda e, m: (e, 0, 0))]
        total = run(fold_body, "fold", (experts,), meta, ins, outs)[0]
        total = total.reshape(experts, ds, tiles, 2, HD).transpose(0, 1, 3, 2, 4)
        return total.reshape(experts, ds, 2, ff)

    expertin_grad = fold(dwin(meta))
    expertout_grad = exchange(dwout(meta))
    proj_grad = exchange(dwproj(meta))
    sums = dwqkv(meta)
    query_grad, kv_grad = exchange(sums[:parts]), exchange(sums[parts:])

    down_totals = wide_sum_z(*down(meta))

    def finish_body(m, *refs):
        t_refs, after_ref, out_ref = refs[:2], refs[2], refs[3]
        for k in range(4):
            span_k = at_row(m, BY_HALF + k, blk)
            for s in pieces:
                total = t_refs[k // 2][s, (k % 2) * blk : (k % 2 + 1) * blk, :]
                out_ref[s, span_k, :] = (
                    after_ref[s, span_k, :] + total.astype(F32)
                ).astype(BF16)

    ins = [(t, None, None) for t in down_totals] + [(after_rows, None, None)]
    out_rows = run(
        finish_body, "finish", (1,), meta, ins, [((parts, rp, ds), BF16, None, None)]
    )[0]

    def unpack_body(dealt, m, other_ref, *refs):
        v_refs, out_ref = refs[:parts], refs[parts]
        packed, other, total, whole = refs[parts + 1 :]
        for s in pieces:
            packed[part_rows(m, s), :] = v_refs[s][...].astype(F32)
        other[...] = other_ref[...].astype(F32)
        line = lax.broadcasted_iota(jnp.int32, (per, ds), 0)

        def one(j, carry):
            window, shift = near_rows(m, j)
            back = jnp.where(shift == 0, 0, seq_len + 8 - shift)
            whole[...] = pltpu.roll(packed[window, :], back, 0)
            for p in range(dp):
                if dealt:
                    spot = m[2 * seqs + j] * seq_len + p * per
                    kept = other[pl.ds(pl.multiple_of(spot, per), per), :]
                else:
                    kept = other[block_rows(p, j), :]
                value = whole[p * per : (p + 1) * per, :]
                total[block_rows(p, j), :] = jnp.where(line < m[seqs + j] - p * per, value, kept)
            return carry

        lax.fori_loop(0, seqs, one, 0)
        out_ref[...] = total[...].astype(BF16)

    def unpack(value, otherwise, dealt):
        mine_all = [value[0]] + [by_part(value[s], s) for s in pieces[1:]]
        ins = [(v, None, None) for v in [otherwise] + mine_all]
        spread_rows = run(
            functools.partial(unpack_body, dealt), "unpack", (1,), table, ins,
            [((rows_all, ds), BF16, None, None)],
            [
                pltpu.VMEM((n, ds), F32)
                for n in (rows + seq_len + 8, rows_all, rows_all, seq_len + 8)
            ],
        )[0]
        landed = lax.all_to_all(
            spread_rows.reshape(dp, seqs * per, ds), "dp", 0, 0, tiled=True
        )
        return landed.transpose(1, 0, 2).reshape(seqs, per, width)

    layer_out = unpack(out_rows, x_all, False)
    input_grad = unpack(dinput, d_all, True)
    return (
        layer_out,
        input_grad,
        attngain_grad,
        attnrouter_grad,
        kv_grad,
        query_grad,
        proj_grad,
        ffngain_grad,
        ffnrouter_grad,
        expertin_grad,
        expertout_grad,
    )


def solution(mesh):
    placed = (
        P(None, "dp", None),
        P("dp", None, None),
        P(),
        P(),
        P(),
        P(),
        P(),
        P(),
        P(None, "dp", "tensor"),
        P(None, "dp", "tensor"),
        P(None, "tensor", "dp"),
        P(),
        P(),
        P(None, "dp", None, "tensor"),
        P(None, "tensor", "dp"),
    )
    return jax.shard_map(
        functools.partial(local, dp=mesh.shape["dp"], tp=mesh.shape["tensor"]),
        mesh=mesh,
        in_specs=placed,
        out_specs=(
            P(None, "dp", None),
            P(None, "dp", None),
            P(),
            P(),
            P(None, "dp", "tensor"),
            P(None, "dp", "tensor"),
            P(None, "tensor", "dp"),
            P(),
            P(),
            P(None, "dp", None, "tensor"),
            P(None, "tensor", "dp"),
        ),
        check_vma=False,
    )
```

```python
import functools

import jax
import jax.numpy as jnp
from jax import lax
from jax.experimental import pallas as pl
from jax.experimental.pallas import tpu as pltpu
from jax.sharding import PartitionSpec as P

HD = 128
EPSILON = 1e-06
ROPE_BASE = 10000.0
BEST = lax.Precision.HIGHEST
F32 = jnp.float32
BF16 = jnp.bfloat16
VMEM_BYTES = 60 * 1024 * 1024


def nn(a, b):
    return lax.dot_general(a, b, (((1,), (0,)), ((), ())), preferred_element_type=F32)


def nt(a, b, precision=None):
    return lax.dot_general(
        a, b, (((1,), (1,)), ((), ())), preferred_element_type=F32, precision=precision
    )


def tn(a, b):
    return lax.dot_general(a, b, (((0,), (0,)), ((), ())), preferred_element_type=F32)


def lane_sums(values):
    ones = jnp.ones((8, values.shape[1]), F32)
    return nt(ones, values, BEST)


def run(body, name, grid, meta, ins, outs, scratch=(), flops=0):
    in_specs = []
    moved = 0
    for array, block, index in ins:
        if block is None:
            rank = array.ndim
            in_specs.append(pl.BlockSpec(array.shape, lambda *a, rank=rank: (0,) * rank))
        else:
            in_specs.append(pl.BlockSpec(block, index))
        moved += array.size * array.dtype.itemsize
    out_specs = []
    out_shape = []
    for shape, dtype, block, index in outs:
        if block is None:
            rank = len(shape)
            out_specs.append(pl.BlockSpec(shape, lambda *a, rank=rank: (0,) * rank))
        else:
            out_specs.append(pl.BlockSpec(block, index))
        out_shape.append(jax.ShapeDtypeStruct(shape, dtype))
        size = jnp.dtype(dtype).itemsize
        for extent in shape:
            size *= extent
        moved += size
    return pl.pallas_call(
        body,
        name=name,
        grid_spec=pltpu.PrefetchScalarGridSpec(
            num_scalar_prefetch=1,
            grid=grid,
            in_specs=in_specs,
            out_specs=out_specs,
            scratch_shapes=list(scratch),
        ),
        out_shape=out_shape,
        compiler_params=pltpu.CompilerParams(
            dimension_semantics=("arbitrary",) * len(grid), vmem_limit_bytes=VMEM_BYTES
        ),
        cost_estimate=pl.CostEstimate(flops=flops, bytes_accessed=moved, transcendentals=0),
    )(meta, *[array for array, _, _ in ins])


def pick(low_id, high_id, expert, low_value, high_value):
    zero = jnp.zeros_like(low_value)
    return jnp.where(
        low_id == expert, low_value, jnp.where(high_id == expert, high_value, zero)
    )


def two_slots(low_id, high_id, products):
    low_value = products[0]
    for expert in range(1, len(products) - 1):
        low_value = jnp.where(low_id == expert, products[expert], low_value)
    high_value = products[1]
    for expert in range(2, len(products)):
        high_value = jnp.where(high_id == expert, products[expert], high_value)
    return low_value, high_value


def turn(values, cosine, sine):
    return values * cosine + pltpu.roll(values, HD // 2, 1) * sine


def local(
    hidden_in,
    cotangent,
    lengths,
    dealing,
    attn_routes,
    ffn_routes,
    attn_gain,
    attn_router,
    kv_weight,
    query_weight,
    proj_weight,
    ffn_gain,
    ffn_router,
    expert_in,
    expert_out,
    *,
    dp,
    tp,
):
    seqs = dealing.shape[0]
    seq_len = cotangent.shape[1]
    slots = cotangent.shape[0]
    per = hidden_in.shape[1]
    width = hidden_in.shape[2]
    heads = query_weight.shape[2] // HD
    groups = heads
    parts = dp // groups
    ds = width // dp
    hw = heads * HD
    rows_all = seqs * seq_len
    rows = rows_all * 3 // 4
    rp = rows // parts
    blk = rp // groups
    experts = query_weight.shape[0]
    ff = expert_out.shape[1]
    scale = HD ** (-0.5)
    pieces = range(parts)

    index = lax.axis_index("dp")
    z = lax.axis_index("tensor")
    g = index // parts
    c = index % parts
    mine = ((z == 1) | (z == 2)).astype(jnp.int32)
    theirs = 1 - mine
    spots = [g, c, g, g ^ 1, g ^ 2, g ^ 3, mine, theirs]
    spots += [g ^ mine, g ^ theirs, g ^ (2 + mine), g ^ (2 + theirs)]
    spots += [g ^ (2 * mine), g ^ (2 * mine + 1), g ^ (2 * theirs), g ^ (2 * theirs + 1)]
    spots += [mine, theirs, 2 + mine, 2 + theirs]
    meta = jnp.stack(spots).astype(jnp.int32)
    BY_CHUNK, BY_HALF, IN_ORDER = 8, 12, 16

    def after(value, *others):
        return lax.optimization_barrier((value,) + others)[0]

    def both(a, b):
        return (a.astype(F32) + b.astype(F32)).astype(BF16)

    def by_group(value, mask):
        pairs = [(a, ((a // parts) ^ mask) * parts + a % parts) for a in range(dp)]
        return lax.ppermute(value, "dp", pairs)

    def by_part(value, mask):
        pairs = [(a, (a // parts) * parts + ((a % parts) ^ mask)) for a in range(dp)]
        return lax.ppermute(value, "dp", pairs)

    def to_next(value):
        pairs = [(a, a + 1) for a in range(dp) if a % parts < parts - 1]
        return lax.ppermute(value, "dp", pairs)

    def to_previous(value):
        pairs = [(a, a - 1) for a in range(dp) if a % parts > 0]
        return lax.ppermute(value, "dp", pairs)

    def by_z(value, mask):
        return lax.ppermute(value, "tensor", [(a, a ^ mask) for a in range(tp)])

    def sum_groups(value):
        return (value + by_group(value, 1)) + (by_group(value, 2) + by_group(value, 3))

    def sum_z(value):
        value = value + by_z(value, 1)
        return value + by_z(value, 3)

    def z_first(keep, send):
        return both(keep, by_z(send, 1))

    def z_second(half):
        return both(half, by_z(half, 3))

    def z_last(half):
        return half, by_z(half, 1)

    def wide_sum_z(keep, send):
        return z_last(z_second(z_first(keep, send)))

    def held(values, *others):
        return lax.optimization_barrier((tuple(values),) + others)[0]

    def reduce_groups(first, second, early=(), late=()):
        if early:
            first, second = held((tuple(first), tuple(second)), early)
        ra = by_group(first[3], 1)
        rb = by_group(second[3], 2)
        ax = by_group(first[1], 1)
        by = by_group(second[2], 2)
        along = held((both(first[2], ra), both(second[1], rb)), (ax, by), late)
        ay = by_group(along[0], 2)
        bx = by_group(along[1], 1)
        return (first[0], ax, ay), (second[0], bx, by), along, (ra, rb)

    def gather_groups(first, second, late=()):
        ax, bx = by_group(first, 1), by_group(second, 1)
        ay, by = by_group(first, 2), by_group(second, 2)
        along = held((ax, by), (bx, ay), late)
        ad, bd = by_group(along[0], 2), by_group(along[1], 1)
        return (first, ax, ay, ad), (second, bx, by, bd)

    def row_of(offset):
        return lambda *a: (a[-1][2 + offset], 0)

    def at_row(m, spot, count):
        return pl.ds(pl.multiple_of(m[spot] * count, count), count)

    wide = ds % 128 == 0

    def nn_pieces(x, weights):
        if not wide:
            return [nn(x, w) for w in weights]
        value = nn(x, jnp.concatenate(weights, axis=1))
        return [value[:, s * ds : (s + 1) * ds] for s in pieces]

    def nt_pieces(x, weights):
        if not wide:
            return [nt(x, w) for w in weights]
        value = nt(x, jnp.concatenate(weights, axis=0))
        return [value[:, s * ds : (s + 1) * ds] for s in pieces]

    ends = jnp.cumsum(lengths)
    starts = ends - lengths
    inverse = jnp.sum(
        (dealing[None, :] == jnp.arange(seqs, dtype=jnp.int32)[:, None])
        * jnp.arange(seqs, dtype=jnp.int32)[None, :],
        axis=1,
    )

    table = jnp.concatenate([starts, lengths, inverse, c[None]]).astype(jnp.int32)

    def places(part):
        packed = part * rp + jnp.arange(rp, dtype=jnp.int32)
        begun = starts[None, :] <= packed[:, None]
        first = jnp.max(jnp.where(begun, starts[None, :], 0), axis=1)
        seq = jnp.sum(begun.astype(jnp.int32), axis=1) - 1
        return seq, packed - first, first

    seq, at, first = places(c)

    def slot_rows(m, j):
        return pl.ds(pl.multiple_of(m[2 * seqs + j] * seq_len, seq_len), seq_len)

    def part_rows(m, s):
        return pl.ds(pl.multiple_of((m[3 * seqs] ^ s) * rp, rp), rp)

    def block_rows(p, j):
        return pl.ds(pl.multiple_of((p * seqs + j) * per, per), per)

    def near_rows(m, j):
        shift = m[j] & 7
        return pl.ds(pl.multiple_of(m[j] - shift, 8), seq_len + 8), shift

    def pack_body(dealt, m, all_ref, *refs):
        outs = refs[:parts]
        source, packed, whole = refs[parts:]
        source[...] = all_ref[...].astype(F32)

        line = lax.broadcasted_iota(jnp.int32, (seq_len + 8, ds), 0)

        def one(j, carry):
            if dealt:
                whole[:seq_len, :] = source[slot_rows(m, j), :]
            else:
                for p in range(dp):
                    whole[p * per : (p + 1) * per, :] = source[block_rows(p, j), :]
            window, shift = near_rows(m, j)
            moved = pltpu.roll(whole[...], shift, 0)
            packed[window, :] = jnp.where(line < shift, packed[window, :], moved)
            return carry

        lax.fori_loop(0, seqs, one, 0)
        for s in pieces:
            outs[s][...] = packed[part_rows(m, s), :].astype(BF16)

    def pack(value, dealt):
        own = run(
            functools.partial(pack_body, dealt), "pack", (1,), table, [(value, None, None)],
            [((rp, ds), BF16, None, None)] * parts,
            [pltpu.VMEM((n, ds), F32) for n in (rows_all, rows + seq_len + 8, seq_len + 8)],
        )
        return [own[0]] + [by_part(own[s], s) for s in pieces[1:]]

    x_send = hidden_in.reshape(seqs * per, dp, ds).transpose(1, 0, 2)
    x_all = lax.all_to_all(x_send, "dp", 0, 0, tiled=True).reshape(rows_all, ds)
    x_pieces = pack(x_all, False)
    d_send = cotangent.reshape(slots * seq_len, dp, ds).transpose(1, 0, 2)
    d_all = lax.all_to_all(d_send, "dp", 0, 0, tiled=True).reshape(rows_all, ds)
    d_pieces = pack(d_all, True)

    def spread(vector):
        tall = vector.reshape((groups, parts, ds) + vector.shape[1:])[g]
        return jnp.stack([tall[c ^ s] for s in pieces])

    gain_a = spread(attn_gain)[:, None, :]
    gain_f = spread(ffn_gain)[:, None, :]
    pad = ((0, 0), (0, 8 - experts), (0, 0))
    router_a = jnp.pad(spread(attn_router).transpose(0, 2, 1), pad)
    router_f = jnp.pad(spread(ffn_router).transpose(0, 2, 1), pad)

    in_own = expert_in.swapaxes(1, 2)
    wq = [query_weight] + [by_part(query_weight, s) for s in pieces[1:]]
    wkv = [kv_weight] + [by_part(kv_weight, s) for s in pieces[1:]]
    wp = [proj_weight] + [by_part(proj_weight, s) for s in pieces[1:]]
    wo = [expert_out] + [by_part(expert_out, s) for s in pieces[1:]]
    wi = [in_own] + [by_part(in_own, s) for s in pieces[1:]]

    routes = jnp.concatenate(
        [attn_routes.reshape(rows_all, 2), ffn_routes.reshape(rows_all, 2)], axis=1
    )
    here = (seq * seq_len + at)[:, None] == jnp.arange(rows_all, dtype=jnp.int32)[None, :]
    mine = jnp.dot(here.astype(BF16), routes.astype(BF16), preferred_element_type=F32)
    low_a, high_a = jnp.minimum(mine[:, 0], mine[:, 1]), jnp.maximum(mine[:, 0], mine[:, 1])
    low_f, high_f = jnp.minimum(mine[:, 2], mine[:, 3]), jnp.maximum(mine[:, 2], mine[:, 3])
    window = (first - c * rp + seq_len).astype(F32)
    nil = jnp.zeros_like(window)
    sel = jnp.stack([low_a, high_a, low_f, high_f, window, nil, nil, nil], axis=1)
    half = HD // 2
    frequency = ROPE_BASE ** (-2.0 * jnp.arange(half, dtype=F32) / HD)
    angles = at.astype(F32)[:, None] * frequency[None, :]
    cosine = jnp.concatenate([jnp.cos(angles)] * 2, axis=1)
    sine = jnp.sin(angles)
    sine = jnp.concatenate([-sine, sine], axis=1)

    def gate_columns(stats, low_id, high_id):
        rms = lax.rsqrt(stats[experts] / width + EPSILON)
        ids = jnp.arange(experts, dtype=F32)[:, None]
        logits = stats[:experts]
        low_logit = jnp.sum(jnp.where(low_id[None] == ids, logits, 0.0), axis=0) * rms
        high_logit = jnp.sum(jnp.where(high_id[None] == ids, logits, 0.0), axis=0) * rms
        gap = low_logit - high_logit
        low_gate, high_gate = jax.nn.sigmoid(gap), jax.nn.sigmoid(-gap)
        zero = jnp.zeros_like(rms)
        flat = jnp.stack([rms, low_gate, high_gate, gap, zero, zero, zero, zero])
        return flat, flat.T

    def rows_pair(refs):
        return jnp.concatenate([ref[...] for ref in refs], axis=0)

    def dhidden_body(m, *refs):
        d_refs = refs[: 2 * parts]
        w_refs, sel_refs = refs[2 * parts : 3 * parts], refs[3 * parts : 3 * parts + 2]
        outs = refs[3 * parts + 2 :]
        ids = rows_pair(sel_refs)
        rows_of = [rows_pair(d_refs[2 * s : 2 * s + 2]) for s in pieces]
        products = []
        for e in range(experts):
            products.append(sum(nt(rows_of[s], w_refs[s][e]) for s in pieces))
        low, high = two_slots(ids[:, 2:3], ids[:, 3:4], products)
        low, high = low.astype(BF16), high.astype(BF16)
        for step, pair in enumerate(((3, 1), (2, 0))):

            @pl.when(pl.program_id(0) == step)
            def _():
                for k, r in enumerate(pair):
                    outs[2 * r][...] = low[k * blk : (k + 1) * blk]
                    outs[2 * r + 1][...] = high[k * blk : (k + 1) * blk]

    def dhidden(meta):
        spots = [lambda i, m: (m[5 - i], 0), lambda i, m: (m[3 - i], 0)]
        ins = [(d, (blk, ds), spot) for d in d_pieces for spot in spots]
        ins += [(w, None, None) for w in wo]
        ins += [(sel, (blk, 8), spot) for spot in spots]
        outs = [((blk, ff), BF16, None, None)] * 8
        return run(
            dhidden_body, "dhidden", (2,), meta, ins, outs,
            flops=2 * rp * experts * parts * ds * ff,
        )

    tile = 256

    def qkv_body(m, *refs):
        x_refs = refs[:parts]
        gain_ref, router_ref = refs[parts : parts + 2]
        q_refs = refs[parts + 2 : 2 * parts + 2]
        kv_refs = refs[2 * parts + 2 : 3 * parts + 2]
        sel_ref = refs[3 * parts + 2]
        outs = refs[3 * parts + 3 : 3 * parts + 11]
        stats_ref, scr = refs[3 * parts + 11 :]
        us = []
        logits = jnp.zeros((8, tile), F32)
        squares = jnp.zeros((8, tile), F32)
        for s in pieces:
            xf = x_refs[s][...].astype(F32)
            us.append((xf * gain_ref[s]).astype(BF16))
            logits += nt(router_ref[s], us[s])
            squares += lane_sums(xf * xf)
        line = lax.broadcasted_iota(jnp.int32, (8, tile), 0)
        stats_ref[...] = jnp.where(line < experts, logits, squares)
        products = []
        for e in range(experts):
            products.append(sum(nn(us[s], q_refs[s][e]) for s in pieces))
        low, high = two_slots(sel_ref[:, 0:1], sel_ref[:, 1:2], products)
        keys = sum(nn(us[s], kv_refs[s][0]) for s in pieces)
        values = sum(nn(us[s], kv_refs[s][1]) for s in pieces)
        for k, value in enumerate((low, high, keys, values)):
            value = value.astype(BF16)
            for h in range(heads):
                scr[h, :, k * HD : (k + 1) * HD] = value[:, h * HD : (h + 1) * HD]
        for r in range(4):
            block = scr[m[2 + r]]
            outs[2 * r][...] = block[:, : 2 * HD]
            outs[2 * r + 1][...] = block[:, 2 * HD :]

    ins = [(x, (tile, ds), lambda i, m: (i, 0)) for x in x_pieces]
    ins += [(gain_a, None, None), (router_a, None, None)]
    ins += [(w, None, None) for w in wq + wkv]
    ins += [(sel, (tile, 8), lambda i, m: (i, 0))]
    outs = [((rp, 2 * HD), BF16, (tile, 2 * HD), lambda i, m: (i, 0))] * 8
    outs += [((8, rp), F32, (8, tile), lambda i, m: (0, i))]
    qkv = run(
        qkv_body, "qkv", (rp // tile,), after(meta, d_pieces[0]), ins, outs,
        [pltpu.VMEM((heads, tile, 4 * HD), BF16)],
        flops=2 * rp * (experts + 2) * parts * ds * hw,
    )
    dh = dhidden(after(meta, qkv[8]))
    q_sum, kv_sum, sent, far = reduce_groups(qkv[0:8:2], qkv[1:8:2], late=dh[0])
    stats_a = sum_groups(after(qkv[8], far))
    flat_a, cols_a = gate_columns(stats_a, low_a, high_a)

    def rope_body(m, a0, a1, a2, b0, b1, b2, cols, cos_ref, sin_ref, q_ref, kv_ref):
        rms = cols[:, 0:1]
        cos, sin = cos_ref[...], sin_ref[...]
        q = (a0[...].astype(F32) + a1[...].astype(F32) + a2[...].astype(F32)) * rms
        kv = (b0[...].astype(F32) + b1[...].astype(F32) + b2[...].astype(F32)) * rms
        q_ref[:, :HD] = turn(q[:, :HD], cos, sin).astype(BF16)
        q_ref[:, HD:] = turn(q[:, HD:], cos, sin).astype(BF16)
        kv_ref[:, :HD] = turn(kv[:, :HD], cos, sin).astype(BF16)
        kv_ref[:, HD:] = kv[:, HD:].astype(BF16)

    ins = [(v, (tile, 2 * HD), lambda i, m: (i, 0)) for v in q_sum + kv_sum]
    ins += [(cols_a, (tile, 8), lambda i, m: (i, 0))]
    ins += [(v, (tile, HD), lambda i, m: (i, 0)) for v in (cosine, sine)]
    outs = [((rp, 2 * HD), BF16, (tile, 2 * HD), lambda i, m: (i, 0))] * 2
    q_rot, kv_rot = run(rope_body, "rope", (rp // tile,), after(meta, dh[0]), ins, outs)
    halo = to_next(kv_rot[rp - seq_len :])

    qt = 128
    span = seq_len + qt

    def window_mask(i, low_key):
        u = i * qt + lax.broadcasted_iota(jnp.int32, (qt, span), 1)
        t = seq_len + i * qt + lax.broadcasted_iota(jnp.int32, (qt, span), 0)
        return (u >= low_key.astype(jnp.int32)) & (u <= t)

    def softmax_of(query, key, allowed):
        score = jnp.where(allowed, nt(query, key) * scale, -1e30)
        top = jnp.max(score, axis=1, keepdims=True)
        raised = jnp.exp(score - top)
        return raised / jnp.sum(raised, axis=1, keepdims=True)

    def attend_body(m, q_ref, kv_ref, halo_ref, sel_ref, cols, ga, gb, ma, mb, ext):
        i = pl.program_id(0)

        @pl.when(i == 0)
        def _():
            ext[:seq_len, :] = halo_ref[...]
            ext[seq_len:, :] = kv_ref[...]

        near = ext[pl.ds(pl.multiple_of(i * qt, qt), span), :]
        allowed = window_mask(i, sel_ref[:, 4:5])
        for k, (g_ref, m_ref) in enumerate(((ga, ma), (gb, mb))):
            probs = softmax_of(q_ref[:, k * HD : (k + 1) * HD], near[:, :HD], allowed)
            mixed = nn(probs.astype(BF16), near[:, HD:]).astype(BF16)
            m_ref[...] = mixed
            g_ref[...] = (mixed.astype(F32) * cols[:, 1 + k : 2 + k]).astype(BF16)

    def qrow(i, m):
        return (i, 0)

    ins = [(q_rot, (qt, 2 * HD), qrow), (kv_rot, None, None), (halo, None, None)]
    ins += [(sel, (qt, 8), qrow), (cols_a, (qt, 8), qrow)]
    outs = [((rp, HD), BF16, (qt, HD), qrow)] * 4
    gated_a, gated_b, mixed_a, mixed_b = run(
        attend_body, "attend", (rp // qt,), meta, ins, outs,
        [pltpu.VMEM((seq_len + rp, 2 * HD), BF16)],
        flops=8 * rp * span * HD,
    )
    gm_a, gm_b = gather_groups(gated_a, gated_b)
    chunks = 2
    zr = rp // chunks // 2
    hold = [((parts, zr, ds), BF16, None, None)] * 2

    def store_halves(i, refs, s, value):
        @pl.when(i == 0)
        def _():
            refs[1][s] = value

        @pl.when(i == 1)
        def _():
            refs[0][s] = value

    def proj_body(m, *refs):
        a_refs, b_refs = refs[:4], refs[4:8]
        sel_ref = refs[8]
        w_refs = refs[9 : 9 + parts]
        outs, xs = refs[9 + parts : 11 + parts], refs[11 + parts]
        for r in range(4):
            lanes = pl.ds(pl.multiple_of(m[2 + r] * HD, HD), HD)
            for e in range(experts):
                xs[e, :, lanes] = pick(
                    sel_ref[:, 0:1], sel_ref[:, 1:2], e, a_refs[r][...], b_refs[r][...]
                )
        acc = nn_pieces(xs[0], [w[0] for w in w_refs])
        for e in range(1, experts):
            for s, value in enumerate(nn_pieces(xs[e], [w[e] for w in w_refs])):
                acc[s] += value
        for s in pieces:
            store_halves(pl.program_id(0), outs, s, acc[s].astype(BF16))

    def project(k, meta):
        half = lambda i, m: (2 * k + m[7 - i], 0)
        ins = [(v, (zr, HD), half) for v in gm_a + gm_b]
        ins += [(sel, (zr, 8), half)]
        ins += [(w, None, None) for w in wp]
        return run(
            proj_body, "proj", (2,), meta, ins, hold,
            [pltpu.VMEM((experts, zr, hw), BF16)],
            flops=4 * zr * experts * hw * parts * ds,
        )

    halves = [z_first(*project(0, meta))]
    dh_a, dh_b = held((dh[0:8:2], dh[1:8:2]), gm_a[3], gm_b[3])
    ra, rb = by_group(dh_a[3], 1), by_group(dh_b[3], 2)
    for k in range(1, chunks):
        halves.append(z_first(*project(k, after(meta, halves[-1], ra, rb))))
    near = held((dh_a[1], dh_b[2]), halves[0])
    ax, by = by_group(near[0], 1), by_group(near[1], 2)
    halves = held([z_second(half) for half in halves], ax, by)
    along = held((both(dh_a[2], ra), both(dh_b[1], rb)), halves)
    dh_a, dh_b = (dh_a[0], ax, by_group(along[0], 2)), (dh_b[0], by_group(along[1], 1), by)
    attn_totals = [half for v in halves for half in z_last(v)]

    def norm_body(m, *refs):
        t_refs = refs[: 2 * chunks]
        x_refs = refs[2 * chunks : 2 * chunks + parts]
        gain_ref, router_ref, after_ref, u_ref, stats_ref = refs[2 * chunks + parts :]
        for k in range(2 * chunks):
            span_k = at_row(m, IN_ORDER + k, zr)
            for s in pieces:
                after_ref[s, span_k, :] = x_refs[s][span_k, :].astype(F32) + t_refs[k][s].astype(F32)
        logits = jnp.zeros((8, rp), F32)
        squares = jnp.zeros((8, rp), F32)
        for s in pieces:
            af = after_ref[s]
            u = (af * gain_ref[s]).astype(BF16)
            u_ref[s] = u
            logits += nt(router_ref[s], u)
            squares += lane_sums(af * af)
        line = lax.broadcasted_iota(jnp.int32, (8, rp), 0)
        stats_ref[...] = jnp.where(line < experts, logits, squares)

    ins = [(t, None, None) for t in attn_totals + x_pieces]
    ins += [(gain_f, None, None), (router_f, None, None)]
    outs = [
        ((parts, rp, ds), F32, None, None),
        ((parts, rp, ds), BF16, None, None),
        ((8, rp), F32, None, None),
    ]
    after_rows, u_f, stats_part = run(norm_body, "norm", (1,), meta, ins, outs)
    stats_f = sum_groups(stats_part)
    flat_f, cols_f = gate_columns(stats_f, low_f, high_f)

    def up_body(m, *refs):
        u_refs, w_refs = refs[:2], refs[2 : 2 + parts]
        sel_refs = refs[2 + parts : 4 + parts]
        outs = refs[4 + parts :]
        ids = rows_pair(sel_refs)
        rows_of = [jnp.concatenate([u[s] for u in u_refs], axis=0) for s in pieces]
        products = []
        for e in range(experts):
            products.append(sum(nn(rows_of[s], w_refs[s][e, 0]) for s in pieces))
        low, high = two_slots(ids[:, 2:3], ids[:, 3:4], products)
        low, high = low.astype(BF16), high.astype(BF16)
        for k in range(2):
            outs[2 * k][0] = low[k * blk : (k + 1) * blk]
            outs[2 * k + 1][0] = high[k * blk : (k + 1) * blk]

    def up(pair, meta):
        def block_of(r):
            return lambda j, m: (0, m[2 + r], 0)

        ins = [(u_f, (parts, blk, ds), block_of(r)) for r in pair]
        ins += [(w, (experts, 1, ds, ff), lambda j, m: (0, j, 0, 0)) for w in wi]
        ins += [(sel, (blk, 8), row_of(r)) for r in pair]
        outs = [((2, blk, ff), BF16, (1, blk, ff), lambda j, m: (j, 0, 0))] * 4
        return run(
            up_body, "up", (2,), meta, ins, outs, flops=8 * blk * experts * parts * ds * ff
        )

    up_far = up((3, 1), after(meta, stats_f, dh_a[2], dh_b[1]))
    up_near = up((2, 0), after(meta, up_far[0]))
    gu_a, gu_b, _, _ = reduce_groups(
        (up_near[2], up_far[2], up_near[0], up_far[0]),
        (up_near[3], up_far[3], up_near[1], up_far[1]),
    )

    mt_rows = blk // 3

    def mid_body(m, *refs):
        gu = (refs[0:3], refs[3:6])
        dhr = (refs[6:9], refs[9:12])
        cols = refs[12]
        acts, grads, dots = refs[13:15], refs[15:17], refs[17]
        rms = cols[:, 0:1]
        column = lax.broadcasted_iota(jnp.int32, (mt_rows, 8), 1)
        found = []
        inner = jnp.zeros((mt_rows, 1), F32)
        for k in range(2):
            gate = cols[:, 1 + k : 2 + k]
            gp = sum(v[0].astype(F32) for v in gu[k]) * rms
            up_pre = sum(v[1].astype(F32) for v in gu[k]) * rms
            raw = sum(v[...].astype(F32) for v in dhr[k])
            sg = jax.nn.sigmoid(gp)
            act = (gp * sg * up_pre).astype(BF16).astype(F32)
            grad = raw * gate
            dgp = (grad * up_pre * sg * (1.0 + gp * (1.0 - sg))).astype(BF16)
            dup = (grad * gp * sg).astype(BF16)
            acts[k][...] = (act * gate).astype(BF16)
            grads[k][0] = dgp
            grads[k][1] = dup
            found.append(jnp.sum(act * raw, axis=1, keepdims=True))
            inner += jnp.sum(
                dgp.astype(F32) * gp + dup.astype(F32) * up_pre, axis=1, keepdims=True
            )
        zero = jnp.zeros((mt_rows, 8), F32)
        for k, value in enumerate(found + [inner]):
            zero = jnp.where(column == k, value, zero)
        dots[...] = zero

    rows_3 = lambda i, m: (0, i, 0)
    rows_2 = lambda i, m: (i, 0)
    ins = [(v, (2, mt_rows, ff), rows_3) for v in gu_a + gu_b]
    ins += [(v, (mt_rows, ff), rows_2) for v in dh_a + dh_b]
    ins += [(cols_f, (mt_rows, 8), lambda i, m: (3 * m[2] + i, 0))]
    outs = [((blk, ff), BF16, (mt_rows, ff), rows_2)] * 2
    outs += [((2, blk, ff), BF16, (2, mt_rows, ff), rows_3)] * 2
    outs += [((blk, 8), F32, (mt_rows, 8), rows_2)]
    act_a, act_b, grad_a, grad_b, dots_f = run(mid_body, "mid", (3,), meta, ins, outs)
    gg_a, gg_b = gather_groups(grad_a, grad_b)
    dots_f = dots_f.T

    dots_f = after(sum_z(dots_f), gg_a[3], gg_b[3])
    dots_f = jnp.stack([dots_f, by_group(dots_f, 1), by_group(dots_f, 2), by_group(dots_f, 3)])
    act_a, act_b, _ = lax.optimization_barrier((act_a, act_b, (gg_a[3], gg_b[3])))
    ag_a = [act_a, by_group(act_a, 1), by_group(act_a, 2)]
    ag_b = [act_b, by_group(act_b, 1), by_group(act_b, 2)]
    dots_f = jnp.take(dots_f, g ^ jnp.arange(4, dtype=jnp.int32), axis=0)
    dots_f = dots_f.transpose(1, 0, 2).reshape(8, rp)

    def back_columns(flat, dots, low_id, high_id):
        delta = flat[1] * flat[2] * (dots[0] - dots[1])
        inner = (dots[2] + delta * flat[3]) / width
        ids = jnp.arange(experts, dtype=F32)[:, None]
        dlogit = jnp.where(low_id[None] == ids, delta[None], 0.0) - jnp.where(
            high_id[None] == ids, delta[None], 0.0
        )
        zero = jnp.zeros((1, rp), F32)
        return jnp.concatenate(
            [dlogit, inner[None], flat[0:1]] + [zero] * (6 - experts), axis=0
        ).T

    back_f = back_columns(flat_f, dots_f, low_f, high_f)

    def dx_body(m, *refs):
        a_refs, b_refs = refs[:2], refs[2:4]
        w_refs = refs[4 : 4 + parts]
        sel_refs = refs[4 + parts : 6 + parts]
        keep_ref, send_ref, acc, xs = refs[6 + parts :]
        e = pl.program_id(0)
        expert = e.astype(F32)

        @pl.when(e == 0)
        def _():
            acc[...] = jnp.zeros_like(acc)

        for j in range(2):
            for k in range(2):
                ids = sel_refs[k]
                xs[k * blk : (k + 1) * blk, :] = pick(
                    ids[:, 2:3], ids[:, 3:4], expert, a_refs[k][j], b_refs[k][j]
                )
            for s, value in enumerate(nt_pieces(xs[...], [w[0, j] for w in w_refs])):
                acc[s] += value

        @pl.when(e == experts - 1)
        def _():
            keep_ref[...] = acc[:, at_row(m, 6, blk), :].astype(BF16)
            send_ref[...] = acc[:, at_row(m, 7, blk), :].astype(BF16)

    def dx(pair, meta):
        ins = [(v[r], None, None) for v in (gg_a, gg_b) for r in pair]
        ins += [(w, (1, 2, ds, ff), lambda e, m: (e, 0, 0, 0)) for w in wi]
        ins += [(sel, (blk, 8), row_of(r)) for r in pair]
        return run(
            dx_body, "dx", (experts,), meta, ins, [((parts, blk, ds), BF16, None, None)] * 2,
            [pltpu.VMEM((parts, 2 * blk, ds), F32), pltpu.VMEM((2 * blk, ff), BF16)],
            flops=8 * blk * experts * parts * ds * ff,
        )

    dx_near = dx((0, 1), meta)
    dx_far = dx((2, 3), meta)
    far_half = z_first(*dx_far)
    dx_totals = wide_sum_z(*dx_near) + z_last(z_second(far_half))

    def exchange(sums):
        total = sums[0].astype(F32)
        for s in pieces[1:]:
            total = total + by_part(sums[s], s).astype(F32)
        return total

    ffn_input = (after_rows * flat_f[0][None, :, None] * gain_f).astype(BF16)

    def t_left(xs, value):
        if not wide:
            return [tn(x, value) for x in xs]
        total = tn(jnp.concatenate(xs, axis=1), value)
        return [total[s * ds : (s + 1) * ds] for s in pieces]

    def t_right(value, xs):
        if not wide:
            return [tn(value, x) for x in xs]
        total = tn(value, jnp.concatenate(xs, axis=1))
        return [total[:, s * ds : (s + 1) * ds] for s in pieces]

    def sort_rows(m, sel_ref, x_refs, xs, ids):
        for r in range(4):
            src, here_r = at_row(m, 2 + r, blk), slice(r * blk, (r + 1) * blk)
            for s in pieces:
                xs[s, here_r, :] = x_refs[s][src, :]
            ids[here_r, :] = sel_ref[src, :]

    def dwin_body(m, *refs):
        a_refs, b_refs = refs[:4], refs[4:8]
        sel_ref, x_ref = refs[8:10]
        outs = refs[10 : 10 + parts]
        xs, ids, mt = refs[10 + parts :]
        e = pl.program_id(0)

        @pl.when(e == 0)
        def _():
            sort_rows(m, sel_ref, [x_ref.at[s] for s in pieces], xs, ids)

        expert = e.astype(F32)
        for r in range(4):
            here_r = slice(r * blk, (r + 1) * blk)
            mt[here_r, :] = pick(
                ids[here_r, 2:3], ids[here_r, 3:4], expert, a_refs[r][0], b_refs[r][0]
            )
        for s, value in enumerate(t_left([xs[s] for s in pieces], mt[...])):
            outs[s][0] = value.astype(BF16)

    def dwin(j, meta):
        ins = [(v, (1, blk, ff), lambda e, m: (j, 0, 0)) for v in gg_a + gg_b]
        ins += [(sel, None, None), (ffn_input, None, None)]
        outs = [((experts, ds, ff), BF16, (1, ds, ff), lambda e, m: (e, 0, 0))] * parts
        return run(
            dwin_body, "dwin", (experts,), meta, ins, outs,
            [pltpu.VMEM((parts, rp, ds), BF16), pltpu.VMEM((rp, 8), F32), pltpu.VMEM((rp, ff), BF16)],
            flops=2 * rp * experts * parts * ds * ff,
        )

    def fold_body(m, *refs):
        out_ref = refs[2 * parts]
        for j in range(2):
            total = refs[j * parts][0].astype(F32)
            for ref in refs[j * parts + 1 : (j + 1) * parts]:
                total = total + ref[0].astype(F32)
            out_ref[0, :, j, :] = total

    def fold(sums, meta):
        ins = []
        for half in sums:
            got = [half[0]] + [by_part(half[s], s) for s in pieces[1:]]
            ins += [(v, (1, ds, ff), lambda e, m: (e, 0, 0)) for v in got]
        outs = [((experts, ds, 2, ff), F32, (1, ds, 2, ff), lambda e, m: (e, 0, 0, 0))]
        return run(fold_body, "fold", (experts,), meta, ins, outs)[0]

    dwin_gate = dwin(0, after(meta, far_half))

    def norm_back_body(low_precision_out, m, *refs):
        t_refs = refs[:4]
        after_ref = refs[4]
        ups = parts if low_precision_out else 1
        up_refs = refs[5 : 5 + ups]
        gain_ref, router_ref, back = refs[5 + ups : 8 + ups]
        outs = refs[8 + ups :]
        small = outs[-1]
        for s in pieces:
            gain = gain_ref[s]
            router = router_ref[s].astype(F32)
            gain_sum = jnp.zeros((1, ds), F32)
            router_sum = [jnp.zeros((1, ds), F32)] * experts
            for r in range(4):
                span_r = at_row(m, (BY_CHUNK if low_precision_out else IN_ORDER) + r, blk)
                up_value = up_refs[s][span_r, :] if low_precision_out else up_refs[0][s, span_r, :]
                x = after_ref[s, span_r, :].astype(F32)
                cols = back[span_r, :]
                rms = cols[:, experts + 1 : experts + 2]
                grad = t_refs[r][s].astype(F32)
                for e in range(experts):
                    grad += cols[:, e : e + 1] * router[e : e + 1]
                normed = x * rms
                token = (normed * gain).astype(BF16).astype(F32)
                gain_sum += jnp.sum(grad * normed, axis=0, keepdims=True)
                for e in range(experts):
                    router_sum[e] = router_sum[e] + jnp.sum(
                        token * cols[:, e : e + 1], axis=0, keepdims=True
                    )
                dn = grad * gain
                total = up_value.astype(F32) + rms * (
                    dn - normed * cols[:, experts : experts + 1]
                )
                if low_precision_out:
                    outs[0][s, span_r, :] = total
                    outs[1][s, span_r, :] = total.astype(BF16)
                else:
                    outs[0][s, span_r, :] = total.astype(BF16)
            for e in range(experts):
                small[e, s] = router_sum[e][0]
            small[experts, s] = gain_sum[0]

    ins = [(t, None, None) for t in dx_totals]
    ins += [(after_rows, None, None)] + [(d, None, None) for d in d_pieces]
    ins += [(gain_f, None, None), (router_f, None, None), (back_f, None, None)]
    outs = [
        ((parts, rp, ds), F32, None, None),
        ((parts, rp, ds), BF16, None, None),
        ((experts + 1, parts, ds), F32, None, None),
    ]
    dafter, dafter_low, small_f = run(
        functools.partial(norm_back_body, True), "norm_back", (1,),
        after(meta, dwin_gate[0], ag_a[1:], ag_b[1:]), ins, outs,
    )

    def whole_vectors(*smalls):
        small = jnp.concatenate(smalls, axis=0)
        full = jnp.zeros((small.shape[0], dp, ds), F32)
        for s in pieces:
            full = lax.dynamic_update_slice_in_dim(
                full, small[:, s : s + 1], g * parts + (c ^ s), axis=1
            )
        mask = 1
        while mask < dp:
            full = full + lax.ppermute(full, "dp", [(a, a ^ mask) for a in range(dp)])
            mask *= 2
        full = full.reshape(len(smalls), experts + 1, width)
        return [(v[:experts].T, v[experts]) for v in full]

    def dmix_body(m, *refs):
        d_ref = refs[0]
        w_refs = refs[1 : 1 + parts]
        sel_ref = refs[1 + parts]
        outs = refs[2 + parts : 10 + parts]
        scr = refs[10 + parts]
        products = []
        for e in range(experts):
            products.append(sum(nt(d_ref[s], w_refs[s][e]) for s in pieces))
        low, high = two_slots(sel_ref[:, 0:1], sel_ref[:, 1:2], products)
        for k, value in enumerate((low, high)):
            value = value.astype(BF16)
            for h in range(heads):
                scr[h, :, k * HD : (k + 1) * HD] = value[:, h * HD : (h + 1) * HD]
        for r in range(4):
            block = scr[m[2 + r]]
            outs[2 * r][...] = block[:, :HD]
            outs[2 * r + 1][...] = block[:, HD:]

    ins = [(dafter_low, (parts, tile, ds), lambda i, m: (0, i, 0))]
    ins += [(w, None, None) for w in wp]
    ins += [(sel, (tile, 8), lambda i, m: (i, 0))]
    outs = [((rp, HD), BF16, (tile, HD), lambda i, m: (i, 0))] * 8
    dm = run(
        dmix_body, "dmix", (rp // tile,), meta, ins, outs,
        [pltpu.VMEM((heads, tile, 2 * HD), BF16)],
        flops=2 * rp * experts * parts * ds * hw,
    )
    dwin_up = dwin(1, after(meta, dm[0]))
    dm_a, dm_b, _, _ = reduce_groups(dm[0:8:2], dm[1:8:2], late=dwin_up[0])
    along = held((ag_a[1], ag_b[2]), dm_a[2], dm_b[1])
    ag_a, ag_b = ag_a + [by_group(along[0], 2)], ag_b + [by_group(along[1], 1)]

    def attend_back_body(m, *refs):
        q_ref, kv_ref, halo_ref, sel_ref, cols, cos_ref, sin_ref = refs[:7]
        d_refs = (refs[7:10], refs[10:13])
        mix_refs = refs[13:15]
        dq_ref, own_ref, far_ref, dots_ref, ext, acc = refs[15:]
        i = pl.program_id(0)

        @pl.when(i == 0)
        def _():
            ext[:seq_len, :] = halo_ref[...]
            ext[seq_len:, :] = kv_ref[...]
            acc[...] = jnp.zeros_like(acc)

        near_rows = pl.ds(pl.multiple_of(i * qt, qt), span)
        near = ext[near_rows, :]
        allowed = window_mask(i, sel_ref[:, 4:5])
        line = lax.broadcasted_iota(jnp.int32, (8, qt), 0)
        inner = jnp.zeros((qt, HD), F32)
        found = []
        dk = jnp.zeros((span, HD), F32)
        dv = jnp.zeros((span, HD), F32)
        for k in range(2):
            query = q_ref[:, k * HD : (k + 1) * HD]
            probs = softmax_of(query, near[:, :HD], allowed)
            raw = sum(v[...].astype(F32) for v in d_refs[k])
            dmixed = (raw * cols[:, 1 + k : 2 + k]).astype(BF16)
            found.append(raw * mix_refs[k][...].astype(F32))
            dv += tn(probs.astype(BF16), dmixed)
            dprob = nt(dmixed, near[:, HD:])
            rest = jnp.sum(probs * dprob, axis=1, keepdims=True)
            dscore = (probs * (dprob - rest)).astype(BF16)
            dk += tn(dscore, query) * scale
            dquery = nn(dscore, near[:, :HD]) * scale
            inner += dquery * query.astype(F32)
            dq_ref[:, k * HD : (k + 1) * HD] = turn(dquery, cos_ref[...], -sin_ref[...]).astype(BF16)
        acc[near_rows, :HD] += dk
        acc[near_rows, HD:] += dv
        dots_ref[...] = jnp.where(
            line == 0, lane_sums(found[0]), jnp.where(line == 1, lane_sums(found[1]), lane_sums(inner))
        )

        @pl.when(i == rp // qt - 1)
        def _():
            far_ref[...] = acc[:seq_len, :]
            own_ref[...] = acc[seq_len:, :]

    ins = [(q_rot, (qt, 2 * HD), qrow), (kv_rot, None, None), (halo, None, None)]
    ins += [(sel, (qt, 8), qrow), (cols_a, (qt, 8), qrow)]
    ins += [(cosine, (qt, HD), qrow), (sine, (qt, HD), qrow)]
    ins += [(v, (qt, HD), qrow) for v in dm_a + dm_b + (mixed_a, mixed_b)]
    outs = [
        ((rp, 2 * HD), BF16, (qt, 2 * HD), qrow),
        ((rp, 2 * HD), F32, None, None),
        ((seq_len, 2 * HD), F32, None, None),
        ((8, rp), F32, (8, qt), lambda i, m: (0, i)),
    ]
    dq, dkv_own, dkv_far, dots_q = run(
        attend_back_body, "attend_back", (rp // qt,), meta, ins, outs,
        [pltpu.VMEM((seq_len + rp, 2 * HD), BF16), pltpu.VMEM((seq_len + rp, 2 * HD), F32)],
        flops=20 * rp * span * HD,
    )
    dkv_in = to_previous(dkv_far)

    def dkv_body(m, own_ref, in_ref, kv_ref, cos_ref, sin_ref, out_ref, dots_ref):
        head = rp - seq_len
        for rows_here in (slice(0, head), slice(head, rp)):
            value = own_ref[rows_here, :]
            if rows_here.start == head:
                value = value + in_ref[...]
            out_ref[rows_here, :HD] = turn(
                value[:, :HD], cos_ref[rows_here, :], -sin_ref[rows_here, :]
            ).astype(BF16)
            out_ref[rows_here, HD:] = value[:, HD:].astype(BF16)
            dots_ref[:, rows_here] = lane_sums(value * kv_ref[rows_here, :].astype(F32))

    ins = [(v, None, None) for v in (dkv_own, dkv_in, kv_rot, cosine, sine)]
    outs = [((rp, 2 * HD), BF16, None, None), ((8, rp), F32, None, None)]
    dkv, dots_kv = run(dkv_body, "dkv", (1,), meta, ins, outs)
    third = jnp.arange(8)[:, None] == 2
    def down_body(m, *refs):
        a_refs, b_refs = refs[:4], refs[4:8]
        sel_ref, d_refs = refs[8], refs[9 : 9 + parts]
        w_refs = refs[9 + parts : 9 + 2 * parts]
        keep_ref, send_ref = refs[9 + 2 * parts : 11 + 2 * parts]
        outs = refs[11 + 2 * parts : 11 + 3 * parts]
        acc, xs, ids, mt = refs[11 + 3 * parts :]
        e = pl.program_id(0)

        @pl.when(e == 0)
        def _():
            acc[...] = jnp.zeros_like(acc)
            sort_rows(m, sel_ref, d_refs, xs, ids)

        expert = e.astype(F32)
        for r in range(4):
            here_r = slice(r * blk, (r + 1) * blk)
            mt[here_r, :] = pick(
                ids[here_r, 2:3], ids[here_r, 3:4], expert, a_refs[r][...], b_refs[r][...]
            )
        for s, value in enumerate(nn_pieces(mt[...], [w[0] for w in w_refs])):
            acc[s] += value
        for s, value in enumerate(t_right(mt[...], [xs[s] for s in pieces])):
            outs[s][0] = value.astype(BF16)

        @pl.when(e == experts - 1)
        def _():
            keep_ref[...] = acc[:, at_row(m, 6, 2 * blk), :].astype(BF16)
            send_ref[...] = acc[:, at_row(m, 7, 2 * blk), :].astype(BF16)

    def down(meta):
        spot = lambda e, m: (e, 0, 0)
        ins = [(v, None, None) for v in ag_a + ag_b]
        ins += [(sel, None, None)] + [(d, None, None) for d in d_pieces]
        ins += [(w, (1, ff, ds), spot) for w in wo]
        outs = [((parts, 2 * blk, ds), BF16, None, None)] * 2
        outs += [((experts, ff, ds), BF16, (1, ff, ds), spot)] * parts
        return run(
            down_body, "down", (experts,), meta, ins, outs,
            [
                pltpu.VMEM((parts, rp, ds), F32),
                pltpu.VMEM((parts, rp, ds), BF16),
                pltpu.VMEM((rp, 8), F32),
                pltpu.VMEM((rp, ff), BF16),
            ],
            flops=4 * rp * experts * parts * ds * ff,
        )

    def dwproj_body(m, *refs):
        a_refs, b_refs = refs[:4], refs[4:8]
        sel_ref, d_ref = refs[8:10]
        outs = refs[10 : 10 + parts]
        lo, hi = refs[10 + parts :]
        e = pl.program_id(0)

        @pl.when(e == 0)
        def _():
            for r in range(4):
                lanes = pl.ds(pl.multiple_of(m[2 + r] * HD, HD), HD)
                lo[:, lanes] = a_refs[r][...]
                hi[:, lanes] = b_refs[r][...]

        x = pick(sel_ref[:, 0:1], sel_ref[:, 1:2], e.astype(F32), lo[...], hi[...])
        for s, value in enumerate(t_right(x, [d_ref[s] for s in pieces])):
            outs[s][0] = value.astype(BF16)

    def dwproj(meta):
        ins = [(v, None, None) for v in gm_a + gm_b]
        ins += [(sel, None, None), (dafter_low, None, None)]
        return run(
            dwproj_body, "dwproj", (experts,), meta, ins,
            [((experts, hw, ds), BF16, (1, hw, ds), lambda e, m: (e, 0, 0))] * parts,
            [pltpu.VMEM((rp, hw), BF16)] * 2,
            flops=2 * rp * experts * hw * parts * ds,
        )

    down_halves = down(after(meta, dkv))
    down_halves, dwout_sums = down_halves[:2], down_halves[2:]
    da_a, da_b = gather_groups(dq, dkv, late=dwout_sums[0])
    dwproj_sums = dwproj(after(meta, dwout_sums[0]))
    dots_a = sum_z(sum_groups(after(dots_q, da_a[3], da_b[3]) + jnp.where(third, dots_kv, 0.0)))
    back_a = back_columns(flat_a, dots_a, low_a, high_a)


    def place_heads(m, refs, lo, hi):
        for r in range(4):
            lanes = pl.ds(pl.multiple_of(m[2 + r] * HD, HD), HD)
            lo[:, lanes] = refs[r][:, :HD]
            hi[:, lanes] = refs[r][:, HD:]

    def dattn_body(m, *refs):
        a_refs, b_refs = refs[:4], refs[4:8]
        sel_ref = refs[8]
        q_refs = refs[9 : 9 + parts]
        kv_refs = refs[9 + parts : 9 + 2 * parts]
        outs = refs[9 + 2 * parts : 11 + 2 * parts]
        lo, hi, dk, dv = refs[11 + 2 * parts :]
        place_heads(m, a_refs, lo, hi)
        place_heads(m, b_refs, dk, dv)
        acc = nt_pieces(dk[...], [w[0] for w in kv_refs])
        for s, value in enumerate(nt_pieces(dv[...], [w[1] for w in kv_refs])):
            acc[s] += value
        for e in range(experts):
            x = pick(sel_ref[:, 0:1], sel_ref[:, 1:2], e, lo[...], hi[...])
            for s, value in enumerate(nt_pieces(x, [w[e] for w in q_refs])):
                acc[s] += value
        for s in pieces:
            store_halves(pl.program_id(0), outs, s, acc[s].astype(BF16))

    def dattn(k, meta):
        half = lambda i, m: (2 * k + m[7 - i], 0)
        ins = [(v, (zr, 2 * HD), half) for v in da_a + da_b]
        ins += [(sel, (zr, 8), half)]
        ins += [(w, None, None) for w in wq + wkv]
        return run(
            dattn_body, "dattn", (2,), meta, ins, hold,
            [pltpu.VMEM((zr, hw), BF16)] * 4,
            flops=4 * zr * (experts + 2) * hw * parts * ds,
        )

    da_halves = [z_first(*dattn(0, after(meta, dwproj_sums[0])))]
    for k in range(1, chunks):
        da_halves.append(z_first(*dattn(k, after(meta, da_halves[-1]))))
    x_stack = jnp.stack(x_pieces)
    attn_input = (x_stack.astype(F32) * flat_a[0][None, :, None] * gain_a).astype(BF16)

    def dwqkv_body(m, *refs):
        a_refs, b_refs = refs[:4], refs[4:8]
        sel_ref, x_ref = refs[8:10]
        q_outs, kv_outs = refs[10 : 10 + parts], refs[10 + parts : 10 + 2 * parts]
        lo, hi, dk, dv = refs[10 + 2 * parts :]
        e = pl.program_id(0)
        xs = [x_ref.at[s] for s in pieces]

        @pl.when(e == 0)
        def _():
            place_heads(m, a_refs, lo, hi)
            place_heads(m, b_refs, dk, dv)

        @pl.when(e < experts)
        def _():
            x = pick(sel_ref[:, 0:1], sel_ref[:, 1:2], e.astype(F32), lo[...], hi[...])
            for s, value in enumerate(t_left([v[...] for v in xs], x)):
                q_outs[s][0] = value.astype(BF16)

        for k, grad in enumerate((dk, dv)):

            @pl.when(e == experts + k)
            def _():
                for s, value in enumerate(t_left([v[...] for v in xs], grad[...])):
                    kv_outs[s][0] = value.astype(BF16)

    def dwqkv(meta):
        q_spot = lambda e, m: (jnp.minimum(e, experts - 1), 0, 0)
        kv_spot = lambda e, m: (jnp.maximum(e - experts, 0), 0, 0)
        ins = [(v, None, None) for v in da_a + da_b]
        ins += [(sel, None, None), (attn_input, None, None)]
        outs = [((experts, ds, hw), BF16, (1, ds, hw), q_spot)] * parts
        outs += [((2, ds, hw), BF16, (1, ds, hw), kv_spot)] * parts
        return run(
            dwqkv_body, "dwqkv", (experts + 2,), meta, ins, outs,
            [pltpu.VMEM((rp, hw), BF16)] * 4,
            flops=2 * rp * (experts + 2) * hw * parts * ds,
        )

    dwqkv_sums = dwqkv(after(meta, da_halves))
    da_halves = held([z_second(half) for half in da_halves], dwqkv_sums[0])
    da_totals = [half for v in da_halves for half in z_last(v)]
    expertin_grad = fold((dwin_gate, dwin_up), after(meta, dwqkv_sums[0]))
    ins = [(t, None, None) for t in da_totals]
    ins += [(x_stack, None, None), (dafter, None, None)]
    ins += [(gain_a, None, None), (router_a, None, None), (back_a, None, None)]
    outs = [((parts, rp, ds), BF16, None, None), ((experts + 1, parts, ds), F32, None, None)]
    dinput, small_a = run(
        functools.partial(norm_back_body, False), "norm_back_first", (1,),
        after(meta, expertin_grad), ins, outs,
    )
    expertout_grad = exchange(dwout_sums)
    proj_grad = exchange(dwproj_sums)
    query_grad, kv_grad = exchange(dwqkv_sums[:parts]), exchange(dwqkv_sums[parts:])
    down_totals = wide_sum_z(*down_halves)

    def finish_body(m, *refs):
        t_refs, after_ref, out_ref = refs[:2], refs[2], refs[3]
        for k in range(4):
            span_k = at_row(m, BY_HALF + k, blk)
            for s in pieces:
                total = t_refs[k // 2][s, (k % 2) * blk : (k % 2 + 1) * blk, :]
                out_ref[s, span_k, :] = (
                    after_ref[s, span_k, :] + total.astype(F32)
                ).astype(BF16)

    ins = [(t, None, None) for t in down_totals] + [(after_rows, None, None)]
    out_rows = run(
        finish_body, "finish", (1,), meta, ins, [((parts, rp, ds), BF16, None, None)]
    )[0]

    def unpack_body(dealt, m, other_ref, *refs):
        v_refs, out_ref = refs[:parts], refs[parts]
        packed, other, total, whole = refs[parts + 1 :]
        for s in pieces:
            packed[part_rows(m, s), :] = v_refs[s][...].astype(F32)
        other[...] = other_ref[...].astype(F32)
        line = lax.broadcasted_iota(jnp.int32, (per, ds), 0)

        def one(j, carry):
            window, shift = near_rows(m, j)
            back = jnp.where(shift == 0, 0, seq_len + 8 - shift)
            whole[...] = pltpu.roll(packed[window, :], back, 0)
            for p in range(dp):
                if dealt:
                    spot = m[2 * seqs + j] * seq_len + p * per
                    kept = other[pl.ds(pl.multiple_of(spot, per), per), :]
                else:
                    kept = other[block_rows(p, j), :]
                value = whole[p * per : (p + 1) * per, :]
                total[block_rows(p, j), :] = jnp.where(line < m[seqs + j] - p * per, value, kept)
            return carry

        lax.fori_loop(0, seqs, one, 0)
        out_ref[...] = total[...].astype(BF16)

    def unpack(value, otherwise, dealt):
        mine_all = [value[0]] + [by_part(value[s], s) for s in pieces[1:]]
        ins = [(v, None, None) for v in [otherwise] + mine_all]
        spread_rows = run(
            functools.partial(unpack_body, dealt), "unpack", (1,), table, ins,
            [((rows_all, ds), BF16, None, None)],
            [
                pltpu.VMEM((n, ds), F32)
                for n in (rows + seq_len + 8, rows_all, rows_all, seq_len + 8)
            ],
        )[0]
        landed = lax.all_to_all(
            spread_rows.reshape(dp, seqs * per, ds), "dp", 0, 0, tiled=True
        )
        return landed.transpose(1, 0, 2).reshape(seqs, per, width), spread_rows

    layer_out, _ = unpack(out_rows, x_all, False)
    input_grad, last_rows = unpack(dinput, d_all, True)
    vectors = whole_vectors(after(small_a, last_rows), small_f)
    (attnrouter_grad, attngain_grad), (ffnrouter_grad, ffngain_grad) = vectors
    return (
        layer_out,
        input_grad,
        attngain_grad,
        attnrouter_grad,
        kv_grad,
        query_grad,
        proj_grad,
        ffngain_grad,
        ffnrouter_grad,
        expertin_grad,
        expertout_grad,
    )


def solution(mesh):
    placed = (
        P(None, "dp", None),
        P("dp", None, None),
        P(),
        P(),
        P(),
        P(),
        P(),
        P(),
        P(None, "dp", "tensor"),
        P(None, "dp", "tensor"),
        P(None, "tensor", "dp"),
        P(),
        P(),
        P(None, "dp", None, "tensor"),
        P(None, "tensor", "dp"),
    )
    return jax.shard_map(
        functools.partial(local, dp=mesh.shape["dp"], tp=mesh.shape["tensor"]),
        mesh=mesh,
        in_specs=placed,
        out_specs=(
            P(None, "dp", None),
            P(None, "dp", None),
            P(),
            P(),
            P(None, "dp", "tensor"),
            P(None, "dp", "tensor"),
            P(None, "tensor", "dp"),
            P(),
            P(),
            P(None, "dp", None, "tensor"),
            P(None, "tensor", "dp"),
        ),
        check_vma=False,
    )
```

```python
import functools

import jax
import jax.numpy as jnp
from jax import lax
from jax.experimental import pallas as pl
from jax.experimental.pallas import tpu as pltpu
from jax.sharding import PartitionSpec as P

HD = 128
EPSILON = 1e-06
ROPE_BASE = 10000.0
BEST = lax.Precision.HIGHEST
F32 = jnp.float32
BF16 = jnp.bfloat16
VMEM_BYTES = 60 * 1024 * 1024


def nn(a, b):
    return lax.dot_general(a, b, (((1,), (0,)), ((), ())), preferred_element_type=F32)


def nt(a, b, precision=None):
    return lax.dot_general(
        a, b, (((1,), (1,)), ((), ())), preferred_element_type=F32, precision=precision
    )


def tn(a, b):
    return lax.dot_general(a, b, (((0,), (0,)), ((), ())), preferred_element_type=F32)


def lane_sums(values):
    ones = jnp.ones((8, values.shape[1]), F32)
    return nt(ones, values, BEST)


def run(body, name, grid, meta, ins, outs, scratch=(), flops=0):
    in_specs = []
    moved = 0
    for array, block, index in ins:
        if block is None:
            rank = array.ndim
            in_specs.append(pl.BlockSpec(array.shape, lambda *a, rank=rank: (0,) * rank))
        else:
            in_specs.append(pl.BlockSpec(block, index))
        moved += array.size * array.dtype.itemsize
    out_specs = []
    out_shape = []
    for shape, dtype, block, index in outs:
        if block is None:
            rank = len(shape)
            out_specs.append(pl.BlockSpec(shape, lambda *a, rank=rank: (0,) * rank))
        else:
            out_specs.append(pl.BlockSpec(block, index))
        out_shape.append(jax.ShapeDtypeStruct(shape, dtype))
        size = jnp.dtype(dtype).itemsize
        for extent in shape:
            size *= extent
        moved += size
    return pl.pallas_call(
        body,
        name=name,
        grid_spec=pltpu.PrefetchScalarGridSpec(
            num_scalar_prefetch=1,
            grid=grid,
            in_specs=in_specs,
            out_specs=out_specs,
            scratch_shapes=list(scratch),
        ),
        out_shape=out_shape,
        compiler_params=pltpu.CompilerParams(
            dimension_semantics=("arbitrary",) * len(grid), vmem_limit_bytes=VMEM_BYTES
        ),
        cost_estimate=pl.CostEstimate(flops=flops, bytes_accessed=moved, transcendentals=0),
    )(meta, *[array for array, _, _ in ins])


def pick(low_id, high_id, expert, low_value, high_value):
    zero = jnp.zeros_like(low_value)
    return jnp.where(
        low_id == expert, low_value, jnp.where(high_id == expert, high_value, zero)
    )


def two_slots(low_id, high_id, products):
    low_value = products[0]
    for expert in range(1, len(products) - 1):
        low_value = jnp.where(low_id == expert, products[expert], low_value)
    high_value = products[1]
    for expert in range(2, len(products)):
        high_value = jnp.where(high_id == expert, products[expert], high_value)
    return low_value, high_value


def turn(values, cosine, sine):
    return values * cosine + pltpu.roll(values, HD // 2, 1) * sine


def local(
    hidden_in,
    cotangent,
    lengths,
    dealing,
    attn_routes,
    ffn_routes,
    attn_gain,
    attn_router,
    kv_weight,
    query_weight,
    proj_weight,
    ffn_gain,
    ffn_router,
    expert_in,
    expert_out,
    *,
    dp,
    tp,
):
    seqs = dealing.shape[0]
    seq_len = cotangent.shape[1]
    slots = cotangent.shape[0]
    per = hidden_in.shape[1]
    width = hidden_in.shape[2]
    heads = query_weight.shape[2] // HD
    groups = heads
    parts = dp // groups
    ds = width // dp
    hw = heads * HD
    rows_all = seqs * seq_len
    rows = rows_all * 3 // 4
    rp = rows // parts
    blk = rp // groups
    experts = query_weight.shape[0]
    ff = expert_out.shape[1]
    scale = HD ** (-0.5)
    pieces = range(parts)

    index = lax.axis_index("dp")
    z = lax.axis_index("tensor")
    g = index // parts
    c = index % parts
    mine = ((z == 1) | (z == 2)).astype(jnp.int32)
    theirs = 1 - mine
    spots = [g, c, g, g ^ 1, g ^ 2, g ^ 3, mine, theirs]
    spots += [g ^ mine, g ^ theirs, g ^ (2 + mine), g ^ (2 + theirs)]
    spots += [g ^ (2 * mine), g ^ (2 * mine + 1), g ^ (2 * theirs), g ^ (2 * theirs + 1)]
    spots += [mine, theirs, 2 + mine, 2 + theirs]
    spots += [2 * mine, 2 * mine + 1, 2 * theirs, 2 * theirs + 1]
    meta = jnp.stack(spots).astype(jnp.int32)
    BY_CHUNK, BY_HALF, IN_ORDER, IN_HALVES = 8, 12, 16, 20

    def after(value, *others):
        return lax.optimization_barrier((value,) + others)[0]

    def both(a, b):
        return (a.astype(F32) + b.astype(F32)).astype(BF16)

    def by_group(value, mask):
        pairs = [(a, ((a // parts) ^ mask) * parts + a % parts) for a in range(dp)]
        return lax.ppermute(value, "dp", pairs)

    def by_part(value, mask):
        pairs = [(a, (a // parts) * parts + ((a % parts) ^ mask)) for a in range(dp)]
        return lax.ppermute(value, "dp", pairs)

    def to_next(value):
        pairs = [(a, a + 1) for a in range(dp) if a % parts < parts - 1]
        return lax.ppermute(value, "dp", pairs)

    def to_previous(value):
        pairs = [(a, a - 1) for a in range(dp) if a % parts > 0]
        return lax.ppermute(value, "dp", pairs)

    def by_z(value, mask):
        return lax.ppermute(value, "tensor", [(a, a ^ mask) for a in range(tp)])

    def sum_groups(value):
        return (value + by_group(value, 1)) + (by_group(value, 2) + by_group(value, 3))

    def sum_z(value):
        return (value + by_z(value, 1)) + (by_z(value, 2) + by_z(value, 3))

    def z_first(keep, send):
        return both(keep, by_z(send, 1))

    def z_second(half):
        return both(half, by_z(half, 3))

    def z_covered(keep, send, mask, cover):
        keep, got = held((keep, by_z(send, mask)), cover)
        return both(keep, got)

    def z_last(half):
        return half, by_z(half, 1)

    def wide_sum_z(keep, send):
        return z_last(z_second(z_first(keep, send)))

    def held(values, *others):
        return lax.optimization_barrier((tuple(values),) + others)[0]

    def reduce_groups(first, second, early=(), late=()):
        if early:
            first, second = held((tuple(first), tuple(second)), early)
        ra = by_group(first[3], 1)
        rb = by_group(second[3], 2)
        ax = by_group(first[1], 1)
        by = by_group(second[2], 2)
        along = held((both(first[2], ra), both(second[1], rb)), (ax, by), late)
        ay = by_group(along[0], 2)
        bx = by_group(along[1], 1)
        return (first[0], ax, ay), (second[0], bx, by), along, (ra, rb)

    def gather_groups(first, second, late=()):
        ax, bx = by_group(first, 1), by_group(second, 1)
        ay, by = by_group(first, 2), by_group(second, 2)
        along = held((ax, by), (bx, ay), late) if len(late) else (ax, by)
        ad, bd = by_group(along[0], 2), by_group(along[1], 1)
        return (first, ax, ay, ad), (second, bx, by, bd), along

    def row_of(offset):
        return lambda *a: (a[-1][2 + offset], 0)

    def at_row(m, spot, count):
        return pl.ds(pl.multiple_of(m[spot] * count, count), count)

    wide = ds % 128 == 0

    def nn_pieces(x, weights):
        if not wide:
            return [nn(x, w) for w in weights]
        value = nn(x, jnp.concatenate(weights, axis=1))
        return [value[:, s * ds : (s + 1) * ds] for s in pieces]

    def nt_pieces(x, weights):
        if not wide:
            return [nt(x, w) for w in weights]
        value = nt(x, jnp.concatenate(weights, axis=0))
        return [value[:, s * ds : (s + 1) * ds] for s in pieces]

    ends = jnp.cumsum(lengths)
    starts = ends - lengths
    inverse = jnp.sum(
        (dealing[None, :] == jnp.arange(seqs, dtype=jnp.int32)[:, None])
        * jnp.arange(seqs, dtype=jnp.int32)[None, :],
        axis=1,
    )

    table = jnp.concatenate([starts, lengths, inverse, c[None]]).astype(jnp.int32)

    def places(part):
        packed = part * rp + jnp.arange(rp, dtype=jnp.int32)
        begun = starts[None, :] <= packed[:, None]
        first = jnp.max(jnp.where(begun, starts[None, :], 0), axis=1)
        seq = jnp.sum(begun.astype(jnp.int32), axis=1) - 1
        return seq, packed - first, first

    seq, at, first = places(c)

    def slot_rows(m, j):
        return pl.ds(pl.multiple_of(m[2 * seqs + j] * seq_len, seq_len), seq_len)

    def part_rows(m, s):
        return pl.ds(pl.multiple_of((m[3 * seqs] ^ s) * rp, rp), rp)

    def block_rows(p, j):
        return pl.ds(pl.multiple_of((p * seqs + j) * per, per), per)

    def near_rows(m, j):
        shift = m[j] & 7
        return pl.ds(pl.multiple_of(m[j] - shift, 8), seq_len + 8), shift

    def take_rows(dealt, source, all_ref):
        count = slots * seq_len if dealt else seqs * per
        start = seqs * per if dealt else 0
        for p in range(dp):
            source[p * count : (p + 1) * count, :] = all_ref[p, start : start + count, :].astype(F32)

    def pack_body(dealt, m, all_ref, *refs):
        outs = refs[:parts]
        source, packed, whole = refs[parts:]
        take_rows(dealt, source, all_ref)

        line = lax.broadcasted_iota(jnp.int32, (seq_len + 8, ds), 0)

        def one(j, carry):
            if dealt:
                whole[:seq_len, :] = source[slot_rows(m, j), :]
            else:
                for p in range(dp):
                    whole[p * per : (p + 1) * per, :] = source[block_rows(p, j), :]
            window, shift = near_rows(m, j)
            moved = pltpu.roll(whole[...], shift, 0)
            packed[window, :] = jnp.where(line < shift, packed[window, :], moved)
            return carry

        lax.fori_loop(0, seqs, one, 0)
        for s in pieces:
            outs[s][...] = packed[part_rows(m, s), :].astype(BF16)

    def pack(value, dealt):
        own = run(
            functools.partial(pack_body, dealt), "pack", (1,), table, [(value, None, None)],
            [((rp, ds), BF16, None, None)] * parts,
            [pltpu.VMEM((n, ds), F32) for n in (rows_all, rows + seq_len + 8, seq_len + 8)],
        )
        return [own[0]] + [by_part(own[s], s) for s in pieces[1:]]

    x_send = hidden_in.reshape(seqs * per, dp, ds).transpose(1, 0, 2)
    d_send = cotangent.reshape(slots * seq_len, dp, ds).transpose(1, 0, 2)
    arrived = lax.all_to_all(
        jnp.concatenate([x_send, d_send], axis=1), "dp", 0, 0, tiled=True
    )
    x_pieces = pack(arrived, False)
    d_pieces = pack(arrived, True)

    def spread(vector):
        tall = vector.reshape((groups, parts, ds) + vector.shape[1:])[g]
        return jnp.stack([tall[c ^ s] for s in pieces])

    gain_a = spread(attn_gain)[:, None, :]
    gain_f = spread(ffn_gain)[:, None, :]
    pad = ((0, 0), (0, 8 - experts), (0, 0))
    router_a = jnp.pad(spread(attn_router).transpose(0, 2, 1), pad)
    router_f = jnp.pad(spread(ffn_router).transpose(0, 2, 1), pad)

    in_own = expert_in.swapaxes(1, 2)
    wq = [query_weight] + [by_part(query_weight, s) for s in pieces[1:]]
    wkv = [kv_weight] + [by_part(kv_weight, s) for s in pieces[1:]]
    wp = [proj_weight] + [by_part(proj_weight, s) for s in pieces[1:]]
    wo = [expert_out] + [by_part(expert_out, s) for s in pieces[1:]]
    wi = [in_own] + [by_part(in_own, s) for s in pieces[1:]]

    routes = jnp.concatenate(
        [attn_routes.reshape(rows_all, 2), ffn_routes.reshape(rows_all, 2)], axis=1
    )
    here = (seq * seq_len + at)[:, None] == jnp.arange(rows_all, dtype=jnp.int32)[None, :]
    mine = jnp.dot(here.astype(BF16), routes.astype(BF16), preferred_element_type=F32)
    low_a, high_a = jnp.minimum(mine[:, 0], mine[:, 1]), jnp.maximum(mine[:, 0], mine[:, 1])
    low_f, high_f = jnp.minimum(mine[:, 2], mine[:, 3]), jnp.maximum(mine[:, 2], mine[:, 3])
    window = (first - c * rp + seq_len).astype(F32)
    nil = jnp.zeros_like(window)
    sel = jnp.stack([low_a, high_a, low_f, high_f, window, nil, nil, nil], axis=1)
    half = HD // 2
    frequency = ROPE_BASE ** (-2.0 * jnp.arange(half, dtype=F32) / HD)
    angles = at.astype(F32)[:, None] * frequency[None, :]
    cosine = jnp.concatenate([jnp.cos(angles)] * 2, axis=1)
    sine = jnp.sin(angles)
    sine = jnp.concatenate([-sine, sine], axis=1)

    def gate_columns(stats, low_id, high_id):
        rms = lax.rsqrt(stats[experts] / width + EPSILON)
        ids = jnp.arange(experts, dtype=F32)[:, None]
        logits = stats[:experts]
        low_logit = jnp.sum(jnp.where(low_id[None] == ids, logits, 0.0), axis=0) * rms
        high_logit = jnp.sum(jnp.where(high_id[None] == ids, logits, 0.0), axis=0) * rms
        gap = low_logit - high_logit
        low_gate, high_gate = jax.nn.sigmoid(gap), jax.nn.sigmoid(-gap)
        zero = jnp.zeros_like(rms)
        flat = jnp.stack([rms, low_gate, high_gate, gap, zero, zero, zero, zero])
        return flat, flat.T

    def rows_pair(refs):
        return jnp.concatenate([ref[...] for ref in refs], axis=0)

    def dhidden_body(m, *refs):
        d_refs = refs[: 2 * parts]
        w_refs, sel_refs = refs[2 * parts : 3 * parts], refs[3 * parts : 3 * parts + 2]
        outs = refs[3 * parts + 2 :]
        ids = rows_pair(sel_refs)
        rows_of = [rows_pair(d_refs[2 * s : 2 * s + 2]) for s in pieces]
        products = []
        for e in range(experts):
            products.append(sum(nt(rows_of[s], w_refs[s][e]) for s in pieces))
        low, high = two_slots(ids[:, 2:3], ids[:, 3:4], products)
        low, high = low.astype(BF16), high.astype(BF16)
        for step, pair in enumerate(((3, 1), (2, 0))):

            @pl.when(pl.program_id(0) == step)
            def _():
                for k, r in enumerate(pair):
                    outs[2 * r][...] = low[k * blk : (k + 1) * blk]
                    outs[2 * r + 1][...] = high[k * blk : (k + 1) * blk]

    def dhidden(meta):
        spots = [lambda i, m: (m[5 - i], 0), lambda i, m: (m[3 - i], 0)]
        ins = [(d, (blk, ds), spot) for d in d_pieces for spot in spots]
        ins += [(w, None, None) for w in wo]
        ins += [(sel, (blk, 8), spot) for spot in spots]
        outs = [((blk, ff), BF16, None, None)] * 8
        return run(
            dhidden_body, "dhidden", (2,), meta, ins, outs,
            flops=2 * rp * experts * parts * ds * ff,
        )

    tile = 256

    def qkv_body(m, *refs):
        x_refs = refs[:parts]
        gain_ref, router_ref = refs[parts : parts + 2]
        q_refs = refs[parts + 2 : 2 * parts + 2]
        kv_refs = refs[2 * parts + 2 : 3 * parts + 2]
        sel_ref = refs[3 * parts + 2]
        outs = refs[3 * parts + 3 : 3 * parts + 11]
        stats_ref, scr = refs[3 * parts + 11 :]
        us = []
        logits = jnp.zeros((8, tile), F32)
        squares = jnp.zeros((8, tile), F32)
        for s in pieces:
            xf = x_refs[s][...].astype(F32)
            us.append((xf * gain_ref[s]).astype(BF16))
            logits += nt(router_ref[s], us[s])
            squares += lane_sums(xf * xf)
        line = lax.broadcasted_iota(jnp.int32, (8, tile), 0)
        stats_ref[...] = jnp.where(line < experts, logits, squares)
        products = []
        for e in range(experts):
            products.append(sum(nn(us[s], q_refs[s][e]) for s in pieces))
        low, high = two_slots(sel_ref[:, 0:1], sel_ref[:, 1:2], products)
        keys = sum(nn(us[s], kv_refs[s][0]) for s in pieces)
        values = sum(nn(us[s], kv_refs[s][1]) for s in pieces)
        for k, value in enumerate((low, high, keys, values)):
            value = value.astype(BF16)
            for h in range(heads):
                scr[h, :, k * HD : (k + 1) * HD] = value[:, h * HD : (h + 1) * HD]
        for r in range(4):
            block = scr[m[2 + r]]
            outs[2 * r][...] = block[:, : 2 * HD]
            outs[2 * r + 1][...] = block[:, 2 * HD :]

    ins = [(x, (tile, ds), lambda i, m: (i, 0)) for x in x_pieces]
    ins += [(gain_a, None, None), (router_a, None, None)]
    ins += [(w, None, None) for w in wq + wkv]
    ins += [(sel, (tile, 8), lambda i, m: (i, 0))]
    outs = [((rp, 2 * HD), BF16, (tile, 2 * HD), lambda i, m: (i, 0))] * 8
    outs += [((8, rp), F32, (8, tile), lambda i, m: (0, i))]
    qkv = run(
        qkv_body, "qkv", (rp // tile,), after(meta, d_pieces[0]), ins, outs,
        [pltpu.VMEM((heads, tile, 4 * HD), BF16)],
        flops=2 * rp * (experts + 2) * parts * ds * hw,
    )
    dh = dhidden(after(meta, qkv[8]))
    q_sum, kv_sum, sent, far = reduce_groups(qkv[0:8:2], qkv[1:8:2])
    stats_a = sum_groups(after(qkv[8], far))
    flat_a, cols_a = gate_columns(stats_a, low_a, high_a)

    def rope_body(m, a0, a1, a2, b0, b1, b2, cols, cos_ref, sin_ref, q_ref, kv_ref):
        rms = cols[:, 0:1]
        cos, sin = cos_ref[...], sin_ref[...]
        q = (a0[...].astype(F32) + a1[...].astype(F32) + a2[...].astype(F32)) * rms
        kv = (b0[...].astype(F32) + b1[...].astype(F32) + b2[...].astype(F32)) * rms
        q_ref[:, :HD] = turn(q[:, :HD], cos, sin).astype(BF16)
        q_ref[:, HD:] = turn(q[:, HD:], cos, sin).astype(BF16)
        kv_ref[:, :HD] = turn(kv[:, :HD], cos, sin).astype(BF16)
        kv_ref[:, HD:] = kv[:, HD:].astype(BF16)

    ins = [(v, (tile, 2 * HD), lambda i, m: (i, 0)) for v in q_sum + kv_sum]
    ins += [(cols_a, (tile, 8), lambda i, m: (i, 0))]
    ins += [(v, (tile, HD), lambda i, m: (i, 0)) for v in (cosine, sine)]
    outs = [((rp, 2 * HD), BF16, (tile, 2 * HD), lambda i, m: (i, 0))] * 2
    q_rot, kv_rot = run(rope_body, "rope", (rp // tile,), after(meta, dh[0]), ins, outs)
    halo = to_next(kv_rot[rp - seq_len :])

    qt = 128
    span = seq_len + qt

    def window_mask(i, low_key):
        u = i * qt + lax.broadcasted_iota(jnp.int32, (qt, span), 1)
        t = seq_len + i * qt + lax.broadcasted_iota(jnp.int32, (qt, span), 0)
        return (u >= low_key.astype(jnp.int32)) & (u <= t)

    def softmax_of(query, key, allowed):
        score = jnp.where(allowed, nt(query, key) * scale, -1e30)
        top = jnp.max(score, axis=1, keepdims=True)
        raised = jnp.exp(score - top)
        return raised / jnp.sum(raised, axis=1, keepdims=True)

    def attend_body(m, q_ref, kv_ref, halo_ref, sel_ref, cols, ga, gb, ma, mb, ext):
        i = pl.program_id(0)

        @pl.when(i == 0)
        def _():
            ext[:seq_len, :] = halo_ref[...]
            ext[seq_len:, :] = kv_ref[...]

        near = ext[pl.ds(pl.multiple_of(i * qt, qt), span), :]
        allowed = window_mask(i, sel_ref[:, 4:5])
        for k, (g_ref, m_ref) in enumerate(((ga, ma), (gb, mb))):
            probs = softmax_of(q_ref[:, k * HD : (k + 1) * HD], near[:, :HD], allowed)
            mixed = nn(probs.astype(BF16), near[:, HD:]).astype(BF16)
            m_ref[...] = mixed
            g_ref[...] = (mixed.astype(F32) * cols[:, 1 + k : 2 + k]).astype(BF16)

    def qrow(i, m):
        return (i, 0)

    ins = [(q_rot, (qt, 2 * HD), qrow), (kv_rot, None, None), (halo, None, None)]
    ins += [(sel, (qt, 8), qrow), (cols_a, (qt, 8), qrow)]
    outs = [((rp, HD), BF16, (qt, HD), qrow)] * 4
    gated_a, gated_b, mixed_a, mixed_b = run(
        attend_body, "attend", (rp // qt,), meta, ins, outs,
        [pltpu.VMEM((seq_len + rp, 2 * HD), BF16)],
        flops=8 * rp * span * HD,
    )
    gm_a, gm_b, _ = gather_groups(gated_a, gated_b)
    chunks = 2
    zr = rp // chunks // 2
    hold = [((parts, zr, ds), BF16, None, None)] * 2

    def store_halves(i, refs, s, value):
        @pl.when(i == 0)
        def _():
            refs[1][s] = value

        @pl.when(i == 1)
        def _():
            refs[0][s] = value

    def proj_body(m, *refs):
        a_refs, b_refs = refs[:4], refs[4:8]
        sel_ref = refs[8]
        w_refs = refs[9 : 9 + parts]
        outs, xs = refs[9 + parts : 11 + parts], refs[11 + parts]
        for r in range(4):
            lanes = pl.ds(pl.multiple_of(m[2 + r] * HD, HD), HD)
            for e in range(experts):
                xs[e, :, lanes] = pick(
                    sel_ref[:, 0:1], sel_ref[:, 1:2], e, a_refs[r][...], b_refs[r][...]
                )
        acc = nn_pieces(xs[0], [w[0] for w in w_refs])
        for e in range(1, experts):
            for s, value in enumerate(nn_pieces(xs[e], [w[e] for w in w_refs])):
                acc[s] += value
        for s in pieces:
            store_halves(pl.program_id(0), outs, s, acc[s].astype(BF16))

    def project(k, meta):
        half = lambda i, m: (2 * k + m[7 - i], 0)
        ins = [(v, (zr, HD), half) for v in gm_a + gm_b]
        ins += [(sel, (zr, 8), half)]
        ins += [(w, None, None) for w in wp]
        return run(
            proj_body, "proj", (2,), meta, ins, hold,
            [pltpu.VMEM((experts, zr, hw), BF16)],
            flops=4 * zr * experts * hw * parts * ds,
        )

    halves = [z_first(*project(0, meta))]
    dh_a, dh_b = held((dh[0:8:2], dh[1:8:2]), gm_a[3], gm_b[3])
    ra, rb = by_group(dh_a[3], 1), by_group(dh_b[3], 2)
    for k in range(1, chunks):
        halves.append(z_first(*project(k, after(meta, halves[-1]))))
    ax, by = by_group(dh_a[1], 1), by_group(dh_b[2], 2)
    halves = [z_second(half) for half in halves]
    along = held((both(dh_a[2], ra), both(dh_b[1], rb)), (ax, by))
    dh_a, dh_b = (dh_a[0], ax, by_group(along[0], 2)), (dh_b[0], by_group(along[1], 1), by)
    attn_totals = [half for v in halves for half in z_last(v)]

    def norm_body(m, *refs):
        t_refs = refs[: 2 * chunks]
        x_refs = refs[2 * chunks : 2 * chunks + parts]
        gain_ref, router_ref, after_ref, u_ref, stats_ref = refs[2 * chunks + parts :]
        for k in range(2 * chunks):
            span_k = at_row(m, IN_ORDER + k, zr)
            for s in pieces:
                after_ref[s, span_k, :] = x_refs[s][span_k, :].astype(F32) + t_refs[k][s].astype(F32)
        logits = jnp.zeros((8, rp), F32)
        squares = jnp.zeros((8, rp), F32)
        for s in pieces:
            af = after_ref[s]
            u = (af * gain_ref[s]).astype(BF16)
            u_ref[s] = u
            logits += nt(router_ref[s], u)
            squares += lane_sums(af * af)
        line = lax.broadcasted_iota(jnp.int32, (8, rp), 0)
        stats_ref[...] = jnp.where(line < experts, logits, squares)

    ins = [(t, None, None) for t in attn_totals + x_pieces]
    ins += [(gain_f, None, None), (router_f, None, None)]
    outs = [
        ((parts, rp, ds), F32, None, None),
        ((parts, rp, ds), BF16, None, None),
        ((8, rp), F32, None, None),
    ]
    after_rows, u_f, stats_part = run(norm_body, "norm", (1,), after(meta, along), ins, outs)
    def up_body(m, *refs):
        u_refs, w_refs = refs[:2], refs[2 : 2 + parts]
        sel_refs = refs[2 + parts : 4 + parts]
        outs = refs[4 + parts :]
        ids = rows_pair(sel_refs)
        rows_of = [jnp.concatenate([u[s] for u in u_refs], axis=0) for s in pieces]
        products = []
        for e in range(experts):
            products.append(sum(nn(rows_of[s], w_refs[s][e, 0]) for s in pieces))
        low, high = two_slots(ids[:, 2:3], ids[:, 3:4], products)
        low, high = low.astype(BF16), high.astype(BF16)
        for k in range(2):
            outs[2 * k][0] = low[k * blk : (k + 1) * blk]
            outs[2 * k + 1][0] = high[k * blk : (k + 1) * blk]

    def up(pair, meta):
        def block_of(r):
            return lambda j, m: (0, m[2 + r], 0)

        ins = [(u_f, (parts, blk, ds), block_of(r)) for r in pair]
        ins += [(w, (experts, 1, ds, ff), lambda j, m: (0, j, 0, 0)) for w in wi]
        ins += [(sel, (blk, 8), row_of(r)) for r in pair]
        outs = [((2, blk, ff), BF16, (1, blk, ff), lambda j, m: (j, 0, 0))] * 4
        return run(
            up_body, "up", (2,), meta, ins, outs, flops=8 * blk * experts * parts * ds * ff
        )

    up_far = up((3, 1), after(meta, dh_a[2], dh_b[1]))
    up_near = up((2, 0), after(meta, up_far[0]))
    gu_a, gu_b, _, far = reduce_groups(
        (up_near[2], up_far[2], up_near[0], up_far[0]),
        (up_near[3], up_far[3], up_near[1], up_far[1]),
    )

    stats_f = sum_groups(after(stats_part, far))
    flat_f, cols_f = gate_columns(stats_f, low_f, high_f)

    mt_rows = blk // 3

    def mid_body(m, *refs):
        gu = (refs[0:3], refs[3:6])
        dhr = (refs[6:9], refs[9:12])
        cols = refs[12]
        acts, grads, dots = refs[13:15], refs[15:17], refs[17]
        rms = cols[:, 0:1]
        column = lax.broadcasted_iota(jnp.int32, (mt_rows, 8), 1)
        found = []
        inner = jnp.zeros((mt_rows, 1), F32)
        for k in range(2):
            gate = cols[:, 1 + k : 2 + k]
            gp = sum(v[0].astype(F32) for v in gu[k]) * rms
            up_pre = sum(v[1].astype(F32) for v in gu[k]) * rms
            raw = sum(v[...].astype(F32) for v in dhr[k])
            sg = jax.nn.sigmoid(gp)
            act = (gp * sg * up_pre).astype(BF16).astype(F32)
            grad = raw * gate
            dgp = (grad * up_pre * sg * (1.0 + gp * (1.0 - sg))).astype(BF16)
            dup = (grad * gp * sg).astype(BF16)
            acts[k][...] = (act * gate).astype(BF16)
            grads[k][0] = dgp
            grads[k][1] = dup
            found.append(jnp.sum(act * raw, axis=1, keepdims=True))
            inner += jnp.sum(
                dgp.astype(F32) * gp + dup.astype(F32) * up_pre, axis=1, keepdims=True
            )
        zero = jnp.zeros((mt_rows, 8), F32)
        for k, value in enumerate(found + [inner]):
            zero = jnp.where(column == k, value, zero)
        dots[...] = zero

    rows_3 = lambda i, m: (0, i, 0)
    rows_2 = lambda i, m: (i, 0)
    ins = [(v, (2, mt_rows, ff), rows_3) for v in gu_a + gu_b]
    ins += [(v, (mt_rows, ff), rows_2) for v in dh_a + dh_b]
    ins += [(cols_f, (mt_rows, 8), lambda i, m: (3 * m[2] + i, 0))]
    outs = [((blk, ff), BF16, (mt_rows, ff), rows_2)] * 2
    outs += [((2, blk, ff), BF16, (2, mt_rows, ff), rows_3)] * 2
    outs += [((blk, 8), F32, (mt_rows, 8), rows_2)]
    act_a, act_b, grad_a, grad_b, dots_f = run(mid_body, "mid", (3,), meta, ins, outs)
    gg_a, gg_b, _ = gather_groups(grad_a, grad_b, late=(act_a,))
    dots_f = dots_f.T

    def dx_body(m, *refs):
        a_refs, b_refs = refs[:2], refs[2:4]
        w_refs = refs[4 : 4 + parts]
        sel_refs = refs[4 + parts : 6 + parts]
        keep_ref, send_ref, acc, xs = refs[6 + parts :]
        e = pl.program_id(0)
        expert = e.astype(F32)

        @pl.when(e == 0)
        def _():
            acc[...] = jnp.zeros_like(acc)

        for j in range(2):
            for k in range(2):
                ids = sel_refs[k]
                xs[k * blk : (k + 1) * blk, :] = pick(
                    ids[:, 2:3], ids[:, 3:4], expert, a_refs[k][j], b_refs[k][j]
                )
            for s, value in enumerate(nt_pieces(xs[...], [w[0, j] for w in w_refs])):
                acc[s] += value

        @pl.when(e == experts - 1)
        def _():
            keep_ref[...] = acc[:, at_row(m, 6, blk), :].astype(BF16)
            send_ref[...] = acc[:, at_row(m, 7, blk), :].astype(BF16)

    def dx(pair, meta):
        ins = [(v[r], None, None) for v in (gg_a, gg_b) for r in pair]
        ins += [(w, (1, 2, ds, ff), lambda e, m: (e, 0, 0, 0)) for w in wi]
        ins += [(sel, (blk, 8), row_of(r)) for r in pair]
        return run(
            dx_body, "dx", (experts,), meta, ins, [((parts, blk, ds), BF16, None, None)] * 2,
            [pltpu.VMEM((parts, 2 * blk, ds), F32), pltpu.VMEM((2 * blk, ff), BF16)],
            flops=8 * blk * experts * parts * ds * ff,
        )

    dx_near = dx((0, 1), after(meta, gg_a[2], gg_b[2]))
    dots_f = after(sum_z(dots_f), gg_a[3], gg_b[3])
    dots_f = jnp.stack([dots_f, by_group(dots_f, 1), by_group(dots_f, 2), by_group(dots_f, 3)])
    dx_far = dx((2, 3), meta)
    near_half = held([z_second(z_first(*dx_near))], dx_far[0])[0]
    far_half = z_first(*dx_far)

    act_a, act_b, _ = lax.optimization_barrier((act_a, act_b, far_half))
    ag_a = [act_a, by_group(act_a, 1), by_group(act_a, 2)]
    ag_b = [act_b, by_group(act_b, 1), by_group(act_b, 2)]
    dots_f = jnp.take(dots_f, g ^ jnp.arange(4, dtype=jnp.int32), axis=0)
    dots_f = dots_f.transpose(1, 0, 2).reshape(8, rp)

    def back_columns(flat, dots, low_id, high_id):
        delta = flat[1] * flat[2] * (dots[0] - dots[1])
        inner = (dots[2] + delta * flat[3]) / width
        ids = jnp.arange(experts, dtype=F32)[:, None]
        dlogit = jnp.where(low_id[None] == ids, delta[None], 0.0) - jnp.where(
            high_id[None] == ids, delta[None], 0.0
        )
        zero = jnp.zeros((1, rp), F32)
        return jnp.concatenate(
            [dlogit, inner[None], flat[0:1]] + [zero] * (6 - experts), axis=0
        ).T

    back_f = back_columns(flat_f, dots_f, low_f, high_f)


    def exchange(sums):
        total = sums[0].astype(F32)
        for s in pieces[1:]:
            total = total + by_part(sums[s], s).astype(F32)
        return total

    ffn_input = (after_rows * flat_f[0][None, :, None] * gain_f).astype(BF16)

    def t_left(xs, value):
        if not wide:
            return [tn(x, value) for x in xs]
        total = tn(jnp.concatenate(xs, axis=1), value)
        return [total[s * ds : (s + 1) * ds] for s in pieces]

    def t_right(value, xs):
        if not wide:
            return [tn(value, x) for x in xs]
        total = tn(value, jnp.concatenate(xs, axis=1))
        return [total[:, s * ds : (s + 1) * ds] for s in pieces]

    def sort_rows(m, sel_ref, x_refs, xs, ids):
        for r in range(4):
            src, here_r = at_row(m, 2 + r, blk), slice(r * blk, (r + 1) * blk)
            for s in pieces:
                xs[s, here_r, :] = x_refs[s][src, :]
            ids[here_r, :] = sel_ref[src, :]

    def dwin_body(m, *refs):
        a_refs, b_refs = refs[:4], refs[4:8]
        sel_ref, x_ref = refs[8:10]
        outs = refs[10 : 10 + parts]
        xs, ids, mt = refs[10 + parts :]
        e = pl.program_id(0)

        @pl.when(e == 0)
        def _():
            sort_rows(m, sel_ref, [x_ref.at[s] for s in pieces], xs, ids)

        expert = e.astype(F32)
        for r in range(4):
            here_r = slice(r * blk, (r + 1) * blk)
            mt[here_r, :] = pick(
                ids[here_r, 2:3], ids[here_r, 3:4], expert, a_refs[r][0], b_refs[r][0]
            )
        for s, value in enumerate(t_left([xs[s] for s in pieces], mt[...])):
            outs[s][0] = value.astype(BF16)

    def dwin(j, meta):
        ins = [(v, (1, blk, ff), lambda e, m: (j, 0, 0)) for v in gg_a + gg_b]
        ins += [(sel, None, None), (ffn_input, None, None)]
        outs = [((experts, ds, ff), BF16, (1, ds, ff), lambda e, m: (e, 0, 0))] * parts
        return run(
            dwin_body, "dwin", (experts,), meta, ins, outs,
            [pltpu.VMEM((parts, rp, ds), BF16), pltpu.VMEM((rp, 8), F32), pltpu.VMEM((rp, ff), BF16)],
            flops=2 * rp * experts * parts * ds * ff,
        )

    def fold_body(m, *refs):
        out_ref = refs[2 * parts]
        for j in range(2):
            total = refs[j * parts][0].astype(F32)
            for ref in refs[j * parts + 1 : (j + 1) * parts]:
                total = total + ref[0].astype(F32)
            out_ref[0, :, j, :] = total

    def fold(sums, meta):
        ins = []
        for half in sums:
            got = [half[0]] + [by_part(half[s], s) for s in pieces[1:]]
            ins += [(v, (1, ds, ff), lambda e, m: (e, 0, 0)) for v in got]
        outs = [((experts, ds, 2, ff), F32, (1, ds, 2, ff), lambda e, m: (e, 0, 0, 0))]
        return run(fold_body, "fold", (experts,), meta, ins, outs)[0]

    dwin_gate = dwin(0, after(meta, far_half))
    dx_totals = z_last(near_half) + z_last(z_covered(far_half, far_half, 3, dwin_gate[0]))

    def norm_back_body(low_precision_out, m, *refs):
        sums = 4 if low_precision_out else 2
        t_refs, after_ref, refs = refs[:sums], refs[sums], refs[sums + 1 :]
        ups = parts if low_precision_out else 1
        up_refs = refs[:ups]
        gain_ref, router_ref, back = refs[ups : 3 + ups]
        outs = refs[3 + ups :]
        small = outs[-1]
        for s in pieces:
            gain = gain_ref[s]
            router = router_ref[s].astype(F32)
            gain_sum = jnp.zeros((1, ds), F32)
            router_sum = [jnp.zeros((1, ds), F32)] * experts
            for r in range(4):
                span_r = at_row(m, (BY_CHUNK if low_precision_out else IN_HALVES) + r, blk)
                up_value = up_refs[s][span_r, :] if low_precision_out else up_refs[0][s, span_r, :]
                x = after_ref[s, span_r, :].astype(F32)
                cols = back[span_r, :]
                rms = cols[:, experts + 1 : experts + 2]
                if low_precision_out:
                    grad = t_refs[r][s].astype(F32)
                else:
                    grad = t_refs[r // 2][s, (r % 2) * blk : (r % 2 + 1) * blk, :].astype(F32)
                for e in range(experts):
                    grad += cols[:, e : e + 1] * router[e : e + 1]
                normed = x * rms
                token = (normed * gain).astype(BF16).astype(F32)
                gain_sum += jnp.sum(grad * normed, axis=0, keepdims=True)
                for e in range(experts):
                    router_sum[e] = router_sum[e] + jnp.sum(
                        token * cols[:, e : e + 1], axis=0, keepdims=True
                    )
                dn = grad * gain
                total = up_value.astype(F32) + rms * (
                    dn - normed * cols[:, experts : experts + 1]
                )
                if low_precision_out:
                    outs[0][s, span_r, :] = total
                    outs[1][s, span_r, :] = total.astype(BF16)
                else:
                    outs[s][span_r, :] = total.astype(BF16)
            for e in range(experts):
                small[e, s] = router_sum[e][0]
            small[experts, s] = gain_sum[0]

    ins = [(t, None, None) for t in dx_totals]
    ins += [(after_rows, None, None)] + [(d, None, None) for d in d_pieces]
    ins += [(gain_f, None, None), (router_f, None, None), (back_f, None, None)]
    outs = [
        ((parts, rp, ds), F32, None, None),
        ((parts, rp, ds), BF16, None, None),
        ((experts + 1, parts, ds), F32, None, None),
    ]
    dafter, dafter_low, small_f = run(
        functools.partial(norm_back_body, True), "norm_back", (1,),
        after(meta, dwin_gate[0], ag_a[1:], ag_b[1:]), ins, outs,
    )

    def whole_vectors(*smalls):
        small = jnp.concatenate(smalls, axis=0)
        full = jnp.zeros((small.shape[0], dp, ds), F32)
        for s in pieces:
            full = lax.dynamic_update_slice_in_dim(
                full, small[:, s : s + 1], g * parts + (c ^ s), axis=1
            )
        mask = 1
        while mask < dp:
            full = full + lax.ppermute(full, "dp", [(a, a ^ mask) for a in range(dp)])
            mask *= 2
        full = full.reshape(len(smalls), experts + 1, width)
        return [(v[:experts].T, v[experts]) for v in full]

    def dmix_body(m, *refs):
        d_ref = refs[0]
        w_refs = refs[1 : 1 + parts]
        sel_ref = refs[1 + parts]
        outs = refs[2 + parts : 10 + parts]
        scr = refs[10 + parts]
        products = []
        for e in range(experts):
            products.append(sum(nt(d_ref[s], w_refs[s][e]) for s in pieces))
        low, high = two_slots(sel_ref[:, 0:1], sel_ref[:, 1:2], products)
        for k, value in enumerate((low, high)):
            value = value.astype(BF16)
            for h in range(heads):
                scr[h, :, k * HD : (k + 1) * HD] = value[:, h * HD : (h + 1) * HD]
        for r in range(4):
            block = scr[m[2 + r]]
            outs[2 * r][...] = block[:, :HD]
            outs[2 * r + 1][...] = block[:, HD:]

    ins = [(dafter_low, (parts, tile, ds), lambda i, m: (0, i, 0))]
    ins += [(w, None, None) for w in wp]
    ins += [(sel, (tile, 8), lambda i, m: (i, 0))]
    outs = [((rp, HD), BF16, (tile, HD), lambda i, m: (i, 0))] * 8
    dm = run(
        dmix_body, "dmix", (rp // tile,), meta, ins, outs,
        [pltpu.VMEM((heads, tile, 2 * HD), BF16)],
        flops=2 * rp * experts * parts * ds * hw,
    )
    dwin_up = dwin(1, after(meta, dm[0]))
    dm_a, dm_b, _, _ = reduce_groups(dm[0:8:2], dm[1:8:2], late=dwin_up[0])
    along = held((ag_a[1], ag_b[2]), dm_a[2], dm_b[1])
    ag_a, ag_b = ag_a + [by_group(along[0], 2)], ag_b + [by_group(along[1], 1)]

    def attend_back_body(m, *refs):
        q_ref, kv_ref, halo_ref, sel_ref, cols, cos_ref, sin_ref = refs[:7]
        d_refs = (refs[7:10], refs[10:13])
        mix_refs = refs[13:15]
        dq_ref, own_ref, far_ref, dots_ref, ext, acc = refs[15:]
        i = pl.program_id(0)

        @pl.when(i == 0)
        def _():
            ext[:seq_len, :] = halo_ref[...]
            ext[seq_len:, :] = kv_ref[...]
            acc[...] = jnp.zeros_like(acc)

        near_rows = pl.ds(pl.multiple_of(i * qt, qt), span)
        near = ext[near_rows, :]
        allowed = window_mask(i, sel_ref[:, 4:5])
        line = lax.broadcasted_iota(jnp.int32, (8, qt), 0)
        inner = jnp.zeros((qt, HD), F32)
        found = []
        dk = jnp.zeros((span, HD), F32)
        dv = jnp.zeros((span, HD), F32)
        for k in range(2):
            query = q_ref[:, k * HD : (k + 1) * HD]
            probs = softmax_of(query, near[:, :HD], allowed)
            raw = sum(v[...].astype(F32) for v in d_refs[k])
            dmixed = (raw * cols[:, 1 + k : 2 + k]).astype(BF16)
            found.append(raw * mix_refs[k][...].astype(F32))
            dv += tn(probs.astype(BF16), dmixed)
            dprob = nt(dmixed, near[:, HD:])
            rest = jnp.sum(probs * dprob, axis=1, keepdims=True)
            dscore = (probs * (dprob - rest)).astype(BF16)
            dk += tn(dscore, query) * scale
            dquery = nn(dscore, near[:, :HD]) * scale
            inner += dquery * query.astype(F32)
            dq_ref[:, k * HD : (k + 1) * HD] = turn(dquery, cos_ref[...], -sin_ref[...]).astype(BF16)
        acc[near_rows, :HD] += dk
        acc[near_rows, HD:] += dv
        dots_ref[...] = jnp.where(
            line == 0, lane_sums(found[0]), jnp.where(line == 1, lane_sums(found[1]), lane_sums(inner))
        )

        @pl.when(i == rp // qt - 1)
        def _():
            far_ref[...] = acc[:seq_len, :]
            own_ref[...] = acc[seq_len:, :]

    ins = [(q_rot, (qt, 2 * HD), qrow), (kv_rot, None, None), (halo, None, None)]
    ins += [(sel, (qt, 8), qrow), (cols_a, (qt, 8), qrow)]
    ins += [(cosine, (qt, HD), qrow), (sine, (qt, HD), qrow)]
    ins += [(v, (qt, HD), qrow) for v in dm_a + dm_b + (mixed_a, mixed_b)]
    outs = [
        ((rp, 2 * HD), BF16, (qt, 2 * HD), qrow),
        ((rp, 2 * HD), F32, None, None),
        ((seq_len, 2 * HD), F32, None, None),
        ((8, rp), F32, (8, qt), lambda i, m: (0, i)),
    ]
    dq, dkv_own, dkv_far, dots_q = run(
        attend_back_body, "attend_back", (rp // qt,), meta, ins, outs,
        [pltpu.VMEM((seq_len + rp, 2 * HD), BF16), pltpu.VMEM((seq_len + rp, 2 * HD), F32)],
        flops=20 * rp * span * HD,
    )
    dkv_in = to_previous(dkv_far)

    def dkv_body(m, own_ref, in_ref, kv_ref, cos_ref, sin_ref, out_ref, dots_ref):
        head = rp - seq_len
        for rows_here in (slice(0, head), slice(head, rp)):
            value = own_ref[rows_here, :]
            if rows_here.start == head:
                value = value + in_ref[...]
            out_ref[rows_here, :HD] = turn(
                value[:, :HD], cos_ref[rows_here, :], -sin_ref[rows_here, :]
            ).astype(BF16)
            out_ref[rows_here, HD:] = value[:, HD:].astype(BF16)
            dots_ref[:, rows_here] = lane_sums(value * kv_ref[rows_here, :].astype(F32))

    ins = [(v, None, None) for v in (dkv_own, dkv_in, kv_rot, cosine, sine)]
    outs = [((rp, 2 * HD), BF16, None, None), ((8, rp), F32, None, None)]
    dkv, dots_kv = run(
        dkv_body, "dkv", (1,), after(meta, ag_a[3], ag_b[3]), ins, outs
    )
    third = jnp.arange(8)[:, None] == 2
    def down_body(m, *refs):
        a_refs, b_refs = refs[:4], refs[4:8]
        sel_ref, d_refs = refs[8], refs[9 : 9 + parts]
        w_refs = refs[9 + parts : 9 + 2 * parts]
        keep_ref, send_ref = refs[9 + 2 * parts : 11 + 2 * parts]
        outs = refs[11 + 2 * parts : 11 + 3 * parts]
        acc, xs, ids, mt = refs[11 + 3 * parts :]
        e = pl.program_id(0)

        @pl.when(e == 0)
        def _():
            acc[...] = jnp.zeros_like(acc)
            sort_rows(m, sel_ref, d_refs, xs, ids)

        expert = e.astype(F32)
        for r in range(4):
            here_r = slice(r * blk, (r + 1) * blk)
            mt[here_r, :] = pick(
                ids[here_r, 2:3], ids[here_r, 3:4], expert, a_refs[r][...], b_refs[r][...]
            )
        for s, value in enumerate(nn_pieces(mt[...], [w[0] for w in w_refs])):
            acc[s] += value
        for s, value in enumerate(t_right(mt[...], [xs[s] for s in pieces])):
            outs[s][0] = value.astype(BF16)

        @pl.when(e == experts - 1)
        def _():
            keep_ref[...] = acc[:, at_row(m, 6, 2 * blk), :].astype(BF16)
            send_ref[...] = acc[:, at_row(m, 7, 2 * blk), :].astype(BF16)

    def down(meta):
        spot = lambda e, m: (e, 0, 0)
        ins = [(v, None, None) for v in ag_a + ag_b]
        ins += [(sel, None, None)] + [(d, None, None) for d in d_pieces]
        ins += [(w, (1, ff, ds), spot) for w in wo]
        outs = [((parts, 2 * blk, ds), BF16, None, None)] * 2
        outs += [((experts, ff, ds), BF16, (1, ff, ds), spot)] * parts
        return run(
            down_body, "down", (experts,), meta, ins, outs,
            [
                pltpu.VMEM((parts, rp, ds), F32),
                pltpu.VMEM((parts, rp, ds), BF16),
                pltpu.VMEM((rp, 8), F32),
                pltpu.VMEM((rp, ff), BF16),
            ],
            flops=4 * rp * experts * parts * ds * ff,
        )

    def dwproj_body(m, *refs):
        a_refs, b_refs = refs[:4], refs[4:8]
        sel_ref, d_ref = refs[8:10]
        outs = refs[10 : 10 + parts]
        lo, hi = refs[10 + parts :]
        e = pl.program_id(0)

        @pl.when(e == 0)
        def _():
            for r in range(4):
                lanes = pl.ds(pl.multiple_of(m[2 + r] * HD, HD), HD)
                lo[:, lanes] = a_refs[r][...]
                hi[:, lanes] = b_refs[r][...]

        x = pick(sel_ref[:, 0:1], sel_ref[:, 1:2], e.astype(F32), lo[...], hi[...])
        for s, value in enumerate(t_right(x, [d_ref[s] for s in pieces])):
            outs[s][0] = value.astype(BF16)

    def dwproj(meta):
        ins = [(v, None, None) for v in gm_a + gm_b]
        ins += [(sel, None, None), (dafter_low, None, None)]
        return run(
            dwproj_body, "dwproj", (experts,), meta, ins,
            [((experts, hw, ds), BF16, (1, hw, ds), lambda e, m: (e, 0, 0))] * parts,
            [pltpu.VMEM((rp, hw), BF16)] * 2,
            flops=2 * rp * experts * hw * parts * ds,
        )

    down_halves = down(after(meta, dkv))
    down_halves, dwout_sums = down_halves[:2], down_halves[2:]
    da_a, da_b, da_along = gather_groups(dq, dkv, late=(dwout_sums[0],))
    dwproj_sums = dwproj(after(meta, da_along))
    def place_heads(m, refs, lo, hi):
        for r in range(4):
            lanes = pl.ds(pl.multiple_of(m[2 + r] * HD, HD), HD)
            lo[:, lanes] = refs[r][:, :HD]
            hi[:, lanes] = refs[r][:, HD:]

    def dattn_body(m, *refs):
        a_refs, b_refs = refs[:4], refs[4:8]
        sel_ref = refs[8]
        q_refs = refs[9 : 9 + parts]
        kv_refs = refs[9 + parts : 9 + 2 * parts]
        outs = refs[9 + 2 * parts : 11 + 2 * parts]
        lo, hi, dk, dv = refs[11 + 2 * parts :]
        place_heads(m, a_refs, lo, hi)
        place_heads(m, b_refs, dk, dv)
        acc = nt_pieces(dk[...], [w[0] for w in kv_refs])
        for s, value in enumerate(nt_pieces(dv[...], [w[1] for w in kv_refs])):
            acc[s] += value
        for e in range(experts):
            x = pick(sel_ref[:, 0:1], sel_ref[:, 1:2], e, lo[...], hi[...])
            for s, value in enumerate(nt_pieces(x, [w[e] for w in q_refs])):
                acc[s] += value
        for s in pieces:
            store_halves(pl.program_id(0), outs, s, acc[s].astype(BF16))

    def dattn(meta):
        half = lambda i, m: (m[7 - i], 0)
        ins = [(v, (2 * zr, 2 * HD), half) for v in da_a + da_b]
        ins += [(sel, (2 * zr, 8), half)]
        ins += [(w, None, None) for w in wq + wkv]
        return run(
            dattn_body, "dattn", (2,), meta, ins, [((parts, 2 * zr, ds), BF16, None, None)] * 2,
            [pltpu.VMEM((2 * zr, hw), BF16)] * 4,
            flops=8 * zr * (experts + 2) * hw * parts * ds,
        )

    dots_a = sum_groups(after(dots_q + jnp.where(third, dots_kv, 0.0), da_along))
    da_halves = dattn(after(meta, dwproj_sums[0], dots_a))
    dots_a = sum_z(dots_a)
    x_stack = jnp.stack(x_pieces)
    attn_input = (x_stack.astype(F32) * flat_a[0][None, :, None] * gain_a).astype(BF16)

    def dwqkv_body(m, *refs):
        a_refs, b_refs = refs[:4], refs[4:8]
        sel_ref, x_ref = refs[8:10]
        q_outs, kv_outs = refs[10 : 10 + parts], refs[10 + parts : 10 + 2 * parts]
        lo, hi, dk, dv = refs[10 + 2 * parts :]
        e = pl.program_id(0)
        xs = [x_ref.at[s] for s in pieces]

        @pl.when(e == 0)
        def _():
            place_heads(m, a_refs, lo, hi)
            place_heads(m, b_refs, dk, dv)

        @pl.when(e < experts)
        def _():
            x = pick(sel_ref[:, 0:1], sel_ref[:, 1:2], e.astype(F32), lo[...], hi[...])
            for s, value in enumerate(t_left([v[...] for v in xs], x)):
                q_outs[s][0] = value.astype(BF16)

        for k, grad in enumerate((dk, dv)):

            @pl.when(e == experts + k)
            def _():
                for s, value in enumerate(t_left([v[...] for v in xs], grad[...])):
                    kv_outs[s][0] = value.astype(BF16)

    def dwqkv(meta):
        q_spot = lambda e, m: (jnp.minimum(e, experts - 1), 0, 0)
        kv_spot = lambda e, m: (jnp.maximum(e - experts, 0), 0, 0)
        ins = [(v, None, None) for v in da_a + da_b]
        ins += [(sel, None, None), (attn_input, None, None)]
        outs = [((experts, ds, hw), BF16, (1, ds, hw), q_spot)] * parts
        outs += [((2, ds, hw), BF16, (1, ds, hw), kv_spot)] * parts
        return run(
            dwqkv_body, "dwqkv", (experts + 2,), meta, ins, outs,
            [pltpu.VMEM((rp, hw), BF16)] * 4,
            flops=2 * rp * (experts + 2) * hw * parts * ds,
        )

    dwqkv_sums = dwqkv(after(meta, da_halves[0], dots_a))


    da_half = z_covered(*da_halves, 1, dwqkv_sums[0])

    down_half = z_covered(*down_halves, 1, dwproj_sums[0])
    down_half = z_covered(down_half, down_half, 3, da_halves[0])
    down_totals = z_last(down_half)

    def finish_body(m, *refs):
        t_refs, after_ref, outs = refs[:2], refs[2], refs[3:]
        for k in range(4):
            span_k = at_row(m, BY_HALF + k, blk)
            for s in pieces:
                total = t_refs[k // 2][s, (k % 2) * blk : (k % 2 + 1) * blk, :]
                outs[s][span_k, :] = (
                    after_ref[s, span_k, :] + total.astype(F32)
                ).astype(BF16)

    ins = [(t, None, None) for t in down_totals] + [(after_rows, None, None)]
    out_rows = run(
        finish_body, "finish", (1,), after(meta, dwqkv_sums[0]), ins,
        [((rp, ds), BF16, None, None)] * parts,
    )

    def unpack_body(dealt, m, other_ref, *refs):
        v_refs, out_ref = refs[:parts], refs[parts]
        packed, other, total, whole = refs[parts + 1 :]
        for s in pieces:
            packed[part_rows(m, s), :] = v_refs[s][...].astype(F32)
        take_rows(dealt, other, other_ref)
        line = lax.broadcasted_iota(jnp.int32, (per, ds), 0)

        def one(j, carry):
            window, shift = near_rows(m, j)
            back = jnp.where(shift == 0, 0, seq_len + 8 - shift)
            whole[...] = pltpu.roll(packed[window, :], back, 0)
            for p in range(dp):
                if dealt:
                    spot = m[2 * seqs + j] * seq_len + p * per
                    kept = other[pl.ds(pl.multiple_of(spot, per), per), :]
                else:
                    kept = other[block_rows(p, j), :]
                value = whole[p * per : (p + 1) * per, :]
                total[block_rows(p, j), :] = jnp.where(line < m[seqs + j] - p * per, value, kept)
            return carry

        lax.fori_loop(0, seqs, one, 0)
        out_ref[...] = total[...].astype(BF16)

    def unpack(value, otherwise, dealt, table):
        mine_all = [value[0]] + [by_part(value[s], s) for s in pieces[1:]]
        ins = [(v, None, None) for v in [otherwise] + mine_all]
        spread_rows = run(
            functools.partial(unpack_body, dealt), "unpack", (1,), table, ins,
            [((rows_all, ds), BF16, None, None)],
            [
                pltpu.VMEM((n, ds), F32)
                for n in (rows + seq_len + 8, rows_all, rows_all, seq_len + 8)
            ],
        )[0]
        landed = lax.all_to_all(
            spread_rows.reshape(dp, seqs * per, ds), "dp", 0, 0, tiled=True
        )
        return landed.transpose(1, 0, 2).reshape(seqs, per, width), spread_rows

    layer_out, layer_rows = unpack(out_rows, arrived, False, table)
    expertin_grad = fold((dwin_gate, dwin_up), after(meta, layer_rows))
    back_a = back_columns(flat_a, dots_a, low_a, high_a)
    da_half = z_covered(da_half, da_half, 3, layer_rows)
    da_totals = z_last(da_half)
    ins = [(t, None, None) for t in da_totals]
    ins += [(x_stack, None, None), (dafter, None, None)]
    ins += [(gain_a, None, None), (router_a, None, None), (back_a, None, None)]
    outs = [((rp, ds), BF16, None, None)] * parts
    outs += [((experts + 1, parts, ds), F32, None, None)]
    *dinput, small_a = run(
        functools.partial(norm_back_body, False), "norm_back_first", (1,),
        after(meta, expertin_grad), ins, outs,
    )
    expertout_grad = exchange(dwout_sums)
    proj_grad = exchange(dwproj_sums)
    query_grad, kv_grad = exchange(dwqkv_sums[:parts]), exchange(dwqkv_sums[parts:])
    input_grad, last_rows = unpack(dinput, arrived, True, after(table, layer_out))
    vectors = whole_vectors(after(small_a, last_rows), small_f)
    (attnrouter_grad, attngain_grad), (ffnrouter_grad, ffngain_grad) = vectors
    return (
        layer_out,
        input_grad,
        attngain_grad,
        attnrouter_grad,
        kv_grad,
        query_grad,
        proj_grad,
        ffngain_grad,
        ffnrouter_grad,
        expertin_grad,
        expertout_grad,
    )


def solution(mesh):
    placed = (
        P(None, "dp", None),
        P("dp", None, None),
        P(),
        P(),
        P(),
        P(),
        P(),
        P(),
        P(None, "dp", "tensor"),
        P(None, "dp", "tensor"),
        P(None, "tensor", "dp"),
        P(),
        P(),
        P(None, "dp", None, "tensor"),
        P(None, "tensor", "dp"),
    )
    return jax.shard_map(
        functools.partial(local, dp=mesh.shape["dp"], tp=mesh.shape["tensor"]),
        mesh=mesh,
        in_specs=placed,
        out_specs=(
            P(None, "dp", None),
            P(None, "dp", None),
            P(),
            P(),
            P(None, "dp", "tensor"),
            P(None, "dp", "tensor"),
            P(None, "tensor", "dp"),
            P(),
            P(),
            P(None, "dp", None, "tensor"),
            P(None, "tensor", "dp"),
        ),
        check_vma=False,
    )
```

```python
import functools

import jax
import jax.numpy as jnp
from jax import lax
from jax.experimental import pallas as pl
from jax.experimental.pallas import tpu as pltpu
from jax.sharding import PartitionSpec as P

HD = 128
EPSILON = 1e-06
ROPE_BASE = 10000.0
BEST = lax.Precision.HIGHEST
F32 = jnp.float32
BF16 = jnp.bfloat16
VMEM_BYTES = 60 * 1024 * 1024


def nn(a, b):
    return lax.dot_general(a, b, (((1,), (0,)), ((), ())), preferred_element_type=F32)


def nt(a, b, precision=None):
    return lax.dot_general(
        a, b, (((1,), (1,)), ((), ())), preferred_element_type=F32, precision=precision
    )


def tn(a, b):
    return lax.dot_general(a, b, (((0,), (0,)), ((), ())), preferred_element_type=F32)


def lane_sums(values):
    ones = jnp.ones((8, values.shape[1]), F32)
    return nt(ones, values, BEST)


def run(body, name, grid, meta, ins, outs, scratch=(), flops=0):
    in_specs = []
    moved = 0
    for array, block, index in ins:
        if block is None:
            rank = array.ndim
            in_specs.append(pl.BlockSpec(array.shape, lambda *a, rank=rank: (0,) * rank))
        else:
            in_specs.append(pl.BlockSpec(block, index))
        moved += array.size * array.dtype.itemsize
    out_specs = []
    out_shape = []
    for shape, dtype, block, index in outs:
        if block is None:
            rank = len(shape)
            out_specs.append(pl.BlockSpec(shape, lambda *a, rank=rank: (0,) * rank))
        else:
            out_specs.append(pl.BlockSpec(block, index))
        out_shape.append(jax.ShapeDtypeStruct(shape, dtype))
        size = jnp.dtype(dtype).itemsize
        for extent in shape:
            size *= extent
        moved += size
    return pl.pallas_call(
        body,
        name=name,
        grid_spec=pltpu.PrefetchScalarGridSpec(
            num_scalar_prefetch=1,
            grid=grid,
            in_specs=in_specs,
            out_specs=out_specs,
            scratch_shapes=list(scratch),
        ),
        out_shape=out_shape,
        compiler_params=pltpu.CompilerParams(
            dimension_semantics=("arbitrary",) * len(grid), vmem_limit_bytes=VMEM_BYTES
        ),
        cost_estimate=pl.CostEstimate(flops=flops, bytes_accessed=moved, transcendentals=0),
    )(meta, *[array for array, _, _ in ins])


def pick(low_id, high_id, expert, low_value, high_value):
    zero = jnp.zeros_like(low_value)
    return jnp.where(
        low_id == expert, low_value, jnp.where(high_id == expert, high_value, zero)
    )


def two_slots(low_id, high_id, products):
    low_value = products[0]
    for expert in range(1, len(products) - 1):
        low_value = jnp.where(low_id == expert, products[expert], low_value)
    high_value = products[1]
    for expert in range(2, len(products)):
        high_value = jnp.where(high_id == expert, products[expert], high_value)
    return low_value, high_value


def turn(values, cosine, sine):
    return values * cosine + pltpu.roll(values, HD // 2, 1) * sine


def local(
    hidden_in,
    cotangent,
    lengths,
    dealing,
    attn_routes,
    ffn_routes,
    attn_gain,
    attn_router,
    kv_weight,
    query_weight,
    proj_weight,
    ffn_gain,
    ffn_router,
    expert_in,
    expert_out,
    *,
    dp,
    tp,
):
    seqs = dealing.shape[0]
    seq_len = cotangent.shape[1]
    slots = cotangent.shape[0]
    per = hidden_in.shape[1]
    width = hidden_in.shape[2]
    heads = query_weight.shape[2] // HD
    groups = heads
    parts = dp // groups
    ds = width // dp
    hw = heads * HD
    rows_all = seqs * seq_len
    rows = rows_all * 3 // 4
    rp = rows // parts
    blk = rp // groups
    experts = query_weight.shape[0]
    ff = expert_out.shape[1]
    scale = HD ** (-0.5)
    pieces = range(parts)

    index = lax.axis_index("dp")
    z = lax.axis_index("tensor")
    g = index // parts
    c = index % parts
    mine = ((z == 1) | (z == 2)).astype(jnp.int32)
    theirs = 1 - mine
    spots = [g, c, g, g ^ 1, g ^ 2, g ^ 3, mine, theirs]
    spots += [g ^ mine, g ^ theirs, g ^ (2 + mine), g ^ (2 + theirs)]
    spots += [g ^ (2 * mine), g ^ (2 * mine + 1), g ^ (2 * theirs), g ^ (2 * theirs + 1)]
    spots += [mine, theirs, 2 + mine, 2 + theirs]
    spots += [2 * mine, 2 * mine + 1, 2 * theirs, 2 * theirs + 1]
    meta = jnp.stack(spots).astype(jnp.int32)
    BY_CHUNK, BY_HALF, IN_ORDER, IN_HALVES = 8, 12, 16, 20

    def after(value, *others):
        return lax.optimization_barrier((value,) + others)[0]

    def both(a, b):
        return (a.astype(F32) + b.astype(F32)).astype(BF16)

    def by_group(value, mask):
        pairs = [(a, ((a // parts) ^ mask) * parts + a % parts) for a in range(dp)]
        return lax.ppermute(value, "dp", pairs)

    def by_part(value, mask):
        pairs = [(a, (a // parts) * parts + ((a % parts) ^ mask)) for a in range(dp)]
        return lax.ppermute(value, "dp", pairs)

    def to_next(value):
        pairs = [(a, a + 1) for a in range(dp) if a % parts < parts - 1]
        return lax.ppermute(value, "dp", pairs)

    def to_previous(value):
        pairs = [(a, a - 1) for a in range(dp) if a % parts > 0]
        return lax.ppermute(value, "dp", pairs)

    def by_z(value, mask):
        return lax.ppermute(value, "tensor", [(a, a ^ mask) for a in range(tp)])

    def sum_groups(value):
        return (value + by_group(value, 1)) + (by_group(value, 2) + by_group(value, 3))

    def sum_z(value):
        return (value + by_z(value, 1)) + (by_z(value, 2) + by_z(value, 3))

    def z_first(keep, send):
        return both(keep, by_z(send, 1))

    def z_second(half):
        return both(half, by_z(half, 3))

    def z_covered(keep, send, mask, cover):
        keep, got = held((keep, by_z(send, mask)), cover)
        return both(keep, got)

    def z_last(half):
        return half, by_z(half, 1)

    def wide_sum_z(keep, send):
        return z_last(z_second(z_first(keep, send)))

    def held(values, *others):
        return lax.optimization_barrier((tuple(values),) + others)[0]

    def reduce_groups(first, second, early=(), late=()):
        if early:
            first, second = held((tuple(first), tuple(second)), early)
        ra = by_group(first[3], 1)
        rb = by_group(second[3], 2)
        ax = by_group(first[1], 1)
        by = by_group(second[2], 2)
        along = held((both(first[2], ra), both(second[1], rb)), (ax, by), late)
        ay = by_group(along[0], 2)
        bx = by_group(along[1], 1)
        return (first[0], ax, ay), (second[0], bx, by), along, (ra, rb)

    def gather_groups(first, second, late=()):
        ax, bx = by_group(first, 1), by_group(second, 1)
        ay, by = by_group(first, 2), by_group(second, 2)
        along = held((ax, by), (bx, ay), late) if len(late) else (ax, by)
        ad, bd = by_group(along[0], 2), by_group(along[1], 1)
        return (first, ax, ay, ad), (second, bx, by, bd), along

    def row_of(offset):
        return lambda *a: (a[-1][2 + offset], 0)

    def at_row(m, spot, count):
        return pl.ds(pl.multiple_of(m[spot] * count, count), count)

    wide = ds % 128 == 0

    def nn_pieces(x, weights):
        if not wide:
            return [nn(x, w) for w in weights]
        value = nn(x, jnp.concatenate(weights, axis=1))
        return [value[:, s * ds : (s + 1) * ds] for s in pieces]

    def nt_pieces(x, weights):
        if not wide:
            return [nt(x, w) for w in weights]
        value = nt(x, jnp.concatenate(weights, axis=0))
        return [value[:, s * ds : (s + 1) * ds] for s in pieces]

    ends = jnp.cumsum(lengths)
    starts = ends - lengths
    inverse = jnp.sum(
        (dealing[None, :] == jnp.arange(seqs, dtype=jnp.int32)[:, None])
        * jnp.arange(seqs, dtype=jnp.int32)[None, :],
        axis=1,
    )

    table = jnp.concatenate([starts, lengths, inverse, c[None]]).astype(jnp.int32)

    def places(part):
        packed = part * rp + jnp.arange(rp, dtype=jnp.int32)
        begun = starts[None, :] <= packed[:, None]
        first = jnp.max(jnp.where(begun, starts[None, :], 0), axis=1)
        seq = jnp.sum(begun.astype(jnp.int32), axis=1) - 1
        return seq, packed - first, first

    seq, at, first = places(c)

    def slot_rows(m, j):
        return pl.ds(pl.multiple_of(m[2 * seqs + j] * seq_len, seq_len), seq_len)

    def part_rows(m, s):
        return pl.ds(pl.multiple_of((m[3 * seqs] ^ s) * rp, rp), rp)

    def block_rows(p, j):
        return pl.ds(pl.multiple_of((p * seqs + j) * per, per), per)

    def near_rows(m, j):
        shift = m[j] & 7
        return pl.ds(pl.multiple_of(m[j] - shift, 8), seq_len + 8), shift

    def pack_body(dealt, m, all_ref, *refs):
        outs = refs[:parts]
        source, packed, whole = refs[parts:]
        source[...] = all_ref[...].astype(F32)

        line = lax.broadcasted_iota(jnp.int32, (seq_len + 8, ds), 0)

        def one(j, carry):
            if dealt:
                whole[:seq_len, :] = source[slot_rows(m, j), :]
            else:
                for p in range(dp):
                    whole[p * per : (p + 1) * per, :] = source[block_rows(p, j), :]
            window, shift = near_rows(m, j)
            moved = pltpu.roll(whole[...], shift, 0)
            packed[window, :] = jnp.where(line < shift, packed[window, :], moved)
            return carry

        lax.fori_loop(0, seqs, one, 0)
        for s in pieces:
            outs[s][...] = packed[part_rows(m, s), :].astype(BF16)

    def pack(value, dealt):
        own = run(
            functools.partial(pack_body, dealt), "pack", (1,), table, [(value, None, None)],
            [((rp, ds), BF16, None, None)] * parts,
            [pltpu.VMEM((n, ds), F32) for n in (rows_all, rows + seq_len + 8, seq_len + 8)],
        )
        return [own[0]] + [by_part(own[s], s) for s in pieces[1:]]

    x_send = hidden_in.reshape(seqs * per, dp, ds).transpose(1, 0, 2)
    d_send = cotangent.reshape(slots * seq_len, dp, ds).transpose(1, 0, 2)
    x_all = lax.all_to_all(x_send, "dp", 0, 0, tiled=True).reshape(rows_all, ds)
    x_pieces = pack(x_all, False)
    d_all = lax.all_to_all(d_send, "dp", 0, 0, tiled=True).reshape(rows_all, ds)
    d_pieces = pack(d_all, True)

    def spread(vector):
        tall = vector.reshape((groups, parts, ds) + vector.shape[1:])[g]
        return jnp.stack([tall[c ^ s] for s in pieces])

    gain_a = spread(attn_gain)[:, None, :]
    gain_f = spread(ffn_gain)[:, None, :]
    pad = ((0, 0), (0, 8 - experts), (0, 0))
    router_a = jnp.pad(spread(attn_router).transpose(0, 2, 1), pad)
    router_f = jnp.pad(spread(ffn_router).transpose(0, 2, 1), pad)

    in_own = expert_in.swapaxes(1, 2)
    wq = [query_weight] + [by_part(query_weight, s) for s in pieces[1:]]
    wkv = [kv_weight] + [by_part(kv_weight, s) for s in pieces[1:]]
    wp = [proj_weight] + [by_part(proj_weight, s) for s in pieces[1:]]
    wo = [expert_out] + [by_part(expert_out, s) for s in pieces[1:]]
    wi = [in_own] + [by_part(in_own, s) for s in pieces[1:]]

    routes = jnp.concatenate(
        [attn_routes.reshape(rows_all, 2), ffn_routes.reshape(rows_all, 2)], axis=1
    )
    here = (seq * seq_len + at)[:, None] == jnp.arange(rows_all, dtype=jnp.int32)[None, :]
    mine = jnp.dot(here.astype(BF16), routes.astype(BF16), preferred_element_type=F32)
    low_a, high_a = jnp.minimum(mine[:, 0], mine[:, 1]), jnp.maximum(mine[:, 0], mine[:, 1])
    low_f, high_f = jnp.minimum(mine[:, 2], mine[:, 3]), jnp.maximum(mine[:, 2], mine[:, 3])
    window = (first - c * rp + seq_len).astype(F32)
    nil = jnp.zeros_like(window)
    sel = jnp.stack([low_a, high_a, low_f, high_f, window, nil, nil, nil], axis=1)
    half = HD // 2
    frequency = ROPE_BASE ** (-2.0 * jnp.arange(half, dtype=F32) / HD)
    angles = at.astype(F32)[:, None] * frequency[None, :]
    cosine = jnp.concatenate([jnp.cos(angles)] * 2, axis=1)
    sine = jnp.sin(angles)
    sine = jnp.concatenate([-sine, sine], axis=1)

    def gate_columns(stats, low_id, high_id):
        rms = lax.rsqrt(stats[experts] / width + EPSILON)
        ids = jnp.arange(experts, dtype=F32)[:, None]
        logits = stats[:experts]
        low_logit = jnp.sum(jnp.where(low_id[None] == ids, logits, 0.0), axis=0) * rms
        high_logit = jnp.sum(jnp.where(high_id[None] == ids, logits, 0.0), axis=0) * rms
        gap = low_logit - high_logit
        low_gate, high_gate = jax.nn.sigmoid(gap), jax.nn.sigmoid(-gap)
        zero = jnp.zeros_like(rms)
        flat = jnp.stack([rms, low_gate, high_gate, gap, zero, zero, zero, zero])
        return flat, flat.T

    def rows_pair(refs):
        return jnp.concatenate([ref[...] for ref in refs], axis=0)

    def dhidden_body(m, *refs):
        d_refs = refs[: 2 * parts]
        w_refs, sel_refs = refs[2 * parts : 3 * parts], refs[3 * parts : 3 * parts + 2]
        outs = refs[3 * parts + 2 :]
        ids = rows_pair(sel_refs)
        rows_of = [rows_pair(d_refs[2 * s : 2 * s + 2]) for s in pieces]
        products = []
        for e in range(experts):
            products.append(sum(nt(rows_of[s], w_refs[s][e]) for s in pieces))
        low, high = two_slots(ids[:, 2:3], ids[:, 3:4], products)
        low, high = low.astype(BF16), high.astype(BF16)
        for step, pair in enumerate(((3, 1), (2, 0))):

            @pl.when(pl.program_id(0) == step)
            def _():
                for k, r in enumerate(pair):
                    outs[2 * r][...] = low[k * blk : (k + 1) * blk]
                    outs[2 * r + 1][...] = high[k * blk : (k + 1) * blk]

    def dhidden(meta):
        spots = [lambda i, m: (m[5 - i], 0), lambda i, m: (m[3 - i], 0)]
        ins = [(d, (blk, ds), spot) for d in d_pieces for spot in spots]
        ins += [(w, None, None) for w in wo]
        ins += [(sel, (blk, 8), spot) for spot in spots]
        outs = [((blk, ff), BF16, None, None)] * 8
        return run(
            dhidden_body, "dhidden", (2,), meta, ins, outs,
            flops=2 * rp * experts * parts * ds * ff,
        )

    tile = 256

    def qkv_body(m, *refs):
        x_refs = refs[:parts]
        gain_ref, router_ref = refs[parts : parts + 2]
        q_refs = refs[parts + 2 : 2 * parts + 2]
        kv_refs = refs[2 * parts + 2 : 3 * parts + 2]
        sel_ref = refs[3 * parts + 2]
        outs = refs[3 * parts + 3 : 3 * parts + 11]
        stats_ref, scr = refs[3 * parts + 11 :]
        us = []
        logits = jnp.zeros((8, tile), F32)
        squares = jnp.zeros((8, tile), F32)
        for s in pieces:
            xf = x_refs[s][...].astype(F32)
            us.append((xf * gain_ref[s]).astype(BF16))
            logits += nt(router_ref[s], us[s])
            squares += lane_sums(xf * xf)
        line = lax.broadcasted_iota(jnp.int32, (8, tile), 0)
        stats_ref[...] = jnp.where(line < experts, logits, squares)
        products = []
        for e in range(experts):
            products.append(sum(nn(us[s], q_refs[s][e]) for s in pieces))
        low, high = two_slots(sel_ref[:, 0:1], sel_ref[:, 1:2], products)
        keys = sum(nn(us[s], kv_refs[s][0]) for s in pieces)
        values = sum(nn(us[s], kv_refs[s][1]) for s in pieces)
        for k, value in enumerate((low, high, keys, values)):
            value = value.astype(BF16)
            for h in range(heads):
                scr[h, :, k * HD : (k + 1) * HD] = value[:, h * HD : (h + 1) * HD]
        for r in range(4):
            block = scr[m[2 + r]]
            outs[2 * r][...] = block[:, : 2 * HD]
            outs[2 * r + 1][...] = block[:, 2 * HD :]

    ins = [(x, (tile, ds), lambda i, m: (i, 0)) for x in x_pieces]
    ins += [(gain_a, None, None), (router_a, None, None)]
    ins += [(w, None, None) for w in wq + wkv]
    ins += [(sel, (tile, 8), lambda i, m: (i, 0))]
    outs = [((rp, 2 * HD), BF16, (tile, 2 * HD), lambda i, m: (i, 0))] * 8
    outs += [((8, rp), F32, (8, tile), lambda i, m: (0, i))]
    qkv = run(
        qkv_body, "qkv", (rp // tile,), after(meta, in_own), ins, outs,
        [pltpu.VMEM((heads, tile, 4 * HD), BF16)],
        flops=2 * rp * (experts + 2) * parts * ds * hw,
    )
    dh = dhidden(after(meta, qkv[8]))
    stats_a = sum_groups(qkv[8])
    flat_a, cols_a = gate_columns(stats_a, low_a, high_a)
    q_sum, kv_sum, _, _ = reduce_groups(qkv[0:8:2], qkv[1:8:2], late=cols_a)

    def rope_body(m, a0, a1, a2, b0, b1, b2, cols, cos_ref, sin_ref, q_ref, kv_ref):
        rms = cols[:, 0:1]
        cos, sin = cos_ref[...], sin_ref[...]
        q = (a0[...].astype(F32) + a1[...].astype(F32) + a2[...].astype(F32)) * rms
        kv = (b0[...].astype(F32) + b1[...].astype(F32) + b2[...].astype(F32)) * rms
        q_ref[:, :HD] = turn(q[:, :HD], cos, sin).astype(BF16)
        q_ref[:, HD:] = turn(q[:, HD:], cos, sin).astype(BF16)
        kv_ref[:, :HD] = turn(kv[:, :HD], cos, sin).astype(BF16)
        kv_ref[:, HD:] = kv[:, HD:].astype(BF16)

    ins = [(v, (tile, 2 * HD), lambda i, m: (i, 0)) for v in q_sum + kv_sum]
    ins += [(cols_a, (tile, 8), lambda i, m: (i, 0))]
    ins += [(v, (tile, HD), lambda i, m: (i, 0)) for v in (cosine, sine)]
    outs = [((rp, 2 * HD), BF16, (tile, 2 * HD), lambda i, m: (i, 0))] * 2
    q_rot, kv_rot = run(rope_body, "rope", (rp // tile,), after(meta, dh[0]), ins, outs)
    halo = to_next(kv_rot[rp - seq_len :])

    qt = 128
    span = seq_len + qt

    def window_mask(i, low_key):
        u = i * qt + lax.broadcasted_iota(jnp.int32, (qt, span), 1)
        t = seq_len + i * qt + lax.broadcasted_iota(jnp.int32, (qt, span), 0)
        return (u >= low_key.astype(jnp.int32)) & (u <= t)

    def softmax_of(query, key, allowed):
        score = jnp.where(allowed, nt(query, key) * scale, -1e30)
        top = jnp.max(score, axis=1, keepdims=True)
        raised = jnp.exp(score - top)
        return raised / jnp.sum(raised, axis=1, keepdims=True)

    def attend_body(m, q_ref, kv_ref, halo_ref, sel_ref, cols, ga, gb, ma, mb, ext):
        i = pl.program_id(0)

        @pl.when(i == 0)
        def _():
            ext[:seq_len, :] = halo_ref[...]
            ext[seq_len:, :] = kv_ref[...]

        near = ext[pl.ds(pl.multiple_of(i * qt, qt), span), :]
        allowed = window_mask(i, sel_ref[:, 4:5])
        for k, (g_ref, m_ref) in enumerate(((ga, ma), (gb, mb))):
            probs = softmax_of(q_ref[:, k * HD : (k + 1) * HD], near[:, :HD], allowed)
            mixed = nn(probs.astype(BF16), near[:, HD:]).astype(BF16)
            m_ref[...] = mixed
            g_ref[...] = (mixed.astype(F32) * cols[:, 1 + k : 2 + k]).astype(BF16)

    def qrow(i, m):
        return (i, 0)

    ins = [(q_rot, (qt, 2 * HD), qrow), (kv_rot, None, None), (halo, None, None)]
    ins += [(sel, (qt, 8), qrow), (cols_a, (qt, 8), qrow)]
    outs = [((rp, HD), BF16, (qt, HD), qrow)] * 4
    gated_a, gated_b, mixed_a, mixed_b = run(
        attend_body, "attend", (rp // qt,), meta, ins, outs,
        [pltpu.VMEM((seq_len + rp, 2 * HD), BF16)],
        flops=8 * rp * span * HD,
    )
    gm_a, gm_b, _ = gather_groups(gated_a, gated_b)
    chunks = 2
    zr = rp // chunks // 2
    hold = [((parts, zr, ds), BF16, None, None)] * 2

    def store_halves(i, refs, s, value):
        @pl.when(i == 0)
        def _():
            refs[1][s] = value

        @pl.when(i == 1)
        def _():
            refs[0][s] = value

    def proj_body(m, *refs):
        a_refs, b_refs = refs[:4], refs[4:8]
        sel_ref = refs[8]
        w_refs = refs[9 : 9 + parts]
        outs, xs = refs[9 + parts : 11 + parts], refs[11 + parts]
        for r in range(4):
            lanes = pl.ds(pl.multiple_of(m[2 + r] * HD, HD), HD)
            for e in range(experts):
                xs[e, :, lanes] = pick(
                    sel_ref[:, 0:1], sel_ref[:, 1:2], e, a_refs[r][...], b_refs[r][...]
                )
        acc = nn_pieces(xs[0], [w[0] for w in w_refs])
        for e in range(1, experts):
            for s, value in enumerate(nn_pieces(xs[e], [w[e] for w in w_refs])):
                acc[s] += value
        for s in pieces:
            store_halves(pl.program_id(0), outs, s, acc[s].astype(BF16))

    def project(k, meta):
        half = lambda i, m: (2 * k + m[7 - i], 0)
        ins = [(v, (zr, HD), half) for v in gm_a + gm_b]
        ins += [(sel, (zr, 8), half)]
        ins += [(w, None, None) for w in wp]
        return run(
            proj_body, "proj", (2,), meta, ins, hold,
            [pltpu.VMEM((experts, zr, hw), BF16)],
            flops=4 * zr * experts * hw * parts * ds,
        )

    sums = [project(0, meta)]
    dh_a, dh_b = held((dh[0:8:2], dh[1:8:2]), gm_a[3], gm_b[3])
    ra, rb = by_group(dh_a[3], 1), by_group(dh_b[3], 2)
    halves = [z_first(*sums[0])]
    for k in range(1, chunks):
        sums.append(project(k, after(meta, halves[-1])))
        halves[-1] = z_covered(halves[-1], halves[-1], 3, sums[-1][0])
        halves.append(z_first(*sums[-1]))
    halves[-1] = z_second(halves[-1])
    ax, by = by_group(dh_a[1], 1), by_group(dh_b[2], 2)
    attn_totals = [half for v in halves for half in z_last(v)]
    near = held((both(dh_a[2], ra), both(dh_b[1], rb)), (ax, by))
    dh_a, dh_b = (dh_a[0], ax, by_group(near[0], 2)), (dh_b[0], by_group(near[1], 1), by)

    def norm_body(m, *refs):
        t_refs = refs[: 2 * chunks]
        x_refs = refs[2 * chunks : 2 * chunks + parts]
        gain_ref, router_ref, after_ref, u_ref, stats_ref = refs[2 * chunks + parts :]
        for k in range(2 * chunks):
            span_k = at_row(m, IN_ORDER + k, zr)
            for s in pieces:
                after_ref[s, span_k, :] = x_refs[s][span_k, :].astype(F32) + t_refs[k][s].astype(F32)
        logits = jnp.zeros((8, rp), F32)
        squares = jnp.zeros((8, rp), F32)
        for s in pieces:
            af = after_ref[s]
            u = (af * gain_ref[s]).astype(BF16)
            u_ref[s] = u
            logits += nt(router_ref[s], u)
            squares += lane_sums(af * af)
        line = lax.broadcasted_iota(jnp.int32, (8, rp), 0)
        stats_ref[...] = jnp.where(line < experts, logits, squares)

    ins = [(t, None, None) for t in attn_totals + x_pieces]
    ins += [(gain_f, None, None), (router_f, None, None)]
    outs = [
        ((parts, rp, ds), F32, None, None),
        ((parts, rp, ds), BF16, None, None),
        ((8, rp), F32, None, None),
    ]
    after_rows, u_f, stats_part = run(norm_body, "norm", (1,), after(meta, near), ins, outs)
    def up_body(m, *refs):
        u_refs, w_refs = refs[:2], refs[2 : 2 + parts]
        sel_refs = refs[2 + parts : 4 + parts]
        outs = refs[4 + parts :]
        ids = rows_pair(sel_refs)
        rows_of = [jnp.concatenate([u[s] for u in u_refs], axis=0) for s in pieces]
        products = []
        for e in range(experts):
            products.append(sum(nn(rows_of[s], w_refs[s][e, 0]) for s in pieces))
        low, high = two_slots(ids[:, 2:3], ids[:, 3:4], products)
        low, high = low.astype(BF16), high.astype(BF16)
        for k in range(2):
            outs[2 * k][0] = low[k * blk : (k + 1) * blk]
            outs[2 * k + 1][0] = high[k * blk : (k + 1) * blk]

    def up(pair, meta):
        def block_of(r):
            return lambda j, m: (0, m[2 + r], 0)

        ins = [(u_f, (parts, blk, ds), block_of(r)) for r in pair]
        ins += [(w, (experts, 1, ds, ff), lambda j, m: (0, j, 0, 0)) for w in wi]
        ins += [(sel, (blk, 8), row_of(r)) for r in pair]
        outs = [((2, blk, ff), BF16, (1, blk, ff), lambda j, m: (j, 0, 0))] * 4
        return run(
            up_body, "up", (2,), meta, ins, outs, flops=8 * blk * experts * parts * ds * ff
        )

    up_far = up((3, 1), after(meta, dh_a[2], dh_b[1]))
    up_near = up((2, 0), after(meta, up_far[0]))
    gu_a, gu_b, _, far = reduce_groups(
        (up_near[2], up_far[2], up_near[0], up_far[0]),
        (up_near[3], up_far[3], up_near[1], up_far[1]),
    )

    stats_f = sum_groups(after(stats_part, far))
    flat_f, cols_f = gate_columns(stats_f, low_f, high_f)

    mt_rows = blk // 3

    def mid_body(m, *refs):
        gu = (refs[0:3], refs[3:6])
        dhr = (refs[6:9], refs[9:12])
        cols = refs[12]
        acts, grads, dots = refs[13:15], refs[15:17], refs[17]
        rms = cols[:, 0:1]
        column = lax.broadcasted_iota(jnp.int32, (mt_rows, 8), 1)
        found = []
        inner = jnp.zeros((mt_rows, 1), F32)
        for k in range(2):
            gate = cols[:, 1 + k : 2 + k]
            gp = sum(v[0].astype(F32) for v in gu[k]) * rms
            up_pre = sum(v[1].astype(F32) for v in gu[k]) * rms
            raw = sum(v[...].astype(F32) for v in dhr[k])
            sg = jax.nn.sigmoid(gp)
            act = (gp * sg * up_pre).astype(BF16).astype(F32)
            grad = raw * gate
            dgp = (grad * up_pre * sg * (1.0 + gp * (1.0 - sg))).astype(BF16)
            dup = (grad * gp * sg).astype(BF16)
            acts[k][...] = (act * gate).astype(BF16)
            grads[k][0] = dgp
            grads[k][1] = dup
            found.append(jnp.sum(act * raw, axis=1, keepdims=True))
            inner += jnp.sum(
                dgp.astype(F32) * gp + dup.astype(F32) * up_pre, axis=1, keepdims=True
            )
        zero = jnp.zeros((mt_rows, 8), F32)
        for k, value in enumerate(found + [inner]):
            zero = jnp.where(column == k, value, zero)
        dots[...] = zero

    rows_3 = lambda i, m: (0, i, 0)
    rows_2 = lambda i, m: (i, 0)
    ins = [(v, (2, mt_rows, ff), rows_3) for v in gu_a + gu_b]
    ins += [(v, (mt_rows, ff), rows_2) for v in dh_a + dh_b]
    ins += [(cols_f, (mt_rows, 8), lambda i, m: (3 * m[2] + i, 0))]
    outs = [((blk, ff), BF16, (mt_rows, ff), rows_2)] * 2
    outs += [((2, blk, ff), BF16, (2, mt_rows, ff), rows_3)] * 2
    outs += [((blk, 8), F32, (mt_rows, 8), rows_2)]
    act_a, act_b, grad_a, grad_b, dots_f = run(mid_body, "mid", (3,), meta, ins, outs)
    gg_a, gg_b, gg_along = gather_groups(grad_a, grad_b, late=(act_a,))
    dots_f = dots_f.T

    def dx_body(m, *refs):
        a_refs, b_refs = refs[:2], refs[2:4]
        w_refs = refs[4 : 4 + parts]
        sel_refs = refs[4 + parts : 6 + parts]
        keep_ref, send_ref, acc, xs = refs[6 + parts :]
        e = pl.program_id(0)
        expert = e.astype(F32)

        @pl.when(e == 0)
        def _():
            acc[...] = jnp.zeros_like(acc)

        for j in range(2):
            for k in range(2):
                ids = sel_refs[k]
                xs[k * blk : (k + 1) * blk, :] = pick(
                    ids[:, 2:3], ids[:, 3:4], expert, a_refs[k][j], b_refs[k][j]
                )
            for s, value in enumerate(nt_pieces(xs[...], [w[0, j] for w in w_refs])):
                acc[s] += value

        @pl.when(e == experts - 1)
        def _():
            keep_ref[...] = acc[:, at_row(m, 6, blk), :].astype(BF16)
            send_ref[...] = acc[:, at_row(m, 7, blk), :].astype(BF16)

    def dx(pair, meta):
        ins = [(v[r], None, None) for v in (gg_a, gg_b) for r in pair]
        ins += [(w, (1, 2, ds, ff), lambda e, m: (e, 0, 0, 0)) for w in wi]
        ins += [(sel, (blk, 8), row_of(r)) for r in pair]
        return run(
            dx_body, "dx", (experts,), meta, ins, [((parts, blk, ds), BF16, None, None)] * 2,
            [pltpu.VMEM((parts, 2 * blk, ds), F32), pltpu.VMEM((2 * blk, ff), BF16)],
            flops=8 * blk * experts * parts * ds * ff,
        )

    dx_near = dx((0, 1), after(meta, gg_a[2], gg_b[2]))
    dots_f = after(sum_z(dots_f), gg_a[3], gg_b[3])
    dots_f = jnp.stack([dots_f, by_group(dots_f, 1), by_group(dots_f, 2), by_group(dots_f, 3)])
    dx_far = dx((2, 3), meta)
    near_half = z_first(*dx_near)
    near_half = z_covered(near_half, near_half, 3, dx_far[0])
    far_half = z_first(*dx_far)

    act_a, act_b, _ = lax.optimization_barrier((act_a, act_b, far_half))
    ag_a = [act_a, by_group(act_a, 1), by_group(act_a, 2)]
    ag_b = [act_b, by_group(act_b, 1), by_group(act_b, 2)]
    dots_f = jnp.take(dots_f, g ^ jnp.arange(4, dtype=jnp.int32), axis=0)
    dots_f = dots_f.transpose(1, 0, 2).reshape(8, rp)

    def back_columns(flat, dots, low_id, high_id):
        delta = flat[1] * flat[2] * (dots[0] - dots[1])
        inner = (dots[2] + delta * flat[3]) / width
        ids = jnp.arange(experts, dtype=F32)[:, None]
        dlogit = jnp.where(low_id[None] == ids, delta[None], 0.0) - jnp.where(
            high_id[None] == ids, delta[None], 0.0
        )
        zero = jnp.zeros((1, rp), F32)
        return jnp.concatenate(
            [dlogit, inner[None], flat[0:1]] + [zero] * (6 - experts), axis=0
        ).T

    back_f = back_columns(flat_f, dots_f, low_f, high_f)


    def exchange(sums):
        total = sums[0].astype(F32)
        for s in pieces[1:]:
            total = total + by_part(sums[s], s).astype(F32)
        return total

    ffn_input = (after_rows * flat_f[0][None, :, None] * gain_f).astype(BF16)

    def t_left(xs, value):
        if not wide:
            return [tn(x, value) for x in xs]
        total = tn(jnp.concatenate(xs, axis=1), value)
        return [total[s * ds : (s + 1) * ds] for s in pieces]

    def t_right(value, xs):
        if not wide:
            return [tn(value, x) for x in xs]
        total = tn(value, jnp.concatenate(xs, axis=1))
        return [total[:, s * ds : (s + 1) * ds] for s in pieces]

    def sort_rows(m, sel_ref, x_refs, xs, ids):
        for r in range(4):
            src, here_r = at_row(m, 2 + r, blk), slice(r * blk, (r + 1) * blk)
            for s in pieces:
                xs[s, here_r, :] = x_refs[s][src, :]
            ids[here_r, :] = sel_ref[src, :]

    def dwin_body(m, *refs):
        a_refs, b_refs = refs[:4], refs[4:8]
        sel_ref, x_ref = refs[8:10]
        outs = refs[10 : 10 + parts]
        xs, ids, mt = refs[10 + parts :]
        e = pl.program_id(0)

        @pl.when(e == 0)
        def _():
            sort_rows(m, sel_ref, [x_ref.at[s] for s in pieces], xs, ids)

        expert = e.astype(F32)
        for r in range(4):
            here_r = slice(r * blk, (r + 1) * blk)
            mt[here_r, :] = pick(
                ids[here_r, 2:3], ids[here_r, 3:4], expert, a_refs[r][0], b_refs[r][0]
            )
        for s, value in enumerate(t_left([xs[s] for s in pieces], mt[...])):
            outs[s][0] = value.astype(BF16)

    def dwin(j, meta):
        ins = [(v, (1, blk, ff), lambda e, m: (j, 0, 0)) for v in gg_a + gg_b]
        ins += [(sel, None, None), (ffn_input, None, None)]
        outs = [((experts, ds, ff), BF16, (1, ds, ff), lambda e, m: (e, 0, 0))] * parts
        return run(
            dwin_body, "dwin", (experts,), meta, ins, outs,
            [pltpu.VMEM((parts, rp, ds), BF16), pltpu.VMEM((rp, 8), F32), pltpu.VMEM((rp, ff), BF16)],
            flops=2 * rp * experts * parts * ds * ff,
        )

    def fold_body(m, *refs):
        out_ref = refs[2 * parts]
        for j in range(2):
            total = refs[j * parts][0].astype(F32)
            for ref in refs[j * parts + 1 : (j + 1) * parts]:
                total = total + ref[0].astype(F32)
            out_ref[0, :, j, :] = total

    def fold(sums, meta):
        ins = []
        for half in sums:
            got = [half[0]] + [by_part(half[s], s) for s in pieces[1:]]
            ins += [(v, (1, ds, ff), lambda e, m: (e, 0, 0)) for v in got]
        outs = [((experts, ds, 2, ff), F32, (1, ds, 2, ff), lambda e, m: (e, 0, 0, 0))]
        return run(fold_body, "fold", (experts,), meta, ins, outs)[0]

    dwin_gate = dwin(0, after(meta, far_half))
    dx_totals = z_last(near_half) + z_last(z_covered(far_half, far_half, 3, dwin_gate[0]))

    def norm_back_body(low_precision_out, m, *refs):
        sums = 4 if low_precision_out else 2
        t_refs, after_ref, refs = refs[:sums], refs[sums], refs[sums + 1 :]
        ups = parts if low_precision_out else 1
        up_refs = refs[:ups]
        gain_ref, router_ref, back = refs[ups : 3 + ups]
        outs = refs[3 + ups :]
        small = outs[-1]
        for s in pieces:
            gain = gain_ref[s]
            router = router_ref[s].astype(F32)
            gain_sum = jnp.zeros((1, ds), F32)
            router_sum = [jnp.zeros((1, ds), F32)] * experts
            for r in range(4):
                span_r = at_row(m, (BY_CHUNK if low_precision_out else IN_HALVES) + r, blk)
                up_value = up_refs[s][span_r, :] if low_precision_out else up_refs[0][s, span_r, :]
                x = after_ref[s, span_r, :].astype(F32)
                cols = back[span_r, :]
                rms = cols[:, experts + 1 : experts + 2]
                if low_precision_out:
                    grad = t_refs[r][s].astype(F32)
                else:
                    grad = t_refs[r // 2][s, (r % 2) * blk : (r % 2 + 1) * blk, :].astype(F32)
                for e in range(experts):
                    grad += cols[:, e : e + 1] * router[e : e + 1]
                normed = x * rms
                token = (normed * gain).astype(BF16).astype(F32)
                gain_sum += jnp.sum(grad * normed, axis=0, keepdims=True)
                for e in range(experts):
                    router_sum[e] = router_sum[e] + jnp.sum(
                        token * cols[:, e : e + 1], axis=0, keepdims=True
                    )
                dn = grad * gain
                total = up_value.astype(F32) + rms * (
                    dn - normed * cols[:, experts : experts + 1]
                )
                if low_precision_out:
                    outs[0][s, span_r, :] = total
                    outs[1][s, span_r, :] = total.astype(BF16)
                else:
                    outs[s][span_r, :] = total.astype(BF16)
            for e in range(experts):
                small[e, s] = router_sum[e][0]
            small[experts, s] = gain_sum[0]

    ins = [(t, None, None) for t in dx_totals]
    ins += [(after_rows, None, None)] + [(d, None, None) for d in d_pieces]
    ins += [(gain_f, None, None), (router_f, None, None), (back_f, None, None)]
    outs = [
        ((parts, rp, ds), F32, None, None),
        ((parts, rp, ds), BF16, None, None),
        ((experts + 1, parts, ds), F32, None, None),
    ]
    dafter, dafter_low, small_f = run(
        functools.partial(norm_back_body, True), "norm_back", (1,),
        after(meta, dwin_gate[0], ag_a[1:], ag_b[1:]), ins, outs,
    )

    def dmix_body(m, *refs):
        d_ref = refs[0]
        w_refs = refs[1 : 1 + parts]
        sel_ref = refs[1 + parts]
        outs = refs[2 + parts : 10 + parts]
        scr = refs[10 + parts]
        products = []
        for e in range(experts):
            products.append(sum(nt(d_ref[s], w_refs[s][e]) for s in pieces))
        low, high = two_slots(sel_ref[:, 0:1], sel_ref[:, 1:2], products)
        for k, value in enumerate((low, high)):
            value = value.astype(BF16)
            for h in range(heads):
                scr[h, :, k * HD : (k + 1) * HD] = value[:, h * HD : (h + 1) * HD]
        for r in range(4):
            block = scr[m[2 + r]]
            outs[2 * r][...] = block[:, :HD]
            outs[2 * r + 1][...] = block[:, HD:]

    ins = [(dafter_low, (parts, tile, ds), lambda i, m: (0, i, 0))]
    ins += [(w, None, None) for w in wp]
    ins += [(sel, (tile, 8), lambda i, m: (i, 0))]
    outs = [((rp, HD), BF16, (tile, HD), lambda i, m: (i, 0))] * 8
    dm = run(
        dmix_body, "dmix", (rp // tile,), meta, ins, outs,
        [pltpu.VMEM((heads, tile, 2 * HD), BF16)],
        flops=2 * rp * experts * parts * ds * hw,
    )
    dwin_up = dwin(1, after(meta, dm[0]))
    dm_a, dm_b, _, _ = reduce_groups(dm[0:8:2], dm[1:8:2], late=dwin_up[0])
    along = held((ag_a[1], ag_b[2]), dm_a[2], dm_b[1])
    ag_a, ag_b = ag_a + [by_group(along[0], 2)], ag_b + [by_group(along[1], 1)]

    def attend_back_body(m, *refs):
        q_ref, kv_ref, halo_ref, sel_ref, cols, cos_ref, sin_ref = refs[:7]
        d_refs = (refs[7:10], refs[10:13])
        mix_refs = refs[13:15]
        dq_ref, own_ref, far_ref, dots_ref, ext, acc = refs[15:]
        i = pl.program_id(0)

        @pl.when(i == 0)
        def _():
            ext[:seq_len, :] = halo_ref[...]
            ext[seq_len:, :] = kv_ref[...]
            acc[...] = jnp.zeros_like(acc)

        near_rows = pl.ds(pl.multiple_of(i * qt, qt), span)
        near = ext[near_rows, :]
        allowed = window_mask(i, sel_ref[:, 4:5])
        line = lax.broadcasted_iota(jnp.int32, (8, qt), 0)
        inner = jnp.zeros((qt, HD), F32)
        found = []
        dk = jnp.zeros((span, HD), F32)
        dv = jnp.zeros((span, HD), F32)
        for k in range(2):
            query = q_ref[:, k * HD : (k + 1) * HD]
            probs = softmax_of(query, near[:, :HD], allowed)
            raw = sum(v[...].astype(F32) for v in d_refs[k])
            dmixed = (raw * cols[:, 1 + k : 2 + k]).astype(BF16)
            found.append(raw * mix_refs[k][...].astype(F32))
            dv += tn(probs.astype(BF16), dmixed)
            dprob = nt(dmixed, near[:, HD:])
            rest = jnp.sum(probs * dprob, axis=1, keepdims=True)
            dscore = (probs * (dprob - rest)).astype(BF16)
            dk += tn(dscore, query) * scale
            dquery = nn(dscore, near[:, :HD]) * scale
            inner += dquery * query.astype(F32)
            dq_ref[:, k * HD : (k + 1) * HD] = turn(dquery, cos_ref[...], -sin_ref[...]).astype(BF16)
        acc[near_rows, :HD] += dk
        acc[near_rows, HD:] += dv
        dots_ref[...] = jnp.where(
            line == 0, lane_sums(found[0]), jnp.where(line == 1, lane_sums(found[1]), lane_sums(inner))
        )

        @pl.when(i == rp // qt - 1)
        def _():
            far_ref[...] = acc[:seq_len, :]
            own_ref[...] = acc[seq_len:, :]

    ins = [(q_rot, (qt, 2 * HD), qrow), (kv_rot, None, None), (halo, None, None)]
    ins += [(sel, (qt, 8), qrow), (cols_a, (qt, 8), qrow)]
    ins += [(cosine, (qt, HD), qrow), (sine, (qt, HD), qrow)]
    ins += [(v, (qt, HD), qrow) for v in dm_a + dm_b + (mixed_a, mixed_b)]
    outs = [
        ((rp, 2 * HD), BF16, (qt, 2 * HD), qrow),
        ((rp, 2 * HD), F32, None, None),
        ((seq_len, 2 * HD), F32, None, None),
        ((8, rp), F32, (8, qt), lambda i, m: (0, i)),
    ]
    dq, dkv_own, dkv_far, dots_q = run(
        attend_back_body, "attend_back", (rp // qt,), meta, ins, outs,
        [pltpu.VMEM((seq_len + rp, 2 * HD), BF16), pltpu.VMEM((seq_len + rp, 2 * HD), F32)],
        flops=20 * rp * span * HD,
    )
    dkv_in = to_previous(dkv_far)

    def dkv_body(m, own_ref, in_ref, kv_ref, cos_ref, sin_ref, out_ref, dots_ref):
        head = rp - seq_len
        for rows_here in (slice(0, head), slice(head, rp)):
            value = own_ref[rows_here, :]
            if rows_here.start == head:
                value = value + in_ref[...]
            out_ref[rows_here, :HD] = turn(
                value[:, :HD], cos_ref[rows_here, :], -sin_ref[rows_here, :]
            ).astype(BF16)
            out_ref[rows_here, HD:] = value[:, HD:].astype(BF16)
            dots_ref[:, rows_here] = lane_sums(value * kv_ref[rows_here, :].astype(F32))

    ins = [(v, None, None) for v in (dkv_own, dkv_in, kv_rot, cosine, sine)]
    outs = [((rp, 2 * HD), BF16, None, None), ((8, rp), F32, None, None)]
    dkv, dots_kv = run(
        dkv_body, "dkv", (1,), after(meta, ag_a[3], ag_b[3]), ins, outs
    )
    third = jnp.arange(8)[:, None] == 2
    def down_body(m, *refs):
        a_refs, b_refs = refs[:4], refs[4:8]
        sel_ref, d_refs = refs[8], refs[9 : 9 + parts]
        w_refs = refs[9 + parts : 9 + 2 * parts]
        keep_ref, send_ref = refs[9 + 2 * parts : 11 + 2 * parts]
        outs = refs[11 + 2 * parts : 11 + 3 * parts]
        acc, xs, ids, mt = refs[11 + 3 * parts :]
        e = pl.program_id(0)

        @pl.when(e == 0)
        def _():
            acc[...] = jnp.zeros_like(acc)
            sort_rows(m, sel_ref, d_refs, xs, ids)

        expert = e.astype(F32)
        for r in range(4):
            here_r = slice(r * blk, (r + 1) * blk)
            mt[here_r, :] = pick(
                ids[here_r, 2:3], ids[here_r, 3:4], expert, a_refs[r][...], b_refs[r][...]
            )
        for s, value in enumerate(nn_pieces(mt[...], [w[0] for w in w_refs])):
            acc[s] += value
        for s, value in enumerate(t_right(mt[...], [xs[s] for s in pieces])):
            outs[s][0] = value.astype(BF16)

        @pl.when(e == experts - 1)
        def _():
            keep_ref[...] = acc[:, at_row(m, 6, 2 * blk), :].astype(BF16)
            send_ref[...] = acc[:, at_row(m, 7, 2 * blk), :].astype(BF16)

    def down(meta):
        spot = lambda e, m: (e, 0, 0)
        ins = [(v, None, None) for v in ag_a + ag_b]
        ins += [(sel, None, None)] + [(d, None, None) for d in d_pieces]
        ins += [(w, (1, ff, ds), spot) for w in wo]
        outs = [((parts, 2 * blk, ds), BF16, None, None)] * 2
        outs += [((experts, ff, ds), BF16, (1, ff, ds), spot)] * parts
        return run(
            down_body, "down", (experts,), meta, ins, outs,
            [
                pltpu.VMEM((parts, rp, ds), F32),
                pltpu.VMEM((parts, rp, ds), BF16),
                pltpu.VMEM((rp, 8), F32),
                pltpu.VMEM((rp, ff), BF16),
            ],
            flops=4 * rp * experts * parts * ds * ff,
        )

    def dwproj_body(m, *refs):
        a_refs, b_refs = refs[:4], refs[4:8]
        sel_ref, d_ref = refs[8:10]
        outs = refs[10 : 10 + parts]
        lo, hi = refs[10 + parts :]
        e = pl.program_id(0)

        @pl.when(e == 0)
        def _():
            for r in range(4):
                lanes = pl.ds(pl.multiple_of(m[2 + r] * HD, HD), HD)
                lo[:, lanes] = a_refs[r][...]
                hi[:, lanes] = b_refs[r][...]

        x = pick(sel_ref[:, 0:1], sel_ref[:, 1:2], e.astype(F32), lo[...], hi[...])
        for s, value in enumerate(t_right(x, [d_ref[s] for s in pieces])):
            outs[s][0] = value.astype(BF16)

    def dwproj(meta):
        ins = [(v, None, None) for v in gm_a + gm_b]
        ins += [(sel, None, None), (dafter_low, None, None)]
        return run(
            dwproj_body, "dwproj", (experts,), meta, ins,
            [((experts, hw, ds), BF16, (1, hw, ds), lambda e, m: (e, 0, 0))] * parts,
            [pltpu.VMEM((rp, hw), BF16)] * 2,
            flops=2 * rp * experts * hw * parts * ds,
        )

    down_halves = down(after(meta, dkv))
    down_halves, dwout_sums = down_halves[:2], down_halves[2:]
    da_a, da_b, da_along = gather_groups(dq, dkv, late=(dwout_sums[0],))
    dwproj_sums = dwproj(after(meta, da_along))
    def place_heads(m, refs, lo, hi):
        for r in range(4):
            lanes = pl.ds(pl.multiple_of(m[2 + r] * HD, HD), HD)
            lo[:, lanes] = refs[r][:, :HD]
            hi[:, lanes] = refs[r][:, HD:]

    def dattn_body(m, *refs):
        a_refs, b_refs = refs[:4], refs[4:8]
        sel_ref = refs[8]
        q_refs = refs[9 : 9 + parts]
        kv_refs = refs[9 + parts : 9 + 2 * parts]
        outs = refs[9 + 2 * parts : 11 + 2 * parts]
        lo, hi, dk, dv = refs[11 + 2 * parts :]
        place_heads(m, a_refs, lo, hi)
        place_heads(m, b_refs, dk, dv)
        acc = nt_pieces(dk[...], [w[0] for w in kv_refs])
        for s, value in enumerate(nt_pieces(dv[...], [w[1] for w in kv_refs])):
            acc[s] += value
        for e in range(experts):
            x = pick(sel_ref[:, 0:1], sel_ref[:, 1:2], e, lo[...], hi[...])
            for s, value in enumerate(nt_pieces(x, [w[e] for w in q_refs])):
                acc[s] += value
        for s in pieces:
            store_halves(pl.program_id(0), outs, s, acc[s].astype(BF16))

    def dattn(meta):
        half = lambda i, m: (m[7 - i], 0)
        ins = [(v, (2 * zr, 2 * HD), half) for v in da_a + da_b]
        ins += [(sel, (2 * zr, 8), half)]
        ins += [(w, None, None) for w in wq + wkv]
        return run(
            dattn_body, "dattn", (2,), meta, ins, [((parts, 2 * zr, ds), BF16, None, None)] * 2,
            [pltpu.VMEM((2 * zr, hw), BF16)] * 4,
            flops=8 * zr * (experts + 2) * hw * parts * ds,
        )

    dots_a = sum_groups(after(dots_q + jnp.where(third, dots_kv, 0.0), dwproj_sums[0]))
    da_halves = dattn(after(meta, dwproj_sums[0]))
    x_stack = jnp.stack(x_pieces)
    attn_input = (x_stack.astype(F32) * flat_a[0][None, :, None] * gain_a).astype(BF16)

    def dwqkv_body(m, *refs):
        a_refs, b_refs = refs[:4], refs[4:8]
        sel_ref, x_ref = refs[8:10]
        q_outs, kv_outs = refs[10 : 10 + parts], refs[10 + parts : 10 + 2 * parts]
        lo, hi, dk, dv = refs[10 + 2 * parts :]
        e = pl.program_id(0)
        xs = [x_ref.at[s] for s in pieces]

        @pl.when(e == 0)
        def _():
            place_heads(m, a_refs, lo, hi)
            place_heads(m, b_refs, dk, dv)

        @pl.when(e < experts)
        def _():
            x = pick(sel_ref[:, 0:1], sel_ref[:, 1:2], e.astype(F32), lo[...], hi[...])
            for s, value in enumerate(t_left([v[...] for v in xs], x)):
                q_outs[s][0] = value.astype(BF16)

        for k, grad in enumerate((dk, dv)):

            @pl.when(e == experts + k)
            def _():
                for s, value in enumerate(t_left([v[...] for v in xs], grad[...])):
                    kv_outs[s][0] = value.astype(BF16)

    def dwqkv(meta):
        q_spot = lambda e, m: (jnp.minimum(e, experts - 1), 0, 0)
        kv_spot = lambda e, m: (jnp.maximum(e - experts, 0), 0, 0)
        ins = [(v, None, None) for v in da_a + da_b]
        ins += [(sel, None, None), (attn_input, None, None)]
        outs = [((experts, ds, hw), BF16, (1, ds, hw), q_spot)] * parts
        outs += [((2, ds, hw), BF16, (1, ds, hw), kv_spot)] * parts
        return run(
            dwqkv_body, "dwqkv", (experts + 2,), meta, ins, outs,
            [pltpu.VMEM((rp, hw), BF16)] * 4,
            flops=2 * rp * (experts + 2) * hw * parts * ds,
        )

    dwqkv_sums = dwqkv(after(meta, da_halves[0], dots_a))
    dots_a = sum_z(dots_a)


    da_half = z_covered(*da_halves, 1, dwqkv_sums[0])

    down_half = z_covered(*down_halves, 1, dwproj_sums[0])
    down_half = z_covered(down_half, down_half, 3, da_halves[0])
    down_totals = z_last(down_half)

    def finish_body(m, *refs):
        t_refs, after_ref, outs = refs[:2], refs[2], refs[3:]
        for k in range(4):
            span_k = at_row(m, BY_HALF + k, blk)
            for s in pieces:
                total = t_refs[k // 2][s, (k % 2) * blk : (k % 2 + 1) * blk, :]
                outs[s][span_k, :] = (
                    after_ref[s, span_k, :] + total.astype(F32)
                ).astype(BF16)

    ins = [(t, None, None) for t in down_totals] + [(after_rows, None, None)]
    out_rows = run(
        finish_body, "finish", (1,), after(meta, dwqkv_sums[0]), ins,
        [((rp, ds), BF16, None, None)] * parts,
    )

    count = rows_all // dp

    def unpack_body(dealt, m, other_ref, *refs):
        v_refs, out_ref = refs[:parts], refs[-5]
        packed, other, total, whole = refs[-4:]
        for s in pieces:
            packed[part_rows(m, s), :] = v_refs[s][...].astype(F32)
        other[...] = other_ref[...].astype(F32)
        line = lax.broadcasted_iota(jnp.int32, (per, ds), 0)

        def one(j, carry):
            window, shift = near_rows(m, j)
            back = jnp.where(shift == 0, 0, seq_len + 8 - shift)
            whole[...] = pltpu.roll(packed[window, :], back, 0)
            for p in range(dp):
                if dealt:
                    spot = m[2 * seqs + j] * seq_len + p * per
                    kept = other[pl.ds(pl.multiple_of(spot, per), per), :]
                else:
                    kept = other[block_rows(p, j), :]
                value = whole[p * per : (p + 1) * per, :]
                total[block_rows(p, j), :] = jnp.where(line < m[seqs + j] - p * per, value, kept)
            return carry

        lax.fori_loop(0, seqs, one, 0)
        for p in range(dp):
            out_ref[p, :count, :] = total[p * count : (p + 1) * count, :].astype(BF16)
            for ref in refs[parts:-5]:
                out_ref[p, count:, :] = ref[...]

    def unpack(value, otherwise, dealt, table, extra=()):
        mine_all = [value[0]] + [by_part(value[s], s) for s in pieces[1:]]
        ins = [(v, None, None) for v in [otherwise] + mine_all + list(extra)]
        tall = count + sum(v.shape[0] for v in extra)
        spread_rows = run(
            functools.partial(unpack_body, dealt), "unpack", (1,), table, ins,
            [((dp, tall, ds), BF16, None, None)],
            [
                pltpu.VMEM((n, ds), F32)
                for n in (rows + seq_len + 8, rows_all, rows_all, seq_len + 8)
            ],
        )[0]
        landed = lax.all_to_all(spread_rows, "dp", 0, 0, tiled=True)
        rows_of = landed[:, :count].transpose(1, 0, 2).reshape(seqs, per, width)
        return rows_of, spread_rows, landed[:, count:]

    layer_out, layer_rows, _ = unpack(out_rows, x_all, False, table)
    expertin_grad = fold((dwin_gate, dwin_up), after(meta, layer_rows, dots_a))
    back_a = back_columns(flat_a, dots_a, low_a, high_a)
    da_half = z_covered(da_half, da_half, 3, layer_rows)
    da_totals = z_last(da_half)
    ins = [(t, None, None) for t in da_totals]
    ins += [(x_stack, None, None), (dafter, None, None)]
    ins += [(gain_a, None, None), (router_a, None, None), (back_a, None, None)]
    outs = [((rp, ds), BF16, None, None)] * parts
    outs += [((experts + 1, parts, ds), F32, None, None)]
    *dinput, small_a = run(
        functools.partial(norm_back_body, False), "norm_back_first", (1,),
        after(meta, expertin_grad), ins, outs,
    )
    expertout_grad = exchange(dwout_sums)
    proj_grad = exchange(dwproj_sums)
    query_grad, kv_grad = exchange(dwqkv_sums[:parts]), exchange(dwqkv_sums[parts:])
    vectors = 2 * (experts + 1)
    small = jnp.concatenate([small_a, small_f], axis=0).reshape(vectors * parts, ds)
    small = jnp.pad(small, ((0, -vectors * parts % 16), (0, 0))).astype(BF16)
    input_grad, _, got = unpack(dinput, d_all, True, after(table, layer_out), [small])
    got = got[:, : vectors * parts].astype(F32).reshape(groups, parts, vectors, parts, ds)
    full = jnp.stack(
        [sum(got[:, k ^ s, :, s] for s in pieces) for k in range(parts)], axis=2
    )
    full = full.transpose(1, 0, 2, 3).reshape(2, experts + 1, width)
    attnrouter_grad, attngain_grad = full[0, :experts].T, full[0, experts]
    ffnrouter_grad, ffngain_grad = full[1, :experts].T, full[1, experts]
    return (
        layer_out,
        input_grad,
        attngain_grad,
        attnrouter_grad,
        kv_grad,
        query_grad,
        proj_grad,
        ffngain_grad,
        ffnrouter_grad,
        expertin_grad,
        expertout_grad,
    )


def solution(mesh):
    placed = (
        P(None, "dp", None),
        P("dp", None, None),
        P(),
        P(),
        P(),
        P(),
        P(),
        P(),
        P(None, "dp", "tensor"),
        P(None, "dp", "tensor"),
        P(None, "tensor", "dp"),
        P(),
        P(),
        P(None, "dp", None, "tensor"),
        P(None, "tensor", "dp"),
    )
    return jax.shard_map(
        functools.partial(local, dp=mesh.shape["dp"], tp=mesh.shape["tensor"]),
        mesh=mesh,
        in_specs=placed,
        out_specs=(
            P(None, "dp", None),
            P(None, "dp", None),
            P(),
            P(),
            P(None, "dp", "tensor"),
            P(None, "dp", "tensor"),
            P(None, "tensor", "dp"),
            P(),
            P(),
            P(None, "dp", None, "tensor"),
            P(None, "tensor", "dp"),
        ),
        check_vma=False,
    )
```

```python
import functools

import jax
import jax.numpy as jnp
from jax import lax
from jax.experimental import pallas as pl
from jax.experimental.pallas import tpu as pltpu
from jax.sharding import PartitionSpec as P

HD = 128
EPSILON = 1e-06
ROPE_BASE = 10000.0
BEST = lax.Precision.HIGHEST
F32 = jnp.float32
BF16 = jnp.bfloat16
VMEM_BYTES = 60 * 1024 * 1024


def nn(a, b):
    return lax.dot_general(a, b, (((1,), (0,)), ((), ())), preferred_element_type=F32)


def nt(a, b, precision=None):
    return lax.dot_general(
        a, b, (((1,), (1,)), ((), ())), preferred_element_type=F32, precision=precision
    )


def tn(a, b):
    return lax.dot_general(a, b, (((0,), (0,)), ((), ())), preferred_element_type=F32)


def lane_sums(values):
    ones = jnp.ones((8, values.shape[1]), F32)
    return nt(ones, values, BEST)


def run(body, name, grid, meta, ins, outs, scratch=(), flops=0):
    in_specs = []
    moved = 0
    for array, block, index in ins:
        if block is None:
            rank = array.ndim
            in_specs.append(pl.BlockSpec(array.shape, lambda *a, rank=rank: (0,) * rank))
        else:
            in_specs.append(pl.BlockSpec(block, index))
        moved += array.size * array.dtype.itemsize
    out_specs = []
    out_shape = []
    for shape, dtype, block, index in outs:
        if block is None:
            rank = len(shape)
            out_specs.append(pl.BlockSpec(shape, lambda *a, rank=rank: (0,) * rank))
        else:
            out_specs.append(pl.BlockSpec(block, index))
        out_shape.append(jax.ShapeDtypeStruct(shape, dtype))
        size = jnp.dtype(dtype).itemsize
        for extent in shape:
            size *= extent
        moved += size
    return pl.pallas_call(
        body,
        name=name,
        grid_spec=pltpu.PrefetchScalarGridSpec(
            num_scalar_prefetch=1,
            grid=grid,
            in_specs=in_specs,
            out_specs=out_specs,
            scratch_shapes=list(scratch),
        ),
        out_shape=out_shape,
        compiler_params=pltpu.CompilerParams(
            dimension_semantics=("arbitrary",) * len(grid), vmem_limit_bytes=VMEM_BYTES
        ),
        cost_estimate=pl.CostEstimate(flops=flops, bytes_accessed=moved, transcendentals=0),
    )(meta, *[array for array, _, _ in ins])


def pick(low_id, high_id, expert, low_value, high_value):
    zero = jnp.zeros_like(low_value)
    return jnp.where(
        low_id == expert, low_value, jnp.where(high_id == expert, high_value, zero)
    )


def two_slots(low_id, high_id, products):
    low_value = products[0]
    for expert in range(1, len(products) - 1):
        low_value = jnp.where(low_id == expert, products[expert], low_value)
    high_value = products[1]
    for expert in range(2, len(products)):
        high_value = jnp.where(high_id == expert, products[expert], high_value)
    return low_value, high_value


def turn(values, cosine, sine):
    return values * cosine + pltpu.roll(values, HD // 2, 1) * sine


def local(
    hidden_in,
    cotangent,
    lengths,
    dealing,
    attn_routes,
    ffn_routes,
    attn_gain,
    attn_router,
    kv_weight,
    query_weight,
    proj_weight,
    ffn_gain,
    ffn_router,
    expert_in,
    expert_out,
    *,
    dp,
    tp,
):
    seqs = dealing.shape[0]
    seq_len = cotangent.shape[1]
    slots = cotangent.shape[0]
    per = hidden_in.shape[1]
    width = hidden_in.shape[2]
    heads = query_weight.shape[2] // HD
    groups = heads
    parts = dp // groups
    ds = width // dp
    hw = heads * HD
    rows_all = seqs * seq_len
    rows = rows_all * 3 // 4
    rp = rows // parts
    blk = rp // groups
    experts = query_weight.shape[0]
    ff = expert_out.shape[1]
    scale = HD ** (-0.5)
    pieces = range(parts)

    index = lax.axis_index("dp")
    z = lax.axis_index("tensor")
    g = index // parts
    c = index % parts
    mine = ((z == 1) | (z == 2)).astype(jnp.int32)
    theirs = 1 - mine
    spots = [g, c, g, g ^ 1, g ^ 2, g ^ 3, mine, theirs]
    spots += [g ^ mine, g ^ theirs, g ^ (2 + mine), g ^ (2 + theirs)]
    spots += [g ^ (2 * mine), g ^ (2 * mine + 1), g ^ (2 * theirs), g ^ (2 * theirs + 1)]
    spots += [mine, theirs, 2 + mine, 2 + theirs]
    spots += [2 * mine, 2 * mine + 1, 2 * theirs, 2 * theirs + 1]
    meta = jnp.stack(spots).astype(jnp.int32)
    BY_CHUNK, BY_HALF, IN_ORDER, IN_HALVES = 8, 12, 16, 20

    def after(value, *others):
        return lax.optimization_barrier((value,) + others)[0]

    def both(a, b):
        return (a.astype(F32) + b.astype(F32)).astype(BF16)

    def by_group(value, mask):
        pairs = [(a, ((a // parts) ^ mask) * parts + a % parts) for a in range(dp)]
        return lax.ppermute(value, "dp", pairs)

    def by_part(value, mask):
        pairs = [(a, (a // parts) * parts + ((a % parts) ^ mask)) for a in range(dp)]
        return lax.ppermute(value, "dp", pairs)

    def to_next(value):
        pairs = [(a, a + 1) for a in range(dp) if a % parts < parts - 1]
        return lax.ppermute(value, "dp", pairs)

    def to_previous(value):
        pairs = [(a, a - 1) for a in range(dp) if a % parts > 0]
        return lax.ppermute(value, "dp", pairs)

    def by_z(value, mask):
        return lax.ppermute(value, "tensor", [(a, a ^ mask) for a in range(tp)])

    def sum_groups(value):
        value = value + by_group(value, 1)
        return value + by_group(value, 2)

    def sum_z(value):
        value = value + by_z(value, 1)
        return value + by_z(value, 3)

    def z_first(keep, send):
        return both(keep, by_z(send, 1))

    def z_second(half):
        return both(half, by_z(half, 3))

    def z_covered(keep, send, mask, cover):
        keep, got = held((keep, by_z(send, mask)), cover)
        return both(keep, got)

    def z_last(half):
        return half, by_z(half, 1)

    def wide_sum_z(keep, send):
        return z_last(z_second(z_first(keep, send)))

    def held(values, *others):
        return lax.optimization_barrier((tuple(values),) + others)[0]

    def reduce_groups(first, second, early=(), late=()):
        if early:
            first, second = held((tuple(first), tuple(second)), early)
        ra = by_group(first[3], 1)
        rb = by_group(second[3], 2)
        ax = by_group(first[1], 1)
        by = by_group(second[2], 2)
        along = held((both(first[2], ra), both(second[1], rb)), (ax, by), late)
        ay = by_group(along[0], 2)
        bx = by_group(along[1], 1)
        return (first[0], ax, ay), (second[0], bx, by), along, (ra, rb)

    def gather_groups(first, second, late=()):
        ax, bx = by_group(first, 1), by_group(second, 1)
        ay, by = by_group(first, 2), by_group(second, 2)
        along = held((ax, by), (bx, ay), late) if len(late) else (ax, by)
        ad, bd = by_group(along[0], 2), by_group(along[1], 1)
        return (first, ax, ay, ad), (second, bx, by, bd), along

    def row_of(offset):
        return lambda *a: (a[-1][2 + offset], 0)

    def at_row(m, spot, count):
        return pl.ds(pl.multiple_of(m[spot] * count, count), count)

    wide = ds % 128 == 0

    def nn_pieces(x, weights):
        if not wide:
            return [nn(x, w) for w in weights]
        value = nn(x, jnp.concatenate(weights, axis=1))
        return [value[:, s * ds : (s + 1) * ds] for s in pieces]

    def nt_pieces(x, weights):
        if not wide:
            return [nt(x, w) for w in weights]
        value = nt(x, jnp.concatenate(weights, axis=0))
        return [value[:, s * ds : (s + 1) * ds] for s in pieces]

    ends = jnp.cumsum(lengths)
    starts = ends - lengths
    inverse = jnp.sum(
        (dealing[None, :] == jnp.arange(seqs, dtype=jnp.int32)[:, None])
        * jnp.arange(seqs, dtype=jnp.int32)[None, :],
        axis=1,
    )

    table = jnp.concatenate([starts, lengths, inverse, c[None]]).astype(jnp.int32)

    def places(part):
        packed = part * rp + jnp.arange(rp, dtype=jnp.int32)
        begun = starts[None, :] <= packed[:, None]
        first = jnp.max(jnp.where(begun, starts[None, :], 0), axis=1)
        seq = jnp.sum(begun.astype(jnp.int32), axis=1) - 1
        return seq, packed - first, first

    seq, at, first = places(c)

    def slot_rows(m, j):
        return pl.ds(pl.multiple_of(m[2 * seqs + j] * seq_len, seq_len), seq_len)

    def part_rows(m, s):
        return pl.ds(pl.multiple_of((m[3 * seqs] ^ s) * rp, rp), rp)

    def block_rows(p, j):
        return pl.ds(pl.multiple_of((p * seqs + j) * per, per), per)

    def near_rows(m, j):
        shift = m[j] & 7
        return pl.ds(pl.multiple_of(m[j] - shift, 8), seq_len + 8), shift

    def pack_body(dealt, m, all_ref, *refs):
        outs = refs[:parts]
        source, packed, whole = refs[parts:]
        source[...] = all_ref[...].astype(F32)

        line = lax.broadcasted_iota(jnp.int32, (seq_len + 8, ds), 0)

        def one(j, carry):
            if dealt:
                whole[:seq_len, :] = source[slot_rows(m, j), :]
            else:
                for p in range(dp):
                    whole[p * per : (p + 1) * per, :] = source[block_rows(p, j), :]
            window, shift = near_rows(m, j)
            moved = pltpu.roll(whole[...], shift, 0)
            packed[window, :] = jnp.where(line < shift, packed[window, :], moved)
            return carry

        lax.fori_loop(0, seqs, one, 0)
        for s in pieces:
            outs[s][...] = packed[part_rows(m, s), :].astype(BF16)

    def pack(value, dealt, table):
        own = run(
            functools.partial(pack_body, dealt), "pack", (1,), table, [(value, None, None)],
            [((rp, ds), BF16, None, None)] * parts,
            [pltpu.VMEM((n, ds), F32) for n in (rows_all, rows + seq_len + 8, seq_len + 8)],
        )
        return [own[0]] + [by_part(own[s], s) for s in pieces[1:]]

    x_send = hidden_in.reshape(seqs * per, dp, ds).transpose(1, 0, 2)
    d_send = cotangent.reshape(slots * seq_len, dp, ds).transpose(1, 0, 2)
    x_all = lax.all_to_all(x_send, "dp", 0, 0, tiled=True).reshape(rows_all, ds)
    x_pieces = pack(x_all, False, table)
    def spread(vector):
        tall = vector.reshape((groups, parts, ds) + vector.shape[1:])[g]
        return jnp.stack([tall[c ^ s] for s in pieces])

    gain_a = spread(attn_gain)[:, None, :]
    gain_f = spread(ffn_gain)[:, None, :]
    pad = ((0, 0), (0, 8 - experts), (0, 0))
    router_a = jnp.pad(spread(attn_router).transpose(0, 2, 1), pad)
    router_f = jnp.pad(spread(ffn_router).transpose(0, 2, 1), pad)

    in_own = expert_in.swapaxes(1, 2)
    wq = [query_weight] + [by_part(query_weight, s) for s in pieces[1:]]
    wkv = [kv_weight] + [by_part(kv_weight, s) for s in pieces[1:]]
    wp = [proj_weight] + [by_part(proj_weight, s) for s in pieces[1:]]
    wo = [expert_out] + [by_part(expert_out, s) for s in pieces[1:]]
    wi = [in_own] + [by_part(in_own, s) for s in pieces[1:]]

    routes = jnp.concatenate(
        [attn_routes.reshape(rows_all, 2), ffn_routes.reshape(rows_all, 2)], axis=1
    )
    here = (seq * seq_len + at)[:, None] == jnp.arange(rows_all, dtype=jnp.int32)[None, :]
    mine = jnp.dot(here.astype(BF16), routes.astype(BF16), preferred_element_type=F32)
    low_a, high_a = jnp.minimum(mine[:, 0], mine[:, 1]), jnp.maximum(mine[:, 0], mine[:, 1])
    low_f, high_f = jnp.minimum(mine[:, 2], mine[:, 3]), jnp.maximum(mine[:, 2], mine[:, 3])
    window = (first - c * rp + seq_len).astype(F32)
    nil = jnp.zeros_like(window)
    sel = jnp.stack([low_a, high_a, low_f, high_f, window, nil, nil, nil], axis=1)
    half = HD // 2
    frequency = ROPE_BASE ** (-2.0 * jnp.arange(half, dtype=F32) / HD)
    angles = at.astype(F32)[:, None] * frequency[None, :]
    cosine = jnp.concatenate([jnp.cos(angles)] * 2, axis=1)
    sine = jnp.sin(angles)
    sine = jnp.concatenate([-sine, sine], axis=1)

    def gate_columns(stats, low_id, high_id):
        rms = lax.rsqrt(stats[experts] / width + EPSILON)
        ids = jnp.arange(experts, dtype=F32)[:, None]
        logits = stats[:experts]
        low_logit = jnp.sum(jnp.where(low_id[None] == ids, logits, 0.0), axis=0) * rms
        high_logit = jnp.sum(jnp.where(high_id[None] == ids, logits, 0.0), axis=0) * rms
        gap = low_logit - high_logit
        low_gate, high_gate = jax.nn.sigmoid(gap), jax.nn.sigmoid(-gap)
        zero = jnp.zeros_like(rms)
        flat = jnp.stack([rms, low_gate, high_gate, gap, zero, zero, zero, zero])
        return flat, flat.T

    tile = 256

    def qkv_body(m, *refs):
        x_refs = refs[:parts]
        gain_ref, router_ref = refs[parts : parts + 2]
        q_refs = refs[parts + 2 : 2 * parts + 2]
        kv_refs = refs[2 * parts + 2 : 3 * parts + 2]
        sel_ref = refs[3 * parts + 2]
        outs = refs[3 * parts + 3 : 3 * parts + 11]
        stats_ref, scr = refs[3 * parts + 11 :]
        us = []
        logits = jnp.zeros((8, tile), F32)
        squares = jnp.zeros((8, tile), F32)
        for s in pieces:
            xf = x_refs[s][...].astype(F32)
            us.append((xf * gain_ref[s]).astype(BF16))
            logits += nt(router_ref[s], us[s])
            squares += lane_sums(xf * xf)
        line = lax.broadcasted_iota(jnp.int32, (8, tile), 0)
        stats_ref[...] = jnp.where(line < experts, logits, squares)
        products = []
        for e in range(experts):
            products.append(sum(nn(us[s], q_refs[s][e]) for s in pieces))
        low, high = two_slots(sel_ref[:, 0:1], sel_ref[:, 1:2], products)
        keys = sum(nn(us[s], kv_refs[s][0]) for s in pieces)
        values = sum(nn(us[s], kv_refs[s][1]) for s in pieces)
        for k, value in enumerate((low, high, keys, values)):
            value = value.astype(BF16)
            for h in range(heads):
                scr[h, :, k * HD : (k + 1) * HD] = value[:, h * HD : (h + 1) * HD]
        for r in range(4):
            block = scr[m[2 + r]]
            outs[2 * r][...] = block[:, : 2 * HD]
            outs[2 * r + 1][...] = block[:, 2 * HD :]

    ins = [(x, (tile, ds), lambda i, m: (i, 0)) for x in x_pieces]
    ins += [(gain_a, None, None), (router_a, None, None)]
    ins += [(w, None, None) for w in wq + wkv]
    ins += [(sel, (tile, 8), lambda i, m: (i, 0))]
    outs = [((rp, 2 * HD), BF16, (tile, 2 * HD), lambda i, m: (i, 0))] * 8
    outs += [((8, rp), F32, (8, tile), lambda i, m: (0, i))]
    qkv = run(
        qkv_body, "qkv", (rp // tile,), after(meta, wo[1:], wi[1:], wp[1:]), ins, outs,
        [pltpu.VMEM((heads, tile, 4 * HD), BF16)],
        flops=2 * rp * (experts + 2) * parts * ds * hw,
    )
    stats_a = sum_groups(qkv[8])
    flat_a, cols_a = gate_columns(stats_a, low_a, high_a)
    q_sum, kv_sum, _, far = reduce_groups(qkv[0:8:2], qkv[1:8:2], late=cols_a)

    d_all = lax.all_to_all(d_send, "dp", 0, 0, tiled=True).reshape(rows_all, ds)
    d_pieces = pack(d_all, True, after(table, far[0]))

    def rows_pair(refs):
        return jnp.concatenate([ref[...] for ref in refs], axis=0)

    def dhidden_body(m, *refs):
        d_refs = refs[: 2 * parts]
        w_refs, sel_refs = refs[2 * parts : 3 * parts], refs[3 * parts : 3 * parts + 2]
        outs = refs[3 * parts + 2 :]
        ids = rows_pair(sel_refs)
        rows_of = [rows_pair(d_refs[2 * s : 2 * s + 2]) for s in pieces]
        products = []
        for e in range(experts):
            products.append(sum(nt(rows_of[s], w_refs[s][e]) for s in pieces))
        low, high = two_slots(ids[:, 2:3], ids[:, 3:4], products)
        low, high = low.astype(BF16), high.astype(BF16)
        for step, pair in enumerate(((3, 1), (2, 0))):

            @pl.when(pl.program_id(0) == step)
            def _():
                for k, r in enumerate(pair):
                    outs[2 * r][...] = low[k * blk : (k + 1) * blk]
                    outs[2 * r + 1][...] = high[k * blk : (k + 1) * blk]

    def dhidden(meta):
        spots = [lambda i, m: (m[5 - i], 0), lambda i, m: (m[3 - i], 0)]
        ins = [(d, (blk, ds), spot) for d in d_pieces for spot in spots]
        ins += [(w, None, None) for w in wo]
        ins += [(sel, (blk, 8), spot) for spot in spots]
        outs = [((blk, ff), BF16, None, None)] * 8
        return run(
            dhidden_body, "dhidden", (2,), meta, ins, outs,
            flops=2 * rp * experts * parts * ds * ff,
        )

    dh = dhidden(meta)

    def rope_body(m, a0, a1, a2, b0, b1, b2, cols, cos_ref, sin_ref, q_ref, kv_ref):
        rms = cols[:, 0:1]
        cos, sin = cos_ref[...], sin_ref[...]
        q = (a0[...].astype(F32) + a1[...].astype(F32) + a2[...].astype(F32)) * rms
        kv = (b0[...].astype(F32) + b1[...].astype(F32) + b2[...].astype(F32)) * rms
        q_ref[:, :HD] = turn(q[:, :HD], cos, sin).astype(BF16)
        q_ref[:, HD:] = turn(q[:, HD:], cos, sin).astype(BF16)
        kv_ref[:, :HD] = turn(kv[:, :HD], cos, sin).astype(BF16)
        kv_ref[:, HD:] = kv[:, HD:].astype(BF16)

    ins = [(v, (tile, 2 * HD), lambda i, m: (i, 0)) for v in q_sum + kv_sum]
    ins += [(cols_a, (tile, 8), lambda i, m: (i, 0))]
    ins += [(v, (tile, HD), lambda i, m: (i, 0)) for v in (cosine, sine)]
    outs = [((rp, 2 * HD), BF16, (tile, 2 * HD), lambda i, m: (i, 0))] * 2
    q_rot, kv_rot = run(rope_body, "rope", (rp // tile,), after(meta, dh[0]), ins, outs)
    halo = to_next(kv_rot[rp - seq_len :])

    qt = 128
    span = seq_len + qt

    def window_mask(i, low_key):
        u = i * qt + lax.broadcasted_iota(jnp.int32, (qt, span), 1)
        t = seq_len + i * qt + lax.broadcasted_iota(jnp.int32, (qt, span), 0)
        return (u >= low_key.astype(jnp.int32)) & (u <= t)

    def softmax_of(query, key, allowed):
        score = jnp.where(allowed, nt(query, key) * scale, -1e30)
        top = jnp.max(score, axis=1, keepdims=True)
        raised = jnp.exp(score - top)
        return raised / jnp.sum(raised, axis=1, keepdims=True)

    def attend_body(m, q_ref, kv_ref, halo_ref, sel_ref, cols, ga, gb, ma, mb, ext):
        i = pl.program_id(0)

        @pl.when(i == 0)
        def _():
            ext[:seq_len, :] = halo_ref[...]
            ext[seq_len:, :] = kv_ref[...]

        near = ext[pl.ds(pl.multiple_of(i * qt, qt), span), :]
        allowed = window_mask(i, sel_ref[:, 4:5])
        for k, (g_ref, m_ref) in enumerate(((ga, ma), (gb, mb))):
            probs = softmax_of(q_ref[:, k * HD : (k + 1) * HD], near[:, :HD], allowed)
            mixed = nn(probs.astype(BF16), near[:, HD:]).astype(BF16)
            m_ref[...] = mixed
            g_ref[...] = (mixed.astype(F32) * cols[:, 1 + k : 2 + k]).astype(BF16)

    def qrow(i, m):
        return (i, 0)

    ins = [(q_rot, (qt, 2 * HD), qrow), (kv_rot, None, None), (halo, None, None)]
    ins += [(sel, (qt, 8), qrow), (cols_a, (qt, 8), qrow)]
    outs = [((rp, HD), BF16, (qt, HD), qrow)] * 4
    gated_a, gated_b, mixed_a, mixed_b = run(
        attend_body, "attend", (rp // qt,), meta, ins, outs,
        [pltpu.VMEM((seq_len + rp, 2 * HD), BF16)],
        flops=8 * rp * span * HD,
    )
    gm_a, gm_b, _ = gather_groups(gated_a, gated_b)
    zr = rp // 2
    hold = [((parts, zr, ds), BF16, None, None)] * 2

    def store_halves(i, refs, s, value):
        @pl.when(i == 0)
        def _():
            refs[1][s] = value

        @pl.when(i == 1)
        def _():
            refs[0][s] = value

    def proj_body(m, *refs):
        a_refs, b_refs = refs[:4], refs[4:8]
        sel_ref = refs[8]
        w_refs = refs[9 : 9 + parts]
        outs, xs = refs[9 + parts : 11 + parts], refs[11 + parts]
        for r in range(4):
            lanes = pl.ds(pl.multiple_of(m[2 + r] * HD, HD), HD)
            for e in range(experts):
                xs[e, :, lanes] = pick(
                    sel_ref[:, 0:1], sel_ref[:, 1:2], e, a_refs[r][...], b_refs[r][...]
                )
        acc = nn_pieces(xs[0], [w[0] for w in w_refs])
        for e in range(1, experts):
            for s, value in enumerate(nn_pieces(xs[e], [w[e] for w in w_refs])):
                acc[s] += value
        for s in pieces:
            store_halves(pl.program_id(0), outs, s, acc[s].astype(BF16))

    def project(meta):
        half = lambda i, m: (m[7 - i], 0)
        ins = [(v, (zr, HD), half) for v in gm_a + gm_b]
        ins += [(sel, (zr, 8), half)]
        ins += [(w, None, None) for w in wp]
        return run(
            proj_body, "proj", (2,), meta, ins, hold,
            [pltpu.VMEM((experts, zr, hw), BF16)],
            flops=4 * zr * experts * hw * parts * ds,
        )

    proj_halves = project(meta)
    dh_a, dh_b = held((dh[0:8:2], dh[1:8:2]), gm_a[3], gm_b[3])
    ra, rb = by_group(dh_a[3], 1), by_group(dh_b[3], 2)
    ax, by = by_group(dh_a[1], 1), by_group(dh_b[2], 2)
    half = z_second(z_first(*proj_halves))
    near = held((both(dh_a[2], ra), both(dh_b[1], rb)), (ax, by), half)
    dh_a, dh_b = (dh_a[0], ax, by_group(near[0], 2)), (dh_b[0], by_group(near[1], 1), by)
    attn_totals = list(z_last(half))

    def norm_body(m, *refs):
        t_refs = refs[: 2]
        x_refs = refs[2 : 2 + parts]
        gain_ref, router_ref, after_ref, u_ref, stats_ref = refs[2 + parts :]
        for k in range(2):
            span_k = at_row(m, IN_ORDER + k, zr)
            for s in pieces:
                after_ref[s, span_k, :] = x_refs[s][span_k, :].astype(F32) + t_refs[k][s].astype(F32)
        logits = jnp.zeros((8, rp), F32)
        squares = jnp.zeros((8, rp), F32)
        for s in pieces:
            af = after_ref[s]
            u = (af * gain_ref[s]).astype(BF16)
            u_ref[s] = u
            logits += nt(router_ref[s], u)
            squares += lane_sums(af * af)
        line = lax.broadcasted_iota(jnp.int32, (8, rp), 0)
        stats_ref[...] = jnp.where(line < experts, logits, squares)

    ins = [(t, None, None) for t in attn_totals + x_pieces]
    ins += [(gain_f, None, None), (router_f, None, None)]
    outs = [
        ((parts, rp, ds), F32, None, None),
        ((parts, rp, ds), BF16, None, None),
        ((8, rp), F32, None, None),
    ]
    after_rows, u_f, stats_part = run(norm_body, "norm", (1,), meta, ins, outs)
    def up_body(m, *refs):
        u_refs, w_refs = refs[:2], refs[2 : 2 + parts]
        sel_refs = refs[2 + parts : 4 + parts]
        outs = refs[4 + parts :]
        ids = rows_pair(sel_refs)
        rows_of = [jnp.concatenate([u[s] for u in u_refs], axis=0) for s in pieces]
        products = []
        for e in range(experts):
            products.append(sum(nn(rows_of[s], w_refs[s][e, 0]) for s in pieces))
        low, high = two_slots(ids[:, 2:3], ids[:, 3:4], products)
        low, high = low.astype(BF16), high.astype(BF16)
        for k in range(2):
            outs[2 * k][0] = low[k * blk : (k + 1) * blk]
            outs[2 * k + 1][0] = high[k * blk : (k + 1) * blk]

    def up(pair, meta):
        def block_of(r):
            return lambda j, m: (0, m[2 + r], 0)

        ins = [(u_f, (parts, blk, ds), block_of(r)) for r in pair]
        ins += [(w, (experts, 1, ds, ff), lambda j, m: (0, j, 0, 0)) for w in wi]
        ins += [(sel, (blk, 8), row_of(r)) for r in pair]
        outs = [((2, blk, ff), BF16, (1, blk, ff), lambda j, m: (j, 0, 0))] * 4
        return run(
            up_body, "up", (2,), meta, ins, outs, flops=8 * blk * experts * parts * ds * ff
        )

    up_far = up((3, 1), after(meta, dh_a[2], dh_b[1]))
    up_near = up((2, 0), after(meta, up_far[0]))
    gu_a, gu_b, _, far = reduce_groups(
        (up_near[2], up_far[2], up_near[0], up_far[0]),
        (up_near[3], up_far[3], up_near[1], up_far[1]),
    )

    stats_f = sum_groups(after(stats_part, far))
    flat_f, cols_f = gate_columns(stats_f, low_f, high_f)

    mt_rows = blk // 3

    def mid_body(m, *refs):
        gu = (refs[0:3], refs[3:6])
        dhr = (refs[6:9], refs[9:12])
        cols = refs[12]
        acts, grads, dots = refs[13:15], refs[15:17], refs[17]
        rms = cols[:, 0:1]
        column = lax.broadcasted_iota(jnp.int32, (mt_rows, 8), 1)
        found = []
        inner = jnp.zeros((mt_rows, 1), F32)
        for k in range(2):
            gate = cols[:, 1 + k : 2 + k]
            gp = sum(v[0].astype(F32) for v in gu[k]) * rms
            up_pre = sum(v[1].astype(F32) for v in gu[k]) * rms
            raw = sum(v[...].astype(F32) for v in dhr[k])
            sg = jax.nn.sigmoid(gp)
            act = (gp * sg * up_pre).astype(BF16).astype(F32)
            grad = raw * gate
            dgp = (grad * up_pre * sg * (1.0 + gp * (1.0 - sg))).astype(BF16)
            dup = (grad * gp * sg).astype(BF16)
            acts[k][...] = (act * gate).astype(BF16)
            grads[k][0] = dgp
            grads[k][1] = dup
            found.append(jnp.sum(act * raw, axis=1, keepdims=True))
            inner += jnp.sum(
                dgp.astype(F32) * gp + dup.astype(F32) * up_pre, axis=1, keepdims=True
            )
        zero = jnp.zeros((mt_rows, 8), F32)
        for k, value in enumerate(found + [inner]):
            zero = jnp.where(column == k, value, zero)
        dots[...] = zero

    rows_3 = lambda i, m: (0, i, 0)
    rows_2 = lambda i, m: (i, 0)
    ins = [(v, (2, mt_rows, ff), rows_3) for v in gu_a + gu_b]
    ins += [(v, (mt_rows, ff), rows_2) for v in dh_a + dh_b]
    ins += [(cols_f, (mt_rows, 8), lambda i, m: (3 * m[2] + i, 0))]
    outs = [((blk, ff), BF16, (mt_rows, ff), rows_2)] * 2
    outs += [((2, blk, ff), BF16, (2, mt_rows, ff), rows_3)] * 2
    outs += [((blk, 8), F32, (mt_rows, 8), rows_2)]
    act_a, act_b, grad_a, grad_b, dots_f = run(mid_body, "mid", (3,), meta, ins, outs)
    gg_a, gg_b, gg_along = gather_groups(grad_a, grad_b, late=(act_a,))
    dots_f = dots_f.T

    def dx_body(m, *refs):
        a_refs, b_refs = refs[:2], refs[2:4]
        w_refs = refs[4 : 4 + parts]
        sel_refs = refs[4 + parts : 6 + parts]
        keep_ref, send_ref, acc, xs = refs[6 + parts :]
        e = pl.program_id(0)
        expert = e.astype(F32)

        @pl.when(e == 0)
        def _():
            acc[...] = jnp.zeros_like(acc)

        for j in range(2):
            for k in range(2):
                ids = sel_refs[k]
                xs[k * blk : (k + 1) * blk, :] = pick(
                    ids[:, 2:3], ids[:, 3:4], expert, a_refs[k][j], b_refs[k][j]
                )
            for s, value in enumerate(nt_pieces(xs[...], [w[0, j] for w in w_refs])):
                acc[s] += value

        @pl.when(e == experts - 1)
        def _():
            keep_ref[...] = acc[:, at_row(m, 6, blk), :].astype(BF16)
            send_ref[...] = acc[:, at_row(m, 7, blk), :].astype(BF16)

    def dx(pair, meta):
        ins = [(v[r], None, None) for v in (gg_a, gg_b) for r in pair]
        ins += [(w, (1, 2, ds, ff), lambda e, m: (e, 0, 0, 0)) for w in wi]
        ins += [(sel, (blk, 8), row_of(r)) for r in pair]
        return run(
            dx_body, "dx", (experts,), meta, ins, [((parts, blk, ds), BF16, None, None)] * 2,
            [pltpu.VMEM((parts, 2 * blk, ds), F32), pltpu.VMEM((2 * blk, ff), BF16)],
            flops=8 * blk * experts * parts * ds * ff,
        )

    dx_near = dx((0, 1), after(meta, gg_a[2], gg_b[2]))
    dx_far = dx((2, 3), meta)
    dots_f = sum_z(dots_f)
    dots_f = jnp.stack([dots_f, held([by_group(dots_f, 1)], dx_near[0])[0]])
    dots_f = jnp.concatenate([dots_f, held([by_group(dots_f, 2)], dx_far[0])[0]])
    near_half = z_first(*dx_near)
    near_half = z_covered(near_half, near_half, 3, dx_far[0])
    far_half = z_first(*dx_far)

    act_a, act_b, _ = lax.optimization_barrier((act_a, act_b, far_half))
    ag_a = [act_a, by_group(act_a, 1), by_group(act_a, 2)]
    ag_b = [act_b, by_group(act_b, 1), by_group(act_b, 2)]
    dots_f = jnp.take(dots_f, g ^ jnp.arange(4, dtype=jnp.int32), axis=0)
    dots_f = dots_f.transpose(1, 0, 2).reshape(8, rp)

    def back_columns(flat, dots, low_id, high_id):
        delta = flat[1] * flat[2] * (dots[0] - dots[1])
        inner = (dots[2] + delta * flat[3]) / width
        ids = jnp.arange(experts, dtype=F32)[:, None]
        dlogit = jnp.where(low_id[None] == ids, delta[None], 0.0) - jnp.where(
            high_id[None] == ids, delta[None], 0.0
        )
        zero = jnp.zeros((1, rp), F32)
        return jnp.concatenate(
            [dlogit, inner[None], flat[0:1]] + [zero] * (6 - experts), axis=0
        ).T

    back_f = back_columns(flat_f, dots_f, low_f, high_f)


    def exchange(sums):
        return [sums[0]] + [by_part(sums[s], s) for s in pieces[1:]]

    def add_up(got):
        return sum(v.astype(F32) for v in got)

    ffn_input = (after_rows * flat_f[0][None, :, None] * gain_f).astype(BF16)

    def t_left(xs, value):
        if not wide:
            return [tn(x, value) for x in xs]
        total = tn(jnp.concatenate(xs, axis=1), value)
        return [total[s * ds : (s + 1) * ds] for s in pieces]

    def t_right(value, xs):
        if not wide:
            return [tn(value, x) for x in xs]
        total = tn(value, jnp.concatenate(xs, axis=1))
        return [total[:, s * ds : (s + 1) * ds] for s in pieces]

    def sort_rows(m, sel_ref, x_refs, xs, ids):
        for r in range(4):
            src, here_r = at_row(m, 2 + r, blk), slice(r * blk, (r + 1) * blk)
            for s in pieces:
                xs[s, here_r, :] = x_refs[s][src, :]
            ids[here_r, :] = sel_ref[src, :]

    def dwin_body(m, *refs):
        a_refs, b_refs = refs[:4], refs[4:8]
        sel_ref, x_ref = refs[8:10]
        outs = refs[10 : 10 + parts]
        xs, ids, mt = refs[10 + parts :]
        e = pl.program_id(0)

        @pl.when(e == 0)
        def _():
            sort_rows(m, sel_ref, [x_ref.at[s] for s in pieces], xs, ids)

        expert = e.astype(F32)
        for r in range(4):
            here_r = slice(r * blk, (r + 1) * blk)
            mt[here_r, :] = pick(
                ids[here_r, 2:3], ids[here_r, 3:4], expert, a_refs[r][0], b_refs[r][0]
            )
        for s, value in enumerate(t_left([xs[s] for s in pieces], mt[...])):
            outs[s][0] = value.astype(BF16)

    def dwin(j, meta):
        ins = [(v, (1, blk, ff), lambda e, m: (j, 0, 0)) for v in gg_a + gg_b]
        ins += [(sel, None, None), (ffn_input, None, None)]
        outs = [((experts, ds, ff), BF16, (1, ds, ff), lambda e, m: (e, 0, 0))] * parts
        return run(
            dwin_body, "dwin", (experts,), meta, ins, outs,
            [pltpu.VMEM((parts, rp, ds), BF16), pltpu.VMEM((rp, 8), F32), pltpu.VMEM((rp, ff), BF16)],
            flops=2 * rp * experts * parts * ds * ff,
        )

    def fold_body(m, *refs):
        out_ref = refs[2 * parts]
        for j in range(2):
            total = refs[j * parts][0].astype(F32)
            for ref in refs[j * parts + 1 : (j + 1) * parts]:
                total = total + ref[0].astype(F32)
            out_ref[0, :, j, :] = total

    def fold(sums, meta):
        ins = [(v, (1, ds, ff), lambda e, m: (e, 0, 0)) for half in sums for v in half]
        outs = [((experts, ds, 2, ff), F32, (1, ds, 2, ff), lambda e, m: (e, 0, 0, 0))]
        return run(fold_body, "fold", (experts,), meta, ins, outs)[0]

    dwin_gate = dwin(0, after(meta, far_half))
    dx_totals = z_last(near_half) + z_last(z_covered(far_half, far_half, 3, dwin_gate[0]))

    def norm_back_body(low_precision_out, m, *refs):
        sums = 4 if low_precision_out else 2
        t_refs, after_ref, refs = refs[:sums], refs[sums], refs[sums + 1 :]
        ups = parts if low_precision_out else 1
        up_refs = refs[:ups]
        gain_ref, router_ref, back = refs[ups : 3 + ups]
        outs = refs[3 + ups :]
        small = outs[-1]
        for s in pieces:
            gain = gain_ref[s]
            router = router_ref[s].astype(F32)
            gain_sum = jnp.zeros((1, ds), F32)
            router_sum = [jnp.zeros((1, ds), F32)] * experts
            for r in range(4):
                span_r = at_row(m, (BY_CHUNK if low_precision_out else IN_HALVES) + r, blk)
                up_value = up_refs[s][span_r, :] if low_precision_out else up_refs[0][s, span_r, :]
                x = after_ref[s, span_r, :].astype(F32)
                cols = back[span_r, :]
                rms = cols[:, experts + 1 : experts + 2]
                if low_precision_out:
                    grad = t_refs[r][s].astype(F32)
                else:
                    grad = t_refs[r // 2][s, (r % 2) * blk : (r % 2 + 1) * blk, :].astype(F32)
                for e in range(experts):
                    grad += cols[:, e : e + 1] * router[e : e + 1]
                normed = x * rms
                token = (normed * gain).astype(BF16).astype(F32)
                gain_sum += jnp.sum(grad * normed, axis=0, keepdims=True)
                for e in range(experts):
                    router_sum[e] = router_sum[e] + jnp.sum(
                        token * cols[:, e : e + 1], axis=0, keepdims=True
                    )
                dn = grad * gain
                total = up_value.astype(F32) + rms * (
                    dn - normed * cols[:, experts : experts + 1]
                )
                if low_precision_out:
                    outs[0][s, span_r, :] = total
                    outs[1][s, span_r, :] = total.astype(BF16)
                else:
                    outs[s][span_r, :] = total.astype(BF16)
            for e in range(experts):
                small[e, s] = router_sum[e][0]
            small[experts, s] = gain_sum[0]

    ins = [(t, None, None) for t in dx_totals]
    ins += [(after_rows, None, None)] + [(d, None, None) for d in d_pieces]
    ins += [(gain_f, None, None), (router_f, None, None), (back_f, None, None)]
    outs = [
        ((parts, rp, ds), F32, None, None),
        ((parts, rp, ds), BF16, None, None),
        ((experts + 1, parts, ds), F32, None, None),
    ]
    dafter, dafter_low, small_f = run(
        functools.partial(norm_back_body, True), "norm_back", (1,),
        after(meta, dwin_gate[0], ag_a[1:], ag_b[1:]), ins, outs,
    )

    def dmix_body(m, *refs):
        d_ref = refs[0]
        w_refs = refs[1 : 1 + parts]
        sel_ref = refs[1 + parts]
        outs = refs[2 + parts : 10 + parts]
        scr = refs[10 + parts]
        products = []
        for e in range(experts):
            products.append(sum(nt(d_ref[s], w_refs[s][e]) for s in pieces))
        low, high = two_slots(sel_ref[:, 0:1], sel_ref[:, 1:2], products)
        for k, value in enumerate((low, high)):
            value = value.astype(BF16)
            for h in range(heads):
                scr[h, :, k * HD : (k + 1) * HD] = value[:, h * HD : (h + 1) * HD]
        for r in range(4):
            block = scr[m[2 + r]]
            outs[2 * r][...] = block[:, :HD]
            outs[2 * r + 1][...] = block[:, HD:]

    ins = [(dafter_low, (parts, tile, ds), lambda i, m: (0, i, 0))]
    ins += [(w, None, None) for w in wp]
    ins += [(sel, (tile, 8), lambda i, m: (i, 0))]
    outs = [((rp, HD), BF16, (tile, HD), lambda i, m: (i, 0))] * 8
    dm = run(
        dmix_body, "dmix", (rp // tile,), meta, ins, outs,
        [pltpu.VMEM((heads, tile, 2 * HD), BF16)],
        flops=2 * rp * experts * parts * ds * hw,
    )
    dwin_up = dwin(1, after(meta, dm[0]))
    dm_a, dm_b, _, _ = reduce_groups(dm[0:8:2], dm[1:8:2], late=dwin_up[0])
    along = held((ag_a[1], ag_b[2]), dm_a[2], dm_b[1])
    ag_a, ag_b = ag_a + [by_group(along[0], 2)], ag_b + [by_group(along[1], 1)]

    def attend_back_body(m, *refs):
        q_ref, kv_ref, halo_ref, sel_ref, cols, cos_ref, sin_ref = refs[:7]
        d_refs = (refs[7:10], refs[10:13])
        mix_refs = refs[13:15]
        dq_ref, own_ref, far_ref, dots_ref, ext, acc = refs[15:]
        i = pl.program_id(0)

        @pl.when(i == 0)
        def _():
            ext[:seq_len, :] = halo_ref[...]
            ext[seq_len:, :] = kv_ref[...]
            acc[...] = jnp.zeros_like(acc)

        near_rows = pl.ds(pl.multiple_of(i * qt, qt), span)
        near = ext[near_rows, :]
        allowed = window_mask(i, sel_ref[:, 4:5])
        line = lax.broadcasted_iota(jnp.int32, (8, qt), 0)
        inner = jnp.zeros((qt, HD), F32)
        found = []
        dk = jnp.zeros((span, HD), F32)
        dv = jnp.zeros((span, HD), F32)
        for k in range(2):
            query = q_ref[:, k * HD : (k + 1) * HD]
            probs = softmax_of(query, near[:, :HD], allowed)
            raw = sum(v[...].astype(F32) for v in d_refs[k])
            dmixed = (raw * cols[:, 1 + k : 2 + k]).astype(BF16)
            found.append(raw * mix_refs[k][...].astype(F32))
            dv += tn(probs.astype(BF16), dmixed)
            dprob = nt(dmixed, near[:, HD:])
            rest = jnp.sum(probs * dprob, axis=1, keepdims=True)
            dscore = (probs * (dprob - rest)).astype(BF16)
            dk += tn(dscore, query) * scale
            dquery = nn(dscore, near[:, :HD]) * scale
            inner += dquery * query.astype(F32)
            dq_ref[:, k * HD : (k + 1) * HD] = turn(dquery, cos_ref[...], -sin_ref[...]).astype(BF16)
        acc[near_rows, :HD] += dk
        acc[near_rows, HD:] += dv
        dots_ref[...] = jnp.where(
            line == 0, lane_sums(found[0]), jnp.where(line == 1, lane_sums(found[1]), lane_sums(inner))
        )

        @pl.when(i == rp // qt - 1)
        def _():
            far_ref[...] = acc[:seq_len, :]
            own_ref[...] = acc[seq_len:, :]

    ins = [(q_rot, (qt, 2 * HD), qrow), (kv_rot, None, None), (halo, None, None)]
    ins += [(sel, (qt, 8), qrow), (cols_a, (qt, 8), qrow)]
    ins += [(cosine, (qt, HD), qrow), (sine, (qt, HD), qrow)]
    ins += [(v, (qt, HD), qrow) for v in dm_a + dm_b + (mixed_a, mixed_b)]
    outs = [
        ((rp, 2 * HD), BF16, (qt, 2 * HD), qrow),
        ((rp, 2 * HD), F32, None, None),
        ((seq_len, 2 * HD), F32, None, None),
        ((8, rp), F32, (8, qt), lambda i, m: (0, i)),
    ]
    dq, dkv_own, dkv_far, dots_q = run(
        attend_back_body, "attend_back", (rp // qt,), meta, ins, outs,
        [pltpu.VMEM((seq_len + rp, 2 * HD), BF16), pltpu.VMEM((seq_len + rp, 2 * HD), F32)],
        flops=20 * rp * span * HD,
    )
    dkv_in = to_previous(dkv_far)

    def dkv_body(m, own_ref, in_ref, kv_ref, cos_ref, sin_ref, out_ref, dots_ref):
        head = rp - seq_len
        for rows_here in (slice(0, head), slice(head, rp)):
            value = own_ref[rows_here, :]
            if rows_here.start == head:
                value = value + in_ref[...]
            out_ref[rows_here, :HD] = turn(
                value[:, :HD], cos_ref[rows_here, :], -sin_ref[rows_here, :]
            ).astype(BF16)
            out_ref[rows_here, HD:] = value[:, HD:].astype(BF16)
            dots_ref[:, rows_here] = lane_sums(value * kv_ref[rows_here, :].astype(F32))

    ins = [(v, None, None) for v in (dkv_own, dkv_in, kv_rot, cosine, sine)]
    outs = [((rp, 2 * HD), BF16, None, None), ((8, rp), F32, None, None)]
    got_in = [exchange(dwin_gate), exchange(held(dwin_up, dm_a[2], dm_b[1]))]
    dkv, dots_kv = run(
        dkv_body, "dkv", (1,), after(meta, ag_a[3], ag_b[3]), ins, outs
    )
    third = jnp.arange(8)[:, None] == 2
    def down_body(m, *refs):
        a_refs, b_refs = refs[:4], refs[4:8]
        sel_ref, d_refs = refs[8], refs[9 : 9 + parts]
        w_refs = refs[9 + parts : 9 + 2 * parts]
        keep_ref, send_ref = refs[9 + 2 * parts : 11 + 2 * parts]
        outs = refs[11 + 2 * parts : 11 + 3 * parts]
        acc, xs, ids, mt = refs[11 + 3 * parts :]
        e = pl.program_id(0)

        @pl.when(e == 0)
        def _():
            acc[...] = jnp.zeros_like(acc)
            sort_rows(m, sel_ref, d_refs, xs, ids)

        expert = e.astype(F32)
        for r in range(4):
            here_r = slice(r * blk, (r + 1) * blk)
            mt[here_r, :] = pick(
                ids[here_r, 2:3], ids[here_r, 3:4], expert, a_refs[r][...], b_refs[r][...]
            )
        for s, value in enumerate(nn_pieces(mt[...], [w[0] for w in w_refs])):
            acc[s] += value
        for s, value in enumerate(t_right(mt[...], [xs[s] for s in pieces])):
            outs[s][0] = value.astype(BF16)

        @pl.when(e == experts - 1)
        def _():
            keep_ref[...] = acc[:, at_row(m, 6, 2 * blk), :].astype(BF16)
            send_ref[...] = acc[:, at_row(m, 7, 2 * blk), :].astype(BF16)

    def down(meta):
        spot = lambda e, m: (e, 0, 0)
        ins = [(v, None, None) for v in ag_a + ag_b]
        ins += [(sel, None, None)] + [(d, None, None) for d in d_pieces]
        ins += [(w, (1, ff, ds), spot) for w in wo]
        outs = [((parts, 2 * blk, ds), BF16, None, None)] * 2
        outs += [((experts, ff, ds), BF16, (1, ff, ds), spot)] * parts
        return run(
            down_body, "down", (experts,), meta, ins, outs,
            [
                pltpu.VMEM((parts, rp, ds), F32),
                pltpu.VMEM((parts, rp, ds), BF16),
                pltpu.VMEM((rp, 8), F32),
                pltpu.VMEM((rp, ff), BF16),
            ],
            flops=4 * rp * experts * parts * ds * ff,
        )

    def dwproj_body(m, *refs):
        a_refs, b_refs = refs[:4], refs[4:8]
        sel_ref, d_ref = refs[8:10]
        outs = refs[10 : 10 + parts]
        lo, hi = refs[10 + parts :]
        e = pl.program_id(0)

        @pl.when(e == 0)
        def _():
            for r in range(4):
                lanes = pl.ds(pl.multiple_of(m[2 + r] * HD, HD), HD)
                lo[:, lanes] = a_refs[r][...]
                hi[:, lanes] = b_refs[r][...]

        x = pick(sel_ref[:, 0:1], sel_ref[:, 1:2], e.astype(F32), lo[...], hi[...])
        for s, value in enumerate(t_right(x, [d_ref[s] for s in pieces])):
            outs[s][0] = value.astype(BF16)

    def dwproj(meta):
        ins = [(v, None, None) for v in gm_a + gm_b]
        ins += [(sel, None, None), (dafter_low, None, None)]
        return run(
            dwproj_body, "dwproj", (experts,), meta, ins,
            [((experts, hw, ds), BF16, (1, hw, ds), lambda e, m: (e, 0, 0))] * parts,
            [pltpu.VMEM((rp, hw), BF16)] * 2,
            flops=2 * rp * experts * hw * parts * ds,
        )

    down_halves = down(after(meta, dkv))
    down_halves, dwout_sums = down_halves[:2], down_halves[2:]
    da_a, da_b, da_along = gather_groups(dq, dkv, late=(dwout_sums[0],))
    dwproj_sums = dwproj(after(meta, da_along, got_in))
    def place_heads(m, refs, lo, hi):
        for r in range(4):
            lanes = pl.ds(pl.multiple_of(m[2 + r] * HD, HD), HD)
            lo[:, lanes] = refs[r][:, :HD]
            hi[:, lanes] = refs[r][:, HD:]

    def dattn_body(m, *refs):
        a_refs, b_refs = refs[:4], refs[4:8]
        sel_ref = refs[8]
        q_refs = refs[9 : 9 + parts]
        kv_refs = refs[9 + parts : 9 + 2 * parts]
        outs = refs[9 + 2 * parts : 11 + 2 * parts]
        lo, hi, dk, dv = refs[11 + 2 * parts :]
        place_heads(m, a_refs, lo, hi)
        place_heads(m, b_refs, dk, dv)
        acc = nt_pieces(dk[...], [w[0] for w in kv_refs])
        for s, value in enumerate(nt_pieces(dv[...], [w[1] for w in kv_refs])):
            acc[s] += value
        for e in range(experts):
            x = pick(sel_ref[:, 0:1], sel_ref[:, 1:2], e, lo[...], hi[...])
            for s, value in enumerate(nt_pieces(x, [w[e] for w in q_refs])):
                acc[s] += value
        for s in pieces:
            store_halves(pl.program_id(0), outs, s, acc[s].astype(BF16))

    def dattn(meta):
        half = lambda i, m: (m[7 - i], 0)
        ins = [(v, (zr, 2 * HD), half) for v in da_a + da_b]
        ins += [(sel, (zr, 8), half)]
        ins += [(w, None, None) for w in wq + wkv]
        return run(
            dattn_body, "dattn", (2,), meta, ins, [((parts, zr, ds), BF16, None, None)] * 2,
            [pltpu.VMEM((zr, hw), BF16)] * 4,
            flops=4 * zr * (experts + 2) * hw * parts * ds,
        )

    dots_a = dots_q + jnp.where(third, dots_kv, 0.0)
    dots_a = sum_groups(after(dots_a, dwproj_sums[0]))
    got_out = exchange(dwout_sums)
    da_halves = dattn(after(meta, dwproj_sums[0]))
    got_proj = exchange(dwproj_sums)
    x_stack = jnp.stack(x_pieces)
    attn_input = (x_stack.astype(F32) * flat_a[0][None, :, None] * gain_a).astype(BF16)

    def dwqkv_body(m, *refs):
        a_refs, b_refs = refs[:4], refs[4:8]
        sel_ref, x_ref = refs[8:10]
        q_outs, kv_outs = refs[10 : 10 + parts], refs[10 + parts : 10 + 2 * parts]
        lo, hi, dk, dv = refs[10 + 2 * parts :]
        e = pl.program_id(0)
        xs = [x_ref.at[s] for s in pieces]

        @pl.when(e == 0)
        def _():
            place_heads(m, a_refs, lo, hi)
            place_heads(m, b_refs, dk, dv)

        @pl.when(e < experts)
        def _():
            x = pick(sel_ref[:, 0:1], sel_ref[:, 1:2], e.astype(F32), lo[...], hi[...])
            for s, value in enumerate(t_left([v[...] for v in xs], x)):
                q_outs[s][0] = value.astype(BF16)

        for k, grad in enumerate((dk, dv)):

            @pl.when(e == experts + k)
            def _():
                for s, value in enumerate(t_left([v[...] for v in xs], grad[...])):
                    kv_outs[s][0] = value.astype(BF16)

    def dwqkv(meta):
        q_spot = lambda e, m: (jnp.minimum(e, experts - 1), 0, 0)
        kv_spot = lambda e, m: (jnp.maximum(e - experts, 0), 0, 0)
        ins = [(v, None, None) for v in da_a + da_b]
        ins += [(sel, None, None), (attn_input, None, None)]
        outs = [((experts, ds, hw), BF16, (1, ds, hw), q_spot)] * parts
        outs += [((2, ds, hw), BF16, (1, ds, hw), kv_spot)] * parts
        return run(
            dwqkv_body, "dwqkv", (experts + 2,), meta, ins, outs,
            [pltpu.VMEM((rp, hw), BF16)] * 4,
            flops=2 * rp * (experts + 2) * hw * parts * ds,
        )

    dwqkv_sums = dwqkv(after(meta, da_halves[0]))


    da_half = z_covered(*da_halves, 1, dwqkv_sums[0])

    down_half = z_covered(*down_halves, 1, dwproj_sums[0])
    down_half = z_covered(down_half, down_half, 3, da_halves[0])
    down_totals = z_last(down_half)

    def finish_body(m, *refs):
        t_refs, after_ref, outs = refs[:2], refs[2], refs[3:]
        for k in range(4):
            span_k = at_row(m, BY_HALF + k, blk)
            for s in pieces:
                total = t_refs[k // 2][s, (k % 2) * blk : (k % 2 + 1) * blk, :]
                outs[s][span_k, :] = (
                    after_ref[s, span_k, :] + total.astype(F32)
                ).astype(BF16)

    ins = [(t, None, None) for t in down_totals] + [(after_rows, None, None)]
    out_rows = run(
        finish_body, "finish", (1,), after(meta, dwqkv_sums[0], dots_a), ins,
        [((rp, ds), BF16, None, None)] * parts,
    )

    count = rows_all // dp

    def unpack_body(dealt, m, other_ref, *refs):
        v_refs, out_ref = refs[:parts], refs[-5]
        packed, other, total, whole = refs[-4:]
        for s in pieces:
            packed[part_rows(m, s), :] = v_refs[s][...].astype(F32)
        other[...] = other_ref[...].astype(F32)
        line = lax.broadcasted_iota(jnp.int32, (per, ds), 0)

        def one(j, carry):
            window, shift = near_rows(m, j)
            back = jnp.where(shift == 0, 0, seq_len + 8 - shift)
            whole[...] = pltpu.roll(packed[window, :], back, 0)
            for p in range(dp):
                if dealt:
                    spot = m[2 * seqs + j] * seq_len + p * per
                    kept = other[pl.ds(pl.multiple_of(spot, per), per), :]
                else:
                    kept = other[block_rows(p, j), :]
                value = whole[p * per : (p + 1) * per, :]
                total[block_rows(p, j), :] = jnp.where(line < m[seqs + j] - p * per, value, kept)
            return carry

        lax.fori_loop(0, seqs, one, 0)
        for p in range(dp):
            out_ref[p, :count, :] = total[p * count : (p + 1) * count, :].astype(BF16)
            for ref in refs[parts:-5]:
                out_ref[p, count:, :] = ref[...]

    def unpack(value, otherwise, dealt, table, extra=()):
        mine_all = [value[0]] + [by_part(value[s], s) for s in pieces[1:]]
        ins = [(v, None, None) for v in [otherwise] + mine_all + list(extra)]
        tall = count + sum(v.shape[0] for v in extra)
        spread_rows = run(
            functools.partial(unpack_body, dealt), "unpack", (1,), table, ins,
            [((dp, tall, ds), BF16, None, None)],
            [
                pltpu.VMEM((n, ds), F32)
                for n in (rows + seq_len + 8, rows_all, rows_all, seq_len + 8)
            ],
        )[0]
        landed = lax.all_to_all(spread_rows, "dp", 0, 0, tiled=True)
        rows_of = landed[:, :count].transpose(1, 0, 2).reshape(seqs, per, width)
        return rows_of, spread_rows, landed[:, count:]

    layer_out, layer_rows, _ = unpack(out_rows, x_all, False, table)
    got_q, got_kv = exchange(dwqkv_sums[:parts]), exchange(dwqkv_sums[parts:])
    expertin_grad = fold(got_in, after(meta, layer_rows))
    da_half = z_covered(da_half, da_half, 3, (expertin_grad, layer_out))
    da_totals = z_last(da_half)
    dots_a = sum_z(after(dots_a, da_half))
    back_a = back_columns(flat_a, dots_a, low_a, high_a)
    ins = [(t, None, None) for t in da_totals]
    ins += [(x_stack, None, None), (dafter, None, None)]
    ins += [(gain_a, None, None), (router_a, None, None), (back_a, None, None)]
    outs = [((rp, ds), BF16, None, None)] * parts
    outs += [((experts + 1, parts, ds), F32, None, None)]
    *dinput, small_a = run(
        functools.partial(norm_back_body, False), "norm_back_first", (1,),
        meta, ins, outs,
    )
    expertout_grad, proj_grad = add_up(got_out), add_up(got_proj)
    query_grad, kv_grad = add_up(got_q), add_up(got_kv)
    vectors = 2 * (experts + 1)
    small = jnp.concatenate([small_a, small_f], axis=0).reshape(vectors * parts, ds)
    small = jnp.pad(small, ((0, -vectors * parts % 16), (0, 0))).astype(BF16)
    input_grad, _, got = unpack(dinput, d_all, True, after(table, layer_out), [small])
    got = got[:, : vectors * parts].astype(F32).reshape(groups, parts, vectors, parts, ds)
    full = jnp.stack(
        [sum(got[:, k ^ s, :, s] for s in pieces) for k in range(parts)], axis=2
    )
    full = full.transpose(1, 0, 2, 3).reshape(2, experts + 1, width)
    attnrouter_grad, attngain_grad = full[0, :experts].T, full[0, experts]
    ffnrouter_grad, ffngain_grad = full[1, :experts].T, full[1, experts]
    return (
        layer_out,
        input_grad,
        attngain_grad,
        attnrouter_grad,
        kv_grad,
        query_grad,
        proj_grad,
        ffngain_grad,
        ffnrouter_grad,
        expertin_grad,
        expertout_grad,
    )


def solution(mesh):
    placed = (
        P(None, "dp", None),
        P("dp", None, None),
        P(),
        P(),
        P(),
        P(),
        P(),
        P(),
        P(None, "dp", "tensor"),
        P(None, "dp", "tensor"),
        P(None, "tensor", "dp"),
        P(),
        P(),
        P(None, "dp", None, "tensor"),
        P(None, "tensor", "dp"),
    )
    return jax.shard_map(
        functools.partial(local, dp=mesh.shape["dp"], tp=mesh.shape["tensor"]),
        mesh=mesh,
        in_specs=placed,
        out_specs=(
            P(None, "dp", None),
            P(None, "dp", None),
            P(),
            P(),
            P(None, "dp", "tensor"),
            P(None, "dp", "tensor"),
            P(None, "tensor", "dp"),
            P(),
            P(),
            P(None, "dp", None, "tensor"),
            P(None, "tensor", "dp"),
        ),
        check_vma=False,
    )
```

```python
import functools

import jax
import jax.numpy as jnp
from jax import lax
from jax.experimental import pallas as pl
from jax.experimental.pallas import tpu as pltpu
from jax.sharding import PartitionSpec as P

HD = 128
EPSILON = 1e-06
ROPE_BASE = 10000.0
BEST = lax.Precision.HIGHEST
F32 = jnp.float32
BF16 = jnp.bfloat16
VMEM_BYTES = 60 * 1024 * 1024


def nn(a, b):
    return lax.dot_general(a, b, (((1,), (0,)), ((), ())), preferred_element_type=F32)


def nt(a, b, precision=None):
    return lax.dot_general(
        a, b, (((1,), (1,)), ((), ())), preferred_element_type=F32, precision=precision
    )


def tn(a, b):
    return lax.dot_general(a, b, (((0,), (0,)), ((), ())), preferred_element_type=F32)


def lane_sums(values):
    ones = jnp.ones((8, values.shape[1]), F32)
    return nt(ones, values, BEST)


def run(body, name, grid, meta, ins, outs, scratch=(), flops=0):
    in_specs = []
    moved = 0
    for array, block, index in ins:
        if block is None:
            rank = array.ndim
            in_specs.append(pl.BlockSpec(array.shape, lambda *a, rank=rank: (0,) * rank))
        else:
            in_specs.append(pl.BlockSpec(block, index))
        moved += array.size * array.dtype.itemsize
    out_specs = []
    out_shape = []
    for shape, dtype, block, index in outs:
        if block is None:
            rank = len(shape)
            out_specs.append(pl.BlockSpec(shape, lambda *a, rank=rank: (0,) * rank))
        else:
            out_specs.append(pl.BlockSpec(block, index))
        out_shape.append(jax.ShapeDtypeStruct(shape, dtype))
        size = jnp.dtype(dtype).itemsize
        for extent in shape:
            size *= extent
        moved += size
    return pl.pallas_call(
        body,
        name=name,
        grid_spec=pltpu.PrefetchScalarGridSpec(
            num_scalar_prefetch=1,
            grid=grid,
            in_specs=in_specs,
            out_specs=out_specs,
            scratch_shapes=list(scratch),
        ),
        out_shape=out_shape,
        compiler_params=pltpu.CompilerParams(
            dimension_semantics=("arbitrary",) * len(grid), vmem_limit_bytes=VMEM_BYTES
        ),
        cost_estimate=pl.CostEstimate(flops=flops, bytes_accessed=moved, transcendentals=0),
    )(meta, *[array for array, _, _ in ins])


def pick(low_id, high_id, expert, low_value, high_value):
    zero = jnp.zeros_like(low_value)
    return jnp.where(
        low_id == expert, low_value, jnp.where(high_id == expert, high_value, zero)
    )


def two_slots(low_id, high_id, products):
    low_value = products[0]
    for expert in range(1, len(products) - 1):
        low_value = jnp.where(low_id == expert, products[expert], low_value)
    high_value = products[1]
    for expert in range(2, len(products)):
        high_value = jnp.where(high_id == expert, products[expert], high_value)
    return low_value, high_value


def turn(values, cosine, sine):
    return values * cosine + pltpu.roll(values, HD // 2, 1) * sine


def local(
    hidden_in,
    cotangent,
    lengths,
    dealing,
    attn_routes,
    ffn_routes,
    attn_gain,
    attn_router,
    kv_weight,
    query_weight,
    proj_weight,
    ffn_gain,
    ffn_router,
    expert_in,
    expert_out,
    *,
    dp,
    tp,
):
    seqs = dealing.shape[0]
    seq_len = cotangent.shape[1]
    slots = cotangent.shape[0]
    per = hidden_in.shape[1]
    width = hidden_in.shape[2]
    heads = query_weight.shape[2] // HD
    groups = heads
    parts = dp // groups
    ds = width // dp
    hw = heads * HD
    rows_all = seqs * seq_len
    rows = rows_all * 3 // 4
    rp = rows // parts
    blk = rp // groups
    experts = query_weight.shape[0]
    ff = expert_out.shape[1]
    scale = HD ** (-0.5)
    pieces = range(parts)

    index = lax.axis_index("dp")
    z = lax.axis_index("tensor")
    g = index // parts
    c = index % parts
    mine = ((z == 1) | (z == 2)).astype(jnp.int32)
    theirs = 1 - mine
    spots = [g, c, g, g ^ 1, g ^ 2, g ^ 3, mine, theirs]
    spots += [g ^ mine, g ^ theirs, g ^ (2 + mine), g ^ (2 + theirs)]
    spots += [g ^ (2 * mine), g ^ (2 * mine + 1), g ^ (2 * theirs), g ^ (2 * theirs + 1)]
    spots += [mine, theirs, 2 + mine, 2 + theirs]
    spots += [2 * mine, 2 * mine + 1, 2 * theirs, 2 * theirs + 1]
    meta = jnp.stack(spots).astype(jnp.int32)
    BY_CHUNK, BY_HALF, IN_ORDER, IN_HALVES = 8, 12, 16, 20

    def after(value, *others):
        return lax.optimization_barrier((value,) + others)[0]

    def both(a, b):
        return (a.astype(F32) + b.astype(F32)).astype(BF16)

    def by_group(value, mask):
        pairs = [(a, ((a // parts) ^ mask) * parts + a % parts) for a in range(dp)]
        return lax.ppermute(value, "dp", pairs)

    def by_part(value, mask):
        pairs = [(a, (a // parts) * parts + ((a % parts) ^ mask)) for a in range(dp)]
        return lax.ppermute(value, "dp", pairs)

    def to_next(value):
        pairs = [(a, a + 1) for a in range(dp) if a % parts < parts - 1]
        return lax.ppermute(value, "dp", pairs)

    def to_previous(value):
        pairs = [(a, a - 1) for a in range(dp) if a % parts > 0]
        return lax.ppermute(value, "dp", pairs)

    def by_z(value, mask):
        return lax.ppermute(value, "tensor", [(a, a ^ mask) for a in range(tp)])

    def sum_groups(value):
        value = value + by_group(value, 1)
        return value + by_group(value, 2)

    def sum_z(value):
        value = value + by_z(value, 1)
        return value + by_z(value, 3)

    def z_first(keep, send):
        return both(keep, by_z(send, 1))

    def z_second(half):
        return both(half, by_z(half, 3))

    def z_covered(keep, send, mask, cover):
        keep, got = held((keep, by_z(send, mask)), cover)
        return both(keep, got)

    def z_last(half):
        return half, by_z(half, 1)

    def wide_sum_z(keep, send):
        return z_last(z_second(z_first(keep, send)))

    def held(values, *others):
        return lax.optimization_barrier((tuple(values),) + others)[0]

    def reduce_groups(first, second, early=(), late=()):
        if early:
            first, second = held((tuple(first), tuple(second)), early)
        ra = by_group(first[3], 1)
        rb = by_group(second[3], 2)
        ax = by_group(first[1], 1)
        by = by_group(second[2], 2)
        along = held((both(first[2], ra), both(second[1], rb)), (ax, by), late)
        ay = by_group(along[0], 2)
        bx = by_group(along[1], 1)
        return (first[0], ax, ay), (second[0], bx, by), along, (ra, rb)

    def gather_groups(first, second, late=()):
        ax, bx = by_group(first, 1), by_group(second, 1)
        ay, by = by_group(first, 2), by_group(second, 2)
        along = held((ax, by), (bx, ay), late) if len(late) else (ax, by)
        ad, bd = by_group(along[0], 2), by_group(along[1], 1)
        return (first, ax, ay, ad), (second, bx, by, bd), along

    def row_of(offset):
        return lambda *a: (a[-1][2 + offset], 0)

    def at_row(m, spot, count):
        return pl.ds(pl.multiple_of(m[spot] * count, count), count)

    wide = ds % 128 == 0

    def nn_pieces(x, weights):
        if not wide:
            return [nn(x, w) for w in weights]
        value = nn(x, jnp.concatenate(weights, axis=1))
        return [value[:, s * ds : (s + 1) * ds] for s in pieces]

    def nt_pieces(x, weights):
        if not wide:
            return [nt(x, w) for w in weights]
        value = nt(x, jnp.concatenate(weights, axis=0))
        return [value[:, s * ds : (s + 1) * ds] for s in pieces]

    ends = jnp.cumsum(lengths)
    starts = ends - lengths
    inverse = jnp.sum(
        (dealing[None, :] == jnp.arange(seqs, dtype=jnp.int32)[:, None])
        * jnp.arange(seqs, dtype=jnp.int32)[None, :],
        axis=1,
    )

    table = jnp.concatenate([starts, lengths, inverse, c[None]]).astype(jnp.int32)

    def places(part):
        packed = part * rp + jnp.arange(rp, dtype=jnp.int32)
        begun = starts[None, :] <= packed[:, None]
        first = jnp.max(jnp.where(begun, starts[None, :], 0), axis=1)
        seq = jnp.sum(begun.astype(jnp.int32), axis=1) - 1
        return seq, packed - first, first

    seq, at, first = places(c)

    def slot_rows(m, j):
        return pl.ds(pl.multiple_of(m[2 * seqs + j] * seq_len, seq_len), seq_len)

    def part_rows(m, s):
        return pl.ds(pl.multiple_of((m[3 * seqs] ^ s) * rp, rp), rp)

    def block_rows(p, j):
        return pl.ds(pl.multiple_of((p * seqs + j) * per, per), per)

    def near_rows(m, j):
        shift = m[j] & 7
        return pl.ds(pl.multiple_of(m[j] - shift, 8), seq_len + 8), shift

    def pack_body(dealt, m, all_ref, *refs):
        outs = refs[:parts]
        source, packed, whole = refs[parts:]
        source[...] = all_ref[...].astype(F32)

        line = lax.broadcasted_iota(jnp.int32, (seq_len + 8, ds), 0)

        def one(j, carry):
            if dealt:
                whole[:seq_len, :] = source[slot_rows(m, j), :]
            else:
                for p in range(dp):
                    whole[p * per : (p + 1) * per, :] = source[block_rows(p, j), :]
            window, shift = near_rows(m, j)
            moved = pltpu.roll(whole[...], shift, 0)
            packed[window, :] = jnp.where(line < shift, packed[window, :], moved)
            return carry

        lax.fori_loop(0, seqs, one, 0)
        for s in pieces:
            outs[s][...] = packed[part_rows(m, s), :].astype(BF16)

    def pack(value, dealt, table):
        own = run(
            functools.partial(pack_body, dealt), "pack", (1,), table, [(value, None, None)],
            [((rp, ds), BF16, None, None)] * parts,
            [pltpu.VMEM((n, ds), F32) for n in (rows_all, rows + seq_len + 8, seq_len + 8)],
        )
        return [own[0]] + [by_part(own[s], s) for s in pieces[1:]]

    x_send = hidden_in.reshape(seqs * per, dp, ds).transpose(1, 0, 2)
    d_send = cotangent.reshape(slots * seq_len, dp, ds).transpose(1, 0, 2)
    x_all = lax.all_to_all(x_send, "dp", 0, 0, tiled=True).reshape(rows_all, ds)
    x_pieces = pack(x_all, False, table)
    def spread(vector):
        tall = vector.reshape((groups, parts, ds) + vector.shape[1:])[g]
        return jnp.stack([tall[c ^ s] for s in pieces])

    gain_a = spread(attn_gain)[:, None, :]
    gain_f = spread(ffn_gain)[:, None, :]
    pad = ((0, 0), (0, 8 - experts), (0, 0))
    router_a = jnp.pad(spread(attn_router).transpose(0, 2, 1), pad)
    router_f = jnp.pad(spread(ffn_router).transpose(0, 2, 1), pad)

    in_own = expert_in.swapaxes(1, 2)
    wq = [query_weight] + [by_part(query_weight, s) for s in pieces[1:]]
    wkv = [kv_weight] + [by_part(kv_weight, s) for s in pieces[1:]]
    wp = [proj_weight] + [by_part(proj_weight, s) for s in pieces[1:]]
    wo = [expert_out] + [by_part(expert_out, s) for s in pieces[1:]]
    wi = [in_own] + [by_part(in_own, s) for s in pieces[1:]]

    routes = jnp.concatenate(
        [attn_routes.reshape(rows_all, 2), ffn_routes.reshape(rows_all, 2)], axis=1
    )
    here = (seq * seq_len + at)[:, None] == jnp.arange(rows_all, dtype=jnp.int32)[None, :]
    mine = jnp.dot(here.astype(BF16), routes.astype(BF16), preferred_element_type=F32)
    low_a, high_a = jnp.minimum(mine[:, 0], mine[:, 1]), jnp.maximum(mine[:, 0], mine[:, 1])
    low_f, high_f = jnp.minimum(mine[:, 2], mine[:, 3]), jnp.maximum(mine[:, 2], mine[:, 3])
    window = (first - c * rp + seq_len).astype(F32)
    nil = jnp.zeros_like(window)
    sel = jnp.stack([low_a, high_a, low_f, high_f, window, nil, nil, nil], axis=1)
    half = HD // 2
    frequency = ROPE_BASE ** (-2.0 * jnp.arange(half, dtype=F32) / HD)
    angles = at.astype(F32)[:, None] * frequency[None, :]
    cosine = jnp.concatenate([jnp.cos(angles)] * 2, axis=1)
    sine = jnp.sin(angles)
    sine = jnp.concatenate([-sine, sine], axis=1)

    def gate_columns(stats, low_id, high_id):
        rms = lax.rsqrt(stats[experts] / width + EPSILON)
        ids = jnp.arange(experts, dtype=F32)[:, None]
        logits = stats[:experts]
        low_logit = jnp.sum(jnp.where(low_id[None] == ids, logits, 0.0), axis=0) * rms
        high_logit = jnp.sum(jnp.where(high_id[None] == ids, logits, 0.0), axis=0) * rms
        gap = low_logit - high_logit
        low_gate, high_gate = jax.nn.sigmoid(gap), jax.nn.sigmoid(-gap)
        zero = jnp.zeros_like(rms)
        flat = jnp.stack([rms, low_gate, high_gate, gap, zero, zero, zero, zero])
        return flat, flat.T

    tile = 256

    def qkv_body(m, *refs):
        x_refs = refs[:parts]
        gain_ref, router_ref = refs[parts : parts + 2]
        q_refs = refs[parts + 2 : 2 * parts + 2]
        kv_refs = refs[2 * parts + 2 : 3 * parts + 2]
        sel_ref = refs[3 * parts + 2]
        outs = refs[3 * parts + 3 : 3 * parts + 11]
        stats_ref, scr = refs[3 * parts + 11 :]
        us = []
        logits = jnp.zeros((8, tile), F32)
        squares = jnp.zeros((8, tile), F32)
        for s in pieces:
            xf = x_refs[s][...].astype(F32)
            us.append((xf * gain_ref[s]).astype(BF16))
            logits += nt(router_ref[s], us[s])
            squares += lane_sums(xf * xf)
        line = lax.broadcasted_iota(jnp.int32, (8, tile), 0)
        stats_ref[...] = jnp.where(line < experts, logits, squares)
        products = []
        for e in range(experts):
            products.append(sum(nn(us[s], q_refs[s][e]) for s in pieces))
        low, high = two_slots(sel_ref[:, 0:1], sel_ref[:, 1:2], products)
        keys = sum(nn(us[s], kv_refs[s][0]) for s in pieces)
        values = sum(nn(us[s], kv_refs[s][1]) for s in pieces)
        for k, value in enumerate((low, high, keys, values)):
            value = value.astype(BF16)
            for h in range(heads):
                scr[h, :, k * HD : (k + 1) * HD] = value[:, h * HD : (h + 1) * HD]
        for r in range(4):
            block = scr[m[2 + r]]
            outs[2 * r][...] = block[:, : 2 * HD]
            outs[2 * r + 1][...] = block[:, 2 * HD :]

    ins = [(x, (tile, ds), lambda i, m: (i, 0)) for x in x_pieces]
    ins += [(gain_a, None, None), (router_a, None, None)]
    ins += [(w, None, None) for w in wq + wkv]
    ins += [(sel, (tile, 8), lambda i, m: (i, 0))]
    outs = [((rp, 2 * HD), BF16, (tile, 2 * HD), lambda i, m: (i, 0))] * 8
    outs += [((8, rp), F32, (8, tile), lambda i, m: (0, i))]
    qkv = run(
        qkv_body, "qkv", (rp // tile,), after(meta, wo[1:], wp[1:]), ins, outs,
        [pltpu.VMEM((heads, tile, 4 * HD), BF16)],
        flops=2 * rp * (experts + 2) * parts * ds * hw,
    )
    stats_a = sum_groups(after(qkv[8], wi[1:]))
    flat_a, cols_a = gate_columns(stats_a, low_a, high_a)
    q_sum, kv_sum, _, far = reduce_groups(qkv[0:8:2], qkv[1:8:2], late=cols_a)

    d_all = lax.all_to_all(d_send, "dp", 0, 0, tiled=True).reshape(rows_all, ds)
    d_pieces = pack(d_all, True, after(table, far[0]))

    def rows_pair(refs):
        return jnp.concatenate([ref[...] for ref in refs], axis=0)

    def dhidden_body(m, *refs):
        d_refs = refs[: 2 * parts]
        w_refs, sel_refs = refs[2 * parts : 3 * parts], refs[3 * parts : 3 * parts + 2]
        outs = refs[3 * parts + 2 :]
        ids = rows_pair(sel_refs)
        rows_of = [rows_pair(d_refs[2 * s : 2 * s + 2]) for s in pieces]
        products = []
        for e in range(experts):
            products.append(sum(nt(rows_of[s], w_refs[s][e]) for s in pieces))
        low, high = two_slots(ids[:, 2:3], ids[:, 3:4], products)
        low, high = low.astype(BF16), high.astype(BF16)
        for step, pair in enumerate(((3, 1), (2, 0))):

            @pl.when(pl.program_id(0) == step)
            def _():
                for k, r in enumerate(pair):
                    outs[2 * r][...] = low[k * blk : (k + 1) * blk]
                    outs[2 * r + 1][...] = high[k * blk : (k + 1) * blk]

    def dhidden(meta):
        spots = [lambda i, m: (m[5 - i], 0), lambda i, m: (m[3 - i], 0)]
        ins = [(d, (blk, ds), spot) for d in d_pieces for spot in spots]
        ins += [(w, None, None) for w in wo]
        ins += [(sel, (blk, 8), spot) for spot in spots]
        outs = [((blk, ff), BF16, None, None)] * 8
        return run(
            dhidden_body, "dhidden", (2,), meta, ins, outs,
            flops=2 * rp * experts * parts * ds * ff,
        )

    dh = dhidden(meta)

    def rope_body(m, a0, a1, a2, b0, b1, b2, cols, cos_ref, sin_ref, q_ref, kv_ref):
        rms = cols[:, 0:1]
        cos, sin = cos_ref[...], sin_ref[...]
        q = (a0[...].astype(F32) + a1[...].astype(F32) + a2[...].astype(F32)) * rms
        kv = (b0[...].astype(F32) + b1[...].astype(F32) + b2[...].astype(F32)) * rms
        q_ref[:, :HD] = turn(q[:, :HD], cos, sin).astype(BF16)
        q_ref[:, HD:] = turn(q[:, HD:], cos, sin).astype(BF16)
        kv_ref[:, :HD] = turn(kv[:, :HD], cos, sin).astype(BF16)
        kv_ref[:, HD:] = kv[:, HD:].astype(BF16)

    ins = [(v, (tile, 2 * HD), lambda i, m: (i, 0)) for v in q_sum + kv_sum]
    ins += [(cols_a, (tile, 8), lambda i, m: (i, 0))]
    ins += [(v, (tile, HD), lambda i, m: (i, 0)) for v in (cosine, sine)]
    outs = [((rp, 2 * HD), BF16, (tile, 2 * HD), lambda i, m: (i, 0))] * 2
    q_rot, kv_rot = run(rope_body, "rope", (rp // tile,), after(meta, dh[0]), ins, outs)
    halo = to_next(kv_rot[rp - seq_len :])

    qt = 128
    span = seq_len + qt

    def window_mask(i, low_key):
        u = i * qt + lax.broadcasted_iota(jnp.int32, (qt, span), 1)
        t = seq_len + i * qt + lax.broadcasted_iota(jnp.int32, (qt, span), 0)
        return (u >= low_key.astype(jnp.int32)) & (u <= t)

    def softmax_of(query, key, allowed):
        score = jnp.where(allowed, nt(query, key) * scale, -1e30)
        top = jnp.max(score, axis=1, keepdims=True)
        raised = jnp.exp(score - top)
        return raised / jnp.sum(raised, axis=1, keepdims=True)

    def attend_body(m, q_ref, kv_ref, halo_ref, sel_ref, cols, ga, gb, ma, mb, ext):
        i = pl.program_id(0)

        @pl.when(i == 0)
        def _():
            ext[:seq_len, :] = halo_ref[...]
            ext[seq_len:, :] = kv_ref[...]

        near = ext[pl.ds(pl.multiple_of(i * qt, qt), span), :]
        allowed = window_mask(i, sel_ref[:, 4:5])
        for k, (g_ref, m_ref) in enumerate(((ga, ma), (gb, mb))):
            probs = softmax_of(q_ref[:, k * HD : (k + 1) * HD], near[:, :HD], allowed)
            mixed = nn(probs.astype(BF16), near[:, HD:]).astype(BF16)
            m_ref[...] = mixed
            g_ref[...] = (mixed.astype(F32) * cols[:, 1 + k : 2 + k]).astype(BF16)

    def qrow(i, m):
        return (i, 0)

    ins = [(q_rot, (qt, 2 * HD), qrow), (kv_rot, None, None), (halo, None, None)]
    ins += [(sel, (qt, 8), qrow), (cols_a, (qt, 8), qrow)]
    outs = [((rp, HD), BF16, (qt, HD), qrow)] * 4
    gated_a, gated_b, mixed_a, mixed_b = run(
        attend_body, "attend", (rp // qt,), meta, ins, outs,
        [pltpu.VMEM((seq_len + rp, 2 * HD), BF16)],
        flops=8 * rp * span * HD,
    )
    gm_a, gm_b, _ = gather_groups(gated_a, gated_b)
    zr = rp // 2
    hold = [((parts, zr, ds), BF16, None, None)] * 2

    def store_halves(i, refs, s, value):
        @pl.when(i == 0)
        def _():
            refs[1][s] = value

        @pl.when(i == 1)
        def _():
            refs[0][s] = value

    def proj_body(m, *refs):
        a_refs, b_refs = refs[:4], refs[4:8]
        sel_ref = refs[8]
        w_refs = refs[9 : 9 + parts]
        outs, xs = refs[9 + parts : 11 + parts], refs[11 + parts]
        for r in range(4):
            lanes = pl.ds(pl.multiple_of(m[2 + r] * HD, HD), HD)
            for e in range(experts):
                xs[e, :, lanes] = pick(
                    sel_ref[:, 0:1], sel_ref[:, 1:2], e, a_refs[r][...], b_refs[r][...]
                )
        acc = nn_pieces(xs[0], [w[0] for w in w_refs])
        for e in range(1, experts):
            for s, value in enumerate(nn_pieces(xs[e], [w[e] for w in w_refs])):
                acc[s] += value
        for s in pieces:
            store_halves(pl.program_id(0), outs, s, acc[s].astype(BF16))

    def project(meta):
        half = lambda i, m: (m[7 - i], 0)
        ins = [(v, (zr, HD), half) for v in gm_a + gm_b]
        ins += [(sel, (zr, 8), half)]
        ins += [(w, None, None) for w in wp]
        return run(
            proj_body, "proj", (2,), meta, ins, hold,
            [pltpu.VMEM((experts, zr, hw), BF16)],
            flops=4 * zr * experts * hw * parts * ds,
        )

    proj_halves = project(meta)
    dh_a, dh_b = held((dh[0:8:2], dh[1:8:2]), gm_a[3], gm_b[3])
    ra, rb = by_group(dh_a[3], 1), by_group(dh_b[3], 2)
    ax, by = by_group(dh_a[1], 1), by_group(dh_b[2], 2)
    half = z_second(z_first(*proj_halves))
    near = held((both(dh_a[2], ra), both(dh_b[1], rb)), (ax, by), half)
    dh_a, dh_b = (dh_a[0], ax, by_group(near[0], 2)), (dh_b[0], by_group(near[1], 1), by)
    attn_totals = list(z_last(half))

    def norm_body(m, *refs):
        t_refs = refs[: 2]
        x_refs = refs[2 : 2 + parts]
        gain_ref, router_ref, after_ref, u_ref, stats_ref = refs[2 + parts :]
        for k in range(2):
            span_k = at_row(m, IN_ORDER + k, zr)
            for s in pieces:
                after_ref[s, span_k, :] = x_refs[s][span_k, :].astype(F32) + t_refs[k][s].astype(F32)
        logits = jnp.zeros((8, rp), F32)
        squares = jnp.zeros((8, rp), F32)
        for s in pieces:
            af = after_ref[s]
            u = (af * gain_ref[s]).astype(BF16)
            u_ref[s] = u
            logits += nt(router_ref[s], u)
            squares += lane_sums(af * af)
        line = lax.broadcasted_iota(jnp.int32, (8, rp), 0)
        stats_ref[...] = jnp.where(line < experts, logits, squares)

    ins = [(t, None, None) for t in attn_totals + x_pieces]
    ins += [(gain_f, None, None), (router_f, None, None)]
    outs = [
        ((parts, rp, ds), F32, None, None),
        ((parts, rp, ds), BF16, None, None),
        ((8, rp), F32, None, None),
    ]
    after_rows, u_f, stats_part = run(norm_body, "norm", (1,), meta, ins, outs)
    def up_body(m, *refs):
        u_refs, w_refs = refs[:2], refs[2 : 2 + parts]
        sel_refs = refs[2 + parts : 4 + parts]
        outs = refs[4 + parts :]
        ids = rows_pair(sel_refs)
        rows_of = [jnp.concatenate([u[s] for u in u_refs], axis=0) for s in pieces]
        products = []
        for e in range(experts):
            products.append(sum(nn(rows_of[s], w_refs[s][e, 0]) for s in pieces))
        low, high = two_slots(ids[:, 2:3], ids[:, 3:4], products)
        low, high = low.astype(BF16), high.astype(BF16)
        for k in range(2):
            outs[2 * k][0] = low[k * blk : (k + 1) * blk]
            outs[2 * k + 1][0] = high[k * blk : (k + 1) * blk]

    def up(pair, meta):
        def block_of(r):
            return lambda j, m: (0, m[2 + r], 0)

        ins = [(u_f, (parts, blk, ds), block_of(r)) for r in pair]
        ins += [(w, (experts, 1, ds, ff), lambda j, m: (0, j, 0, 0)) for w in wi]
        ins += [(sel, (blk, 8), row_of(r)) for r in pair]
        outs = [((2, blk, ff), BF16, (1, blk, ff), lambda j, m: (j, 0, 0))] * 4
        return run(
            up_body, "up", (2,), meta, ins, outs, flops=8 * blk * experts * parts * ds * ff
        )

    up_far = up((3, 1), after(meta, dh_a[2], dh_b[1]))
    up_near = up((2, 0), after(meta, up_far[0]))
    gu_a, gu_b, _, far = reduce_groups(
        (up_near[2], up_far[2], up_near[0], up_far[0]),
        (up_near[3], up_far[3], up_near[1], up_far[1]),
    )

    stats_f = sum_groups(after(stats_part, far))
    flat_f, cols_f = gate_columns(stats_f, low_f, high_f)

    mt_rows = blk // 3

    def mid_body(m, *refs):
        gu = (refs[0:3], refs[3:6])
        dhr = (refs[6:9], refs[9:12])
        cols = refs[12]
        acts, grads, dots = refs[13:15], refs[15:17], refs[17]
        rms = cols[:, 0:1]
        column = lax.broadcasted_iota(jnp.int32, (mt_rows, 8), 1)
        found = []
        inner = jnp.zeros((mt_rows, 1), F32)
        for k in range(2):
            gate = cols[:, 1 + k : 2 + k]
            gp = sum(v[0].astype(F32) for v in gu[k]) * rms
            up_pre = sum(v[1].astype(F32) for v in gu[k]) * rms
            raw = sum(v[...].astype(F32) for v in dhr[k])
            sg = jax.nn.sigmoid(gp)
            act = (gp * sg * up_pre).astype(BF16).astype(F32)
            grad = raw * gate
            dgp = (grad * up_pre * sg * (1.0 + gp * (1.0 - sg))).astype(BF16)
            dup = (grad * gp * sg).astype(BF16)
            acts[k][...] = (act * gate).astype(BF16)
            grads[k][0] = dgp
            grads[k][1] = dup
            found.append(jnp.sum(act * raw, axis=1, keepdims=True))
            inner += jnp.sum(
                dgp.astype(F32) * gp + dup.astype(F32) * up_pre, axis=1, keepdims=True
            )
        zero = jnp.zeros((mt_rows, 8), F32)
        for k, value in enumerate(found + [inner]):
            zero = jnp.where(column == k, value, zero)
        dots[...] = zero

    rows_3 = lambda i, m: (0, i, 0)
    rows_2 = lambda i, m: (i, 0)
    ins = [(v, (2, mt_rows, ff), rows_3) for v in gu_a + gu_b]
    ins += [(v, (mt_rows, ff), rows_2) for v in dh_a + dh_b]
    ins += [(cols_f, (mt_rows, 8), lambda i, m: (3 * m[2] + i, 0))]
    outs = [((blk, ff), BF16, (mt_rows, ff), rows_2)] * 2
    outs += [((2, blk, ff), BF16, (2, mt_rows, ff), rows_3)] * 2
    outs += [((blk, 8), F32, (mt_rows, 8), rows_2)]
    act_a, act_b, grad_a, grad_b, dots_f = run(mid_body, "mid", (3,), meta, ins, outs)
    gg_a, gg_b, gg_along = gather_groups(grad_a, grad_b, late=(act_a,))
    dots_f = dots_f.T

    def dx_body(m, *refs):
        a_refs, b_refs = refs[:2], refs[2:4]
        w_refs = refs[4 : 4 + parts]
        sel_refs = refs[4 + parts : 6 + parts]
        keep_ref, send_ref, acc, xs = refs[6 + parts :]
        e = pl.program_id(0)
        expert = e.astype(F32)

        @pl.when(e == 0)
        def _():
            acc[...] = jnp.zeros_like(acc)

        for j in range(2):
            for k in range(2):
                ids = sel_refs[k]
                xs[k * blk : (k + 1) * blk, :] = pick(
                    ids[:, 2:3], ids[:, 3:4], expert, a_refs[k][j], b_refs[k][j]
                )
            for s, value in enumerate(nt_pieces(xs[...], [w[0, j] for w in w_refs])):
                acc[s] += value

        @pl.when(e == experts - 1)
        def _():
            keep_ref[...] = acc[:, at_row(m, 6, blk), :].astype(BF16)
            send_ref[...] = acc[:, at_row(m, 7, blk), :].astype(BF16)

    def dx(pair, meta):
        ins = [(v[r], None, None) for v in (gg_a, gg_b) for r in pair]
        ins += [(w, (1, 2, ds, ff), lambda e, m: (e, 0, 0, 0)) for w in wi]
        ins += [(sel, (blk, 8), row_of(r)) for r in pair]
        return run(
            dx_body, "dx", (experts,), meta, ins, [((parts, blk, ds), BF16, None, None)] * 2,
            [pltpu.VMEM((parts, 2 * blk, ds), F32), pltpu.VMEM((2 * blk, ff), BF16)],
            flops=8 * blk * experts * parts * ds * ff,
        )

    dx_near = dx((0, 1), after(meta, gg_a[2], gg_b[2]))
    dx_far = dx((2, 3), meta)
    dots_f = sum_z(dots_f)
    dots_f = jnp.stack([dots_f, held([by_group(dots_f, 1)], dx_near[0])[0]])
    dots_f = jnp.concatenate([dots_f, held([by_group(dots_f, 2)], dx_far[0])[0]])
    near_half = z_first(*dx_near)
    near_half = z_covered(near_half, near_half, 3, dx_far[0])
    far_half = z_first(*dx_far)

    act_a, act_b, _ = lax.optimization_barrier((act_a, act_b, far_half))
    ag_a = [act_a, by_group(act_a, 1), by_group(act_a, 2)]
    ag_b = [act_b, by_group(act_b, 1), by_group(act_b, 2)]
    dots_f = jnp.take(dots_f, g ^ jnp.arange(4, dtype=jnp.int32), axis=0)
    dots_f = dots_f.transpose(1, 0, 2).reshape(8, rp)

    def back_columns(flat, dots, low_id, high_id):
        delta = flat[1] * flat[2] * (dots[0] - dots[1])
        inner = (dots[2] + delta * flat[3]) / width
        ids = jnp.arange(experts, dtype=F32)[:, None]
        dlogit = jnp.where(low_id[None] == ids, delta[None], 0.0) - jnp.where(
            high_id[None] == ids, delta[None], 0.0
        )
        zero = jnp.zeros((1, rp), F32)
        return jnp.concatenate(
            [dlogit, inner[None], flat[0:1]] + [zero] * (6 - experts), axis=0
        ).T

    back_f = back_columns(flat_f, dots_f, low_f, high_f)


    def exchange(sums):
        return [sums[0]] + [by_part(sums[s], s) for s in pieces[1:]]

    def add_up(got):
        return sum(v.astype(F32) for v in got)

    ffn_input = (after_rows * flat_f[0][None, :, None] * gain_f).astype(BF16)

    def t_left(xs, value):
        if not wide:
            return [tn(x, value) for x in xs]
        total = tn(jnp.concatenate(xs, axis=1), value)
        return [total[s * ds : (s + 1) * ds] for s in pieces]

    def t_right(value, xs):
        if not wide:
            return [tn(value, x) for x in xs]
        total = tn(value, jnp.concatenate(xs, axis=1))
        return [total[:, s * ds : (s + 1) * ds] for s in pieces]

    def sort_rows(m, sel_ref, x_refs, xs, ids):
        for r in range(4):
            src, here_r = at_row(m, 2 + r, blk), slice(r * blk, (r + 1) * blk)
            for s in pieces:
                xs[s, here_r, :] = x_refs[s][src, :]
            ids[here_r, :] = sel_ref[src, :]

    def dwin_body(m, *refs):
        a_refs, b_refs = refs[:4], refs[4:8]
        sel_ref, x_ref = refs[8:10]
        outs = refs[10 : 10 + parts]
        xs, ids, mt = refs[10 + parts :]
        e = pl.program_id(0)

        @pl.when(e == 0)
        def _():
            sort_rows(m, sel_ref, [x_ref.at[s] for s in pieces], xs, ids)

        expert = e.astype(F32)
        for r in range(4):
            here_r = slice(r * blk, (r + 1) * blk)
            mt[here_r, :] = pick(
                ids[here_r, 2:3], ids[here_r, 3:4], expert, a_refs[r][0], b_refs[r][0]
            )
        for s, value in enumerate(t_left([xs[s] for s in pieces], mt[...])):
            outs[s][0] = value.astype(BF16)

    def dwin(j, meta):
        ins = [(v, (1, blk, ff), lambda e, m: (j, 0, 0)) for v in gg_a + gg_b]
        ins += [(sel, None, None), (ffn_input, None, None)]
        outs = [((experts, ds, ff), BF16, (1, ds, ff), lambda e, m: (e, 0, 0))] * parts
        return run(
            dwin_body, "dwin", (experts,), meta, ins, outs,
            [pltpu.VMEM((parts, rp, ds), BF16), pltpu.VMEM((rp, 8), F32), pltpu.VMEM((rp, ff), BF16)],
            flops=2 * rp * experts * parts * ds * ff,
        )

    def fold_body(m, *refs):
        out_ref = refs[2 * parts]
        for j in range(2):
            total = refs[j * parts][0].astype(F32)
            for ref in refs[j * parts + 1 : (j + 1) * parts]:
                total = total + ref[0].astype(F32)
            out_ref[0, :, j, :] = total

    def fold(sums, meta):
        ins = [(v, (1, ds, ff), lambda e, m: (e, 0, 0)) for half in sums for v in half]
        outs = [((experts, ds, 2, ff), F32, (1, ds, 2, ff), lambda e, m: (e, 0, 0, 0))]
        return run(fold_body, "fold", (experts,), meta, ins, outs)[0]

    dwin_gate = dwin(0, after(meta, far_half))
    dx_totals = z_last(near_half) + z_last(z_covered(far_half, far_half, 3, dwin_gate[0]))

    def norm_back_body(low_precision_out, m, *refs):
        sums = 4 if low_precision_out else 2
        t_refs, after_ref, refs = refs[:sums], refs[sums], refs[sums + 1 :]
        ups = parts if low_precision_out else 1
        up_refs = refs[:ups]
        gain_ref, router_ref, back = refs[ups : 3 + ups]
        outs = refs[3 + ups :]
        small = outs[-1]
        for s in pieces:
            gain = gain_ref[s]
            router = router_ref[s].astype(F32)
            gain_sum = jnp.zeros((1, ds), F32)
            router_sum = [jnp.zeros((1, ds), F32)] * experts
            for r in range(4):
                span_r = at_row(m, (BY_CHUNK if low_precision_out else IN_HALVES) + r, blk)
                up_value = up_refs[s][span_r, :] if low_precision_out else up_refs[0][s, span_r, :]
                x = after_ref[s, span_r, :].astype(F32)
                cols = back[span_r, :]
                rms = cols[:, experts + 1 : experts + 2]
                if low_precision_out:
                    grad = t_refs[r][s].astype(F32)
                else:
                    grad = t_refs[r // 2][s, (r % 2) * blk : (r % 2 + 1) * blk, :].astype(F32)
                for e in range(experts):
                    grad += cols[:, e : e + 1] * router[e : e + 1]
                normed = x * rms
                token = (normed * gain).astype(BF16).astype(F32)
                gain_sum += jnp.sum(grad * normed, axis=0, keepdims=True)
                for e in range(experts):
                    router_sum[e] = router_sum[e] + jnp.sum(
                        token * cols[:, e : e + 1], axis=0, keepdims=True
                    )
                dn = grad * gain
                total = up_value.astype(F32) + rms * (
                    dn - normed * cols[:, experts : experts + 1]
                )
                if low_precision_out:
                    outs[0][s, span_r, :] = total
                    outs[1][s, span_r, :] = total.astype(BF16)
                else:
                    outs[s][span_r, :] = total.astype(BF16)
            for e in range(experts):
                small[e, s] = router_sum[e][0]
            small[experts, s] = gain_sum[0]

    ins = [(t, None, None) for t in dx_totals]
    ins += [(after_rows, None, None)] + [(d, None, None) for d in d_pieces]
    ins += [(gain_f, None, None), (router_f, None, None), (back_f, None, None)]
    outs = [
        ((parts, rp, ds), F32, None, None),
        ((parts, rp, ds), BF16, None, None),
        ((experts + 1, parts, ds), F32, None, None),
    ]
    dafter, dafter_low, small_f = run(
        functools.partial(norm_back_body, True), "norm_back", (1,),
        after(meta, dwin_gate[0], ag_a[1:], ag_b[1:]), ins, outs,
    )

    def dmix_body(m, *refs):
        d_ref = refs[0]
        w_refs = refs[1 : 1 + parts]
        sel_ref = refs[1 + parts]
        outs = refs[2 + parts : 10 + parts]
        scr = refs[10 + parts]
        products = []
        for e in range(experts):
            products.append(sum(nt(d_ref[s], w_refs[s][e]) for s in pieces))
        low, high = two_slots(sel_ref[:, 0:1], sel_ref[:, 1:2], products)
        for k, value in enumerate((low, high)):
            value = value.astype(BF16)
            for h in range(heads):
                scr[h, :, k * HD : (k + 1) * HD] = value[:, h * HD : (h + 1) * HD]
        for r in range(4):
            block = scr[m[2 + r]]
            outs[2 * r][...] = block[:, :HD]
            outs[2 * r + 1][...] = block[:, HD:]

    ins = [(dafter_low, (parts, tile, ds), lambda i, m: (0, i, 0))]
    ins += [(w, None, None) for w in wp]
    ins += [(sel, (tile, 8), lambda i, m: (i, 0))]
    outs = [((rp, HD), BF16, (tile, HD), lambda i, m: (i, 0))] * 8
    dm = run(
        dmix_body, "dmix", (rp // tile,), meta, ins, outs,
        [pltpu.VMEM((heads, tile, 2 * HD), BF16)],
        flops=2 * rp * experts * parts * ds * hw,
    )
    dwin_up = dwin(1, after(meta, dm[0]))
    dm_a, dm_b, _, _ = reduce_groups(dm[0:8:2], dm[1:8:2], late=dwin_up[0])
    along = held((ag_a[1], ag_b[2]), dm_a[2], dm_b[1])
    ag_a, ag_b = ag_a + [by_group(along[0], 2)], ag_b + [by_group(along[1], 1)]

    def attend_back_body(m, *refs):
        q_ref, kv_ref, halo_ref, sel_ref, cols, cos_ref, sin_ref = refs[:7]
        d_refs = (refs[7:10], refs[10:13])
        mix_refs = refs[13:15]
        dq_ref, own_ref, far_ref, dots_ref, ext, acc = refs[15:]
        i = pl.program_id(0)

        @pl.when(i == 0)
        def _():
            ext[:seq_len, :] = halo_ref[...]
            ext[seq_len:, :] = kv_ref[...]
            acc[...] = jnp.zeros_like(acc)

        near_rows = pl.ds(pl.multiple_of(i * qt, qt), span)
        near = ext[near_rows, :]
        allowed = window_mask(i, sel_ref[:, 4:5])
        line = lax.broadcasted_iota(jnp.int32, (8, qt), 0)
        inner = jnp.zeros((qt, HD), F32)
        found = []
        dk = jnp.zeros((span, HD), F32)
        dv = jnp.zeros((span, HD), F32)
        for k in range(2):
            query = q_ref[:, k * HD : (k + 1) * HD]
            probs = softmax_of(query, near[:, :HD], allowed)
            raw = sum(v[...].astype(F32) for v in d_refs[k])
            dmixed = (raw * cols[:, 1 + k : 2 + k]).astype(BF16)
            found.append(raw * mix_refs[k][...].astype(F32))
            dv += tn(probs.astype(BF16), dmixed)
            dprob = nt(dmixed, near[:, HD:])
            rest = jnp.sum(probs * dprob, axis=1, keepdims=True)
            dscore = (probs * (dprob - rest)).astype(BF16)
            dk += tn(dscore, query) * scale
            dquery = nn(dscore, near[:, :HD]) * scale
            inner += dquery * query.astype(F32)
            dq_ref[:, k * HD : (k + 1) * HD] = turn(dquery, cos_ref[...], -sin_ref[...]).astype(BF16)
        acc[near_rows, :HD] += dk
        acc[near_rows, HD:] += dv
        dots_ref[...] = jnp.where(
            line == 0, lane_sums(found[0]), jnp.where(line == 1, lane_sums(found[1]), lane_sums(inner))
        )

        @pl.when(i == rp // qt - 1)
        def _():
            far_ref[...] = acc[:seq_len, :]
            own_ref[...] = acc[seq_len:, :]

    ins = [(q_rot, (qt, 2 * HD), qrow), (kv_rot, None, None), (halo, None, None)]
    ins += [(sel, (qt, 8), qrow), (cols_a, (qt, 8), qrow)]
    ins += [(cosine, (qt, HD), qrow), (sine, (qt, HD), qrow)]
    ins += [(v, (qt, HD), qrow) for v in dm_a + dm_b + (mixed_a, mixed_b)]
    outs = [
        ((rp, 2 * HD), BF16, (qt, 2 * HD), qrow),
        ((rp, 2 * HD), F32, None, None),
        ((seq_len, 2 * HD), F32, None, None),
        ((8, rp), F32, (8, qt), lambda i, m: (0, i)),
    ]
    dq, dkv_own, dkv_far, dots_q = run(
        attend_back_body, "attend_back", (rp // qt,), meta, ins, outs,
        [pltpu.VMEM((seq_len + rp, 2 * HD), BF16), pltpu.VMEM((seq_len + rp, 2 * HD), F32)],
        flops=20 * rp * span * HD,
    )
    dkv_in = to_previous(dkv_far)

    def dkv_body(m, own_ref, in_ref, kv_ref, cos_ref, sin_ref, out_ref, dots_ref):
        head = rp - seq_len
        for rows_here in (slice(0, head), slice(head, rp)):
            value = own_ref[rows_here, :]
            if rows_here.start == head:
                value = value + in_ref[...]
            out_ref[rows_here, :HD] = turn(
                value[:, :HD], cos_ref[rows_here, :], -sin_ref[rows_here, :]
            ).astype(BF16)
            out_ref[rows_here, HD:] = value[:, HD:].astype(BF16)
            dots_ref[:, rows_here] = lane_sums(value * kv_ref[rows_here, :].astype(F32))

    ins = [(v, None, None) for v in (dkv_own, dkv_in, kv_rot, cosine, sine)]
    outs = [((rp, 2 * HD), BF16, None, None), ((8, rp), F32, None, None)]
    got_in = [exchange(dwin_gate), exchange(held(dwin_up, dm_a[2], dm_b[1]))]
    dkv, dots_kv = run(
        dkv_body, "dkv", (1,), after(meta, ag_a[3], ag_b[3]), ins, outs
    )
    third = jnp.arange(8)[:, None] == 2
    def down_body(m, *refs):
        a_refs, b_refs = refs[:4], refs[4:8]
        sel_ref, d_refs = refs[8], refs[9 : 9 + parts]
        w_refs = refs[9 + parts : 9 + 2 * parts]
        keep_ref, send_ref = refs[9 + 2 * parts : 11 + 2 * parts]
        outs = refs[11 + 2 * parts : 11 + 3 * parts]
        acc, xs, ids, mt = refs[11 + 3 * parts :]
        e = pl.program_id(0)

        @pl.when(e == 0)
        def _():
            acc[...] = jnp.zeros_like(acc)
            sort_rows(m, sel_ref, d_refs, xs, ids)

        expert = e.astype(F32)
        for r in range(4):
            here_r = slice(r * blk, (r + 1) * blk)
            mt[here_r, :] = pick(
                ids[here_r, 2:3], ids[here_r, 3:4], expert, a_refs[r][...], b_refs[r][...]
            )
        for s, value in enumerate(nn_pieces(mt[...], [w[0] for w in w_refs])):
            acc[s] += value
        for s, value in enumerate(t_right(mt[...], [xs[s] for s in pieces])):
            outs[s][0] = value.astype(BF16)

        @pl.when(e == experts - 1)
        def _():
            keep_ref[...] = acc[:, at_row(m, 6, 2 * blk), :].astype(BF16)
            send_ref[...] = acc[:, at_row(m, 7, 2 * blk), :].astype(BF16)

    def down(meta):
        spot = lambda e, m: (e, 0, 0)
        ins = [(v, None, None) for v in ag_a + ag_b]
        ins += [(sel, None, None)] + [(d, None, None) for d in d_pieces]
        ins += [(w, (1, ff, ds), spot) for w in wo]
        outs = [((parts, 2 * blk, ds), BF16, None, None)] * 2
        outs += [((experts, ff, ds), BF16, (1, ff, ds), spot)] * parts
        return run(
            down_body, "down", (experts,), meta, ins, outs,
            [
                pltpu.VMEM((parts, rp, ds), F32),
                pltpu.VMEM((parts, rp, ds), BF16),
                pltpu.VMEM((rp, 8), F32),
                pltpu.VMEM((rp, ff), BF16),
            ],
            flops=4 * rp * experts * parts * ds * ff,
        )

    def dwproj_body(m, *refs):
        a_refs, b_refs = refs[:4], refs[4:8]
        sel_ref, d_ref = refs[8:10]
        outs = refs[10 : 10 + parts]
        lo, hi = refs[10 + parts :]
        e = pl.program_id(0)

        @pl.when(e == 0)
        def _():
            for r in range(4):
                lanes = pl.ds(pl.multiple_of(m[2 + r] * HD, HD), HD)
                lo[:, lanes] = a_refs[r][...]
                hi[:, lanes] = b_refs[r][...]

        x = pick(sel_ref[:, 0:1], sel_ref[:, 1:2], e.astype(F32), lo[...], hi[...])
        for s, value in enumerate(t_right(x, [d_ref[s] for s in pieces])):
            outs[s][0] = value.astype(BF16)

    def dwproj(meta):
        ins = [(v, None, None) for v in gm_a + gm_b]
        ins += [(sel, None, None), (dafter_low, None, None)]
        return run(
            dwproj_body, "dwproj", (experts,), meta, ins,
            [((experts, hw, ds), BF16, (1, hw, ds), lambda e, m: (e, 0, 0))] * parts,
            [pltpu.VMEM((rp, hw), BF16)] * 2,
            flops=2 * rp * experts * hw * parts * ds,
        )

    down_halves = down(after(meta, dkv))
    down_halves, dwout_sums = down_halves[:2], down_halves[2:]
    da_a, da_b, da_along = gather_groups(dq, dkv, late=(dwout_sums[0],))
    dwproj_sums = dwproj(after(meta, da_along, got_in))
    def place_heads(m, refs, lo, hi):
        for r in range(4):
            lanes = pl.ds(pl.multiple_of(m[2 + r] * HD, HD), HD)
            lo[:, lanes] = refs[r][:, :HD]
            hi[:, lanes] = refs[r][:, HD:]

    def dattn_body(m, *refs):
        a_refs, b_refs = refs[:4], refs[4:8]
        sel_ref = refs[8]
        q_refs = refs[9 : 9 + parts]
        kv_refs = refs[9 + parts : 9 + 2 * parts]
        outs = refs[9 + 2 * parts : 11 + 2 * parts]
        lo, hi, dk, dv = refs[11 + 2 * parts :]
        place_heads(m, a_refs, lo, hi)
        place_heads(m, b_refs, dk, dv)
        acc = nt_pieces(dk[...], [w[0] for w in kv_refs])
        for s, value in enumerate(nt_pieces(dv[...], [w[1] for w in kv_refs])):
            acc[s] += value
        for e in range(experts):
            x = pick(sel_ref[:, 0:1], sel_ref[:, 1:2], e, lo[...], hi[...])
            for s, value in enumerate(nt_pieces(x, [w[e] for w in q_refs])):
                acc[s] += value
        for s in pieces:
            store_halves(pl.program_id(0), outs, s, acc[s].astype(BF16))

    def dattn(meta):
        half = lambda i, m: (m[7 - i], 0)
        ins = [(v, (zr, 2 * HD), half) for v in da_a + da_b]
        ins += [(sel, (zr, 8), half)]
        ins += [(w, None, None) for w in wq + wkv]
        return run(
            dattn_body, "dattn", (2,), meta, ins, [((parts, zr, ds), BF16, None, None)] * 2,
            [pltpu.VMEM((zr, hw), BF16)] * 4,
            flops=4 * zr * (experts + 2) * hw * parts * ds,
        )

    dots_a = dots_q + jnp.where(third, dots_kv, 0.0)
    dots_a = sum_groups(after(dots_a, dwproj_sums[0]))
    got_out = exchange(dwout_sums)
    da_halves = dattn(after(meta, dwproj_sums[0]))
    got_proj = exchange(dwproj_sums)
    x_stack = jnp.stack(x_pieces)
    attn_input = (x_stack.astype(F32) * flat_a[0][None, :, None] * gain_a).astype(BF16)

    def dwqkv_body(m, *refs):
        a_refs, b_refs = refs[:4], refs[4:8]
        sel_ref, x_ref = refs[8:10]
        q_outs, kv_outs = refs[10 : 10 + parts], refs[10 + parts : 10 + 2 * parts]
        lo, hi, dk, dv = refs[10 + 2 * parts :]
        e = pl.program_id(0)
        xs = [x_ref.at[s] for s in pieces]

        @pl.when(e == 0)
        def _():
            place_heads(m, a_refs, lo, hi)
            place_heads(m, b_refs, dk, dv)

        @pl.when(e < experts)
        def _():
            x = pick(sel_ref[:, 0:1], sel_ref[:, 1:2], e.astype(F32), lo[...], hi[...])
            for s, value in enumerate(t_left([v[...] for v in xs], x)):
                q_outs[s][0] = value.astype(BF16)

        for k, grad in enumerate((dk, dv)):

            @pl.when(e == experts + k)
            def _():
                for s, value in enumerate(t_left([v[...] for v in xs], grad[...])):
                    kv_outs[s][0] = value.astype(BF16)

    def dwqkv(meta):
        q_spot = lambda e, m: (jnp.minimum(e, experts - 1), 0, 0)
        kv_spot = lambda e, m: (jnp.maximum(e - experts, 0), 0, 0)
        ins = [(v, None, None) for v in da_a + da_b]
        ins += [(sel, None, None), (attn_input, None, None)]
        outs = [((experts, ds, hw), BF16, (1, ds, hw), q_spot)] * parts
        outs += [((2, ds, hw), BF16, (1, ds, hw), kv_spot)] * parts
        return run(
            dwqkv_body, "dwqkv", (experts + 2,), meta, ins, outs,
            [pltpu.VMEM((rp, hw), BF16)] * 4,
            flops=2 * rp * (experts + 2) * hw * parts * ds,
        )

    dwqkv_sums = dwqkv(after(meta, da_halves[0]))


    da_half = z_covered(*da_halves, 1, dwqkv_sums[0])

    down_half = z_covered(*down_halves, 1, dwproj_sums[0])

    def finish_body(m, *refs):
        t_refs, after_ref, outs = refs[:2], refs[2], refs[3:]
        for k in range(4):
            span_k = at_row(m, BY_HALF + k, blk)
            for s in pieces:
                total = t_refs[k // 2][s, (k % 2) * blk : (k % 2 + 1) * blk, :]
                outs[s][span_k, :] = (
                    after_ref[s, span_k, :] + total.astype(F32)
                ).astype(BF16)

    got_q, got_kv = exchange(dwqkv_sums[:parts]), exchange(dwqkv_sums[parts:])
    dots_a = sum_z(dots_a)
    back_a = back_columns(flat_a, dots_a, low_a, high_a)
    down_totals = z_last(z_covered(down_half, down_half, 3, da_half))
    ins = [(t, None, None) for t in down_totals] + [(after_rows, None, None)]
    out_rows = run(
        finish_body, "finish", (1,), after(meta, dots_a), ins,
        [((rp, ds), BF16, None, None)] * parts,
    )

    count = rows_all // dp

    def unpack_body(dealt, m, other_ref, *refs):
        v_refs, out_ref = refs[:parts], refs[-5]
        packed, other, total, whole = refs[-4:]
        for s in pieces:
            packed[part_rows(m, s), :] = v_refs[s][...].astype(F32)
        other[...] = other_ref[...].astype(F32)
        line = lax.broadcasted_iota(jnp.int32, (per, ds), 0)

        def one(j, carry):
            window, shift = near_rows(m, j)
            back = jnp.where(shift == 0, 0, seq_len + 8 - shift)
            whole[...] = pltpu.roll(packed[window, :], back, 0)
            for p in range(dp):
                if dealt:
                    spot = m[2 * seqs + j] * seq_len + p * per
                    kept = other[pl.ds(pl.multiple_of(spot, per), per), :]
                else:
                    kept = other[block_rows(p, j), :]
                value = whole[p * per : (p + 1) * per, :]
                total[block_rows(p, j), :] = jnp.where(line < m[seqs + j] - p * per, value, kept)
            return carry

        lax.fori_loop(0, seqs, one, 0)
        for p in range(dp):
            out_ref[p, :count, :] = total[p * count : (p + 1) * count, :].astype(BF16)
            for ref in refs[parts:-5]:
                out_ref[p, count:, :] = ref[...]

    def unpack(value, otherwise, dealt, table, extra=()):
        mine_all = [value[0]] + [by_part(value[s], s) for s in pieces[1:]]
        ins = [(v, None, None) for v in [otherwise] + mine_all + list(extra)]
        tall = count + sum(v.shape[0] for v in extra)
        spread_rows = run(
            functools.partial(unpack_body, dealt), "unpack", (1,), table, ins,
            [((dp, tall, ds), BF16, None, None)],
            [
                pltpu.VMEM((n, ds), F32)
                for n in (rows + seq_len + 8, rows_all, rows_all, seq_len + 8)
            ],
        )[0]
        landed = lax.all_to_all(spread_rows, "dp", 0, 0, tiled=True)
        rows_of = landed[:, :count].transpose(1, 0, 2).reshape(seqs, per, width)
        return rows_of, spread_rows, landed[:, count:]

    da_half = z_covered(da_half, da_half, 3, out_rows[0])
    expertin_grad = fold(got_in, after(meta, da_half))
    layer_out, layer_rows, _ = unpack(out_rows, x_all, False, table)
    da_totals = z_last(da_half)
    ins = [(t, None, None) for t in da_totals]
    ins += [(x_stack, None, None), (dafter, None, None)]
    ins += [(gain_a, None, None), (router_a, None, None), (back_a, None, None)]
    outs = [((rp, ds), BF16, None, None)] * parts
    outs += [((experts + 1, parts, ds), F32, None, None)]
    *dinput, small_a = run(
        functools.partial(norm_back_body, False), "norm_back_first", (1,),
        after(meta, expertin_grad), ins, outs,
    )
    expertout_grad, proj_grad = add_up(got_out), add_up(got_proj)
    query_grad, kv_grad = add_up(got_q), add_up(got_kv)
    vectors = 2 * (experts + 1)
    small = jnp.concatenate([small_a, small_f], axis=0).reshape(vectors * parts, ds)
    small = jnp.pad(small, ((0, -vectors * parts % 16), (0, 0))).astype(BF16)
    input_grad, _, got = unpack(dinput, d_all, True, after(table, layer_out), [small])
    got = got[:, : vectors * parts].astype(F32).reshape(groups, parts, vectors, parts, ds)
    full = jnp.stack(
        [sum(got[:, k ^ s, :, s] for s in pieces) for k in range(parts)], axis=2
    )
    full = full.transpose(1, 0, 2, 3).reshape(2, experts + 1, width)
    attnrouter_grad, attngain_grad = full[0, :experts].T, full[0, experts]
    ffnrouter_grad, ffngain_grad = full[1, :experts].T, full[1, experts]
    return (
        layer_out,
        input_grad,
        attngain_grad,
        attnrouter_grad,
        kv_grad,
        query_grad,
        proj_grad,
        ffngain_grad,
        ffnrouter_grad,
        expertin_grad,
        expertout_grad,
    )


def solution(mesh):
    placed = (
        P(None, "dp", None),
        P("dp", None, None),
        P(),
        P(),
        P(),
        P(),
        P(),
        P(),
        P(None, "dp", "tensor"),
        P(None, "dp", "tensor"),
        P(None, "tensor", "dp"),
        P(),
        P(),
        P(None, "dp", None, "tensor"),
        P(None, "tensor", "dp"),
    )
    return jax.shard_map(
        functools.partial(local, dp=mesh.shape["dp"], tp=mesh.shape["tensor"]),
        mesh=mesh,
        in_specs=placed,
        out_specs=(
            P(None, "dp", None),
            P(None, "dp", None),
            P(),
            P(),
            P(None, "dp", "tensor"),
            P(None, "dp", "tensor"),
            P(None, "tensor", "dp"),
            P(),
            P(),
            P(None, "dp", None, "tensor"),
            P(None, "tensor", "dp"),
        ),
        check_vma=False,
    )
```

```python
import functools

import jax
import jax.numpy as jnp
from jax import lax
from jax.experimental import pallas as pl
from jax.experimental.pallas import tpu as pltpu
from jax.sharding import PartitionSpec as P

HD = 128
EPSILON = 1e-06
ROPE_BASE = 10000.0
BEST = lax.Precision.HIGHEST
F32 = jnp.float32
BF16 = jnp.bfloat16
VMEM_BYTES = 60 * 1024 * 1024


def nn(a, b):
    return lax.dot_general(a, b, (((1,), (0,)), ((), ())), preferred_element_type=F32)


def nt(a, b, precision=None):
    return lax.dot_general(
        a, b, (((1,), (1,)), ((), ())), preferred_element_type=F32, precision=precision
    )


def tn(a, b):
    return lax.dot_general(a, b, (((0,), (0,)), ((), ())), preferred_element_type=F32)


def lane_sums(values):
    ones = jnp.ones((8, values.shape[1]), F32)
    return nt(ones, values, BEST)


def run(body, name, grid, meta, ins, outs, scratch=(), flops=0):
    in_specs = []
    moved = 0
    for array, block, index in ins:
        if block is None:
            rank = array.ndim
            in_specs.append(pl.BlockSpec(array.shape, lambda *a, rank=rank: (0,) * rank))
        else:
            in_specs.append(pl.BlockSpec(block, index))
        moved += array.size * array.dtype.itemsize
    out_specs = []
    out_shape = []
    for shape, dtype, block, index in outs:
        if block is None:
            rank = len(shape)
            out_specs.append(pl.BlockSpec(shape, lambda *a, rank=rank: (0,) * rank))
        else:
            out_specs.append(pl.BlockSpec(block, index))
        out_shape.append(jax.ShapeDtypeStruct(shape, dtype))
        size = jnp.dtype(dtype).itemsize
        for extent in shape:
            size *= extent
        moved += size
    return pl.pallas_call(
        body,
        name=name,
        grid_spec=pltpu.PrefetchScalarGridSpec(
            num_scalar_prefetch=1,
            grid=grid,
            in_specs=in_specs,
            out_specs=out_specs,
            scratch_shapes=list(scratch),
        ),
        out_shape=out_shape,
        compiler_params=pltpu.CompilerParams(
            dimension_semantics=("arbitrary",) * len(grid), vmem_limit_bytes=VMEM_BYTES
        ),
        cost_estimate=pl.CostEstimate(flops=flops, bytes_accessed=moved, transcendentals=0),
    )(meta, *[array for array, _, _ in ins])


def pick(low_id, high_id, expert, low_value, high_value):
    zero = jnp.zeros_like(low_value)
    return jnp.where(
        low_id == expert, low_value, jnp.where(high_id == expert, high_value, zero)
    )


def two_slots(low_id, high_id, products):
    low_value = products[0]
    for expert in range(1, len(products) - 1):
        low_value = jnp.where(low_id == expert, products[expert], low_value)
    high_value = products[1]
    for expert in range(2, len(products)):
        high_value = jnp.where(high_id == expert, products[expert], high_value)
    return low_value, high_value


def turn(values, cosine, sine):
    return values * cosine + pltpu.roll(values, HD // 2, 1) * sine


def local(
    hidden_in,
    cotangent,
    lengths,
    dealing,
    attn_routes,
    ffn_routes,
    attn_gain,
    attn_router,
    kv_weight,
    query_weight,
    proj_weight,
    ffn_gain,
    ffn_router,
    expert_in,
    expert_out,
    *,
    dp,
    tp,
):
    seqs = dealing.shape[0]
    seq_len = cotangent.shape[1]
    slots = cotangent.shape[0]
    per = hidden_in.shape[1]
    width = hidden_in.shape[2]
    heads = query_weight.shape[2] // HD
    groups = heads
    parts = dp // groups
    ds = width // dp
    hw = heads * HD
    rows_all = seqs * seq_len
    rows = rows_all * 3 // 4
    rp = rows // parts
    blk = rp // groups
    experts = query_weight.shape[0]
    ff = expert_out.shape[1]
    scale = HD ** (-0.5)
    pieces = range(parts)

    index = lax.axis_index("dp")
    z = lax.axis_index("tensor")
    g = index // parts
    c = index % parts
    mine = ((z == 1) | (z == 2)).astype(jnp.int32)
    theirs = 1 - mine
    spots = [g, c, g, g ^ 1, g ^ 2, g ^ 3, mine, theirs]
    spots += [g ^ mine, g ^ theirs, g ^ (2 + mine), g ^ (2 + theirs)]
    spots += [g ^ (2 * mine), g ^ (2 * mine + 1), g ^ (2 * theirs), g ^ (2 * theirs + 1)]
    spots += [mine, theirs, 2 + mine, 2 + theirs]
    spots += [2 * mine, 2 * mine + 1, 2 * theirs, 2 * theirs + 1]
    meta = jnp.stack(spots).astype(jnp.int32)
    BY_CHUNK, BY_HALF, IN_ORDER, IN_HALVES = 8, 12, 16, 20

    def after(value, *others):
        return lax.optimization_barrier((value,) + others)[0]

    def both(a, b):
        return (a.astype(F32) + b.astype(F32)).astype(BF16)

    def by_group(value, mask):
        pairs = [(a, ((a // parts) ^ mask) * parts + a % parts) for a in range(dp)]
        return lax.ppermute(value, "dp", pairs)

    def by_part(value, mask):
        pairs = [(a, (a // parts) * parts + ((a % parts) ^ mask)) for a in range(dp)]
        return lax.ppermute(value, "dp", pairs)

    def to_next(value):
        pairs = [(a, a + 1) for a in range(dp) if a % parts < parts - 1]
        return lax.ppermute(value, "dp", pairs)

    def to_previous(value):
        pairs = [(a, a - 1) for a in range(dp) if a % parts > 0]
        return lax.ppermute(value, "dp", pairs)

    def by_z(value, mask):
        return lax.ppermute(value, "tensor", [(a, a ^ mask) for a in range(tp)])

    def sum_groups(value):
        value = value + by_group(value, 1)
        return value + by_group(value, 2)

    def sum_z(value):
        value = value + by_z(value, 1)
        return value + by_z(value, 3)

    def z_first(keep, send):
        return both(keep, by_z(send, 1))

    def z_second(half):
        return both(half, by_z(half, 3))

    def z_covered(keep, send, mask, cover):
        keep, got = held((keep, by_z(send, mask)), cover)
        return both(keep, got)

    def z_last(half):
        return half, by_z(half, 1)

    def wide_sum_z(keep, send):
        return z_last(z_second(z_first(keep, send)))

    def held(values, *others):
        return lax.optimization_barrier((tuple(values),) + others)[0]

    def reduce_groups(first, second, early=(), late=()):
        if early:
            first, second = held((tuple(first), tuple(second)), early)
        ra = by_group(first[3], 1)
        rb = by_group(second[3], 2)
        ax = by_group(first[1], 1)
        by = by_group(second[2], 2)
        along = held((both(first[2], ra), both(second[1], rb)), (ax, by), late)
        ay = by_group(along[0], 2)
        bx = by_group(along[1], 1)
        return (first[0], ax, ay), (second[0], bx, by), along, (ra, rb)

    def gather_groups(first, second, late=()):
        ax, bx = by_group(first, 1), by_group(second, 1)
        ay, by = by_group(first, 2), by_group(second, 2)
        along = held((ax, by), (bx, ay), late) if len(late) else (ax, by)
        ad, bd = by_group(along[0], 2), by_group(along[1], 1)
        return (first, ax, ay, ad), (second, bx, by, bd), along

    def row_of(offset):
        return lambda *a: (a[-1][2 + offset], 0)

    def at_row(m, spot, count):
        return pl.ds(pl.multiple_of(m[spot] * count, count), count)

    wide = ds % 128 == 0

    def nn_pieces(x, weights):
        if not wide:
            return [nn(x, w) for w in weights]
        value = nn(x, jnp.concatenate(weights, axis=1))
        return [value[:, s * ds : (s + 1) * ds] for s in pieces]

    def nt_pieces(x, weights):
        if not wide:
            return [nt(x, w) for w in weights]
        value = nt(x, jnp.concatenate(weights, axis=0))
        return [value[:, s * ds : (s + 1) * ds] for s in pieces]

    ends = jnp.cumsum(lengths)
    starts = ends - lengths
    inverse = jnp.sum(
        (dealing[None, :] == jnp.arange(seqs, dtype=jnp.int32)[:, None])
        * jnp.arange(seqs, dtype=jnp.int32)[None, :],
        axis=1,
    )

    table = jnp.concatenate([starts, lengths, inverse, c[None]]).astype(jnp.int32)

    def places(part):
        packed = part * rp + jnp.arange(rp, dtype=jnp.int32)
        begun = starts[None, :] <= packed[:, None]
        first = jnp.max(jnp.where(begun, starts[None, :], 0), axis=1)
        seq = jnp.sum(begun.astype(jnp.int32), axis=1) - 1
        return seq, packed - first, first

    seq, at, first = places(c)

    def slot_rows(m, j):
        return pl.ds(pl.multiple_of(m[2 * seqs + j] * seq_len, seq_len), seq_len)

    def part_rows(m, s):
        return pl.ds(pl.multiple_of((m[3 * seqs] ^ s) * rp, rp), rp)

    def block_rows(p, j):
        return pl.ds(pl.multiple_of((p * seqs + j) * per, per), per)

    def near_rows(m, j):
        shift = m[j] & 7
        return pl.ds(pl.multiple_of(m[j] - shift, 8), seq_len + 8), shift

    def pack_body(dealt, m, all_ref, *refs):
        outs = refs[:parts]
        source, packed, whole = refs[parts:]
        source[...] = all_ref[...].astype(F32)

        line = lax.broadcasted_iota(jnp.int32, (seq_len + 8, ds), 0)

        def one(j, carry):
            if dealt:
                whole[:seq_len, :] = source[slot_rows(m, j), :]
            else:
                for p in range(dp):
                    whole[p * per : (p + 1) * per, :] = source[block_rows(p, j), :]
            window, shift = near_rows(m, j)
            moved = pltpu.roll(whole[...], shift, 0)
            packed[window, :] = jnp.where(line < shift, packed[window, :], moved)
            return carry

        lax.fori_loop(0, seqs, one, 0)
        for s in pieces:
            outs[s][...] = packed[part_rows(m, s), :].astype(BF16)

    def pack(value, dealt, table):
        own = run(
            functools.partial(pack_body, dealt), "pack", (1,), table, [(value, None, None)],
            [((rp, ds), BF16, None, None)] * parts,
            [pltpu.VMEM((n, ds), F32) for n in (rows_all, rows + seq_len + 8, seq_len + 8)],
        )
        return [own[0]] + [by_part(own[s], s) for s in pieces[1:]]

    x_send = hidden_in.reshape(seqs * per, dp, ds).transpose(1, 0, 2)
    d_send = cotangent.reshape(slots * seq_len, dp, ds).transpose(1, 0, 2)
    x_all = lax.all_to_all(x_send, "dp", 0, 0, tiled=True).reshape(rows_all, ds)
    x_pieces = pack(x_all, False, table)
    def spread(vector):
        tall = vector.reshape((groups, parts, ds) + vector.shape[1:])[g]
        return jnp.stack([tall[c ^ s] for s in pieces])

    gain_a = spread(attn_gain)[:, None, :]
    gain_f = spread(ffn_gain)[:, None, :]
    pad = ((0, 0), (0, 8 - experts), (0, 0))
    router_a = jnp.pad(spread(attn_router).transpose(0, 2, 1), pad)
    router_f = jnp.pad(spread(ffn_router).transpose(0, 2, 1), pad)

    in_own = after(expert_in, x_send).swapaxes(1, 2)
    wq = [query_weight] + [by_part(query_weight, s) for s in pieces[1:]]
    wkv = [kv_weight] + [by_part(kv_weight, s) for s in pieces[1:]]
    wp = [proj_weight] + [by_part(proj_weight, s) for s in pieces[1:]]
    wo = [expert_out] + [by_part(expert_out, s) for s in pieces[1:]]
    wi = [in_own] + [by_part(in_own, s) for s in pieces[1:]]

    routes = jnp.concatenate(
        [attn_routes.reshape(rows_all, 2), ffn_routes.reshape(rows_all, 2)], axis=1
    )
    here = (seq * seq_len + at)[:, None] == jnp.arange(rows_all, dtype=jnp.int32)[None, :]
    mine = jnp.dot(here.astype(BF16), routes.astype(BF16), preferred_element_type=F32)
    low_a, high_a = jnp.minimum(mine[:, 0], mine[:, 1]), jnp.maximum(mine[:, 0], mine[:, 1])
    low_f, high_f = jnp.minimum(mine[:, 2], mine[:, 3]), jnp.maximum(mine[:, 2], mine[:, 3])
    window = (first - c * rp + seq_len).astype(F32)
    nil = jnp.zeros_like(window)
    sel = jnp.stack([low_a, high_a, low_f, high_f, window, nil, nil, nil], axis=1)
    half = HD // 2
    frequency = ROPE_BASE ** (-2.0 * jnp.arange(half, dtype=F32) / HD)
    angles = at.astype(F32)[:, None] * frequency[None, :]
    cosine = jnp.concatenate([jnp.cos(angles)] * 2, axis=1)
    sine = jnp.sin(angles)
    sine = jnp.concatenate([-sine, sine], axis=1)

    def gate_columns(stats, low_id, high_id):
        rms = lax.rsqrt(stats[experts] / width + EPSILON)
        ids = jnp.arange(experts, dtype=F32)[:, None]
        logits = stats[:experts]
        low_logit = jnp.sum(jnp.where(low_id[None] == ids, logits, 0.0), axis=0) * rms
        high_logit = jnp.sum(jnp.where(high_id[None] == ids, logits, 0.0), axis=0) * rms
        gap = low_logit - high_logit
        low_gate, high_gate = jax.nn.sigmoid(gap), jax.nn.sigmoid(-gap)
        zero = jnp.zeros_like(rms)
        flat = jnp.stack([rms, low_gate, high_gate, gap, zero, zero, zero, zero])
        return flat, flat.T

    tile = 256

    def qkv_body(m, *refs):
        x_refs = refs[:parts]
        gain_ref, router_ref = refs[parts : parts + 2]
        q_refs = refs[parts + 2 : 2 * parts + 2]
        kv_refs = refs[2 * parts + 2 : 3 * parts + 2]
        sel_ref = refs[3 * parts + 2]
        outs = refs[3 * parts + 3 : 3 * parts + 11]
        stats_ref, scr = refs[3 * parts + 11 :]
        us = []
        logits = jnp.zeros((8, tile), F32)
        squares = jnp.zeros((8, tile), F32)
        for s in pieces:
            xf = x_refs[s][...].astype(F32)
            us.append((xf * gain_ref[s]).astype(BF16))
            logits += nt(router_ref[s], us[s])
            squares += lane_sums(xf * xf)
        line = lax.broadcasted_iota(jnp.int32, (8, tile), 0)
        stats_ref[...] = jnp.where(line < experts, logits, squares)
        products = []
        for e in range(experts):
            products.append(sum(nn(us[s], q_refs[s][e]) for s in pieces))
        low, high = two_slots(sel_ref[:, 0:1], sel_ref[:, 1:2], products)
        keys = sum(nn(us[s], kv_refs[s][0]) for s in pieces)
        values = sum(nn(us[s], kv_refs[s][1]) for s in pieces)
        for k, value in enumerate((low, high, keys, values)):
            value = value.astype(BF16)
            for h in range(heads):
                scr[h, :, k * HD : (k + 1) * HD] = value[:, h * HD : (h + 1) * HD]
        for r in range(4):
            block = scr[m[2 + r]]
            outs[2 * r][...] = block[:, : 2 * HD]
            outs[2 * r + 1][...] = block[:, 2 * HD :]

    ins = [(x, (tile, ds), lambda i, m: (i, 0)) for x in x_pieces]
    ins += [(gain_a, None, None), (router_a, None, None)]
    ins += [(w, None, None) for w in wq + wkv]
    ins += [(sel, (tile, 8), lambda i, m: (i, 0))]
    outs = [((rp, 2 * HD), BF16, (tile, 2 * HD), lambda i, m: (i, 0))] * 8
    outs += [((8, rp), F32, (8, tile), lambda i, m: (0, i))]
    qkv = run(
        qkv_body, "qkv", (rp // tile,), after(meta, wo[1:], wp[1:]), ins, outs,
        [pltpu.VMEM((heads, tile, 4 * HD), BF16)],
        flops=2 * rp * (experts + 2) * parts * ds * hw,
    )
    stats_a = sum_groups(after(qkv[8], wi[1:]))
    flat_a, cols_a = gate_columns(stats_a, low_a, high_a)
    q_sum, kv_sum, _, far = reduce_groups(qkv[0:8:2], qkv[1:8:2], late=cols_a)

    d_all = lax.all_to_all(d_send, "dp", 0, 0, tiled=True).reshape(rows_all, ds)
    d_pieces = pack(d_all, True, after(table, far[0]))

    def rows_pair(refs):
        return jnp.concatenate([ref[...] for ref in refs], axis=0)

    def dhidden_body(m, *refs):
        d_refs = refs[: 2 * parts]
        w_refs, sel_refs = refs[2 * parts : 3 * parts], refs[3 * parts : 3 * parts + 2]
        outs = refs[3 * parts + 2 :]
        ids = rows_pair(sel_refs)
        rows_of = [rows_pair(d_refs[2 * s : 2 * s + 2]) for s in pieces]
        products = []
        for e in range(experts):
            products.append(sum(nt(rows_of[s], w_refs[s][e]) for s in pieces))
        low, high = two_slots(ids[:, 2:3], ids[:, 3:4], products)
        low, high = low.astype(BF16), high.astype(BF16)
        for step, pair in enumerate(((3, 1), (2, 0))):

            @pl.when(pl.program_id(0) == step)
            def _():
                for k, r in enumerate(pair):
                    outs[2 * r][...] = low[k * blk : (k + 1) * blk]
                    outs[2 * r + 1][...] = high[k * blk : (k + 1) * blk]

    def dhidden(meta):
        spots = [lambda i, m: (m[5 - i], 0), lambda i, m: (m[3 - i], 0)]
        ins = [(d, (blk, ds), spot) for d in d_pieces for spot in spots]
        ins += [(w, None, None) for w in wo]
        ins += [(sel, (blk, 8), spot) for spot in spots]
        outs = [((blk, ff), BF16, None, None)] * 8
        return run(
            dhidden_body, "dhidden", (2,), meta, ins, outs,
            flops=2 * rp * experts * parts * ds * ff,
        )

    dh = dhidden(meta)

    def rope_body(m, a0, a1, a2, b0, b1, b2, cols, cos_ref, sin_ref, q_ref, kv_ref):
        rms = cols[:, 0:1]
        cos, sin = cos_ref[...], sin_ref[...]
        q = (a0[...].astype(F32) + a1[...].astype(F32) + a2[...].astype(F32)) * rms
        kv = (b0[...].astype(F32) + b1[...].astype(F32) + b2[...].astype(F32)) * rms
        q_ref[:, :HD] = turn(q[:, :HD], cos, sin).astype(BF16)
        q_ref[:, HD:] = turn(q[:, HD:], cos, sin).astype(BF16)
        kv_ref[:, :HD] = turn(kv[:, :HD], cos, sin).astype(BF16)
        kv_ref[:, HD:] = kv[:, HD:].astype(BF16)

    ins = [(v, (tile, 2 * HD), lambda i, m: (i, 0)) for v in q_sum + kv_sum]
    ins += [(cols_a, (tile, 8), lambda i, m: (i, 0))]
    ins += [(v, (tile, HD), lambda i, m: (i, 0)) for v in (cosine, sine)]
    outs = [((rp, 2 * HD), BF16, (tile, 2 * HD), lambda i, m: (i, 0))] * 2
    q_rot, kv_rot = run(rope_body, "rope", (rp // tile,), after(meta, dh[0]), ins, outs)
    halo = to_next(kv_rot[rp - seq_len :])

    qt = 128
    span = seq_len + qt

    def window_mask(i, low_key):
        u = i * qt + lax.broadcasted_iota(jnp.int32, (qt, span), 1)
        t = seq_len + i * qt + lax.broadcasted_iota(jnp.int32, (qt, span), 0)
        return (u >= low_key.astype(jnp.int32)) & (u <= t)

    def softmax_of(query, key, allowed):
        score = jnp.where(allowed, nt(query, key) * scale, -1e30)
        top = jnp.max(score, axis=1, keepdims=True)
        raised = jnp.exp(score - top)
        return raised / jnp.sum(raised, axis=1, keepdims=True)

    def attend_body(m, q_ref, kv_ref, halo_ref, sel_ref, cols, ga, gb, ma, mb, ext):
        i = pl.program_id(0)

        @pl.when(i == 0)
        def _():
            ext[:seq_len, :] = halo_ref[...]
            ext[seq_len:, :] = kv_ref[...]

        near = ext[pl.ds(pl.multiple_of(i * qt, qt), span), :]
        allowed = window_mask(i, sel_ref[:, 4:5])
        for k, (g_ref, m_ref) in enumerate(((ga, ma), (gb, mb))):
            probs = softmax_of(q_ref[:, k * HD : (k + 1) * HD], near[:, :HD], allowed)
            mixed = nn(probs.astype(BF16), near[:, HD:]).astype(BF16)
            m_ref[...] = mixed
            g_ref[...] = (mixed.astype(F32) * cols[:, 1 + k : 2 + k]).astype(BF16)

    def qrow(i, m):
        return (i, 0)

    ins = [(q_rot, (qt, 2 * HD), qrow), (kv_rot, None, None), (halo, None, None)]
    ins += [(sel, (qt, 8), qrow), (cols_a, (qt, 8), qrow)]
    outs = [((rp, HD), BF16, (qt, HD), qrow)] * 4
    gated_a, gated_b, mixed_a, mixed_b = run(
        attend_body, "attend", (rp // qt,), meta, ins, outs,
        [pltpu.VMEM((seq_len + rp, 2 * HD), BF16)],
        flops=8 * rp * span * HD,
    )
    gm_a, gm_b, _ = gather_groups(gated_a, gated_b)
    zr = rp // 2
    hold = [((parts, zr, ds), BF16, None, None)] * 2

    def store_halves(i, refs, s, value):
        @pl.when(i == 0)
        def _():
            refs[1][s] = value

        @pl.when(i == 1)
        def _():
            refs[0][s] = value

    def proj_body(m, *refs):
        a_refs, b_refs = refs[:4], refs[4:8]
        sel_ref = refs[8]
        w_refs = refs[9 : 9 + parts]
        outs, xs = refs[9 + parts : 11 + parts], refs[11 + parts]
        for r in range(4):
            lanes = pl.ds(pl.multiple_of(m[2 + r] * HD, HD), HD)
            for e in range(experts):
                xs[e, :, lanes] = pick(
                    sel_ref[:, 0:1], sel_ref[:, 1:2], e, a_refs[r][...], b_refs[r][...]
                )
        acc = nn_pieces(xs[0], [w[0] for w in w_refs])
        for e in range(1, experts):
            for s, value in enumerate(nn_pieces(xs[e], [w[e] for w in w_refs])):
                acc[s] += value
        for s in pieces:
            store_halves(pl.program_id(0), outs, s, acc[s].astype(BF16))

    def project(meta):
        half = lambda i, m: (m[7 - i], 0)
        ins = [(v, (zr, HD), half) for v in gm_a + gm_b]
        ins += [(sel, (zr, 8), half)]
        ins += [(w, None, None) for w in wp]
        return run(
            proj_body, "proj", (2,), meta, ins, hold,
            [pltpu.VMEM((experts, zr, hw), BF16)],
            flops=4 * zr * experts * hw * parts * ds,
        )

    proj_halves = project(meta)
    dh_a, dh_b = held((dh[0:8:2], dh[1:8:2]), gm_a[3], gm_b[3])
    ra, rb = by_group(dh_a[3], 1), by_group(dh_b[3], 2)
    ax, by = by_group(dh_a[1], 1), by_group(dh_b[2], 2)
    half = z_second(z_first(*proj_halves))
    near = held((both(dh_a[2], ra), both(dh_b[1], rb)), (ax, by), half)
    dh_a, dh_b = (dh_a[0], ax, by_group(near[0], 2)), (dh_b[0], by_group(near[1], 1), by)
    attn_totals = list(z_last(half))

    def norm_body(m, *refs):
        t_refs = refs[: 2]
        x_refs = refs[2 : 2 + parts]
        gain_ref, router_ref, after_ref, u_ref, stats_ref = refs[2 + parts :]
        for k in range(2):
            span_k = at_row(m, IN_ORDER + k, zr)
            for s in pieces:
                after_ref[s, span_k, :] = x_refs[s][span_k, :].astype(F32) + t_refs[k][s].astype(F32)
        logits = jnp.zeros((8, rp), F32)
        squares = jnp.zeros((8, rp), F32)
        for s in pieces:
            af = after_ref[s]
            u = (af * gain_ref[s]).astype(BF16)
            u_ref[s] = u
            logits += nt(router_ref[s], u)
            squares += lane_sums(af * af)
        line = lax.broadcasted_iota(jnp.int32, (8, rp), 0)
        stats_ref[...] = jnp.where(line < experts, logits, squares)

    ins = [(t, None, None) for t in attn_totals + x_pieces]
    ins += [(gain_f, None, None), (router_f, None, None)]
    outs = [
        ((parts, rp, ds), F32, None, None),
        ((parts, rp, ds), BF16, None, None),
        ((8, rp), F32, None, None),
    ]
    after_rows, u_f, stats_part = run(norm_body, "norm", (1,), meta, ins, outs)
    def up_body(m, *refs):
        u_refs, w_refs = refs[:2], refs[2 : 2 + parts]
        sel_refs = refs[2 + parts : 4 + parts]
        outs = refs[4 + parts :]
        ids = rows_pair(sel_refs)
        rows_of = [jnp.concatenate([u[s] for u in u_refs], axis=0) for s in pieces]
        products = []
        for e in range(experts):
            products.append(sum(nn(rows_of[s], w_refs[s][e, 0]) for s in pieces))
        low, high = two_slots(ids[:, 2:3], ids[:, 3:4], products)
        low, high = low.astype(BF16), high.astype(BF16)
        for k in range(2):
            outs[2 * k][0] = low[k * blk : (k + 1) * blk]
            outs[2 * k + 1][0] = high[k * blk : (k + 1) * blk]

    def up(pair, meta):
        def block_of(r):
            return lambda j, m: (0, m[2 + r], 0)

        ins = [(u_f, (parts, blk, ds), block_of(r)) for r in pair]
        ins += [(w, (experts, 1, ds, ff), lambda j, m: (0, j, 0, 0)) for w in wi]
        ins += [(sel, (blk, 8), row_of(r)) for r in pair]
        outs = [((2, blk, ff), BF16, (1, blk, ff), lambda j, m: (j, 0, 0))] * 4
        return run(
            up_body, "up", (2,), meta, ins, outs, flops=8 * blk * experts * parts * ds * ff
        )

    up_far = up((3, 1), after(meta, dh_a[2], dh_b[1]))
    up_near = up((2, 0), after(meta, up_far[0]))
    gu_a, gu_b, _, far = reduce_groups(
        (up_near[2], up_far[2], up_near[0], up_far[0]),
        (up_near[3], up_far[3], up_near[1], up_far[1]),
    )

    stats_f = sum_groups(after(stats_part, far))
    flat_f, cols_f = gate_columns(stats_f, low_f, high_f)

    mt_rows = blk // 3

    def mid_body(m, *refs):
        gu = (refs[0:3], refs[3:6])
        dhr = (refs[6:9], refs[9:12])
        cols = refs[12]
        acts, grads, dots = refs[13:15], refs[15:17], refs[17]
        rms = cols[:, 0:1]
        column = lax.broadcasted_iota(jnp.int32, (mt_rows, 8), 1)
        found = []
        inner = jnp.zeros((mt_rows, 1), F32)
        for k in range(2):
            gate = cols[:, 1 + k : 2 + k]
            gp = sum(v[0].astype(F32) for v in gu[k]) * rms
            up_pre = sum(v[1].astype(F32) for v in gu[k]) * rms
            raw = sum(v[...].astype(F32) for v in dhr[k])
            sg = jax.nn.sigmoid(gp)
            act = (gp * sg * up_pre).astype(BF16).astype(F32)
            grad = raw * gate
            dgp = (grad * up_pre * sg * (1.0 + gp * (1.0 - sg))).astype(BF16)
            dup = (grad * gp * sg).astype(BF16)
            acts[k][...] = (act * gate).astype(BF16)
            grads[k][0] = dgp
            grads[k][1] = dup
            found.append(jnp.sum(act * raw, axis=1, keepdims=True))
            inner += jnp.sum(
                dgp.astype(F32) * gp + dup.astype(F32) * up_pre, axis=1, keepdims=True
            )
        zero = jnp.zeros((mt_rows, 8), F32)
        for k, value in enumerate(found + [inner]):
            zero = jnp.where(column == k, value, zero)
        dots[...] = zero

    rows_3 = lambda i, m: (0, i, 0)
    rows_2 = lambda i, m: (i, 0)
    ins = [(v, (2, mt_rows, ff), rows_3) for v in gu_a + gu_b]
    ins += [(v, (mt_rows, ff), rows_2) for v in dh_a + dh_b]
    ins += [(cols_f, (mt_rows, 8), lambda i, m: (3 * m[2] + i, 0))]
    outs = [((blk, ff), BF16, (mt_rows, ff), rows_2)] * 2
    outs += [((2, blk, ff), BF16, (2, mt_rows, ff), rows_3)] * 2
    outs += [((blk, 8), F32, (mt_rows, 8), rows_2)]
    act_a, act_b, grad_a, grad_b, dots_f = run(mid_body, "mid", (3,), meta, ins, outs)
    gg_a, gg_b, gg_along = gather_groups(grad_a, grad_b, late=(act_a,))
    dots_f = dots_f.T

    def dx_body(m, *refs):
        a_refs, b_refs = refs[:2], refs[2:4]
        w_refs = refs[4 : 4 + parts]
        sel_refs = refs[4 + parts : 6 + parts]
        keep_ref, send_ref, acc, xs = refs[6 + parts :]
        e = pl.program_id(0)
        expert = e.astype(F32)

        @pl.when(e == 0)
        def _():
            acc[...] = jnp.zeros_like(acc)

        for j in range(2):
            for k in range(2):
                ids = sel_refs[k]
                xs[k * blk : (k + 1) * blk, :] = pick(
                    ids[:, 2:3], ids[:, 3:4], expert, a_refs[k][j], b_refs[k][j]
                )
            for s, value in enumerate(nt_pieces(xs[...], [w[0, j] for w in w_refs])):
                acc[s] += value

        @pl.when(e == experts - 1)
        def _():
            keep_ref[...] = acc[:, at_row(m, 6, blk), :].astype(BF16)
            send_ref[...] = acc[:, at_row(m, 7, blk), :].astype(BF16)

    def dx(pair, meta):
        ins = [(v[r], None, None) for v in (gg_a, gg_b) for r in pair]
        ins += [(w, (1, 2, ds, ff), lambda e, m: (e, 0, 0, 0)) for w in wi]
        ins += [(sel, (blk, 8), row_of(r)) for r in pair]
        return run(
            dx_body, "dx", (experts,), meta, ins, [((parts, blk, ds), BF16, None, None)] * 2,
            [pltpu.VMEM((parts, 2 * blk, ds), F32), pltpu.VMEM((2 * blk, ff), BF16)],
            flops=8 * blk * experts * parts * ds * ff,
        )

    dx_near = dx((0, 1), after(meta, gg_a[2], gg_b[2]))
    dx_far = dx((2, 3), meta)
    dots_f = sum_z(dots_f)
    dots_f = jnp.stack([dots_f, held([by_group(dots_f, 1)], dx_near[0])[0]])
    dots_f = jnp.concatenate([dots_f, held([by_group(dots_f, 2)], dx_far[0])[0]])
    near_half = z_first(*dx_near)
    near_half = z_covered(near_half, near_half, 3, dx_far[0])
    far_half = z_first(*dx_far)

    act_a, act_b, _ = lax.optimization_barrier((act_a, act_b, far_half))
    ag_a = [act_a, by_group(act_a, 1), by_group(act_a, 2)]
    ag_b = [act_b, by_group(act_b, 1), by_group(act_b, 2)]
    dots_f = jnp.take(dots_f, g ^ jnp.arange(4, dtype=jnp.int32), axis=0)
    dots_f = dots_f.transpose(1, 0, 2).reshape(8, rp)

    def back_columns(flat, dots, low_id, high_id):
        delta = flat[1] * flat[2] * (dots[0] - dots[1])
        inner = (dots[2] + delta * flat[3]) / width
        ids = jnp.arange(experts, dtype=F32)[:, None]
        dlogit = jnp.where(low_id[None] == ids, delta[None], 0.0) - jnp.where(
            high_id[None] == ids, delta[None], 0.0
        )
        zero = jnp.zeros((1, rp), F32)
        return jnp.concatenate(
            [dlogit, inner[None], flat[0:1]] + [zero] * (6 - experts), axis=0
        ).T

    back_f = back_columns(flat_f, dots_f, low_f, high_f)


    def exchange(sums):
        return [sums[0]] + [by_part(sums[s], s) for s in pieces[1:]]

    def add_up(got):
        return sum(v.astype(F32) for v in got)

    ffn_input = (after_rows * flat_f[0][None, :, None] * gain_f).astype(BF16)

    def t_left(xs, value):
        if not wide:
            return [tn(x, value) for x in xs]
        total = tn(jnp.concatenate(xs, axis=1), value)
        return [total[s * ds : (s + 1) * ds] for s in pieces]

    def t_right(value, xs):
        if not wide:
            return [tn(value, x) for x in xs]
        total = tn(value, jnp.concatenate(xs, axis=1))
        return [total[:, s * ds : (s + 1) * ds] for s in pieces]

    def sort_rows(m, sel_ref, x_refs, xs, ids):
        for r in range(4):
            src, here_r = at_row(m, 2 + r, blk), slice(r * blk, (r + 1) * blk)
            for s in pieces:
                xs[s, here_r, :] = x_refs[s][src, :]
            ids[here_r, :] = sel_ref[src, :]

    def dwin_body(m, *refs):
        a_refs, b_refs = refs[:4], refs[4:8]
        sel_ref, x_ref = refs[8:10]
        outs = refs[10 : 10 + parts]
        xs, ids, mt = refs[10 + parts :]
        e = pl.program_id(0)

        @pl.when(e == 0)
        def _():
            sort_rows(m, sel_ref, [x_ref.at[s] for s in pieces], xs, ids)

        expert = e.astype(F32)
        for r in range(4):
            here_r = slice(r * blk, (r + 1) * blk)
            mt[here_r, :] = pick(
                ids[here_r, 2:3], ids[here_r, 3:4], expert, a_refs[r][0], b_refs[r][0]
            )
        for s, value in enumerate(t_left([xs[s] for s in pieces], mt[...])):
            outs[s][0] = value.astype(BF16)

    def dwin(j, meta):
        ins = [(v, (1, blk, ff), lambda e, m: (j, 0, 0)) for v in gg_a + gg_b]
        ins += [(sel, None, None), (ffn_input, None, None)]
        outs = [((experts, ds, ff), BF16, (1, ds, ff), lambda e, m: (e, 0, 0))] * parts
        return run(
            dwin_body, "dwin", (experts,), meta, ins, outs,
            [pltpu.VMEM((parts, rp, ds), BF16), pltpu.VMEM((rp, 8), F32), pltpu.VMEM((rp, ff), BF16)],
            flops=2 * rp * experts * parts * ds * ff,
        )

    def fold_body(m, *refs):
        out_ref = refs[2 * parts]
        for j in range(2):
            total = refs[j * parts][0].astype(F32)
            for ref in refs[j * parts + 1 : (j + 1) * parts]:
                total = total + ref[0].astype(F32)
            out_ref[0, :, j, :] = total

    def fold(sums, meta):
        ins = [(v, (1, ds, ff), lambda e, m: (e, 0, 0)) for half in sums for v in half]
        outs = [((experts, ds, 2, ff), F32, (1, ds, 2, ff), lambda e, m: (e, 0, 0, 0))]
        return run(fold_body, "fold", (experts,), meta, ins, outs)[0]

    dwin_gate = dwin(0, after(meta, far_half))
    dx_totals = z_last(near_half) + z_last(z_covered(far_half, far_half, 3, dwin_gate[0]))

    def norm_back_body(low_precision_out, m, *refs):
        sums = 4 if low_precision_out else 2
        t_refs, after_ref, refs = refs[:sums], refs[sums], refs[sums + 1 :]
        ups = parts if low_precision_out else 1
        up_refs = refs[:ups]
        gain_ref, router_ref, back = refs[ups : 3 + ups]
        outs = refs[3 + ups :]
        small = outs[-1]
        for s in pieces:
            gain = gain_ref[s]
            router = router_ref[s].astype(F32)
            gain_sum = jnp.zeros((1, ds), F32)
            router_sum = [jnp.zeros((1, ds), F32)] * experts
            for r in range(4):
                span_r = at_row(m, (BY_CHUNK if low_precision_out else IN_HALVES) + r, blk)
                up_value = up_refs[s][span_r, :] if low_precision_out else up_refs[0][s, span_r, :]
                x = after_ref[s, span_r, :].astype(F32)
                cols = back[span_r, :]
                rms = cols[:, experts + 1 : experts + 2]
                if low_precision_out:
                    grad = t_refs[r][s].astype(F32)
                else:
                    grad = t_refs[r // 2][s, (r % 2) * blk : (r % 2 + 1) * blk, :].astype(F32)
                for e in range(experts):
                    grad += cols[:, e : e + 1] * router[e : e + 1]
                normed = x * rms
                token = (normed * gain).astype(BF16).astype(F32)
                gain_sum += jnp.sum(grad * normed, axis=0, keepdims=True)
                for e in range(experts):
                    router_sum[e] = router_sum[e] + jnp.sum(
                        token * cols[:, e : e + 1], axis=0, keepdims=True
                    )
                dn = grad * gain
                total = up_value.astype(F32) + rms * (
                    dn - normed * cols[:, experts : experts + 1]
                )
                if low_precision_out:
                    outs[0][s, span_r, :] = total
                    outs[1][s, span_r, :] = total.astype(BF16)
                else:
                    outs[s][span_r, :] = total.astype(BF16)
            for e in range(experts):
                small[e, s] = router_sum[e][0]
            small[experts, s] = gain_sum[0]

    ins = [(t, None, None) for t in dx_totals]
    ins += [(after_rows, None, None)] + [(d, None, None) for d in d_pieces]
    ins += [(gain_f, None, None), (router_f, None, None), (back_f, None, None)]
    outs = [
        ((parts, rp, ds), F32, None, None),
        ((parts, rp, ds), BF16, None, None),
        ((experts + 1, parts, ds), F32, None, None),
    ]
    dafter, dafter_low, small_f = run(
        functools.partial(norm_back_body, True), "norm_back", (1,),
        after(meta, dwin_gate[0], ag_a[1:], ag_b[1:]), ins, outs,
    )

    def dmix_body(m, *refs):
        d_ref = refs[0]
        w_refs = refs[1 : 1 + parts]
        sel_ref = refs[1 + parts]
        outs = refs[2 + parts : 10 + parts]
        scr = refs[10 + parts]
        products = []
        for e in range(experts):
            products.append(sum(nt(d_ref[s], w_refs[s][e]) for s in pieces))
        low, high = two_slots(sel_ref[:, 0:1], sel_ref[:, 1:2], products)
        for k, value in enumerate((low, high)):
            value = value.astype(BF16)
            for h in range(heads):
                scr[h, :, k * HD : (k + 1) * HD] = value[:, h * HD : (h + 1) * HD]
        for r in range(4):
            block = scr[m[2 + r]]
            outs[2 * r][...] = block[:, :HD]
            outs[2 * r + 1][...] = block[:, HD:]

    ins = [(dafter_low, (parts, tile, ds), lambda i, m: (0, i, 0))]
    ins += [(w, None, None) for w in wp]
    ins += [(sel, (tile, 8), lambda i, m: (i, 0))]
    outs = [((rp, HD), BF16, (tile, HD), lambda i, m: (i, 0))] * 8
    dm = run(
        dmix_body, "dmix", (rp // tile,), meta, ins, outs,
        [pltpu.VMEM((heads, tile, 2 * HD), BF16)],
        flops=2 * rp * experts * parts * ds * hw,
    )
    dwin_up = dwin(1, after(meta, dm[0]))
    dm_a, dm_b, _, _ = reduce_groups(dm[0:8:2], dm[1:8:2], late=dwin_up[0])
    along = held((ag_a[1], ag_b[2]), dm_a[2], dm_b[1])
    ag_a, ag_b = ag_a + [by_group(along[0], 2)], ag_b + [by_group(along[1], 1)]

    def attend_back_body(m, *refs):
        q_ref, kv_ref, halo_ref, sel_ref, cols, cos_ref, sin_ref = refs[:7]
        d_refs = (refs[7:10], refs[10:13])
        mix_refs = refs[13:15]
        dq_ref, own_ref, far_ref, dots_ref, ext, acc = refs[15:]
        i = pl.program_id(0)

        @pl.when(i == 0)
        def _():
            ext[:seq_len, :] = halo_ref[...]
            ext[seq_len:, :] = kv_ref[...]
            acc[...] = jnp.zeros_like(acc)

        near_rows = pl.ds(pl.multiple_of(i * qt, qt), span)
        near = ext[near_rows, :]
        allowed = window_mask(i, sel_ref[:, 4:5])
        line = lax.broadcasted_iota(jnp.int32, (8, qt), 0)
        inner = jnp.zeros((qt, HD), F32)
        found = []
        dk = jnp.zeros((span, HD), F32)
        dv = jnp.zeros((span, HD), F32)
        for k in range(2):
            query = q_ref[:, k * HD : (k + 1) * HD]
            probs = softmax_of(query, near[:, :HD], allowed)
            raw = sum(v[...].astype(F32) for v in d_refs[k])
            dmixed = (raw * cols[:, 1 + k : 2 + k]).astype(BF16)
            found.append(raw * mix_refs[k][...].astype(F32))
            dv += tn(probs.astype(BF16), dmixed)
            dprob = nt(dmixed, near[:, HD:])
            rest = jnp.sum(probs * dprob, axis=1, keepdims=True)
            dscore = (probs * (dprob - rest)).astype(BF16)
            dk += tn(dscore, query) * scale
            dquery = nn(dscore, near[:, :HD]) * scale
            inner += dquery * query.astype(F32)
            dq_ref[:, k * HD : (k + 1) * HD] = turn(dquery, cos_ref[...], -sin_ref[...]).astype(BF16)
        acc[near_rows, :HD] += dk
        acc[near_rows, HD:] += dv
        dots_ref[...] = jnp.where(
            line == 0, lane_sums(found[0]), jnp.where(line == 1, lane_sums(found[1]), lane_sums(inner))
        )

        @pl.when(i == rp // qt - 1)
        def _():
            far_ref[...] = acc[:seq_len, :]
            own_ref[...] = acc[seq_len:, :]

    ins = [(q_rot, (qt, 2 * HD), qrow), (kv_rot, None, None), (halo, None, None)]
    ins += [(sel, (qt, 8), qrow), (cols_a, (qt, 8), qrow)]
    ins += [(cosine, (qt, HD), qrow), (sine, (qt, HD), qrow)]
    ins += [(v, (qt, HD), qrow) for v in dm_a + dm_b + (mixed_a, mixed_b)]
    outs = [
        ((rp, 2 * HD), BF16, (qt, 2 * HD), qrow),
        ((rp, 2 * HD), F32, None, None),
        ((seq_len, 2 * HD), F32, None, None),
        ((8, rp), F32, (8, qt), lambda i, m: (0, i)),
    ]
    dq, dkv_own, dkv_far, dots_q = run(
        attend_back_body, "attend_back", (rp // qt,), meta, ins, outs,
        [pltpu.VMEM((seq_len + rp, 2 * HD), BF16), pltpu.VMEM((seq_len + rp, 2 * HD), F32)],
        flops=20 * rp * span * HD,
    )
    dkv_in = to_previous(dkv_far)

    def dkv_body(m, own_ref, in_ref, kv_ref, cos_ref, sin_ref, out_ref, dots_ref):
        head = rp - seq_len
        for rows_here in (slice(0, head), slice(head, rp)):
            value = own_ref[rows_here, :]
            if rows_here.start == head:
                value = value + in_ref[...]
            out_ref[rows_here, :HD] = turn(
                value[:, :HD], cos_ref[rows_here, :], -sin_ref[rows_here, :]
            ).astype(BF16)
            out_ref[rows_here, HD:] = value[:, HD:].astype(BF16)
            dots_ref[:, rows_here] = lane_sums(value * kv_ref[rows_here, :].astype(F32))

    ins = [(v, None, None) for v in (dkv_own, dkv_in, kv_rot, cosine, sine)]
    outs = [((rp, 2 * HD), BF16, None, None), ((8, rp), F32, None, None)]
    got_in = [exchange(dwin_gate), exchange(held(dwin_up, dm_a[2], dm_b[1]))]
    dkv, dots_kv = run(
        dkv_body, "dkv", (1,), after(meta, ag_a[3], ag_b[3]), ins, outs
    )
    third = jnp.arange(8)[:, None] == 2
    def down_body(m, *refs):
        a_refs, b_refs = refs[:4], refs[4:8]
        sel_ref, d_refs = refs[8], refs[9 : 9 + parts]
        w_refs = refs[9 + parts : 9 + 2 * parts]
        keep_ref, send_ref = refs[9 + 2 * parts : 11 + 2 * parts]
        outs = refs[11 + 2 * parts : 11 + 3 * parts]
        acc, xs, ids, mt = refs[11 + 3 * parts :]
        e = pl.program_id(0)

        @pl.when(e == 0)
        def _():
            acc[...] = jnp.zeros_like(acc)
            sort_rows(m, sel_ref, d_refs, xs, ids)

        expert = e.astype(F32)
        for r in range(4):
            here_r = slice(r * blk, (r + 1) * blk)
            mt[here_r, :] = pick(
                ids[here_r, 2:3], ids[here_r, 3:4], expert, a_refs[r][...], b_refs[r][...]
            )
        for s, value in enumerate(nn_pieces(mt[...], [w[0] for w in w_refs])):
            acc[s] += value
        for s, value in enumerate(t_right(mt[...], [xs[s] for s in pieces])):
            outs[s][0] = value.astype(BF16)

        @pl.when(e == experts - 1)
        def _():
            keep_ref[...] = acc[:, at_row(m, 6, 2 * blk), :].astype(BF16)
            send_ref[...] = acc[:, at_row(m, 7, 2 * blk), :].astype(BF16)

    def down(meta):
        spot = lambda e, m: (e, 0, 0)
        ins = [(v, None, None) for v in ag_a + ag_b]
        ins += [(sel, None, None)] + [(d, None, None) for d in d_pieces]
        ins += [(w, (1, ff, ds), spot) for w in wo]
        outs = [((parts, 2 * blk, ds), BF16, None, None)] * 2
        outs += [((experts, ff, ds), BF16, (1, ff, ds), spot)] * parts
        return run(
            down_body, "down", (experts,), meta, ins, outs,
            [
                pltpu.VMEM((parts, rp, ds), F32),
                pltpu.VMEM((parts, rp, ds), BF16),
                pltpu.VMEM((rp, 8), F32),
                pltpu.VMEM((rp, ff), BF16),
            ],
            flops=4 * rp * experts * parts * ds * ff,
        )

    def dwproj_body(m, *refs):
        a_refs, b_refs = refs[:4], refs[4:8]
        sel_ref, d_ref = refs[8:10]
        outs = refs[10 : 10 + parts]
        lo, hi = refs[10 + parts :]
        e = pl.program_id(0)

        @pl.when(e == 0)
        def _():
            for r in range(4):
                lanes = pl.ds(pl.multiple_of(m[2 + r] * HD, HD), HD)
                lo[:, lanes] = a_refs[r][...]
                hi[:, lanes] = b_refs[r][...]

        x = pick(sel_ref[:, 0:1], sel_ref[:, 1:2], e.astype(F32), lo[...], hi[...])
        for s, value in enumerate(t_right(x, [d_ref[s] for s in pieces])):
            outs[s][0] = value.astype(BF16)

    def dwproj(meta):
        ins = [(v, None, None) for v in gm_a + gm_b]
        ins += [(sel, None, None), (dafter_low, None, None)]
        return run(
            dwproj_body, "dwproj", (experts,), meta, ins,
            [((experts, hw, ds), BF16, (1, hw, ds), lambda e, m: (e, 0, 0))] * parts,
            [pltpu.VMEM((rp, hw), BF16)] * 2,
            flops=2 * rp * experts * hw * parts * ds,
        )

    down_halves = down(after(meta, dkv))
    down_halves, dwout_sums = down_halves[:2], down_halves[2:]
    da_a, da_b, da_along = gather_groups(dq, dkv, late=(dwout_sums[0],))
    dwproj_sums = dwproj(after(meta, da_along, got_in))
    def place_heads(m, refs, lo, hi):
        for r in range(4):
            lanes = pl.ds(pl.multiple_of(m[2 + r] * HD, HD), HD)
            lo[:, lanes] = refs[r][:, :HD]
            hi[:, lanes] = refs[r][:, HD:]

    def dattn_body(m, *refs):
        a_refs, b_refs = refs[:4], refs[4:8]
        sel_ref = refs[8]
        q_refs = refs[9 : 9 + parts]
        kv_refs = refs[9 + parts : 9 + 2 * parts]
        outs = refs[9 + 2 * parts : 11 + 2 * parts]
        lo, hi, dk, dv = refs[11 + 2 * parts :]
        place_heads(m, a_refs, lo, hi)
        place_heads(m, b_refs, dk, dv)
        acc = nt_pieces(dk[...], [w[0] for w in kv_refs])
        for s, value in enumerate(nt_pieces(dv[...], [w[1] for w in kv_refs])):
            acc[s] += value
        for e in range(experts):
            x = pick(sel_ref[:, 0:1], sel_ref[:, 1:2], e, lo[...], hi[...])
            for s, value in enumerate(nt_pieces(x, [w[e] for w in q_refs])):
                acc[s] += value
        for s in pieces:
            store_halves(pl.program_id(0), outs, s, acc[s].astype(BF16))

    def dattn(meta):
        half = lambda i, m: (m[7 - i], 0)
        ins = [(v, (zr, 2 * HD), half) for v in da_a + da_b]
        ins += [(sel, (zr, 8), half)]
        ins += [(w, None, None) for w in wq + wkv]
        return run(
            dattn_body, "dattn", (2,), meta, ins, [((parts, zr, ds), BF16, None, None)] * 2,
            [pltpu.VMEM((zr, hw), BF16)] * 4,
            flops=4 * zr * (experts + 2) * hw * parts * ds,
        )

    dots_a = dots_q + jnp.where(third, dots_kv, 0.0)
    dots_a = after(dots_a, dwproj_sums[0])
    dots_a = (dots_a + by_group(dots_a, 1)) + (by_group(dots_a, 2) + by_group(dots_a, 3))
    got_out = exchange(dwout_sums)
    da_halves = dattn(after(meta, dwproj_sums[0]))
    got_proj = exchange(dwproj_sums)
    x_stack = jnp.stack(x_pieces)
    attn_input = (x_stack.astype(F32) * flat_a[0][None, :, None] * gain_a).astype(BF16)

    def dwqkv_body(m, *refs):
        a_refs, b_refs = refs[:4], refs[4:8]
        sel_ref, x_ref = refs[8:10]
        q_outs, kv_outs = refs[10 : 10 + parts], refs[10 + parts : 10 + 2 * parts]
        lo, hi, dk, dv = refs[10 + 2 * parts :]
        e = pl.program_id(0)
        xs = [x_ref.at[s] for s in pieces]

        @pl.when(e == 0)
        def _():
            place_heads(m, a_refs, lo, hi)
            place_heads(m, b_refs, dk, dv)

        @pl.when(e < experts)
        def _():
            x = pick(sel_ref[:, 0:1], sel_ref[:, 1:2], e.astype(F32), lo[...], hi[...])
            for s, value in enumerate(t_left([v[...] for v in xs], x)):
                q_outs[s][0] = value.astype(BF16)

        for k, grad in enumerate((dk, dv)):

            @pl.when(e == experts + k)
            def _():
                for s, value in enumerate(t_left([v[...] for v in xs], grad[...])):
                    kv_outs[s][0] = value.astype(BF16)

    def dwqkv(meta):
        q_spot = lambda e, m: (jnp.minimum(e, experts - 1), 0, 0)
        kv_spot = lambda e, m: (jnp.maximum(e - experts, 0), 0, 0)
        ins = [(v, None, None) for v in da_a + da_b]
        ins += [(sel, None, None), (attn_input, None, None)]
        outs = [((experts, ds, hw), BF16, (1, ds, hw), q_spot)] * parts
        outs += [((2, ds, hw), BF16, (1, ds, hw), kv_spot)] * parts
        return run(
            dwqkv_body, "dwqkv", (experts + 2,), meta, ins, outs,
            [pltpu.VMEM((rp, hw), BF16)] * 4,
            flops=2 * rp * (experts + 2) * hw * parts * ds,
        )

    dwqkv_sums = dwqkv(after(meta, da_halves[0], dots_a))


    da_half = z_covered(*da_halves, 1, dwqkv_sums[0])

    down_half = z_covered(*down_halves, 1, dwproj_sums[0])

    def finish_body(m, *refs):
        t_refs, after_ref, outs = refs[:2], refs[2], refs[3:]
        for k in range(4):
            span_k = at_row(m, BY_HALF + k, blk)
            for s in pieces:
                total = t_refs[k // 2][s, (k % 2) * blk : (k % 2 + 1) * blk, :]
                outs[s][span_k, :] = (
                    after_ref[s, span_k, :] + total.astype(F32)
                ).astype(BF16)

    got_q, got_kv = exchange(dwqkv_sums[:parts]), exchange(dwqkv_sums[parts:])
    dots_a = (dots_a + by_z(dots_a, 1)) + (by_z(dots_a, 2) + by_z(dots_a, 3))
    back_a = back_columns(flat_a, dots_a, low_a, high_a)
    down_totals = z_last(z_covered(down_half, down_half, 3, da_half))
    ins = [(t, None, None) for t in down_totals] + [(after_rows, None, None)]
    out_rows = run(
        finish_body, "finish", (1,), after(meta, dots_a), ins,
        [((rp, ds), BF16, None, None)] * parts,
    )

    count = rows_all // dp

    def unpack_body(dealt, m, other_ref, *refs):
        v_refs, out_ref = refs[:parts], refs[-5]
        packed, other, total, whole = refs[-4:]
        for s in pieces:
            packed[part_rows(m, s), :] = v_refs[s][...].astype(F32)
        other[...] = other_ref[...].astype(F32)
        line = lax.broadcasted_iota(jnp.int32, (per, ds), 0)

        def one(j, carry):
            window, shift = near_rows(m, j)
            back = jnp.where(shift == 0, 0, seq_len + 8 - shift)
            whole[...] = pltpu.roll(packed[window, :], back, 0)
            for p in range(dp):
                if dealt:
                    spot = m[2 * seqs + j] * seq_len + p * per
                    kept = other[pl.ds(pl.multiple_of(spot, per), per), :]
                else:
                    kept = other[block_rows(p, j), :]
                value = whole[p * per : (p + 1) * per, :]
                total[block_rows(p, j), :] = jnp.where(line < m[seqs + j] - p * per, value, kept)
            return carry

        lax.fori_loop(0, seqs, one, 0)
        for p in range(dp):
            out_ref[p, :count, :] = total[p * count : (p + 1) * count, :].astype(BF16)
            for ref in refs[parts:-5]:
                out_ref[p, count:, :] = ref[...]

    def unpack(value, otherwise, dealt, table, extra=()):
        mine_all = [value[0]] + [by_part(value[s], s) for s in pieces[1:]]
        ins = [(v, None, None) for v in [otherwise] + mine_all + list(extra)]
        tall = count + sum(v.shape[0] for v in extra)
        spread_rows = run(
            functools.partial(unpack_body, dealt), "unpack", (1,), table, ins,
            [((dp, tall, ds), BF16, None, None)],
            [
                pltpu.VMEM((n, ds), F32)
                for n in (rows + seq_len + 8, rows_all, rows_all, seq_len + 8)
            ],
        )[0]
        return spread_rows

    def land(spread_rows):
        landed = lax.all_to_all(spread_rows, "dp", 0, 0, tiled=True)
        rows_of = landed[:, :count].transpose(1, 0, 2).reshape(seqs, per, width)
        return rows_of, landed[:, count:]

    da_half = z_covered(da_half, da_half, 3, out_rows[0])
    layer_rows = unpack(out_rows, x_all, False, table)
    expertin_grad = fold(got_in, after(meta, da_half, layer_rows))
    da_totals = z_last(da_half)
    layer_out, _ = land(after(layer_rows, expertin_grad, da_totals[1]))
    ins = [(t, None, None) for t in da_totals]
    ins += [(x_stack, None, None), (dafter, None, None)]
    ins += [(gain_a, None, None), (router_a, None, None), (back_a, None, None)]
    outs = [((rp, ds), BF16, None, None)] * parts
    outs += [((experts + 1, parts, ds), F32, None, None)]
    *dinput, small_a = run(
        functools.partial(norm_back_body, False), "norm_back_first", (1,),
        after(meta, expertin_grad), ins, outs,
    )
    expertout_grad, proj_grad = add_up(got_out), add_up(got_proj)
    query_grad, kv_grad = add_up(got_q), add_up(got_kv)
    vectors = 2 * (experts + 1)
    small = jnp.concatenate([small_a, small_f], axis=0).reshape(vectors * parts, ds)
    small = jnp.pad(small, ((0, -vectors * parts % 16), (0, 0))).astype(BF16)
    input_grad, got = land(unpack(dinput, d_all, True, table, [small]))
    got = got[:, : vectors * parts].astype(F32).reshape(groups, parts, vectors, parts, ds)
    full = jnp.stack(
        [sum(got[:, k ^ s, :, s] for s in pieces) for k in range(parts)], axis=2
    )
    full = full.transpose(1, 0, 2, 3).reshape(2, experts + 1, width)
    attnrouter_grad, attngain_grad = full[0, :experts].T, full[0, experts]
    ffnrouter_grad, ffngain_grad = full[1, :experts].T, full[1, experts]
    return (
        layer_out,
        input_grad,
        attngain_grad,
        attnrouter_grad,
        kv_grad,
        query_grad,
        proj_grad,
        ffngain_grad,
        ffnrouter_grad,
        expertin_grad,
        expertout_grad,
    )


def solution(mesh):
    placed = (
        P(None, "dp", None),
        P("dp", None, None),
        P(),
        P(),
        P(),
        P(),
        P(),
        P(),
        P(None, "dp", "tensor"),
        P(None, "dp", "tensor"),
        P(None, "tensor", "dp"),
        P(),
        P(),
        P(None, "dp", None, "tensor"),
        P(None, "tensor", "dp"),
    )
    return jax.shard_map(
        functools.partial(local, dp=mesh.shape["dp"], tp=mesh.shape["tensor"]),
        mesh=mesh,
        in_specs=placed,
        out_specs=(
            P(None, "dp", None),
            P(None, "dp", None),
            P(),
            P(),
            P(None, "dp", "tensor"),
            P(None, "dp", "tensor"),
            P(None, "tensor", "dp"),
            P(),
            P(),
            P(None, "dp", None, "tensor"),
            P(None, "tensor", "dp"),
        ),
        check_vma=False,
    )
```

```python
import functools

import jax
import jax.numpy as jnp
from jax import lax
from jax.experimental import pallas as pl
from jax.experimental.pallas import tpu as pltpu
from jax.sharding import PartitionSpec as P

HD = 128
EPSILON = 1e-06
ROPE_BASE = 10000.0
BEST = lax.Precision.HIGHEST
F32 = jnp.float32
BF16 = jnp.bfloat16
VMEM_BYTES = 60 * 1024 * 1024


def nn(a, b):
    return lax.dot_general(a, b, (((1,), (0,)), ((), ())), preferred_element_type=F32)


def nt(a, b, precision=None):
    return lax.dot_general(
        a, b, (((1,), (1,)), ((), ())), preferred_element_type=F32, precision=precision
    )


def tn(a, b):
    return lax.dot_general(a, b, (((0,), (0,)), ((), ())), preferred_element_type=F32)


def lane_sums(values):
    ones = jnp.ones((8, values.shape[1]), F32)
    return nt(ones, values, BEST)


def run(body, name, grid, meta, ins, outs, scratch=(), flops=0):
    in_specs = []
    moved = 0
    for array, block, index in ins:
        if block is None:
            rank = array.ndim
            in_specs.append(pl.BlockSpec(array.shape, lambda *a, rank=rank: (0,) * rank))
        else:
            in_specs.append(pl.BlockSpec(block, index))
        moved += array.size * array.dtype.itemsize
    out_specs = []
    out_shape = []
    for shape, dtype, block, index in outs:
        if block is None:
            rank = len(shape)
            out_specs.append(pl.BlockSpec(shape, lambda *a, rank=rank: (0,) * rank))
        else:
            out_specs.append(pl.BlockSpec(block, index))
        out_shape.append(jax.ShapeDtypeStruct(shape, dtype))
        size = jnp.dtype(dtype).itemsize
        for extent in shape:
            size *= extent
        moved += size
    return pl.pallas_call(
        body,
        name=name,
        grid_spec=pltpu.PrefetchScalarGridSpec(
            num_scalar_prefetch=1,
            grid=grid,
            in_specs=in_specs,
            out_specs=out_specs,
            scratch_shapes=list(scratch),
        ),
        out_shape=out_shape,
        compiler_params=pltpu.CompilerParams(
            dimension_semantics=("arbitrary",) * len(grid), vmem_limit_bytes=VMEM_BYTES
        ),
        cost_estimate=pl.CostEstimate(flops=flops, bytes_accessed=moved, transcendentals=0),
    )(meta, *[array for array, _, _ in ins])


def pick(low_id, high_id, expert, low_value, high_value):
    zero = jnp.zeros_like(low_value)
    return jnp.where(
        low_id == expert, low_value, jnp.where(high_id == expert, high_value, zero)
    )


def two_slots(low_id, high_id, products):
    low_value = products[0]
    for expert in range(1, len(products) - 1):
        low_value = jnp.where(low_id == expert, products[expert], low_value)
    high_value = products[1]
    for expert in range(2, len(products)):
        high_value = jnp.where(high_id == expert, products[expert], high_value)
    return low_value, high_value


def turn(values, cosine, sine):
    return values * cosine + pltpu.roll(values, HD // 2, 1) * sine


def local(
    hidden_in,
    cotangent,
    lengths,
    dealing,
    attn_routes,
    ffn_routes,
    attn_gain,
    attn_router,
    kv_weight,
    query_weight,
    proj_weight,
    ffn_gain,
    ffn_router,
    expert_in,
    expert_out,
    *,
    dp,
    tp,
):
    seqs = dealing.shape[0]
    seq_len = cotangent.shape[1]
    slots = cotangent.shape[0]
    per = hidden_in.shape[1]
    width = hidden_in.shape[2]
    heads = query_weight.shape[2] // HD
    groups = heads
    parts = dp // groups
    ds = width // dp
    hw = heads * HD
    rows_all = seqs * seq_len
    rows = rows_all * 3 // 4
    rp = rows // parts
    blk = rp // groups
    experts = query_weight.shape[0]
    ff = expert_out.shape[1]
    scale = HD ** (-0.5)
    pieces = range(parts)

    index = lax.axis_index("dp")
    z = lax.axis_index("tensor")
    g = index // parts
    c = index % parts
    mine = ((z == 1) | (z == 2)).astype(jnp.int32)
    theirs = 1 - mine
    spots = [g, c, g, g ^ 1, g ^ 2, g ^ 3, mine, theirs]
    spots += [g ^ mine, g ^ theirs, g ^ (2 + mine), g ^ (2 + theirs)]
    spots += [g ^ (2 * mine), g ^ (2 * mine + 1), g ^ (2 * theirs), g ^ (2 * theirs + 1)]
    spots += [mine, theirs, 2 + mine, 2 + theirs]
    spots += [2 * mine, 2 * mine + 1, 2 * theirs, 2 * theirs + 1]
    meta = jnp.stack(spots).astype(jnp.int32)
    BY_CHUNK, BY_HALF, IN_ORDER, IN_HALVES = 8, 12, 16, 20

    def after(value, *others):
        return lax.optimization_barrier((value,) + others)[0]

    def both(a, b):
        return (a.astype(F32) + b.astype(F32)).astype(BF16)

    def by_group(value, mask):
        pairs = [(a, ((a // parts) ^ mask) * parts + a % parts) for a in range(dp)]
        return lax.ppermute(value, "dp", pairs)

    def by_part(value, mask):
        pairs = [(a, (a // parts) * parts + ((a % parts) ^ mask)) for a in range(dp)]
        return lax.ppermute(value, "dp", pairs)

    def to_next(value):
        pairs = [(a, a + 1) for a in range(dp) if a % parts < parts - 1]
        return lax.ppermute(value, "dp", pairs)

    def to_previous(value):
        pairs = [(a, a - 1) for a in range(dp) if a % parts > 0]
        return lax.ppermute(value, "dp", pairs)

    def by_z(value, mask):
        return lax.ppermute(value, "tensor", [(a, a ^ mask) for a in range(tp)])

    def sum_groups(value):
        value = value + by_group(value, 1)
        return value + by_group(value, 2)

    def sum_z(value):
        value = value + by_z(value, 1)
        return value + by_z(value, 3)

    def z_first(keep, send):
        return both(keep, by_z(send, 1))

    def z_second(half):
        return both(half, by_z(half, 3))

    def z_covered(keep, send, mask, cover):
        keep, got = held((keep, by_z(send, mask)), cover)
        return both(keep, got)

    def z_last(half):
        return half, by_z(half, 1)

    def wide_sum_z(keep, send):
        return z_last(z_second(z_first(keep, send)))

    def held(values, *others):
        return lax.optimization_barrier((tuple(values),) + others)[0]

    def reduce_groups(first, second, early=(), late=()):
        if early:
            first, second = held((tuple(first), tuple(second)), early)
        ra = by_group(first[3], 1)
        rb = by_group(second[3], 2)
        ax = by_group(first[1], 1)
        by = by_group(second[2], 2)
        along = held((both(first[2], ra), both(second[1], rb)), (ax, by), late)
        ay = by_group(along[0], 2)
        bx = by_group(along[1], 1)
        return (first[0], ax, ay), (second[0], bx, by), along, (ra, rb)

    def gather_groups(first, second, late=()):
        ax, bx = by_group(first, 1), by_group(second, 1)
        ay, by = by_group(first, 2), by_group(second, 2)
        along = held((ax, by), (bx, ay), late) if len(late) else (ax, by)
        ad, bd = by_group(along[0], 2), by_group(along[1], 1)
        return (first, ax, ay, ad), (second, bx, by, bd), along

    def row_of(offset):
        return lambda *a: (a[-1][2 + offset], 0)

    def at_row(m, spot, count):
        return pl.ds(pl.multiple_of(m[spot] * count, count), count)

    wide = ds % 128 == 0

    def nn_pieces(x, weights):
        if not wide:
            return [nn(x, w) for w in weights]
        value = nn(x, jnp.concatenate(weights, axis=1))
        return [value[:, s * ds : (s + 1) * ds] for s in pieces]

    def nt_pieces(x, weights):
        if not wide:
            return [nt(x, w) for w in weights]
        value = nt(x, jnp.concatenate(weights, axis=0))
        return [value[:, s * ds : (s + 1) * ds] for s in pieces]

    ends = jnp.cumsum(lengths)
    starts = ends - lengths
    inverse = jnp.sum(
        (dealing[None, :] == jnp.arange(seqs, dtype=jnp.int32)[:, None])
        * jnp.arange(seqs, dtype=jnp.int32)[None, :],
        axis=1,
    )

    table = jnp.concatenate([starts, lengths, inverse, c[None]]).astype(jnp.int32)

    def places(part):
        packed = part * rp + jnp.arange(rp, dtype=jnp.int32)
        begun = starts[None, :] <= packed[:, None]
        first = jnp.max(jnp.where(begun, starts[None, :], 0), axis=1)
        seq = jnp.sum(begun.astype(jnp.int32), axis=1) - 1
        return seq, packed - first, first

    seq, at, first = places(c)

    def slot_rows(m, j):
        return pl.ds(pl.multiple_of(m[2 * seqs + j] * seq_len, seq_len), seq_len)

    def part_rows(m, s):
        return pl.ds(pl.multiple_of((m[3 * seqs] ^ s) * rp, rp), rp)

    def block_rows(p, j):
        return pl.ds(pl.multiple_of((p * seqs + j) * per, per), per)

    def near_rows(m, j):
        shift = m[j] & 7
        return pl.ds(pl.multiple_of(m[j] - shift, 8), seq_len + 8), shift

    def pack_body(dealt, m, all_ref, *refs):
        outs = refs[:parts]
        source, packed, whole = refs[parts:]
        source[...] = all_ref[...].astype(F32)

        line = lax.broadcasted_iota(jnp.int32, (seq_len + 8, ds), 0)

        def one(j, carry):
            if dealt:
                whole[:seq_len, :] = source[slot_rows(m, j), :]
            else:
                for p in range(dp):
                    whole[p * per : (p + 1) * per, :] = source[block_rows(p, j), :]
            window, shift = near_rows(m, j)
            moved = pltpu.roll(whole[...], shift, 0)
            packed[window, :] = jnp.where(line < shift, packed[window, :], moved)
            return carry

        lax.fori_loop(0, seqs, one, 0)
        for s in pieces:
            outs[s][...] = packed[part_rows(m, s), :].astype(BF16)

    def pack(value, dealt, table):
        own = run(
            functools.partial(pack_body, dealt), "pack", (1,), table, [(value, None, None)],
            [((rp, ds), BF16, None, None)] * parts,
            [pltpu.VMEM((n, ds), F32) for n in (rows_all, rows + seq_len + 8, seq_len + 8)],
        )
        return [own[0]] + [by_part(own[s], s) for s in pieces[1:]]

    x_send = hidden_in.reshape(seqs * per, dp, ds).transpose(1, 0, 2)
    d_send = cotangent.reshape(slots * seq_len, dp, ds).transpose(1, 0, 2)
    x_all = lax.all_to_all(x_send, "dp", 0, 0, tiled=True).reshape(rows_all, ds)
    x_pieces = pack(x_all, False, table)
    def spread(vector):
        tall = vector.reshape((groups, parts, ds) + vector.shape[1:])[g]
        return jnp.stack([tall[c ^ s] for s in pieces])

    gain_a = spread(attn_gain)[:, None, :]
    gain_f = spread(ffn_gain)[:, None, :]
    pad = ((0, 0), (0, 8 - experts), (0, 0))
    router_a = jnp.pad(spread(attn_router).transpose(0, 2, 1), pad)
    router_f = jnp.pad(spread(ffn_router).transpose(0, 2, 1), pad)

    in_own = after(expert_in, x_send).swapaxes(1, 2)
    wq = [query_weight] + [by_part(query_weight, s) for s in pieces[1:]]
    wkv = [kv_weight] + [by_part(kv_weight, s) for s in pieces[1:]]
    wp = [proj_weight] + [by_part(proj_weight, s) for s in pieces[1:]]
    wo = [expert_out] + [by_part(expert_out, s) for s in pieces[1:]]
    wi = [in_own] + [by_part(in_own, s) for s in pieces[1:]]

    routes = jnp.concatenate(
        [attn_routes.reshape(rows_all, 2), ffn_routes.reshape(rows_all, 2)], axis=1
    )
    here = (seq * seq_len + at)[:, None] == jnp.arange(rows_all, dtype=jnp.int32)[None, :]
    mine = jnp.dot(here.astype(BF16), routes.astype(BF16), preferred_element_type=F32)
    low_a, high_a = jnp.minimum(mine[:, 0], mine[:, 1]), jnp.maximum(mine[:, 0], mine[:, 1])
    low_f, high_f = jnp.minimum(mine[:, 2], mine[:, 3]), jnp.maximum(mine[:, 2], mine[:, 3])
    window = (first - c * rp + seq_len).astype(F32)
    nil = jnp.zeros_like(window)
    sel = jnp.stack([low_a, high_a, low_f, high_f, window, nil, nil, nil], axis=1)
    half = HD // 2
    frequency = ROPE_BASE ** (-2.0 * jnp.arange(half, dtype=F32) / HD)
    angles = at.astype(F32)[:, None] * frequency[None, :]
    cosine = jnp.concatenate([jnp.cos(angles)] * 2, axis=1)
    sine = jnp.sin(angles)
    sine = jnp.concatenate([-sine, sine], axis=1)

    def gate_columns(stats, low_id, high_id):
        rms = lax.rsqrt(stats[experts] / width + EPSILON)
        ids = jnp.arange(experts, dtype=F32)[:, None]
        logits = stats[:experts]
        low_logit = jnp.sum(jnp.where(low_id[None] == ids, logits, 0.0), axis=0) * rms
        high_logit = jnp.sum(jnp.where(high_id[None] == ids, logits, 0.0), axis=0) * rms
        gap = low_logit - high_logit
        low_gate, high_gate = jax.nn.sigmoid(gap), jax.nn.sigmoid(-gap)
        zero = jnp.zeros_like(rms)
        flat = jnp.stack([rms, low_gate, high_gate, gap, zero, zero, zero, zero])
        return flat, flat.T

    tile = 256

    def qkv_body(m, *refs):
        x_refs = refs[:parts]
        gain_ref, router_ref = refs[parts : parts + 2]
        q_refs = refs[parts + 2 : 2 * parts + 2]
        kv_refs = refs[2 * parts + 2 : 3 * parts + 2]
        sel_ref = refs[3 * parts + 2]
        outs = refs[3 * parts + 3 : 3 * parts + 11]
        stats_ref, scr = refs[3 * parts + 11 :]
        us = []
        logits = jnp.zeros((8, tile), F32)
        squares = jnp.zeros((8, tile), F32)
        for s in pieces:
            xf = x_refs[s][...].astype(F32)
            us.append((xf * gain_ref[s]).astype(BF16))
            logits += nt(router_ref[s], us[s])
            squares += lane_sums(xf * xf)
        line = lax.broadcasted_iota(jnp.int32, (8, tile), 0)
        stats_ref[...] = jnp.where(line < experts, logits, squares)
        products = []
        for e in range(experts):
            products.append(sum(nn(us[s], q_refs[s][e]) for s in pieces))
        low, high = two_slots(sel_ref[:, 0:1], sel_ref[:, 1:2], products)
        keys = sum(nn(us[s], kv_refs[s][0]) for s in pieces)
        values = sum(nn(us[s], kv_refs[s][1]) for s in pieces)
        for k, value in enumerate((low, high, keys, values)):
            value = value.astype(BF16)
            for h in range(heads):
                scr[h, :, k * HD : (k + 1) * HD] = value[:, h * HD : (h + 1) * HD]
        for r in range(4):
            block = scr[m[2 + r]]
            outs[2 * r][...] = block[:, : 2 * HD]
            outs[2 * r + 1][...] = block[:, 2 * HD :]

    ins = [(x, (tile, ds), lambda i, m: (i, 0)) for x in x_pieces]
    ins += [(gain_a, None, None), (router_a, None, None)]
    ins += [(w, None, None) for w in wq + wkv]
    ins += [(sel, (tile, 8), lambda i, m: (i, 0))]
    outs = [((rp, 2 * HD), BF16, (tile, 2 * HD), lambda i, m: (i, 0))] * 8
    outs += [((8, rp), F32, (8, tile), lambda i, m: (0, i))]
    qkv = run(
        qkv_body, "qkv", (rp // tile,), after(meta, wo[1:], wp[1:]), ins, outs,
        [pltpu.VMEM((heads, tile, 4 * HD), BF16)],
        flops=2 * rp * (experts + 2) * parts * ds * hw,
    )
    stats_a = sum_groups(after(qkv[8], wi[1:]))
    flat_a, cols_a = gate_columns(stats_a, low_a, high_a)
    q_sum, kv_sum, _, far = reduce_groups(qkv[0:8:2], qkv[1:8:2], late=cols_a)

    d_all = lax.all_to_all(d_send, "dp", 0, 0, tiled=True).reshape(rows_all, ds)
    d_pieces = pack(d_all, True, after(table, far[0]))

    def rows_pair(refs):
        return jnp.concatenate([ref[...] for ref in refs], axis=0)

    def dhidden_body(m, *refs):
        d_refs = refs[: 2 * parts]
        w_refs, sel_refs = refs[2 * parts : 3 * parts], refs[3 * parts : 3 * parts + 2]
        outs = refs[3 * parts + 2 :]
        ids = rows_pair(sel_refs)
        rows_of = [rows_pair(d_refs[2 * s : 2 * s + 2]) for s in pieces]
        products = []
        for e in range(experts):
            products.append(sum(nt(rows_of[s], w_refs[s][e]) for s in pieces))
        low, high = two_slots(ids[:, 2:3], ids[:, 3:4], products)
        low, high = low.astype(BF16), high.astype(BF16)
        for step, pair in enumerate(((3, 1), (2, 0))):

            @pl.when(pl.program_id(0) == step)
            def _():
                for k, r in enumerate(pair):
                    outs[2 * r][...] = low[k * blk : (k + 1) * blk]
                    outs[2 * r + 1][...] = high[k * blk : (k + 1) * blk]

    def dhidden(meta):
        spots = [lambda i, m: (m[5 - i], 0), lambda i, m: (m[3 - i], 0)]
        ins = [(d, (blk, ds), spot) for d in d_pieces for spot in spots]
        ins += [(w, None, None) for w in wo]
        ins += [(sel, (blk, 8), spot) for spot in spots]
        outs = [((blk, ff), BF16, None, None)] * 8
        return run(
            dhidden_body, "dhidden", (2,), meta, ins, outs,
            flops=2 * rp * experts * parts * ds * ff,
        )

    dh = dhidden(meta)

    def rope_body(m, a0, a1, a2, b0, b1, b2, cols, cos_ref, sin_ref, q_ref, kv_ref):
        rms = cols[:, 0:1]
        cos, sin = cos_ref[...], sin_ref[...]
        q = (a0[...].astype(F32) + a1[...].astype(F32) + a2[...].astype(F32)) * rms
        kv = (b0[...].astype(F32) + b1[...].astype(F32) + b2[...].astype(F32)) * rms
        q_ref[:, :HD] = turn(q[:, :HD], cos, sin).astype(BF16)
        q_ref[:, HD:] = turn(q[:, HD:], cos, sin).astype(BF16)
        kv_ref[:, :HD] = turn(kv[:, :HD], cos, sin).astype(BF16)
        kv_ref[:, HD:] = kv[:, HD:].astype(BF16)

    ins = [(v, (tile, 2 * HD), lambda i, m: (i, 0)) for v in q_sum + kv_sum]
    ins += [(cols_a, (tile, 8), lambda i, m: (i, 0))]
    ins += [(v, (tile, HD), lambda i, m: (i, 0)) for v in (cosine, sine)]
    outs = [((rp, 2 * HD), BF16, (tile, 2 * HD), lambda i, m: (i, 0))] * 2
    q_rot, kv_rot = run(rope_body, "rope", (rp // tile,), after(meta, dh[0]), ins, outs)
    halo = to_next(kv_rot[rp - seq_len :])

    qt = 128
    span = seq_len + qt

    def window_mask(i, low_key):
        u = i * qt + lax.broadcasted_iota(jnp.int32, (qt, span), 1)
        t = seq_len + i * qt + lax.broadcasted_iota(jnp.int32, (qt, span), 0)
        return (u >= low_key.astype(jnp.int32)) & (u <= t)

    def softmax_of(query, key, allowed):
        score = jnp.where(allowed, nt(query, key) * scale, -1e30)
        top = jnp.max(score, axis=1, keepdims=True)
        raised = jnp.exp(score - top)
        return raised / jnp.sum(raised, axis=1, keepdims=True)

    def attend_body(m, q_ref, kv_ref, halo_ref, sel_ref, cols, ga, gb, ma, mb, ext):
        i = pl.program_id(0)

        @pl.when(i == 0)
        def _():
            ext[:seq_len, :] = halo_ref[...]
            ext[seq_len:, :] = kv_ref[...]

        near = ext[pl.ds(pl.multiple_of(i * qt, qt), span), :]
        allowed = window_mask(i, sel_ref[:, 4:5])
        for k, (g_ref, m_ref) in enumerate(((ga, ma), (gb, mb))):
            probs = softmax_of(q_ref[:, k * HD : (k + 1) * HD], near[:, :HD], allowed)
            mixed = nn(probs.astype(BF16), near[:, HD:]).astype(BF16)
            m_ref[...] = mixed
            g_ref[...] = (mixed.astype(F32) * cols[:, 1 + k : 2 + k]).astype(BF16)

    def qrow(i, m):
        return (i, 0)

    ins = [(q_rot, (qt, 2 * HD), qrow), (kv_rot, None, None), (halo, None, None)]
    ins += [(sel, (qt, 8), qrow), (cols_a, (qt, 8), qrow)]
    outs = [((rp, HD), BF16, (qt, HD), qrow)] * 4
    gated_a, gated_b, mixed_a, mixed_b = run(
        attend_body, "attend", (rp // qt,), meta, ins, outs,
        [pltpu.VMEM((seq_len + rp, 2 * HD), BF16)],
        flops=8 * rp * span * HD,
    )
    gm_a, gm_b, _ = gather_groups(gated_a, gated_b)
    zr = rp // 2
    hold = [((parts, zr, ds), BF16, None, None)] * 2

    def store_halves(i, refs, s, value):
        @pl.when(i == 0)
        def _():
            refs[1][s] = value

        @pl.when(i == 1)
        def _():
            refs[0][s] = value

    def proj_body(m, *refs):
        a_refs, b_refs = refs[:4], refs[4:8]
        sel_ref = refs[8]
        w_refs = refs[9 : 9 + parts]
        outs, xs = refs[9 + parts : 11 + parts], refs[11 + parts]
        for r in range(4):
            lanes = pl.ds(pl.multiple_of(m[2 + r] * HD, HD), HD)
            for e in range(experts):
                xs[e, :, lanes] = pick(
                    sel_ref[:, 0:1], sel_ref[:, 1:2], e, a_refs[r][...], b_refs[r][...]
                )
        acc = nn_pieces(xs[0], [w[0] for w in w_refs])
        for e in range(1, experts):
            for s, value in enumerate(nn_pieces(xs[e], [w[e] for w in w_refs])):
                acc[s] += value
        for s in pieces:
            store_halves(pl.program_id(0), outs, s, acc[s].astype(BF16))

    def project(meta):
        half = lambda i, m: (m[7 - i], 0)
        ins = [(v, (zr, HD), half) for v in gm_a + gm_b]
        ins += [(sel, (zr, 8), half)]
        ins += [(w, None, None) for w in wp]
        return run(
            proj_body, "proj", (2,), meta, ins, hold,
            [pltpu.VMEM((experts, zr, hw), BF16)],
            flops=4 * zr * experts * hw * parts * ds,
        )

    proj_halves = project(meta)
    dh_a, dh_b = held((dh[0:8:2], dh[1:8:2]), gm_a[3], gm_b[3])
    ra, rb = by_group(dh_a[3], 1), by_group(dh_b[3], 2)
    ax, by = by_group(dh_a[1], 1), by_group(dh_b[2], 2)
    half = z_second(z_first(*proj_halves))
    near = held((both(dh_a[2], ra), both(dh_b[1], rb)), (ax, by), half)
    dh_a, dh_b = (dh_a[0], ax, by_group(near[0], 2)), (dh_b[0], by_group(near[1], 1), by)
    attn_totals = list(z_last(half))

    def norm_body(m, *refs):
        t_refs = refs[: 2]
        x_refs = refs[2 : 2 + parts]
        gain_ref, router_ref, after_ref, u_ref, stats_ref = refs[2 + parts :]
        for k in range(2):
            span_k = at_row(m, IN_ORDER + k, zr)
            for s in pieces:
                after_ref[s, span_k, :] = x_refs[s][span_k, :].astype(F32) + t_refs[k][s].astype(F32)
        logits = jnp.zeros((8, rp), F32)
        squares = jnp.zeros((8, rp), F32)
        for s in pieces:
            af = after_ref[s]
            u = (af * gain_ref[s]).astype(BF16)
            u_ref[s] = u
            logits += nt(router_ref[s], u)
            squares += lane_sums(af * af)
        line = lax.broadcasted_iota(jnp.int32, (8, rp), 0)
        stats_ref[...] = jnp.where(line < experts, logits, squares)

    ins = [(t, None, None) for t in attn_totals + x_pieces]
    ins += [(gain_f, None, None), (router_f, None, None)]
    outs = [
        ((parts, rp, ds), F32, None, None),
        ((parts, rp, ds), BF16, None, None),
        ((8, rp), F32, None, None),
    ]
    after_rows, u_f, stats_part = run(norm_body, "norm", (1,), meta, ins, outs)
    def up_body(m, *refs):
        u_refs, w_refs = refs[:2], refs[2 : 2 + parts]
        sel_refs = refs[2 + parts : 4 + parts]
        outs = refs[4 + parts :]
        ids = rows_pair(sel_refs)
        rows_of = [jnp.concatenate([u[s] for u in u_refs], axis=0) for s in pieces]
        products = []
        for e in range(experts):
            products.append(sum(nn(rows_of[s], w_refs[s][e, 0]) for s in pieces))
        low, high = two_slots(ids[:, 2:3], ids[:, 3:4], products)
        low, high = low.astype(BF16), high.astype(BF16)
        for k in range(2):
            outs[2 * k][0] = low[k * blk : (k + 1) * blk]
            outs[2 * k + 1][0] = high[k * blk : (k + 1) * blk]

    def up(pair, meta):
        def block_of(r):
            return lambda j, m: (0, m[2 + r], 0)

        ins = [(u_f, (parts, blk, ds), block_of(r)) for r in pair]
        ins += [(w, (experts, 1, ds, ff), lambda j, m: (0, j, 0, 0)) for w in wi]
        ins += [(sel, (blk, 8), row_of(r)) for r in pair]
        outs = [((2, blk, ff), BF16, (1, blk, ff), lambda j, m: (j, 0, 0))] * 4
        return run(
            up_body, "up", (2,), meta, ins, outs, flops=8 * blk * experts * parts * ds * ff
        )

    up_far = up((3, 1), after(meta, dh_a[2], dh_b[1]))
    up_near = up((2, 0), after(meta, up_far[0]))
    gu_a, gu_b, _, far = reduce_groups(
        (up_near[2], up_far[2], up_near[0], up_far[0]),
        (up_near[3], up_far[3], up_near[1], up_far[1]),
    )

    stats_f = sum_groups(after(stats_part, far))
    flat_f, cols_f = gate_columns(stats_f, low_f, high_f)

    mt_rows = blk // 3

    def mid_body(m, *refs):
        gu = (refs[0:3], refs[3:6])
        dhr = (refs[6:9], refs[9:12])
        cols = refs[12]
        acts, grads, dots = refs[13:15], refs[15:17], refs[17]
        rms = cols[:, 0:1]
        column = lax.broadcasted_iota(jnp.int32, (mt_rows, 8), 1)
        found = []
        inner = jnp.zeros((mt_rows, 1), F32)
        for k in range(2):
            gate = cols[:, 1 + k : 2 + k]
            gp = sum(v[0].astype(F32) for v in gu[k]) * rms
            up_pre = sum(v[1].astype(F32) for v in gu[k]) * rms
            raw = sum(v[...].astype(F32) for v in dhr[k])
            sg = jax.nn.sigmoid(gp)
            act = (gp * sg * up_pre).astype(BF16).astype(F32)
            grad = raw * gate
            dgp = (grad * up_pre * sg * (1.0 + gp * (1.0 - sg))).astype(BF16)
            dup = (grad * gp * sg).astype(BF16)
            acts[k][...] = (act * gate).astype(BF16)
            grads[k][0] = dgp
            grads[k][1] = dup
            found.append(jnp.sum(act * raw, axis=1, keepdims=True))
            inner += jnp.sum(
                dgp.astype(F32) * gp + dup.astype(F32) * up_pre, axis=1, keepdims=True
            )
        zero = jnp.zeros((mt_rows, 8), F32)
        for k, value in enumerate(found + [inner]):
            zero = jnp.where(column == k, value, zero)
        dots[...] = zero

    rows_3 = lambda i, m: (0, i, 0)
    rows_2 = lambda i, m: (i, 0)
    ins = [(v, (2, mt_rows, ff), rows_3) for v in gu_a + gu_b]
    ins += [(v, (mt_rows, ff), rows_2) for v in dh_a + dh_b]
    ins += [(cols_f, (mt_rows, 8), lambda i, m: (3 * m[2] + i, 0))]
    outs = [((blk, ff), BF16, (mt_rows, ff), rows_2)] * 2
    outs += [((2, blk, ff), BF16, (2, mt_rows, ff), rows_3)] * 2
    outs += [((blk, 8), F32, (mt_rows, 8), rows_2)]
    act_a, act_b, grad_a, grad_b, dots_f = run(mid_body, "mid", (3,), meta, ins, outs)
    gg_a, gg_b, gg_along = gather_groups(grad_a, grad_b, late=(act_a,))
    dots_f = dots_f.T

    def dx_body(m, *refs):
        a_refs, b_refs = refs[:2], refs[2:4]
        w_refs = refs[4 : 4 + parts]
        sel_refs = refs[4 + parts : 6 + parts]
        keep_ref, send_ref, acc, xs = refs[6 + parts :]
        e = pl.program_id(0)
        expert = e.astype(F32)

        @pl.when(e == 0)
        def _():
            acc[...] = jnp.zeros_like(acc)

        for j in range(2):
            for k in range(2):
                ids = sel_refs[k]
                xs[k * blk : (k + 1) * blk, :] = pick(
                    ids[:, 2:3], ids[:, 3:4], expert, a_refs[k][j], b_refs[k][j]
                )
            for s, value in enumerate(nt_pieces(xs[...], [w[0, j] for w in w_refs])):
                acc[s] += value

        @pl.when(e == experts - 1)
        def _():
            keep_ref[...] = acc[:, at_row(m, 6, blk), :].astype(BF16)
            send_ref[...] = acc[:, at_row(m, 7, blk), :].astype(BF16)

    def dx(pair, meta):
        ins = [(v[r], None, None) for v in (gg_a, gg_b) for r in pair]
        ins += [(w, (1, 2, ds, ff), lambda e, m: (e, 0, 0, 0)) for w in wi]
        ins += [(sel, (blk, 8), row_of(r)) for r in pair]
        return run(
            dx_body, "dx", (experts,), meta, ins, [((parts, blk, ds), BF16, None, None)] * 2,
            [pltpu.VMEM((parts, 2 * blk, ds), F32), pltpu.VMEM((2 * blk, ff), BF16)],
            flops=8 * blk * experts * parts * ds * ff,
        )

    dx_near = dx((0, 1), after(meta, gg_a[2], gg_b[2]))
    dx_far = dx((2, 3), meta)
    dots_f = sum_z(dots_f)
    dots_f = jnp.stack([dots_f, held([by_group(dots_f, 1)], dx_near[0])[0]])
    dots_f = jnp.concatenate([dots_f, held([by_group(dots_f, 2)], dx_far[0])[0]])
    near_half = z_first(*dx_near)
    near_half = z_covered(near_half, near_half, 3, dx_far[0])
    far_half = z_first(*dx_far)

    act_a, act_b, _ = lax.optimization_barrier((act_a, act_b, far_half))
    ag_a = [act_a, by_group(act_a, 1), by_group(act_a, 2)]
    ag_b = [act_b, by_group(act_b, 1), by_group(act_b, 2)]
    dots_f = jnp.take(dots_f, g ^ jnp.arange(4, dtype=jnp.int32), axis=0)
    dots_f = dots_f.transpose(1, 0, 2).reshape(8, rp)

    def back_columns(flat, dots, low_id, high_id):
        delta = flat[1] * flat[2] * (dots[0] - dots[1])
        inner = (dots[2] + delta * flat[3]) / width
        ids = jnp.arange(experts, dtype=F32)[:, None]
        dlogit = jnp.where(low_id[None] == ids, delta[None], 0.0) - jnp.where(
            high_id[None] == ids, delta[None], 0.0
        )
        zero = jnp.zeros((1, rp), F32)
        return jnp.concatenate(
            [dlogit, inner[None], flat[0:1]] + [zero] * (6 - experts), axis=0
        ).T

    back_f = back_columns(flat_f, dots_f, low_f, high_f)


    def exchange(sums):
        return [sums[0]] + [by_part(sums[s], s) for s in pieces[1:]]

    def add_up(got):
        return sum(v.astype(F32) for v in got)

    ffn_input = (after_rows * flat_f[0][None, :, None] * gain_f).astype(BF16)

    def t_left(xs, value):
        if not wide:
            return [tn(x, value) for x in xs]
        total = tn(jnp.concatenate(xs, axis=1), value)
        return [total[s * ds : (s + 1) * ds] for s in pieces]

    def t_right(value, xs):
        if not wide:
            return [tn(value, x) for x in xs]
        total = tn(value, jnp.concatenate(xs, axis=1))
        return [total[:, s * ds : (s + 1) * ds] for s in pieces]

    def sort_rows(m, sel_ref, x_refs, xs, ids):
        for r in range(4):
            src, here_r = at_row(m, 2 + r, blk), slice(r * blk, (r + 1) * blk)
            for s in pieces:
                xs[s, here_r, :] = x_refs[s][src, :]
            ids[here_r, :] = sel_ref[src, :]

    def dwin_body(m, *refs):
        a_refs, b_refs = refs[:4], refs[4:8]
        sel_ref, x_ref = refs[8:10]
        outs = refs[10 : 10 + parts]
        xs, ids, mt = refs[10 + parts :]
        e = pl.program_id(0)

        @pl.when(e == 0)
        def _():
            sort_rows(m, sel_ref, [x_ref.at[s] for s in pieces], xs, ids)

        expert = e.astype(F32)
        for r in range(4):
            here_r = slice(r * blk, (r + 1) * blk)
            mt[here_r, :] = pick(
                ids[here_r, 2:3], ids[here_r, 3:4], expert, a_refs[r][0], b_refs[r][0]
            )
        for s, value in enumerate(t_left([xs[s] for s in pieces], mt[...])):
            outs[s][0] = value.astype(BF16)

    def dwin(j, meta):
        ins = [(v, (1, blk, ff), lambda e, m: (j, 0, 0)) for v in gg_a + gg_b]
        ins += [(sel, None, None), (ffn_input, None, None)]
        outs = [((experts, ds, ff), BF16, (1, ds, ff), lambda e, m: (e, 0, 0))] * parts
        return run(
            dwin_body, "dwin", (experts,), meta, ins, outs,
            [pltpu.VMEM((parts, rp, ds), BF16), pltpu.VMEM((rp, 8), F32), pltpu.VMEM((rp, ff), BF16)],
            flops=2 * rp * experts * parts * ds * ff,
        )

    def fold_body(m, *refs):
        out_ref = refs[2 * parts]
        for j in range(2):
            total = refs[j * parts][0].astype(F32)
            for ref in refs[j * parts + 1 : (j + 1) * parts]:
                total = total + ref[0].astype(F32)
            out_ref[0, :, j, :] = total

    def fold(sums, meta):
        ins = [(v, (1, ds, ff), lambda e, m: (e, 0, 0)) for half in sums for v in half]
        outs = [((experts, ds, 2, ff), F32, (1, ds, 2, ff), lambda e, m: (e, 0, 0, 0))]
        return run(fold_body, "fold", (experts,), meta, ins, outs)[0]

    dwin_gate = dwin(0, after(meta, far_half))
    dx_totals = z_last(near_half) + z_last(z_covered(far_half, far_half, 3, dwin_gate[0]))

    def norm_back_body(low_precision_out, m, *refs):
        sums = 4 if low_precision_out else 2
        t_refs, after_ref, refs = refs[:sums], refs[sums], refs[sums + 1 :]
        ups = parts if low_precision_out else 1
        up_refs = refs[:ups]
        gain_ref, router_ref, back = refs[ups : 3 + ups]
        outs = refs[3 + ups :]
        small = outs[-1]
        for s in pieces:
            gain = gain_ref[s]
            router = router_ref[s].astype(F32)
            gain_sum = jnp.zeros((1, ds), F32)
            router_sum = [jnp.zeros((1, ds), F32)] * experts
            for r in range(4):
                span_r = at_row(m, (BY_CHUNK if low_precision_out else IN_HALVES) + r, blk)
                up_value = up_refs[s][span_r, :] if low_precision_out else up_refs[0][s, span_r, :]
                x = after_ref[s, span_r, :].astype(F32)
                cols = back[span_r, :]
                rms = cols[:, experts + 1 : experts + 2]
                if low_precision_out:
                    grad = t_refs[r][s].astype(F32)
                else:
                    grad = t_refs[r // 2][s, (r % 2) * blk : (r % 2 + 1) * blk, :].astype(F32)
                for e in range(experts):
                    grad += cols[:, e : e + 1] * router[e : e + 1]
                normed = x * rms
                token = (normed * gain).astype(BF16).astype(F32)
                gain_sum += jnp.sum(grad * normed, axis=0, keepdims=True)
                for e in range(experts):
                    router_sum[e] = router_sum[e] + jnp.sum(
                        token * cols[:, e : e + 1], axis=0, keepdims=True
                    )
                dn = grad * gain
                total = up_value.astype(F32) + rms * (
                    dn - normed * cols[:, experts : experts + 1]
                )
                if low_precision_out:
                    outs[0][s, span_r, :] = total
                    outs[1][s, span_r, :] = total.astype(BF16)
                else:
                    outs[s][span_r, :] = total.astype(BF16)
            for e in range(experts):
                small[e, s] = router_sum[e][0]
            small[experts, s] = gain_sum[0]

    ins = [(t, None, None) for t in dx_totals]
    ins += [(after_rows, None, None)] + [(d, None, None) for d in d_pieces]
    ins += [(gain_f, None, None), (router_f, None, None), (back_f, None, None)]
    outs = [
        ((parts, rp, ds), F32, None, None),
        ((parts, rp, ds), BF16, None, None),
        ((experts + 1, parts, ds), F32, None, None),
    ]
    dafter, dafter_low, small_f = run(
        functools.partial(norm_back_body, True), "norm_back", (1,),
        after(meta, dwin_gate[0], ag_a[1:], ag_b[1:]), ins, outs,
    )

    def dmix_body(m, *refs):
        d_ref = refs[0]
        w_refs = refs[1 : 1 + parts]
        sel_ref = refs[1 + parts]
        outs = refs[2 + parts : 10 + parts]
        scr = refs[10 + parts]
        products = []
        for e in range(experts):
            products.append(sum(nt(d_ref[s], w_refs[s][e]) for s in pieces))
        low, high = two_slots(sel_ref[:, 0:1], sel_ref[:, 1:2], products)
        for k, value in enumerate((low, high)):
            value = value.astype(BF16)
            for h in range(heads):
                scr[h, :, k * HD : (k + 1) * HD] = value[:, h * HD : (h + 1) * HD]
        for r in range(4):
            block = scr[m[2 + r]]
            outs[2 * r][...] = block[:, :HD]
            outs[2 * r + 1][...] = block[:, HD:]

    ins = [(dafter_low, (parts, tile, ds), lambda i, m: (0, i, 0))]
    ins += [(w, None, None) for w in wp]
    ins += [(sel, (tile, 8), lambda i, m: (i, 0))]
    outs = [((rp, HD), BF16, (tile, HD), lambda i, m: (i, 0))] * 8
    dm = run(
        dmix_body, "dmix", (rp // tile,), meta, ins, outs,
        [pltpu.VMEM((heads, tile, 2 * HD), BF16)],
        flops=2 * rp * experts * parts * ds * hw,
    )
    dwin_up = dwin(1, after(meta, dm[0]))
    dm_a, dm_b, _, _ = reduce_groups(dm[0:8:2], dm[1:8:2], late=dwin_up[0])
    along = held((ag_a[1], ag_b[2]), dm_a[2], dm_b[1])
    ag_a, ag_b = ag_a + [by_group(along[0], 2)], ag_b + [by_group(along[1], 1)]

    def attend_back_body(m, *refs):
        q_ref, kv_ref, halo_ref, sel_ref, cols, cos_ref, sin_ref = refs[:7]
        d_refs = (refs[7:10], refs[10:13])
        mix_refs = refs[13:15]
        dq_ref, own_ref, far_ref, dots_ref, ext, acc = refs[15:]
        i = pl.program_id(0)

        @pl.when(i == 0)
        def _():
            ext[:seq_len, :] = halo_ref[...]
            ext[seq_len:, :] = kv_ref[...]
            acc[...] = jnp.zeros_like(acc)

        near_rows = pl.ds(pl.multiple_of(i * qt, qt), span)
        near = ext[near_rows, :]
        allowed = window_mask(i, sel_ref[:, 4:5])
        line = lax.broadcasted_iota(jnp.int32, (8, qt), 0)
        inner = jnp.zeros((qt, HD), F32)
        found = []
        dk = jnp.zeros((span, HD), F32)
        dv = jnp.zeros((span, HD), F32)
        for k in range(2):
            query = q_ref[:, k * HD : (k + 1) * HD]
            probs = softmax_of(query, near[:, :HD], allowed)
            raw = sum(v[...].astype(F32) for v in d_refs[k])
            dmixed = (raw * cols[:, 1 + k : 2 + k]).astype(BF16)
            found.append(raw * mix_refs[k][...].astype(F32))
            dv += tn(probs.astype(BF16), dmixed)
            dprob = nt(dmixed, near[:, HD:])
            rest = jnp.sum(probs * dprob, axis=1, keepdims=True)
            dscore = (probs * (dprob - rest)).astype(BF16)
            dk += tn(dscore, query) * scale
            dquery = nn(dscore, near[:, :HD]) * scale
            inner += dquery * query.astype(F32)
            dq_ref[:, k * HD : (k + 1) * HD] = turn(dquery, cos_ref[...], -sin_ref[...]).astype(BF16)
        acc[near_rows, :HD] += dk
        acc[near_rows, HD:] += dv
        dots_ref[...] = jnp.where(
            line == 0, lane_sums(found[0]), jnp.where(line == 1, lane_sums(found[1]), lane_sums(inner))
        )

        @pl.when(i == rp // qt - 1)
        def _():
            far_ref[...] = acc[:seq_len, :]
            own_ref[...] = acc[seq_len:, :]

    ins = [(q_rot, (qt, 2 * HD), qrow), (kv_rot, None, None), (halo, None, None)]
    ins += [(sel, (qt, 8), qrow), (cols_a, (qt, 8), qrow)]
    ins += [(cosine, (qt, HD), qrow), (sine, (qt, HD), qrow)]
    ins += [(v, (qt, HD), qrow) for v in dm_a + dm_b + (mixed_a, mixed_b)]
    outs = [
        ((rp, 2 * HD), BF16, (qt, 2 * HD), qrow),
        ((rp, 2 * HD), F32, None, None),
        ((seq_len, 2 * HD), F32, None, None),
        ((8, rp), F32, (8, qt), lambda i, m: (0, i)),
    ]
    dq, dkv_own, dkv_far, dots_q = run(
        attend_back_body, "attend_back", (rp // qt,), meta, ins, outs,
        [pltpu.VMEM((seq_len + rp, 2 * HD), BF16), pltpu.VMEM((seq_len + rp, 2 * HD), F32)],
        flops=20 * rp * span * HD,
    )
    dkv_in = to_previous(dkv_far)

    def dkv_body(m, own_ref, in_ref, kv_ref, cos_ref, sin_ref, out_ref, dots_ref):
        head = rp - seq_len
        for rows_here in (slice(0, head), slice(head, rp)):
            value = own_ref[rows_here, :]
            if rows_here.start == head:
                value = value + in_ref[...]
            out_ref[rows_here, :HD] = turn(
                value[:, :HD], cos_ref[rows_here, :], -sin_ref[rows_here, :]
            ).astype(BF16)
            out_ref[rows_here, HD:] = value[:, HD:].astype(BF16)
            dots_ref[:, rows_here] = lane_sums(value * kv_ref[rows_here, :].astype(F32))

    ins = [(v, None, None) for v in (dkv_own, dkv_in, kv_rot, cosine, sine)]
    outs = [((rp, 2 * HD), BF16, None, None), ((8, rp), F32, None, None)]
    got_in = [exchange(dwin_gate), exchange(held(dwin_up, dm_a[2], dm_b[1]))]
    dkv, dots_kv = run(
        dkv_body, "dkv", (1,), after(meta, ag_a[3], ag_b[3]), ins, outs
    )
    third = jnp.arange(8)[:, None] == 2
    def down_body(m, *refs):
        a_refs, b_refs = refs[:4], refs[4:8]
        sel_ref, d_refs = refs[8], refs[9 : 9 + parts]
        w_refs = refs[9 + parts : 9 + 2 * parts]
        keep_ref, send_ref = refs[9 + 2 * parts : 11 + 2 * parts]
        outs = refs[11 + 2 * parts : 11 + 3 * parts]
        acc, xs, ids, mt = refs[11 + 3 * parts :]
        e = pl.program_id(0)

        @pl.when(e == 0)
        def _():
            acc[...] = jnp.zeros_like(acc)
            sort_rows(m, sel_ref, d_refs, xs, ids)

        expert = e.astype(F32)
        for r in range(4):
            here_r = slice(r * blk, (r + 1) * blk)
            mt[here_r, :] = pick(
                ids[here_r, 2:3], ids[here_r, 3:4], expert, a_refs[r][...], b_refs[r][...]
            )
        for s, value in enumerate(nn_pieces(mt[...], [w[0] for w in w_refs])):
            acc[s] += value
        for s, value in enumerate(t_right(mt[...], [xs[s] for s in pieces])):
            outs[s][0] = value.astype(BF16)

        @pl.when(e == experts - 1)
        def _():
            keep_ref[...] = acc[:, at_row(m, 6, 2 * blk), :].astype(BF16)
            send_ref[...] = acc[:, at_row(m, 7, 2 * blk), :].astype(BF16)

    def down(meta):
        spot = lambda e, m: (e, 0, 0)
        ins = [(v, None, None) for v in ag_a + ag_b]
        ins += [(sel, None, None)] + [(d, None, None) for d in d_pieces]
        ins += [(w, (1, ff, ds), spot) for w in wo]
        outs = [((parts, 2 * blk, ds), BF16, None, None)] * 2
        outs += [((experts, ff, ds), BF16, (1, ff, ds), spot)] * parts
        return run(
            down_body, "down", (experts,), meta, ins, outs,
            [
                pltpu.VMEM((parts, rp, ds), F32),
                pltpu.VMEM((parts, rp, ds), BF16),
                pltpu.VMEM((rp, 8), F32),
                pltpu.VMEM((rp, ff), BF16),
            ],
            flops=4 * rp * experts * parts * ds * ff,
        )

    def dwproj_body(m, *refs):
        a_refs, b_refs = refs[:4], refs[4:8]
        sel_ref, d_ref = refs[8:10]
        outs = refs[10 : 10 + parts]
        lo, hi = refs[10 + parts :]
        e = pl.program_id(0)

        @pl.when(e == 0)
        def _():
            for r in range(4):
                lanes = pl.ds(pl.multiple_of(m[2 + r] * HD, HD), HD)
                lo[:, lanes] = a_refs[r][...]
                hi[:, lanes] = b_refs[r][...]

        x = pick(sel_ref[:, 0:1], sel_ref[:, 1:2], e.astype(F32), lo[...], hi[...])
        for s, value in enumerate(t_right(x, [d_ref[s] for s in pieces])):
            outs[s][0] = value.astype(BF16)

    def dwproj(meta):
        ins = [(v, None, None) for v in gm_a + gm_b]
        ins += [(sel, None, None), (dafter_low, None, None)]
        return run(
            dwproj_body, "dwproj", (experts,), meta, ins,
            [((experts, hw, ds), BF16, (1, hw, ds), lambda e, m: (e, 0, 0))] * parts,
            [pltpu.VMEM((rp, hw), BF16)] * 2,
            flops=2 * rp * experts * hw * parts * ds,
        )

    down_halves = down(after(meta, dkv))
    down_halves, dwout_sums = down_halves[:2], down_halves[2:]
    da_a, da_b, da_along = gather_groups(dq, dkv, late=(dwout_sums[0],))
    dwproj_sums = dwproj(after(meta, da_along, got_in))
    def place_heads(m, refs, lo, hi):
        for r in range(4):
            lanes = pl.ds(pl.multiple_of(m[2 + r] * HD, HD), HD)
            lo[:, lanes] = refs[r][:, :HD]
            hi[:, lanes] = refs[r][:, HD:]

    def dattn_body(m, *refs):
        a_refs, b_refs = refs[:4], refs[4:8]
        sel_ref = refs[8]
        q_refs = refs[9 : 9 + parts]
        kv_refs = refs[9 + parts : 9 + 2 * parts]
        outs = refs[9 + 2 * parts : 11 + 2 * parts]
        lo, hi, dk, dv = refs[11 + 2 * parts :]
        place_heads(m, a_refs, lo, hi)
        place_heads(m, b_refs, dk, dv)
        acc = nt_pieces(dk[...], [w[0] for w in kv_refs])
        for s, value in enumerate(nt_pieces(dv[...], [w[1] for w in kv_refs])):
            acc[s] += value
        for e in range(experts):
            x = pick(sel_ref[:, 0:1], sel_ref[:, 1:2], e, lo[...], hi[...])
            for s, value in enumerate(nt_pieces(x, [w[e] for w in q_refs])):
                acc[s] += value
        for s in pieces:
            store_halves(pl.program_id(0), outs, s, acc[s].astype(BF16))

    def dattn(meta):
        half = lambda i, m: (m[7 - i], 0)
        ins = [(v, (zr, 2 * HD), half) for v in da_a + da_b]
        ins += [(sel, (zr, 8), half)]
        ins += [(w, None, None) for w in wq + wkv]
        return run(
            dattn_body, "dattn", (2,), meta, ins, [((parts, zr, ds), BF16, None, None)] * 2,
            [pltpu.VMEM((zr, hw), BF16)] * 4,
            flops=4 * zr * (experts + 2) * hw * parts * ds,
        )

    dots_a = dots_q + jnp.where(third, dots_kv, 0.0)
    dots_a = after(dots_a, dwproj_sums[0])
    dots_a = (dots_a + by_group(dots_a, 1)) + (by_group(dots_a, 2) + by_group(dots_a, 3))
    got_out = exchange(dwout_sums)
    da_halves = dattn(after(meta, dwproj_sums[0]))
    got_proj = exchange(dwproj_sums)
    x_stack = jnp.stack(x_pieces)
    attn_input = (x_stack.astype(F32) * flat_a[0][None, :, None] * gain_a).astype(BF16)

    def dwqkv_body(m, *refs):
        a_refs, b_refs = refs[:4], refs[4:8]
        sel_ref, x_ref = refs[8:10]
        q_outs, kv_outs = refs[10 : 10 + parts], refs[10 + parts : 10 + 2 * parts]
        lo, hi, dk, dv = refs[10 + 2 * parts :]
        e = pl.program_id(0)
        xs = [x_ref.at[s] for s in pieces]

        @pl.when(e == 0)
        def _():
            place_heads(m, a_refs, lo, hi)
            place_heads(m, b_refs, dk, dv)

        @pl.when(e < experts)
        def _():
            x = pick(sel_ref[:, 0:1], sel_ref[:, 1:2], e.astype(F32), lo[...], hi[...])
            for s, value in enumerate(t_left([v[...] for v in xs], x)):
                q_outs[s][0] = value.astype(BF16)

        for k, grad in enumerate((dk, dv)):

            @pl.when(e == experts + k)
            def _():
                for s, value in enumerate(t_left([v[...] for v in xs], grad[...])):
                    kv_outs[s][0] = value.astype(BF16)

    def dwqkv(meta):
        q_spot = lambda e, m: (jnp.minimum(e, experts - 1), 0, 0)
        kv_spot = lambda e, m: (jnp.maximum(e - experts, 0), 0, 0)
        ins = [(v, None, None) for v in da_a + da_b]
        ins += [(sel, None, None), (attn_input, None, None)]
        outs = [((experts, ds, hw), BF16, (1, ds, hw), q_spot)] * parts
        outs += [((2, ds, hw), BF16, (1, ds, hw), kv_spot)] * parts
        return run(
            dwqkv_body, "dwqkv", (experts + 2,), meta, ins, outs,
            [pltpu.VMEM((rp, hw), BF16)] * 4,
            flops=2 * rp * (experts + 2) * hw * parts * ds,
        )

    dwqkv_sums = dwqkv(after(meta, da_halves[0], dots_a))


    da_half = z_covered(*da_halves, 1, dwqkv_sums[0])

    down_half = z_covered(*down_halves, 1, dwproj_sums[0])

    def finish_body(m, *refs):
        t_refs, after_ref, outs = refs[:2], refs[2], refs[3:]
        for k in range(4):
            span_k = at_row(m, BY_HALF + k, blk)
            for s in pieces:
                total = t_refs[k // 2][s, (k % 2) * blk : (k % 2 + 1) * blk, :]
                outs[s][span_k, :] = (
                    after_ref[s, span_k, :] + total.astype(F32)
                ).astype(BF16)

    got_q, got_kv = exchange(dwqkv_sums[:parts]), exchange(dwqkv_sums[parts:])
    down_totals = z_last(z_covered(down_half, down_half, 3, da_half))
    ins = [(t, None, None) for t in down_totals] + [(after_rows, None, None)]
    out_rows = run(
        finish_body, "finish", (1,), meta, ins,
        [((rp, ds), BF16, None, None)] * parts,
    )

    count = rows_all // dp

    def unpack_body(dealt, m, other_ref, *refs):
        v_refs, out_ref = refs[:parts], refs[-5]
        packed, other, total, whole = refs[-4:]
        for s in pieces:
            packed[part_rows(m, s), :] = v_refs[s][...].astype(F32)
        other[...] = other_ref[...].astype(F32)
        line = lax.broadcasted_iota(jnp.int32, (per, ds), 0)

        def one(j, carry):
            window, shift = near_rows(m, j)
            back = jnp.where(shift == 0, 0, seq_len + 8 - shift)
            whole[...] = pltpu.roll(packed[window, :], back, 0)
            for p in range(dp):
                if dealt:
                    spot = m[2 * seqs + j] * seq_len + p * per
                    kept = other[pl.ds(pl.multiple_of(spot, per), per), :]
                else:
                    kept = other[block_rows(p, j), :]
                value = whole[p * per : (p + 1) * per, :]
                total[block_rows(p, j), :] = jnp.where(line < m[seqs + j] - p * per, value, kept)
            return carry

        lax.fori_loop(0, seqs, one, 0)
        for p in range(dp):
            out_ref[p, :count, :] = total[p * count : (p + 1) * count, :].astype(BF16)
            for ref in refs[parts:-5]:
                out_ref[p, count:, :] = ref[...]

    def unpack(value, otherwise, dealt, table, extra=()):
        mine_all = [value[0]] + [by_part(value[s], s) for s in pieces[1:]]
        ins = [(v, None, None) for v in [otherwise] + mine_all + list(extra)]
        tall = count + sum(v.shape[0] for v in extra)
        spread_rows = run(
            functools.partial(unpack_body, dealt), "unpack", (1,), table, ins,
            [((dp, tall, ds), BF16, None, None)],
            [
                pltpu.VMEM((n, ds), F32)
                for n in (rows + seq_len + 8, rows_all, rows_all, seq_len + 8)
            ],
        )[0]
        return spread_rows

    def land(spread_rows):
        landed = lax.all_to_all(spread_rows, "dp", 0, 0, tiled=True)
        rows_of = landed[:, :count].transpose(1, 0, 2).reshape(seqs, per, width)
        return rows_of, landed[:, count:]

    da_half = z_covered(da_half, da_half, 3, out_rows[0])
    layer_rows = unpack(out_rows, x_all, False, table)
    dots_a = after(dots_a, out_rows[0])
    dots_a = (dots_a + by_z(dots_a, 1)) + (by_z(dots_a, 2) + by_z(dots_a, 3))
    back_a = back_columns(flat_a, dots_a, low_a, high_a)
    expertin_grad = fold(got_in, after(meta, da_half, layer_rows))
    da_totals = z_last(da_half)
    layer_out, _ = land(after(layer_rows, expertin_grad, da_totals[1]))
    ins = [(t, None, None) for t in da_totals]
    ins += [(x_stack, None, None), (dafter, None, None)]
    ins += [(gain_a, None, None), (router_a, None, None), (back_a, None, None)]
    outs = [((rp, ds), BF16, None, None)] * parts
    outs += [((experts + 1, parts, ds), F32, None, None)]
    *dinput, small_a = run(
        functools.partial(norm_back_body, False), "norm_back_first", (1,),
        after(meta, expertin_grad), ins, outs,
    )
    expertout_grad, proj_grad = add_up(got_out), add_up(got_proj)
    query_grad, kv_grad = add_up(got_q), add_up(got_kv)
    vectors = 2 * (experts + 1)
    small = jnp.concatenate([small_a, small_f], axis=0).reshape(vectors * parts, ds)
    small = jnp.pad(small, ((0, -vectors * parts % 16), (0, 0))).astype(BF16)
    input_grad, got = land(unpack(dinput, d_all, True, table, [small]))
    got = got[:, : vectors * parts].astype(F32).reshape(groups, parts, vectors, parts, ds)
    full = jnp.stack(
        [sum(got[:, k ^ s, :, s] for s in pieces) for k in range(parts)], axis=2
    )
    full = full.transpose(1, 0, 2, 3).reshape(2, experts + 1, width)
    attnrouter_grad, attngain_grad = full[0, :experts].T, full[0, experts]
    ffnrouter_grad, ffngain_grad = full[1, :experts].T, full[1, experts]
    return (
        layer_out,
        input_grad,
        attngain_grad,
        attnrouter_grad,
        kv_grad,
        query_grad,
        proj_grad,
        ffngain_grad,
        ffnrouter_grad,
        expertin_grad,
        expertout_grad,
    )


def solution(mesh):
    placed = (
        P(None, "dp", None),
        P("dp", None, None),
        P(),
        P(),
        P(),
        P(),
        P(),
        P(),
        P(None, "dp", "tensor"),
        P(None, "dp", "tensor"),
        P(None, "tensor", "dp"),
        P(),
        P(),
        P(None, "dp", None, "tensor"),
        P(None, "tensor", "dp"),
    )
    return jax.shard_map(
        functools.partial(local, dp=mesh.shape["dp"], tp=mesh.shape["tensor"]),
        mesh=mesh,
        in_specs=placed,
        out_specs=(
            P(None, "dp", None),
            P(None, "dp", None),
            P(),
            P(),
            P(None, "dp", "tensor"),
            P(None, "dp", "tensor"),
            P(None, "tensor", "dp"),
            P(),
            P(),
            P(None, "dp", None, "tensor"),
            P(None, "tensor", "dp"),
        ),
        check_vma=False,
    )
```
